32 devices in a mesh: frame: 8 (over z, x), batch: 4 (over y, core).
Axes of the slice: x: 2, y: 2, z: 4, core: 2. Of those that a mesh axis runs over, the one named last changes fastest.
Arguments:
- frames_in: bfloat16 [4, 32, 256, 512], P('batch', 'frame'), may hold values from -6 to 6
- spat_gain_a: float32 [512], replicated, may hold values from 0.5 to 1.5
- spat_qkv: bfloat16 [512, 1536], replicated, may hold values from -0.25 to 0.25
- spat_out: bfloat16 [512, 512], replicated, may hold values from -2 to 2
- spat_gain_b: float32 [512], replicated, may hold values from 0.5 to 1.5
- spat_up: bfloat16 [512, 2048], replicated, may hold values from -0.25 to 0.25
- spat_down: bfloat16 [2048, 512], replicated, may hold values from -0.125 to 0.125
- temp_gain_a: float32 [512], replicated, may hold values from 0.5 to 1.5
- temp_qkv: bfloat16 [512, 1536], replicated, may hold values from -0.25 to 0.25
- temp_out: bfloat16 [512, 512], replicated, may hold values from -0.375 to 0.375
- temp_gain_b: float32 [512], replicated, may hold values from 0.5 to 1.5
- temp_up: bfloat16 [512, 2048], replicated, may hold values from -0.25 to 0.25
- temp_down: bfloat16 [2048, 512], replicated, may hold values from -0.125 to 0.125
- quant_proj: bfloat16 [512, 32], replicated, may hold values from -0.25 to 0.25
- codebook: float32 [8192, 32], replicated, may hold values from -6 to 6
- code_index: int32 [4, 32, 256], P('batch', 'frame'), may hold values from 0 to 8191
- clip_index: int32 [4, 32], P('batch'), may hold values from 0 to 7, never falling along the last dimension, each value on 1 to 5 neighbouring positions
- dead_codes: int32 [64], replicated, may hold values from 0 to 8191, as said below
- source_rows: int32 [64], replicated, may hold values from 0 to 32767
- latent_cot: float32 [4, 32, 256, 32], P('batch', 'frame'), may hold values from -6 to 6
Outputs:
- latents: float32 [4, 32, 256, 32], P('batch', 'frame')
- commit_loss: float32 [], replicated
- frames_grad: bfloat16 [4, 32, 256, 512], P('batch', 'frame')
- spat_gain_a_grad: float32 [512], replicated
- spat_qkv_grad: float32 [512, 1536], P('frame')
- spat_out_grad: float32 [512, 512], P('frame')
- spat_gain_b_grad: float32 [512], replicated
- spat_up_grad: float32 [512, 2048], P('frame')
- spat_down_grad: float32 [2048, 512], P('frame')
- temp_gain_a_grad: float32 [512], replicated
- temp_qkv_grad: float32 [512, 1536], P('frame')
- temp_out_grad: float32 [512, 512], P('frame')
- temp_gain_b_grad: float32 [512], replicated
- temp_up_grad: float32 [512, 2048], P('frame')
- temp_down_grad: float32 [2048, 512], P('frame')
- quant_proj_grad: float32 [512, 32], P('frame')
- codebook_grad: float32 [8192, 32], P('frame')
- refreshed_codebook: float32 [8192, 32], replicated
The draws below stay inside these ranges and needn't reach their ends.
Inputs may be any that keep to these rules, and one draw needn't show every extreme that they name: `dead_codes`: distinct codes; half of them are used by at most one patch of all groups, the others by many. `clip_index`: each clip is 1 to 5 consecutive frames; clip numbers never fall.
All inputs are finite; a program needn't handle non-finite values.
Results may differ from the reference program's by a relative error of at most 0.017.
Values may be sent and summed in bfloat16 or wider, within the bound.
A program may use at most 256 MiB of HBM per device.

```python
import math
import jax
import jax.numpy as jnp
import numpy as np
from jax import lax

D = 512
HEADS = 8
FF = 2048
KCODES = 8192
CDIM = 32
P_SIZE = 256
RDEAD = 64
HD = 64
GROUPS = 4
FRAMES = 32
CLIPS = 8


def code_order(key):
    return (1 + jax.random.permutation(jax.random.fold_in(key, 11), KCODES - 2)).astype(jnp.int32)


def draw_dead_codes(key, part):
    return code_order(key)[:RDEAD].astype(jnp.int32)


def draw_code_index(key, part):
    order = code_order(key)
    half_dead = RDEAD // 2
    active = jnp.concatenate([order[half_dead:], jnp.array([0, KCODES - 1], jnp.int32)])
    active_count = KCODES - half_dead
    shape = (GROUPS, FRAMES, P_SIZE)
    subkeys = jax.random.split(jax.random.fold_in(key, 13), 5)
    ceiling = jax.random.randint(subkeys[0], shape, 1, active_count + 1)
    skewed = jax.random.randint(subkeys[1], shape, 0, ceiling)
    evenly = jax.random.randint(subkeys[2], shape, 0, active_count)
    coin_flip = jax.random.randint(subkeys[3], shape, 0, 2)
    ranks = jnp.where(coin_flip == 0, skewed, evenly)
    codes = jnp.take(active, ranks.reshape(-1), axis=0)
    single_spot = jax.random.randint(subkeys[4], (), 0, GROUPS * FRAMES * P_SIZE)
    codes = codes.at[single_spot].set(order[half_dead - 1])
    return codes.reshape(shape).astype(jnp.int32)


def touch_ends(drawn, stream_key, low, largest):
    spot = [jax.random.randint(jax.random.fold_in(stream_key, axis), (), 0, length) for axis, length in enumerate(drawn.shape)]
    widest = drawn.shape.index(max(drawn.shape))
    neighbour = spot[:widest] + [(spot[widest] + 1) % drawn.shape[widest]] + spot[widest + 1:]
    return drawn.at[tuple(spot)].set(low).at[tuple(neighbour)].set(largest)


def block_levels(own_key, dims, cuts, smallest, high):
    def one(dim, shards_of):
        draws = jax.random.uniform(jax.random.fold_in(jax.random.fold_in(own_key, 6), dim), (shards_of,), jnp.float32, smallest / len(cuts), high / len(cuts))
        return jnp.repeat(jnp.exp(draws), dims[dim] // shards_of).reshape((-1,) + (1,) * (len(dims) - dim - 1))

    loudness = one(*cuts[0])
    for cut in cuts[1:]:
        loudness = loudness * one(*cut)
    return loudness


def profile(count, total, most, slope):
    loads = [(1 << 20) // math.isqrt(grade ** slope) + 1 for grade in range(2, count + 1)]
    surplus, given = total - most - (count - 1), [1] * (count - 1)
    while surplus > 0:
        free = [i for i in range(count - 1) if given[i] < most]
        pool, budget = sum([loads[i] for i in free]), surplus
        for i in free:
            addition = min(most - given[i], max(1, budget * loads[i] // pool), surplus)
            given[i] = given[i] + addition
            surplus = surplus - addition
    return np.array([most] + given)


def ragged_sizes(stream_key, count, total, reach, skew):
    if count == 2:
        one = jax.random.randint(stream_key, (), max(1, total - reach), min(reach, total - 1) + 1)
        return jnp.stack([one, total - one])
    tallies = jnp.asarray(profile(count, total, reach, skew), jnp.int32)
    twos = (count - 1) // 2
    giver, taker = tallies[1:1 + 2 * twos:2], tallies[2:2 + 2 * twos:2]
    slack = jnp.minimum(giver - 1, reach - taker)
    shifted = jax.random.randint(jax.random.fold_in(stream_key, 1), (twos,), 0, 1 << 20) % (slack + 1)
    tallies = tallies.at[1:1 + 2 * twos:2].set(giver - shifted).at[2:2 + 2 * twos:2].set(taker + shifted)
    return tallies[jax.random.permutation(jax.random.fold_in(stream_key, 2), count)]


def normal_values(key, extent, width, limit, shards=(), held_as=jnp.bfloat16):
    values = jax.random.normal(key, extent, jnp.float32) * width
    if len(shards) > 0:
        values = block_levels(key, extent, shards, -0.22, 0.18) * values
    return jnp.clip(values, min=-limit, max=limit).astype(held_as)


def setup_inputs(seed: int = 0) -> dict:
    arg_keys = jax.random.split(jax.random.key(seed), 21)
    return {
        "frames_in": normal_values(arg_keys[0], (GROUPS, FRAMES, P_SIZE, D), 1.0, 6.0, ((0, 4), (1, 8))),
        "spat_gain_a": jnp.clip(1.0 + 0.1 * jax.random.normal(arg_keys[1], (D,), jnp.float32), 0.5, 1.5),
        "spat_qkv": normal_values(arg_keys[2], (D, 3 * D), D ** -0.5, 0.25),
        "spat_out": normal_values(arg_keys[3], (D, D), (max(D // 64, 1)) ** -0.5, 2.0),
        "spat_gain_b": jnp.clip(1.0 + 0.1 * jax.random.normal(arg_keys[4], (D,), jnp.float32), 0.5, 1.5),
        "spat_up": normal_values(arg_keys[5], (D, FF), D ** -0.5, 0.25),
        "spat_down": normal_values(arg_keys[6], (FF, D), FF ** -0.5, 0.125),
        "temp_gain_a": jnp.clip(1.0 + 0.1 * jax.random.normal(arg_keys[7], (D,), jnp.float32), 0.5, 1.5),
        "temp_qkv": normal_values(arg_keys[8], (D, 3 * D), D ** -0.5, 0.25),
        "temp_out": normal_values(arg_keys[9], (D, D), (max(D // 2, 1)) ** -0.5, 0.375),
        "temp_gain_b": jnp.clip(1.0 + 0.1 * jax.random.normal(arg_keys[10], (D,), jnp.float32), 0.5, 1.5),
        "temp_up": normal_values(arg_keys[11], (D, FF), D ** -0.5, 0.25),
        "temp_down": normal_values(arg_keys[12], (FF, D), FF ** -0.5, 0.125),
        "quant_proj": normal_values(arg_keys[13], (D, CDIM), D ** -0.5, 0.25),
        "codebook": normal_values(arg_keys[14], (KCODES, CDIM), 1.0, 6.0, (), jnp.float32),
        "code_index": draw_code_index(jax.random.fold_in(arg_keys[20], 71), 0),
        "clip_index": jax.vmap(lambda own: jnp.searchsorted(jnp.cumsum(ragged_sizes(own, CLIPS, FRAMES, 5, 0)), jnp.arange(FRAMES), side="right"))(jax.random.split(arg_keys[16], GROUPS)).reshape((GROUPS, FRAMES)).astype(jnp.int32),
        "dead_codes": draw_dead_codes(jax.random.fold_in(arg_keys[20], 71), 0),
        "source_rows": touch_ends(jax.random.randint(arg_keys[18], (RDEAD,), 0, GROUPS * FRAMES * P_SIZE), jax.random.fold_in(arg_keys[18], 1), 0, (GROUPS * FRAMES * P_SIZE) - 1).astype(jnp.int32),
        "latent_cot": normal_values(arg_keys[19], (GROUPS, FRAMES, P_SIZE, CDIM), 1.0, 6.0, ((0, 4), (1, 8)), jnp.float32),
    }


@jax.custom_vjp
def low(v):
    return lax.optimization_barrier(v.astype(jnp.bfloat16)).astype(jnp.float32)

@jax.custom_vjp
def low_back(v):
    return v

def low_keep(v):
    return (low(v), None)

def low_pass(kept, grad):
    return (grad,)

def back_keep(v):
    return (v, None)

def back_low(kept, grad):
    return (low(grad),)
low.defvjp(low_keep, low_pass)
low_back.defvjp(back_keep, back_low)
EPS = 1e-05
BETA = 0.25
USE_MIN = 2.0
NEG = -1e+30
HIGH = lax.Precision.HIGHEST
prior_span = 4

def normalize(values, gain_vec):
    row_mean = lax.optimization_barrier(jnp.mean(values, -1, keepdims=True))
    centred = values - row_mean
    spread = lax.optimization_barrier(jnp.mean(centred * centred, -1, keepdims=True))
    return centred * lax.rsqrt(spread + EPS) * gain_vec

def matmul_high(left, right):
    return jnp.matmul(left, right, precision=HIGH)

def attend_one(packed):
    seq_len = packed.shape[0]
    pieces = packed.reshape(seq_len, 3, HEADS, HD)
    queries = pieces[:, 0]
    key_rows = pieces[:, 1]
    values = pieces[:, 2]
    scores = jnp.einsum('qhd,khd->hqk', queries, key_rows, precision=HIGH) * HD ** (-0.5)
    scores = low_back(scores)
    attn_probs = low(jax.nn.softmax(scores, axis=-1))
    attended = jnp.einsum('hqk,khd->qhd', attn_probs, values, precision=HIGH)
    return attended.reshape(seq_len, HEADS * HD)

def spatial_mix(packed, clip_index):
    frame_rows = packed.reshape(-1, P_SIZE, 3 * D)
    attended = lax.map(jax.checkpoint(attend_one), frame_rows)
    return attended.reshape(packed.shape[:-1] + (D,))

def temporal_group(pair_args):
    packed_group, clip_group = pair_args
    pieces = packed_group.reshape(FRAMES, P_SIZE, 3, HEADS, HD)
    queries = pieces[:, :, 0]
    zeros_before = jnp.zeros((prior_span, P_SIZE, HEADS, HD), jnp.float32)
    keys_all = jnp.concatenate([zeros_before, pieces[:, :, 1]], 0)
    values_all = jnp.concatenate([zeros_before, pieces[:, :, 2]], 0)
    clips_all = jnp.concatenate([jnp.full((prior_span,), -1, jnp.int32), clip_group.astype(jnp.int32)])
    key_stack = jnp.stack([keys_all[prior_span - offset:prior_span - offset + FRAMES] for offset in range(prior_span + 1)])
    value_stack = jnp.stack([values_all[prior_span - offset:prior_span - offset + FRAMES] for offset in range(prior_span + 1)])
    allowed = jnp.stack([clips_all[prior_span - offset:prior_span - offset + FRAMES] == clips_all[prior_span:] for offset in range(prior_span + 1)])[:, :, None, None]
    scores = jnp.einsum('fphd,ofphd->ofph', queries, key_stack, precision=HIGH) * HD ** (-0.5)
    scores = low_back(scores)
    scores = jnp.where(allowed, scores, NEG)
    attn_probs = low(jax.nn.softmax(scores, axis=0))
    attended = jnp.einsum('ofph,ofphd->fphd', attn_probs, value_stack, precision=HIGH)
    return attended.reshape(FRAMES, P_SIZE, D)

def temporal_mix(packed, clip_index):
    return lax.map(jax.checkpoint(temporal_group), (packed, clip_index))

def block(stream, weights, mix, clip_index):
    gain_a, w_qkv, w_out, gain_b, w_up, w_down = weights
    input_a = low(normalize(stream, gain_a))
    packed = low(low_back(matmul_high(input_a, w_qkv)))
    attended = low(low_back(mix(packed, clip_index)))
    middle = stream + low_back(matmul_high(attended, w_out))
    input_b = low(normalize(middle, gain_b))
    upward = low_back(matmul_high(input_b, w_up))
    hidden = low(jax.nn.gelu(upward, approximate=True))
    return middle + low_back(matmul_high(hidden, w_down))

def reference(frames_in, spat_gain_a, spat_qkv, spat_out, spat_gain_b, spat_up, spat_down, temp_gain_a, temp_qkv, temp_out, temp_gain_b, temp_up, temp_down, quant_proj, codebook, code_index, clip_index, dead_codes, source_rows, latent_cot):
    spat_weights = (spat_gain_a, spat_qkv.astype(jnp.float32), spat_out.astype(jnp.float32), spat_gain_b, spat_up.astype(jnp.float32), spat_down.astype(jnp.float32))
    temp_weights = (temp_gain_a, temp_qkv.astype(jnp.float32), temp_out.astype(jnp.float32), temp_gain_b, temp_up.astype(jnp.float32), temp_down.astype(jnp.float32))

    def forward(frames, spat_set, temp_set, projection, book):
        after_spatial = low(low_back(block(frames, spat_set, spatial_mix, clip_index)))
        after_temporal = low(low_back(block(after_spatial, temp_set, temporal_mix, clip_index)))
        latent = low_back(matmul_high(after_temporal, projection))
        chosen = jnp.take(book, code_index, axis=0)
        differ = latent - chosen
        return (latent, jnp.sum(differ * differ))
    (latent, commit), pullback = jax.vjp(forward, frames_in.astype(jnp.float32), spat_weights, temp_weights, quant_proj.astype(jnp.float32), codebook)
    grad_frames, grad_spat, grad_temp, grad_proj, grad_book = pullback((latent_cot, jnp.float32(BETA)))
    commit_loss = commit / (GROUPS * FRAMES * P_SIZE * CDIM)
    codes_flat = code_index.reshape(-1)
    usage_count = lax.optimization_barrier(jnp.sum((codes_flat[:, None] == dead_codes[None, :]).astype(jnp.float32), 0))
    candidate = jnp.take(latent.reshape(-1, CDIM), source_rows, axis=0)
    old_rows = jnp.take(codebook, dead_codes, axis=0)
    fresh_rows = jnp.where((usage_count < USE_MIN)[:, None], candidate, old_rows)
    refreshed = codebook.at[dead_codes].set(fresh_rows)
    return (latent, commit_loss, grad_frames.astype(jnp.bfloat16), grad_spat[0], grad_spat[1], grad_spat[2], grad_spat[3], grad_spat[4], grad_spat[5], grad_temp[0], grad_temp[1], grad_temp[2], grad_temp[3], grad_temp[4], grad_temp[5], grad_proj, grad_book, refreshed)
```

```python
import jax
import jax.numpy as jnp
from jax import lax
from jax.experimental import pallas as pl
from jax.experimental.pallas import tpu as pltpu
from jax.sharding import PartitionSpec as P

HEADS = 8
EPS = 1e-05
BETA = 0.25
USE_MIN = 2.0
NEG = -1e30
HIGH = lax.Precision.HIGHEST
SPAN = 4
F32 = jnp.float32
BF16 = jnp.bfloat16
GELU_C = 0.7978845608028654
GELU_A = 0.044715
VMEM_BYTES = 56 * 1024 * 1024
SUB = 32
GROUP = 64


def mm(a, b):
    return jnp.dot(a, b, preferred_element_type=F32)


def mm_t(a, b):
    return lax.dot_general(a, b, (((1,), (1,)), ((), ())), preferred_element_type=F32)


def t_mm(a, b):
    return lax.dot_general(a, b, (((0,), (0,)), ((), ())), preferred_element_type=F32)


def norm(x):
    c = x - jnp.mean(x, -1, keepdims=True)
    r = lax.rsqrt(jnp.mean(c * c, -1, keepdims=True) + EPS)
    return c * r, r


def norm_back(dy, xhat, r, gain):
    d = dy * gain
    return r * (d - jnp.mean(d, -1, keepdims=True) - xhat * jnp.mean(d * xhat, -1, keepdims=True))


def add_row(ref, rows):
    ref[...] += jnp.sum(rows, 0, keepdims=True)


def head_masks(rows, width):
    lane = lax.broadcasted_iota(jnp.int32, (rows, width), 1)
    return (lane < width // 2, lane >= width // 2)


def attend_pair(q, k, v, bias):
    width = q.shape[1]
    scale = (width // 2) ** -0.5
    zero = jnp.zeros((), BF16)
    qs = q * jnp.asarray(scale, BF16)
    v_ext = jnp.concatenate([v, jnp.ones_like(v)], axis=1)
    masks = head_masks(q.shape[0], width)
    halves = []
    for mask in masks:
        s = mm_t(jnp.where(mask, qs, zero), k)
        if bias is not None:
            s = s + bias
        e = jnp.exp(s - jnp.max(s, -1, keepdims=True)).astype(BF16)
        r = mm(e, v_ext)
        halves.append(r[:, :width] / r[:, width:])
    return jnp.where(masks[0], halves[0], halves[1]).astype(BF16)


def attend_pair_back(q, k, v, do, bias_t):
    width = q.shape[1]
    scale = jnp.asarray((width // 2) ** -0.5, BF16)
    zero = jnp.zeros((), BF16)
    qs = q * scale
    ks = k * scale
    q_masks = head_masks(q.shape[0], width)
    k_masks = head_masks(k.shape[0], width)
    dq = dk = dv = None
    for q_mask, k_mask in zip(q_masks, k_masks):
        qm = jnp.where(q_mask, qs, zero)
        dom = jnp.where(q_mask, do, zero)
        st = mm_t(k, qm)
        if bias_t is not None:
            st = st + bias_t
        e = jnp.exp(st - jnp.max(st, 0, keepdims=True))
        p = e * (1.0 / jnp.sum(e, 0, keepdims=True))
        dp = mm_t(v, dom)
        inner = jnp.sum(p * dp, 0, keepdims=True)
        ds = (p * (dp - inner)).astype(BF16)
        dv_one = mm(p.astype(BF16), dom)
        dk_one = mm(ds, qm)
        dq_one = t_mm(ds, jnp.where(k_mask, ks, zero))
        dq = dq_one if dq is None else dq + dq_one
        dk = dk_one if dk is None else dk + dk_one
        dv = dv_one if dv is None else dv + dv_one
    return dq, dk, dv


def mlp_forward(mid, gain, w_up, w_down, bt_ref, h_ref, gp_ref, tile=512):
    xhat, _ = norm(mid)
    b = (xhat * gain).astype(BF16)
    bt_ref[...] = b.T
    out = mid
    for start in range(0, w_up.shape[1], tile):
        cols = slice(start, start + tile)
        u = mm(b, w_up[:, cols])
        u2 = u * u
        th = jnp.tanh(u * (GELU_C + (GELU_C * GELU_A) * u2))
        half = 0.5 + 0.5 * th
        h = (u * half).astype(BF16)
        slope = half + u * (half * (1.0 - th)) * (GELU_C + (3.0 * GELU_C * GELU_A) * u2)
        h_ref[:, cols] = h
        gp_ref[:, cols] = slope.astype(BF16)
        out = out + mm(h, w_down[cols, :])
    return out


def mlp_backward(dy, dy_low, mid, gain, w_up, w_down, gp_ref, du_ref, dgain_ref, tile=512):
    db = None
    for start in range(0, w_up.shape[1], tile):
        cols = slice(start, start + tile)
        dh = mm_t(dy_low, w_down[cols, :])
        du = (gp_ref[:, cols].astype(F32) * dh).astype(BF16)
        du_ref[:, cols] = du
        one = mm_t(du, w_up[:, cols])
        db = one if db is None else db + one
    xhat, r = norm(mid)
    add_row(dgain_ref, db * xhat)
    return dy + norm_back(db, xhat, r, gain)


def spat_fwd_kernel(
    x_ref, ga, w_qkv, w_out, gb, w_up, w_down,
    y_ref, at_ref, pk_ref, att_t_ref, mid_ref, bt_ref, h_ref, gp_ref, att_ref,
):
    feature = x_ref.shape[-1]
    x = x_ref[0].astype(F32)
    xhat, _ = norm(x)
    a = (xhat * ga[...]).astype(BF16)
    at_ref[...] = a.T
    for start in range(0, 3 * feature, 512):
        pk_ref[:, start : start + 512] = mm(a, w_qkv[:, start : start + 512]).astype(BF16)
    for lane in range(0, feature, 128):
        att_ref[:, lane : lane + 128] = attend_pair(
            pk_ref[:, lane : lane + 128],
            pk_ref[:, feature + lane : feature + lane + 128],
            pk_ref[:, 2 * feature + lane : 2 * feature + lane + 128],
            None,
        )
    att = att_ref[...]
    att_t_ref[...] = att.T
    mid = x + mm(att, w_out[...])
    mid_ref[...] = mid
    y_ref[0] = mlp_forward(mid, gb[...], w_up, w_down, bt_ref, h_ref, gp_ref).astype(BF16)


def temp_fwd_kernel(
    x_ref, halo_ref, bias_ref, ga, w_qkv, w_out, gb, w_up, w_down, proj,
    lat_ref, x3_ref, at_ref, aht_ref, pk_ref, kvh_ref, att_t_ref, mid_ref, bt_ref, h_ref, gp_ref, att_ref,
):
    frames, group, feature = x_ref.shape
    rows = frames * group
    x = x_ref[...].reshape(rows, feature).astype(F32)
    xhat, _ = norm(x)
    a = (xhat * ga[...]).astype(BF16)
    at_ref[...] = a.T
    for start in range(0, 3 * feature, 512):
        pk_ref[:, :, start : start + 512] = (
            mm(a, w_qkv[:, start : start + 512]).astype(BF16).reshape(frames, group, 512)
        )
    xhat_h, _ = norm(halo_ref[...].reshape(rows, feature).astype(F32))
    ah = (xhat_h * ga[...]).astype(BF16)
    aht_ref[...] = ah.T
    for start in range(0, 2 * feature, 512):
        kvh_ref[:, :, start : start + 512] = (
            mm(ah, w_qkv[:, feature + start : feature + start + 512])
            .astype(BF16)
            .reshape(frames, group, 512)
        )
    bias = bias_ref[...]
    for sub in range(0, group, SUB):
        here = slice(sub, sub + SUB)
        for lane in range(0, feature, 128):
            q = pk_ref[:, here, lane : lane + 128].reshape(frames * SUB, 128)
            k = jnp.concatenate(
                [kvh_ref[:, here, lane : lane + 128],
                 pk_ref[:, here, feature + lane : feature + lane + 128]], 0
            ).reshape(2 * frames * SUB, 128)
            v = jnp.concatenate(
                [kvh_ref[:, here, feature + lane : feature + lane + 128],
                 pk_ref[:, here, 2 * feature + lane : 2 * feature + lane + 128]], 0
            ).reshape(2 * frames * SUB, 128)
            att_ref[:, here, lane : lane + 128] = attend_pair(q, k, v, bias).reshape(frames, SUB, 128)
    att = att_ref[...].reshape(rows, feature)
    att_t_ref[...] = att.T
    mid = x + mm(att, w_out[...])
    mid_ref[...] = mid
    y = mlp_forward(mid, gb[...], w_up, w_down, bt_ref, h_ref, gp_ref).astype(BF16)
    x3_ref[...] = y
    lat_ref[...] = mm(y, proj[...]).reshape(frames, group, proj.shape[1])


def temp_bwd_kernel(
    gl_ref, proj, x3_ref, x_ref, mid_ref, gp_ref, pk_ref, kvh_ref, bias_ref,
    ga, w_qkv, w_out, gb, w_up, w_down,
    dyt_ref, du_ref, dmid_ref, dpk_ref, dkvh_ref, base_ref, dah_ref, dga_ref, dgb_ref, dproj_ref,
    datt_ref,
):
    frames, group, feature = x_ref.shape
    rows = frames * group

    @pl.when(pl.program_id(0) == 0)
    def _():
        for ref in (dga_ref, dgb_ref, dproj_ref):
            ref[...] = jnp.zeros_like(ref)

    gl = gl_ref[...].reshape(rows, gl_ref.shape[2])
    dproj_ref[...] += t_mm(gl, x3_ref[...])
    dy_low = mm_t(gl, proj[...]).astype(BF16)
    dyt_ref[...] = dy_low.T
    dmid = mlp_backward(
        dy_low.astype(F32), dy_low, mid_ref[...], gb[...], w_up, w_down, gp_ref, du_ref, dgb_ref
    )
    dmid_low = dmid.astype(BF16)
    dmid_ref[...] = dmid_low
    datt_ref[...] = mm_t(dmid_low, w_out[...]).astype(BF16).reshape(frames, group, feature)
    bias = bias_ref[...]
    half = frames * SUB
    for sub in range(0, group, SUB):
        here = slice(sub, sub + SUB)
        for lane in range(0, feature, 128):
            l0 = slice(lane, lane + 128)
            l1 = slice(feature + lane, feature + lane + 128)
            l2 = slice(2 * feature + lane, 2 * feature + lane + 128)
            q = pk_ref[:, here, l0].reshape(half, 128)
            k = jnp.concatenate([kvh_ref[:, here, l0], pk_ref[:, here, l1]], 0).reshape(2 * half, 128)
            v = jnp.concatenate([kvh_ref[:, here, l1], pk_ref[:, here, l2]], 0).reshape(2 * half, 128)
            do = datt_ref[:, here, l0].reshape(half, 128)
            dq, dk, dv = attend_pair_back(q, k, v, do, bias)
            dk, dv = dk.astype(BF16), dv.astype(BF16)
            dpk_ref[:, here, l0] = dq.astype(BF16).reshape(frames, SUB, 128)
            dpk_ref[:, here, l1] = dk[half:].reshape(frames, SUB, 128)
            dpk_ref[:, here, l2] = dv[half:].reshape(frames, SUB, 128)
            dkvh_ref[:, here, l0] = dk[:half].reshape(frames, SUB, 128)
            dkvh_ref[:, here, l1] = dv[:half].reshape(frames, SUB, 128)
    da = mm_t(dpk_ref[...].reshape(rows, 3 * feature), w_qkv[...])
    dah = mm_t(dkvh_ref[...].reshape(rows, 2 * feature), w_qkv[:, feature:])
    dah_ref[...] = dah.astype(BF16).reshape(frames, group, feature)
    xhat, r = norm(x_ref[...].reshape(rows, feature).astype(F32))
    add_row(dga_ref, da * xhat)
    base_ref[...] = (dmid + norm_back(da, xhat, r, ga[...])).reshape(frames, group, feature)


def spat_bwd_kernel(
    base_ref, dah_ref, x2_ref, gta, x_ref, mid_ref, gp_ref, pk_ref,
    ga, w_qkv, w_out, gb, w_up, w_down,
    dx_ref, dyt_ref, du_ref, dmid_ref, dpk_ref, dgt_ref, dga_ref, dgb_ref,
    datt_ref,
):
    feature = x_ref.shape[-1]

    @pl.when(pl.program_id(0) == 0)
    def _():
        for ref in (dgt_ref, dga_ref, dgb_ref):
            ref[...] = jnp.zeros_like(ref)

    xhat2, r2 = norm(x2_ref[0].astype(F32))
    dah = dah_ref[0].astype(F32)
    add_row(dgt_ref, dah * xhat2)
    dy_low = (base_ref[0] + norm_back(dah, xhat2, r2, gta[...])).astype(BF16)
    dyt_ref[...] = dy_low.T
    dmid = mlp_backward(
        dy_low.astype(F32), dy_low, mid_ref[...], gb[...], w_up, w_down, gp_ref, du_ref, dgb_ref
    )
    dmid_low = dmid.astype(BF16)
    dmid_ref[...] = dmid_low
    datt_ref[...] = mm_t(dmid_low, w_out[...]).astype(BF16)
    for lane in range(0, feature, 128):
        l0 = slice(lane, lane + 128)
        l1 = slice(feature + lane, feature + lane + 128)
        l2 = slice(2 * feature + lane, 2 * feature + lane + 128)
        dq, dk, dv = attend_pair_back(pk_ref[:, l0], pk_ref[:, l1], pk_ref[:, l2], datt_ref[:, l0], None)
        dpk_ref[:, l0] = dq.astype(BF16)
        dpk_ref[:, l1] = dk.astype(BF16)
        dpk_ref[:, l2] = dv.astype(BF16)
    da = mm_t(dpk_ref[...], w_qkv[...])
    xhat, r = norm(x_ref[0].astype(F32))
    add_row(dga_ref, da * xhat)
    dx_ref[0] = (dmid + norm_back(da, xhat, r, ga[...])).astype(BF16)


def mlp_grad_kernel(bt_ref, du_ref, dyt_ref, h_ref, up_ref, down_ref):
    up_ref[0] = mm(bt_ref[...], du_ref[...]).astype(BF16)
    width = down_ref.shape[2]
    for j in range(down_ref.shape[0]):
        down_ref[j] = mm(dyt_ref[...], h_ref[:, j * width : (j + 1) * width]).astype(BF16)


def att_grad_kernel(halo, *refs):
    if halo:
        at_ref, att_t_ref, dq_ref, dk_ref, dv_ref, dm_ref, aht_ref, dkh_ref, dvh_ref, out_ref = refs
    else:
        at_ref, att_t_ref, dq_ref, dk_ref, dv_ref, dm_ref, out_ref = refs
    dq = mm(at_ref[...], dq_ref[...])
    dk = mm(at_ref[...], dk_ref[...])
    dv = mm(at_ref[...], dv_ref[...])
    if halo:
        dk = dk + mm(aht_ref[...], dkh_ref[...])
        dv = dv + mm(aht_ref[...], dvh_ref[...])
    do = mm(att_t_ref[...], dm_ref[...])
    for i, part in enumerate((dq, dk, dv, do)):
        part = part.astype(BF16)
        for j in range(2):
            out_ref[j, :, 128 * i : 128 * (i + 1)] = part[:, 128 * j : 128 * (j + 1)]


def whole(shape):
    zeros = (0,) * len(shape)
    return pl.BlockSpec(shape, lambda i: zeros)


def col_block(rows, width, offset=0):
    return pl.BlockSpec((rows, width), lambda i: (0, i + offset))


def row_block(rows, width):
    return pl.BlockSpec((rows, width), lambda i: (i, 0))


def shape_of(shape, dtype):
    return jax.ShapeDtypeStruct(shape, dtype)


def params():
    return pltpu.CompilerParams(vmem_limit_bytes=VMEM_BYTES, dimension_semantics=("arbitrary",))


def cost(flops, nbytes):
    return pl.CostEstimate(flops=int(flops), bytes_accessed=int(nbytes), transcendentals=0)


def weight_specs(feature, hidden):
    return [
        whole((1, feature)), whole((feature, 3 * feature)), whole((feature, feature)),
        whole((1, feature)), whole((feature, hidden)), whole((hidden, feature)),
    ]


def spat_forward(x, weights):
    frames, patches, d = x.shape
    hidden = weights[4].shape[1]
    n = frames * patches
    blk = pl.BlockSpec((1, patches, d), lambda i: (i, 0, 0))
    return pl.pallas_call(
        spat_fwd_kernel,
        grid=(frames,),
        in_specs=[blk] + weight_specs(d, hidden),
        out_specs=[
            blk, col_block(d, patches), row_block(patches, 3 * d), col_block(d, patches),
            row_block(patches, d), col_block(d, patches), row_block(patches, hidden), row_block(patches, hidden),
        ],
        out_shape=[
            shape_of(x.shape, BF16), shape_of((d, n), BF16), shape_of((n, 3 * d), BF16), shape_of((d, n), BF16),
            shape_of((n, d), F32), shape_of((d, n), BF16), shape_of((n, hidden), BF16), shape_of((n, hidden), BF16),
        ],
        scratch_shapes=[pltpu.VMEM((patches, d), BF16)],
        compiler_params=params(),
        cost_estimate=cost(2 * n * d * (4 * d + 2 * hidden + 2 * patches), 24 * n * d),
        name="spat_forward",
    )(x, *weights)


def temp_forward(x, halo, bias, weights, proj):
    frames, patches, d = x.shape
    hidden = weights[4].shape[1]
    n = frames * patches
    steps = patches // GROUP
    rows = frames * GROUP
    cdim = proj.shape[1]
    blk = pl.BlockSpec((frames, GROUP, d), lambda i: (0, i, 0))
    stacked = lambda width: pl.BlockSpec((frames, GROUP, width), lambda i: (i, 0, 0))
    return pl.pallas_call(
        temp_fwd_kernel,
        grid=(steps,),
        in_specs=[blk, blk, whole(bias.shape)] + weight_specs(d, hidden) + [whole(proj.shape)],
        out_specs=[
            pl.BlockSpec((frames, GROUP, cdim), lambda i: (0, i, 0)), row_block(rows, d),
            col_block(d, rows), col_block(d, rows), stacked(3 * d), stacked(2 * d), col_block(d, rows),
            row_block(rows, d), col_block(d, rows), row_block(rows, hidden), row_block(rows, hidden),
        ],
        out_shape=[
            shape_of((frames, patches, cdim), F32), shape_of((n, d), BF16),
            shape_of((d, n), BF16), shape_of((d, n), BF16),
            shape_of((frames * steps, GROUP, 3 * d), BF16), shape_of((frames * steps, GROUP, 2 * d), BF16),
            shape_of((d, n), BF16), shape_of((n, d), F32), shape_of((d, n), BF16),
            shape_of((n, hidden), BF16), shape_of((n, hidden), BF16),
        ],
        scratch_shapes=[pltpu.VMEM((frames, GROUP, d), BF16)],
        compiler_params=params(),
        cost_estimate=cost(2 * n * d * (6 * d + 2 * hidden + 2 * patches), 30 * n * d),
        name="temp_forward",
    )(x, halo, bias, *weights, proj)


def temp_backward(gl, proj, x3, x, mid, gp, pk, kvh, bias_t, weights):
    frames, patches, d = x.shape
    hidden = weights[4].shape[1]
    n = frames * patches
    steps = patches // GROUP
    rows = frames * GROUP
    cdim = proj.shape[1]
    nat = lambda width: pl.BlockSpec((frames, GROUP, width), lambda i: (0, i, 0))
    stacked = lambda width: pl.BlockSpec((frames, GROUP, width), lambda i: (i, 0, 0))
    return pl.pallas_call(
        temp_bwd_kernel,
        grid=(steps,),
        in_specs=[
            nat(cdim), whole(proj.shape), row_block(rows, d), nat(d), row_block(rows, d),
            row_block(rows, hidden), stacked(3 * d), stacked(2 * d), whole(bias_t.shape),
        ] + weight_specs(d, hidden),
        out_specs=[
            col_block(d, rows), row_block(rows, hidden), row_block(rows, d), stacked(3 * d), stacked(2 * d),
            nat(d), nat(d), whole((1, d)), whole((1, d)), whole((cdim, d)),
        ],
        out_shape=[
            shape_of((d, n), BF16), shape_of((n, hidden), BF16), shape_of((n, d), BF16),
            shape_of((frames * steps, GROUP, 3 * d), BF16), shape_of((frames * steps, GROUP, 2 * d), BF16),
            shape_of((frames, patches, d), F32), shape_of((frames, patches, d), BF16),
            shape_of((1, d), F32), shape_of((1, d), F32), shape_of((cdim, d), F32),
        ],
        scratch_shapes=[pltpu.VMEM((frames, GROUP, d), BF16)],
        compiler_params=params(),
        cost_estimate=cost(2 * n * d * (6 * d + 2 * hidden + 5 * patches), 40 * n * d),
        name="temp_backward",
    )(gl, proj, x3, x, mid, gp, pk, kvh, bias_t, *weights)


def spat_backward(base, dah, x2, gta, x, mid, gp, pk, weights):
    frames, patches, d = x.shape
    hidden = weights[4].shape[1]
    n = frames * patches
    blk = pl.BlockSpec((1, patches, d), lambda i: (i, 0, 0))
    return pl.pallas_call(
        spat_bwd_kernel,
        grid=(frames,),
        in_specs=[
            blk, blk, blk, whole((1, d)), blk, row_block(patches, d), row_block(patches, hidden),
            row_block(patches, 3 * d),
        ] + weight_specs(d, hidden),
        out_specs=[
            blk, col_block(d, patches), row_block(patches, hidden), row_block(patches, d),
            row_block(patches, 3 * d), whole((1, d)), whole((1, d)), whole((1, d)),
        ],
        out_shape=[
            shape_of(x.shape, BF16), shape_of((d, n), BF16), shape_of((n, hidden), BF16), shape_of((n, d), BF16),
            shape_of((n, 3 * d), BF16), shape_of((1, d), F32), shape_of((1, d), F32), shape_of((1, d), F32),
        ],
        scratch_shapes=[pltpu.VMEM((patches, d), BF16)],
        compiler_params=params(),
        cost_estimate=cost(2 * n * d * (4 * d + 2 * hidden + 5 * patches), 30 * n * d),
        name="spat_backward",
    )(base, dah, x2, gta, x, mid, gp, pk, *weights)


def mlp_grads(bt, du, dyt, h):
    d, n = bt.shape
    hidden = du.shape[1]
    steps = 4
    wide = hidden // steps
    return pl.pallas_call(
        mlp_grad_kernel,
        grid=(steps,),
        in_specs=[whole((d, n)), col_block(n, wide), whole((d, n)), col_block(n, wide)],
        out_specs=[
            pl.BlockSpec((1, d, wide), lambda i: (i, 0, 0)),
            pl.BlockSpec((2, d, wide // 2), lambda i: (i, 0, 0)),
        ],
        out_shape=[shape_of((steps, d, wide), BF16), shape_of((2 * steps, d, wide // 2), BF16)],
        compiler_params=params(),
        cost_estimate=cost(4 * n * d * hidden, 8 * n * d + 4 * n * hidden),
        name="mlp_grads",
    )(bt, du, dyt, h)


def att_grads(at, att_t, dpk, dmid, aht=None, dkvh=None):
    d, n = at.shape
    halo = aht is not None
    wide = 256
    args = [at, att_t, dpk, dpk, dpk, dmid]
    specs = [
        whole((d, n)), whole((d, n)), col_block(n, wide), col_block(n, wide, d // wide),
        col_block(n, wide, 2 * d // wide), col_block(n, wide),
    ]
    if halo:
        args += [aht, dkvh, dkvh]
        specs += [whole((d, n)), col_block(n, wide), col_block(n, wide, d // wide)]
    return pl.pallas_call(
        lambda *refs: att_grad_kernel(halo, *refs),
        grid=(d // wide,),
        in_specs=specs,
        out_specs=pl.BlockSpec((2, d, 512), lambda i: (i, 0, 0)),
        out_shape=shape_of((d // 128, d, 512), BF16),
        compiler_params=params(),
        cost_estimate=cost(2 * n * d * d * (6 if halo else 4), 16 * n * d),
        name="att_grads",
    )(*args)


def bits_of(count):
    bits = count.bit_length() - 1
    assert count == 1 << bits
    return bits


def swap(value, axis, bit):
    count = lax.axis_size(axis)
    return lax.ppermute(value, axis, [(i, i ^ (1 << bit)) for i in range(count)])


def my_bit(axis, bit):
    return (lax.axis_index(axis) >> bit) & 1


def reduce_pieces(grad, labels, order):
    names = []
    for axis in labels:
        names += [(axis, b) for b in reversed(range(bits_of(lax.axis_size(axis))))]
    tail = grad.shape[len(labels) :]
    cur = grad.reshape((2,) * len(names) + tail)
    for axis, bit in order:
        at = names.index((axis, bit))
        me = my_bit(axis, bit)
        kept = lax.dynamic_index_in_dim(cur, me, at, keepdims=False)
        sent = lax.dynamic_index_in_dim(cur, 1 - me, at, keepdims=False)
        cur = (kept.astype(F32) + swap(sent, axis, bit).astype(F32)).astype(BF16)
        names.pop(at)
    cur = cur[None]
    for bit in reversed(range(bits_of(lax.axis_size("batch")))):
        other = swap(cur, "batch", bit)
        low = my_bit("batch", bit) == 0
        cur = jnp.stack([jnp.where(low, cur, other), jnp.where(low, other, cur)], 1)
        cur = cur.reshape((-1,) + tail)
    return cur.astype(F32)


def orders():
    fb, bb = bits_of(lax.axis_size("frame")), bits_of(lax.axis_size("batch"))
    frame = [("frame", b) for b in [0] + list(reversed(range(1, fb)))]
    batch = [("batch", b) for b in range(bb)]
    return batch + frame, batch[:1] + frame[:1] + batch[1:] + frame[1:]


def local(
    frames_in, spat_gain_a, spat_qkv, spat_out, spat_gain_b, spat_up, spat_down,
    temp_gain_a, temp_qkv, temp_out, temp_gain_b, temp_up, temp_down,
    quant_proj, codebook, code_index, clip_index, dead_codes, source_rows, latent_cot,
):
    frame_count, patches, d = frames_in.shape[1:]
    cdim = quant_proj.shape[1]
    row_count = frame_count * patches
    frame_size, batch_size = lax.axis_size("frame"), lax.axis_size("batch")
    assert frame_count == SPAN
    spat = (spat_gain_a.reshape(1, d), spat_qkv, spat_out, spat_gain_b.reshape(1, d), spat_up, spat_down)
    temp = (temp_gain_a.reshape(1, d), temp_qkv, temp_out, temp_gain_b.reshape(1, d), temp_up, temp_down)
    x = frames_in[0]

    first = lax.axis_index("frame") * frame_count
    clips = jnp.concatenate([jnp.full((SPAN,), -1, jnp.int32), clip_index[0]])
    key_clips = lax.dynamic_slice_in_dim(clips, first, SPAN + frame_count)
    query_clips = key_clips[SPAN:]
    qi, qp = jnp.arange(frame_count * SUB) // SUB, jnp.arange(frame_count * SUB) % SUB
    kj, kp = jnp.arange((SPAN + frame_count) * SUB) // SUB, jnp.arange((SPAN + frame_count) * SUB) % SUB
    offset = qi[:, None] + SPAN - kj[None, :]
    allowed = (
        (qp[:, None] == kp[None, :]) & (offset >= 0) & (offset <= SPAN)
        & (jnp.repeat(query_clips, SUB)[:, None] == jnp.repeat(key_clips, SUB)[None, :])
    )
    bias = jnp.where(allowed, 0.0, NEG).astype(F32)

    x2, s_at, s_pk, s_att_t, s_mid, s_bt, s_h, s_gp = spat_forward(x, spat)
    halo = lax.ppermute(x2, "frame", [(i, i + 1) for i in range(frame_size - 1)])
    latent3, x3, t_at, t_aht, t_pk, t_kvh, t_att_t, t_mid, t_bt, t_h, t_gp = temp_forward(
        x2, halo, bias, temp, quant_proj
    )

    latent = latent3.reshape(-1, cdim)
    codes_flat = code_index.reshape(-1)
    chosen = jnp.take(codebook, codes_flat, axis=0)
    differ = latent - chosen
    commit_part = jnp.sum(differ * differ)
    grad_latent = (latent_cot.reshape(-1, cdim) + 2.0 * BETA * differ).astype(BF16)
    grad_book = jax.ops.segment_sum(-2.0 * BETA * differ, codes_flat, num_segments=codebook.shape[0])

    dyt, du, dmid, dpk, dkvh, base, dah, dg_ta, dg_tb, dproj = temp_backward(
        grad_latent.reshape(latent3.shape), quant_proj, x3, x2, t_mid, t_gp, t_pk, t_kvh, bias.T, temp
    )
    dah_back = lax.ppermute(dah, "frame", [(i + 1, i) for i in range(frame_size - 1)])
    t_up, t_down = mlp_grads(t_bt, du, dyt, t_h)
    t_att = att_grads(
        t_at, t_att_t, dpk.reshape(row_count, -1), dmid, t_aht, dkvh.reshape(row_count, -1)
    )
    dx, dyt, du, dmid, dpk, dg_ta2, dg_sa, dg_sb = spat_backward(
        base, dah_back, x2, temp[0], x, s_mid, s_gp, s_pk, spat
    )
    s_up, s_down = mlp_grads(s_bt, du, dyt, s_h)
    s_att = att_grads(s_at, s_att_t, dpk, dmid)

    dead_match = (codes_flat[:, None] == dead_codes[None, :]).astype(F32)
    usage_part = jnp.sum(dead_match, 0)
    row_base = (lax.axis_index("batch") * frame_size + lax.axis_index("frame")) * row_count
    pick_table = ((source_rows - row_base)[:, None] == jnp.arange(row_count)[None, :]).astype(F32)
    picked = jnp.dot(pick_table, latent, precision=HIGH)
    usage_count, candidate, commit_total = lax.psum((usage_part, picked, commit_part), ("frame", "batch"))
    gain_ta, gain_tb, gain_sa, gain_sb = lax.psum(
        ((dg_ta + dg_ta2)[0], dg_tb[0], dg_sa[0], dg_sb[0]), ("frame", "batch")
    )
    old_rows = jnp.take(codebook, dead_codes, axis=0)
    fresh_rows = jnp.where((usage_count < USE_MIN)[:, None], candidate, old_rows)
    refreshed = codebook.at[dead_codes].set(fresh_rows)
    commit_loss = commit_total / (frame_size * batch_size * row_count * cdim)

    one, two = orders()
    piece = d // frame_size

    def by_rows(grad, order):
        return reduce_pieces(
            grad.reshape(batch_size, frame_size, -1, grad.shape[-1]), ("batch", "frame"), order
        )

    def finish_up(grad):
        return by_rows(grad, one).transpose(1, 0, 2).reshape(piece, -1)

    def finish_down(grad):
        hidden = grad.shape[0] * grad.shape[2]
        wide = hidden // frame_size
        if grad.shape[2] != wide:
            grad = grad.transpose(1, 0, 2).reshape(d, frame_size, wide).transpose(1, 0, 2)
        out = reduce_pieces(
            grad.reshape(frame_size, batch_size, d // batch_size, wide), ("frame", "batch"), two
        )
        return out.reshape(d, wide).T

    def finish_att(grad, order):
        out = by_rows(grad, order)
        qkv = out[:, :, :384].reshape(batch_size, piece, 3, -1).transpose(1, 2, 0, 3).reshape(piece, 3 * d)
        return qkv, out[:, :, 384:].transpose(1, 0, 2).reshape(piece, d)

    book = grad_book.reshape(frame_size, batch_size, -1, 128)
    proj = dproj.T.reshape(frame_size, batch_size, -1)
    proj_size = proj.shape[2]
    proj = jnp.pad(proj, ((0, 0), (0, 0), (0, -proj_size % 128))).reshape(frame_size, batch_size, -1, 128)
    small = jnp.concatenate([book, proj], 2).astype(BF16)
    small = reduce_pieces(small, ("frame", "batch"), two)
    book_rows = book.shape[2]
    g_book = small[:, :book_rows].reshape(-1, cdim)
    g_proj = small[:, book_rows:].reshape(batch_size, -1)[:, :proj_size].reshape(piece, cdim)
    gt_qkv, gt_out = finish_att(t_att, one)
    gs_qkv, gs_out = finish_att(s_att, one)
    return (
        latent.reshape(latent_cot.shape),
        commit_loss,
        dx[None],
        gain_sa,
        gs_qkv,
        gs_out,
        gain_sb,
        finish_up(s_up),
        finish_down(s_down),
        gain_ta,
        gt_qkv,
        gt_out,
        gain_tb,
        finish_up(t_up),
        finish_down(t_down),
        g_proj,
        g_book,
        refreshed,
    )


def solution(mesh):
    return jax.shard_map(
        local,
        mesh=mesh,
        in_specs=(
            P("batch", "frame", None, None),
            *([P()] * 14),
            P("batch", "frame", None),
            P("batch", None),
            P(),
            P(),
            P("batch", "frame", None, None),
        ),
        out_specs=(
            P("batch", "frame", None, None),
            P(),
            P("batch", "frame", None, None),
            P(),
            P("frame", None),
            P("frame", None),
            P(),
            P("frame", None),
            P("frame", None),
            P(),
            P("frame", None),
            P("frame", None),
            P(),
            P("frame", None),
            P("frame", None),
            P("frame", None),
            P("frame", None),
            P(),
        ),
        check_vma=False,
    )
```

```python
import jax
import jax.numpy as jnp
from jax import lax
from jax.experimental import pallas as pl
from jax.experimental.pallas import tpu as pltpu
from jax.sharding import PartitionSpec as P

HEADS = 8
EPS = 1e-05
BETA = 0.25
USE_MIN = 2.0
NEG = -1e30
HIGH = lax.Precision.HIGHEST
SPAN = 4
F32 = jnp.float32
BF16 = jnp.bfloat16
MESH = pl.DeviceIdType.MESH
GELU_C = 0.7978845608028654
GELU_A = 0.044715
VMEM_BYTES = 56 * 1024 * 1024
SUB = 32
GROUP = 64


def mm(a, b):
    return jnp.dot(a, b, preferred_element_type=F32)


def mm_t(a, b):
    return lax.dot_general(a, b, (((1,), (1,)), ((), ())), preferred_element_type=F32)


def t_mm(a, b):
    return lax.dot_general(a, b, (((0,), (0,)), ((), ())), preferred_element_type=F32)


def norm(x):
    c = x - jnp.mean(x, -1, keepdims=True)
    r = lax.rsqrt(jnp.mean(c * c, -1, keepdims=True) + EPS)
    return c * r, r


def norm_back(dy, xhat, r, gain):
    d = dy * gain
    return r * (d - jnp.mean(d, -1, keepdims=True) - xhat * jnp.mean(d * xhat, -1, keepdims=True))


def add_row(ref, rows):
    ref[...] += jnp.sum(rows, 0, keepdims=True)


def head_masks(rows, width):
    lane = lax.broadcasted_iota(jnp.int32, (rows, width), 1)
    return (lane < width // 2, lane >= width // 2)


def attend_pair(q, k, v, bias):
    width = q.shape[1]
    scale = (width // 2) ** -0.5
    zero = jnp.zeros((), BF16)
    qs = q * jnp.asarray(scale, BF16)
    v_ext = jnp.concatenate([v, jnp.ones_like(v)], axis=1)
    masks = head_masks(q.shape[0], width)
    halves = []
    for mask in masks:
        s = mm_t(jnp.where(mask, qs, zero), k)
        if bias is not None:
            s = s + bias
        e = jnp.exp(s - jnp.max(s, -1, keepdims=True)).astype(BF16)
        r = mm(e, v_ext)
        halves.append(r[:, :width] / r[:, width:])
    return jnp.where(masks[0], halves[0], halves[1]).astype(BF16)


def attend_pair_back(q, k, v, do, bias_t):
    width = q.shape[1]
    scale = jnp.asarray((width // 2) ** -0.5, BF16)
    zero = jnp.zeros((), BF16)
    qs = q * scale
    ks = k * scale
    q_masks = head_masks(q.shape[0], width)
    k_masks = head_masks(k.shape[0], width)
    dq = dk = dv = None
    for q_mask, k_mask in zip(q_masks, k_masks):
        qm = jnp.where(q_mask, qs, zero)
        dom = jnp.where(q_mask, do, zero)
        st = mm_t(k, qm)
        if bias_t is not None:
            st = st + bias_t
        e = jnp.exp(st - jnp.max(st, 0, keepdims=True))
        p = e * (1.0 / jnp.sum(e, 0, keepdims=True))
        dp = mm_t(v, dom)
        inner = jnp.sum(p * dp, 0, keepdims=True)
        ds = (p * (dp - inner)).astype(BF16)
        dv_one = mm(p.astype(BF16), dom)
        dk_one = mm(ds, qm)
        dq_one = t_mm(ds, jnp.where(k_mask, ks, zero))
        dq = dq_one if dq is None else dq + dq_one
        dk = dk_one if dk is None else dk + dk_one
        dv = dv_one if dv is None else dv + dv_one
    return dq, dk, dv


def mlp_forward(mid, gain, w_up, w_down, bt_ref, h_ref, gp_ref, tile=512):
    xhat, _ = norm(mid)
    b = (xhat * gain).astype(BF16)
    bt_ref[...] = b.T
    out = mid
    for start in range(0, w_up.shape[1], tile):
        cols = slice(start, start + tile)
        u = mm(b, w_up[:, cols])
        u2 = u * u
        th = jnp.tanh(u * (GELU_C + (GELU_C * GELU_A) * u2))
        half = 0.5 + 0.5 * th
        h = (u * half).astype(BF16)
        slope = half + u * (half * (1.0 - th)) * (GELU_C + (3.0 * GELU_C * GELU_A) * u2)
        h_ref[:, cols] = h
        gp_ref[:, cols] = slope.astype(BF16)
        out = out + mm(h, w_down[cols, :])
    return out


def mlp_backward(dy, dy_low, mid, gain, w_up, w_down, gp_ref, du_ref, dgain_ref, tile=512):
    db = None
    for start in range(0, w_up.shape[1], tile):
        cols = slice(start, start + tile)
        dh = mm_t(dy_low, w_down[cols, :])
        du = (gp_ref[:, cols].astype(F32) * dh).astype(BF16)
        du_ref[:, cols] = du
        one = mm_t(du, w_up[:, cols])
        db = one if db is None else db + one
    xhat, r = norm(mid)
    add_row(dgain_ref, db * xhat)
    return dy + norm_back(db, xhat, r, gain)


def greet_ring(step):
    n = lax.axis_size("frame")
    me = lax.axis_index("frame")
    left, right = lax.rem(me + n - 1, n), lax.rem(me + 1, n)

    @pl.when(step == 0)
    def _():
        barrier = pltpu.get_barrier_semaphore()
        for peer in (left, right):
            pl.semaphore_signal(barrier, inc=1, device_id={"frame": peer}, device_id_type=MESH)

    return left, right


def meet_ring(step):
    @pl.when(step == 0)
    def _():
        pl.semaphore_wait(pltpu.get_barrier_semaphore(), 2)


def ring_copy(src, dst, send_sem, recv_sem, peer):
    return pltpu.make_async_remote_copy(
        src_ref=src, dst_ref=dst, send_sem=send_sem, recv_sem=recv_sem,
        device_id={"frame": peer}, device_id_type=MESH,
    )


def spat_fwd_kernel(
    x_ref, ga, w_qkv, w_out, gb, w_up, w_down,
    y_ref, at_ref, pk_ref, att_t_ref, mid_ref, bt_ref, h_ref, gp_ref, halo_ref,
    att_ref, keep_ref, send_sem, recv_sem,
):
    step = pl.program_id(0)
    steps = pl.num_programs(0)
    feature = x_ref.shape[-1]
    left, right = greet_ring(step)
    x = x_ref[0].astype(F32)
    xhat, _ = norm(x)
    a = (xhat * ga[...]).astype(BF16)
    at_ref[...] = a.T
    for start in range(0, 3 * feature, 512):
        pk_ref[:, start : start + 512] = mm(a, w_qkv[:, start : start + 512]).astype(BF16)
    for lane in range(0, feature, 128):
        att_ref[:, lane : lane + 128] = attend_pair(
            pk_ref[:, lane : lane + 128],
            pk_ref[:, feature + lane : feature + lane + 128],
            pk_ref[:, 2 * feature + lane : 2 * feature + lane + 128],
            None,
        )
    att = att_ref[...]
    att_t_ref[...] = att.T
    mid = x + mm(att, w_out[...])
    mid_ref[...] = mid
    y = mlp_forward(mid, gb[...], w_up, w_down, bt_ref, h_ref, gp_ref).astype(BF16)
    y_ref[0] = y
    keep_ref[step] = y
    meet_ring(step)

    def copy(i):
        return ring_copy(keep_ref.at[i], halo_ref.at[i], send_sem.at[i], recv_sem.at[i], right)

    copy(step).start()

    @pl.when(step == steps - 1)
    def _():
        for i in range(keep_ref.shape[0]):
            copy(i).wait()


def temp_fwd_kernel(
    x_ref, halo_ref, bias_ref, ga, w_qkv, w_out, gb, w_up, w_down, proj,
    lat_ref, x3_ref, at_ref, aht_ref, pk_ref, kvh_ref, att_t_ref, mid_ref, bt_ref, h_ref, gp_ref, att_ref,
):
    frames, group, feature = x_ref.shape
    rows = frames * group
    x = x_ref[...].reshape(rows, feature).astype(F32)
    xhat, _ = norm(x)
    a = (xhat * ga[...]).astype(BF16)
    at_ref[...] = a.T
    for start in range(0, 3 * feature, 512):
        pk_ref[:, :, start : start + 512] = (
            mm(a, w_qkv[:, start : start + 512]).astype(BF16).reshape(frames, group, 512)
        )
    xhat_h, _ = norm(halo_ref[...].reshape(rows, feature).astype(F32))
    ah = (xhat_h * ga[...]).astype(BF16)
    aht_ref[...] = ah.T
    for start in range(0, 2 * feature, 512):
        kvh_ref[:, :, start : start + 512] = (
            mm(ah, w_qkv[:, feature + start : feature + start + 512])
            .astype(BF16)
            .reshape(frames, group, 512)
        )
    bias = bias_ref[...]
    for sub in range(0, group, SUB):
        here = slice(sub, sub + SUB)
        for lane in range(0, feature, 128):
            q = pk_ref[:, here, lane : lane + 128].reshape(frames * SUB, 128)
            k = jnp.concatenate(
                [kvh_ref[:, here, lane : lane + 128],
                 pk_ref[:, here, feature + lane : feature + lane + 128]], 0
            ).reshape(2 * frames * SUB, 128)
            v = jnp.concatenate(
                [kvh_ref[:, here, feature + lane : feature + lane + 128],
                 pk_ref[:, here, 2 * feature + lane : 2 * feature + lane + 128]], 0
            ).reshape(2 * frames * SUB, 128)
            att_ref[:, here, lane : lane + 128] = attend_pair(q, k, v, bias).reshape(frames, SUB, 128)
    att = att_ref[...].reshape(rows, feature)
    att_t_ref[...] = att.T
    mid = x + mm(att, w_out[...])
    mid_ref[...] = mid
    y = mlp_forward(mid, gb[...], w_up, w_down, bt_ref, h_ref, gp_ref).astype(BF16)
    x3_ref[...] = y
    lat_ref[...] = mm(y, proj[...]).reshape(frames, group, proj.shape[1])


def temp_bwd_kernel(
    gl_ref, proj, x3_ref, x_ref, mid_ref, gp_ref, pk_ref, kvh_ref, bias_ref,
    ga, w_qkv, w_out, gb, w_up, w_down,
    dyt_ref, du_ref, dmid_ref, dpk_ref, dkvh_ref, base_ref, back_ref, dga_ref, dgb_ref, dproj_ref,
    datt_ref, dah_ref, send_sem, recv_sem,
):
    step = pl.program_id(0)
    steps = pl.num_programs(0)
    frames, group, feature = x_ref.shape
    rows = frames * group
    left, right = greet_ring(step)

    @pl.when(step == 0)
    def _():
        for ref in (dga_ref, dgb_ref, dproj_ref):
            ref[...] = jnp.zeros_like(ref)

    gl = gl_ref[...].reshape(rows, gl_ref.shape[2])
    dproj_ref[...] += t_mm(gl, x3_ref[...])
    dy_low = mm_t(gl, proj[...]).astype(BF16)
    dyt_ref[...] = dy_low.T
    dmid = mlp_backward(
        dy_low.astype(F32), dy_low, mid_ref[...], gb[...], w_up, w_down, gp_ref, du_ref, dgb_ref
    )
    dmid_low = dmid.astype(BF16)
    dmid_ref[...] = dmid_low
    datt_ref[...] = mm_t(dmid_low, w_out[...]).astype(BF16).reshape(frames, group, feature)
    bias = bias_ref[...]
    half = frames * SUB
    for sub in range(0, group, SUB):
        here = slice(sub, sub + SUB)
        for lane in range(0, feature, 128):
            l0 = slice(lane, lane + 128)
            l1 = slice(feature + lane, feature + lane + 128)
            l2 = slice(2 * feature + lane, 2 * feature + lane + 128)
            q = pk_ref[:, here, l0].reshape(half, 128)
            k = jnp.concatenate([kvh_ref[:, here, l0], pk_ref[:, here, l1]], 0).reshape(2 * half, 128)
            v = jnp.concatenate([kvh_ref[:, here, l1], pk_ref[:, here, l2]], 0).reshape(2 * half, 128)
            do = datt_ref[:, here, l0].reshape(half, 128)
            dq, dk, dv = attend_pair_back(q, k, v, do, bias)
            dk, dv = dk.astype(BF16), dv.astype(BF16)
            dpk_ref[:, here, l0] = dq.astype(BF16).reshape(frames, SUB, 128)
            dpk_ref[:, here, l1] = dk[half:].reshape(frames, SUB, 128)
            dpk_ref[:, here, l2] = dv[half:].reshape(frames, SUB, 128)
            dkvh_ref[:, here, l0] = dk[:half].reshape(frames, SUB, 128)
            dkvh_ref[:, here, l1] = dv[:half].reshape(frames, SUB, 128)
    da = mm_t(dpk_ref[...].reshape(rows, 3 * feature), w_qkv[...])
    dah = mm_t(dkvh_ref[...].reshape(rows, 2 * feature), w_qkv[:, feature:])
    dah_ref[step] = dah.astype(BF16).reshape(frames, group, feature)
    meet_ring(step)

    def copy(i):
        there = back_ref.at[:, pl.ds(i * group, group), :]
        return ring_copy(dah_ref.at[i], there, send_sem.at[i], recv_sem.at[i], left)

    copy(step).start()
    xhat, r = norm(x_ref[...].reshape(rows, feature).astype(F32))
    add_row(dga_ref, da * xhat)
    base_ref[...] = (dmid + norm_back(da, xhat, r, ga[...])).reshape(frames, group, feature)

    @pl.when(step == steps - 1)
    def _():
        for i in range(dah_ref.shape[0]):
            copy(i).wait()


def spat_bwd_kernel(
    base_ref, dah_ref, x2_ref, gta, x_ref, mid_ref, gp_ref, pk_ref,
    ga, w_qkv, w_out, gb, w_up, w_down,
    dx_ref, dyt_ref, du_ref, dmid_ref, dpk_ref, dgt_ref, dga_ref, dgb_ref,
    datt_ref,
):
    feature = x_ref.shape[-1]

    @pl.when(pl.program_id(0) == 0)
    def _():
        for ref in (dgt_ref, dga_ref, dgb_ref):
            ref[...] = jnp.zeros_like(ref)

    xhat2, r2 = norm(x2_ref[0].astype(F32))
    dah = dah_ref[0].astype(F32)
    add_row(dgt_ref, dah * xhat2)
    dy_low = (base_ref[0] + norm_back(dah, xhat2, r2, gta[...])).astype(BF16)
    dyt_ref[...] = dy_low.T
    dmid = mlp_backward(
        dy_low.astype(F32), dy_low, mid_ref[...], gb[...], w_up, w_down, gp_ref, du_ref, dgb_ref
    )
    dmid_low = dmid.astype(BF16)
    dmid_ref[...] = dmid_low
    datt_ref[...] = mm_t(dmid_low, w_out[...]).astype(BF16)
    for lane in range(0, feature, 128):
        l0 = slice(lane, lane + 128)
        l1 = slice(feature + lane, feature + lane + 128)
        l2 = slice(2 * feature + lane, 2 * feature + lane + 128)
        dq, dk, dv = attend_pair_back(pk_ref[:, l0], pk_ref[:, l1], pk_ref[:, l2], datt_ref[:, l0], None)
        dpk_ref[:, l0] = dq.astype(BF16)
        dpk_ref[:, l1] = dk.astype(BF16)
        dpk_ref[:, l2] = dv.astype(BF16)
    da = mm_t(dpk_ref[...], w_qkv[...])
    xhat, r = norm(x_ref[0].astype(F32))
    add_row(dga_ref, da * xhat)
    dx_ref[0] = (dmid + norm_back(da, xhat, r, ga[...])).astype(BF16)


def mlp_grad_kernel(bt_ref, du_ref, dyt_ref, h_ref, up_ref, down_ref):
    up_ref[0] = mm(bt_ref[...], du_ref[...]).astype(BF16)
    width = down_ref.shape[2]
    for j in range(down_ref.shape[0]):
        down_ref[j] = mm(dyt_ref[...], h_ref[:, j * width : (j + 1) * width]).astype(BF16)


def att_grad_kernel(halo, *refs):
    if halo:
        at_ref, att_t_ref, dq_ref, dk_ref, dv_ref, dm_ref, aht_ref, dkh_ref, dvh_ref, out_ref = refs
    else:
        at_ref, att_t_ref, dq_ref, dk_ref, dv_ref, dm_ref, out_ref = refs
    dq = mm(at_ref[...], dq_ref[...])
    dk = mm(at_ref[...], dk_ref[...])
    dv = mm(at_ref[...], dv_ref[...])
    if halo:
        dk = dk + mm(aht_ref[...], dkh_ref[...])
        dv = dv + mm(aht_ref[...], dvh_ref[...])
    do = mm(att_t_ref[...], dm_ref[...])
    for i, part in enumerate((dq, dk, dv, do)):
        part = part.astype(BF16)
        for j in range(2):
            out_ref[j, :, 128 * i : 128 * (i + 1)] = part[:, 128 * j : 128 * (j + 1)]


def whole(shape):
    zeros = (0,) * len(shape)
    return pl.BlockSpec(shape, lambda i: zeros)


def col_block(rows, width, offset=0):
    return pl.BlockSpec((rows, width), lambda i: (0, i + offset))


def row_block(rows, width):
    return pl.BlockSpec((rows, width), lambda i: (i, 0))


def shape_of(shape, dtype):
    return jax.ShapeDtypeStruct(shape, dtype)


def params(collective=None):
    return pltpu.CompilerParams(
        vmem_limit_bytes=VMEM_BYTES, dimension_semantics=("arbitrary",), collective_id=collective,
        has_side_effects=collective is not None,
    )


def cost(flops, nbytes):
    return pl.CostEstimate(flops=int(flops), bytes_accessed=int(nbytes), transcendentals=0)


def weight_specs(feature, hidden):
    return [
        whole((1, feature)), whole((feature, 3 * feature)), whole((feature, feature)),
        whole((1, feature)), whole((feature, hidden)), whole((hidden, feature)),
    ]


def spat_forward(x, weights):
    frames, patches, d = x.shape
    hidden = weights[4].shape[1]
    n = frames * patches
    blk = pl.BlockSpec((1, patches, d), lambda i: (i, 0, 0))
    return pl.pallas_call(
        spat_fwd_kernel,
        grid=(frames,),
        in_specs=[blk] + weight_specs(d, hidden),
        out_specs=[
            blk, col_block(d, patches), row_block(patches, 3 * d), col_block(d, patches),
            row_block(patches, d), col_block(d, patches), row_block(patches, hidden), row_block(patches, hidden),
            pl.BlockSpec(memory_space=pl.ANY),
        ],
        out_shape=[
            shape_of(x.shape, BF16), shape_of((d, n), BF16), shape_of((n, 3 * d), BF16), shape_of((d, n), BF16),
            shape_of((n, d), F32), shape_of((d, n), BF16), shape_of((n, hidden), BF16), shape_of((n, hidden), BF16),
            shape_of(x.shape, BF16),
        ],
        scratch_shapes=[
            pltpu.VMEM((patches, d), BF16), pltpu.VMEM(x.shape, BF16),
            pltpu.SemaphoreType.DMA((frames,)), pltpu.SemaphoreType.DMA((frames,)),
        ],
        compiler_params=params(1),
        cost_estimate=cost(2 * n * d * (4 * d + 2 * hidden + 2 * patches), 24 * n * d),
        name="spat_forward",
    )(x, *weights)


def temp_forward(x, halo, bias, weights, proj):
    frames, patches, d = x.shape
    hidden = weights[4].shape[1]
    n = frames * patches
    steps = patches // GROUP
    rows = frames * GROUP
    cdim = proj.shape[1]
    blk = pl.BlockSpec((frames, GROUP, d), lambda i: (0, i, 0))
    stacked = lambda width: pl.BlockSpec((frames, GROUP, width), lambda i: (i, 0, 0))
    return pl.pallas_call(
        temp_fwd_kernel,
        grid=(steps,),
        in_specs=[blk, blk, whole(bias.shape)] + weight_specs(d, hidden) + [whole(proj.shape)],
        out_specs=[
            pl.BlockSpec((frames, GROUP, cdim), lambda i: (0, i, 0)), row_block(rows, d),
            col_block(d, rows), col_block(d, rows), stacked(3 * d), stacked(2 * d), col_block(d, rows),
            row_block(rows, d), col_block(d, rows), row_block(rows, hidden), row_block(rows, hidden),
        ],
        out_shape=[
            shape_of((frames, patches, cdim), F32), shape_of((n, d), BF16),
            shape_of((d, n), BF16), shape_of((d, n), BF16),
            shape_of((frames * steps, GROUP, 3 * d), BF16), shape_of((frames * steps, GROUP, 2 * d), BF16),
            shape_of((d, n), BF16), shape_of((n, d), F32), shape_of((d, n), BF16),
            shape_of((n, hidden), BF16), shape_of((n, hidden), BF16),
        ],
        scratch_shapes=[pltpu.VMEM((frames, GROUP, d), BF16)],
        compiler_params=params(),
        cost_estimate=cost(2 * n * d * (6 * d + 2 * hidden + 2 * patches), 30 * n * d),
        name="temp_forward",
    )(x, halo, bias, *weights, proj)


def temp_backward(gl, proj, x3, x, mid, gp, pk, kvh, bias_t, weights):
    frames, patches, d = x.shape
    hidden = weights[4].shape[1]
    n = frames * patches
    steps = patches // GROUP
    rows = frames * GROUP
    cdim = proj.shape[1]
    nat = lambda width: pl.BlockSpec((frames, GROUP, width), lambda i: (0, i, 0))
    stacked = lambda width: pl.BlockSpec((frames, GROUP, width), lambda i: (i, 0, 0))
    return pl.pallas_call(
        temp_bwd_kernel,
        grid=(steps,),
        in_specs=[
            nat(cdim), whole(proj.shape), row_block(rows, d), nat(d), row_block(rows, d),
            row_block(rows, hidden), stacked(3 * d), stacked(2 * d), whole(bias_t.shape),
        ] + weight_specs(d, hidden),
        out_specs=[
            col_block(d, rows), row_block(rows, hidden), row_block(rows, d), stacked(3 * d), stacked(2 * d),
            nat(d), pl.BlockSpec(memory_space=pl.ANY), whole((1, d)), whole((1, d)), whole((cdim, d)),
        ],
        out_shape=[
            shape_of((d, n), BF16), shape_of((n, hidden), BF16), shape_of((n, d), BF16),
            shape_of((frames * steps, GROUP, 3 * d), BF16), shape_of((frames * steps, GROUP, 2 * d), BF16),
            shape_of((frames, patches, d), F32), shape_of((frames, patches, d), BF16),
            shape_of((1, d), F32), shape_of((1, d), F32), shape_of((cdim, d), F32),
        ],
        scratch_shapes=[
            pltpu.VMEM((frames, GROUP, d), BF16), pltpu.VMEM((steps, frames, GROUP, d), BF16),
            pltpu.SemaphoreType.DMA((steps,)), pltpu.SemaphoreType.DMA((steps,)),
        ],
        compiler_params=params(2),
        cost_estimate=cost(2 * n * d * (6 * d + 2 * hidden + 5 * patches), 40 * n * d),
        name="temp_backward",
    )(gl, proj, x3, x, mid, gp, pk, kvh, bias_t, *weights)


def spat_backward(base, dah, x2, gta, x, mid, gp, pk, weights):
    frames, patches, d = x.shape
    hidden = weights[4].shape[1]
    n = frames * patches
    blk = pl.BlockSpec((1, patches, d), lambda i: (i, 0, 0))
    return pl.pallas_call(
        spat_bwd_kernel,
        grid=(frames,),
        in_specs=[
            blk, blk, blk, whole((1, d)), blk, row_block(patches, d), row_block(patches, hidden),
            row_block(patches, 3 * d),
        ] + weight_specs(d, hidden),
        out_specs=[
            blk, col_block(d, patches), row_block(patches, hidden), row_block(patches, d),
            row_block(patches, 3 * d), whole((1, d)), whole((1, d)), whole((1, d)),
        ],
        out_shape=[
            shape_of(x.shape, BF16), shape_of((d, n), BF16), shape_of((n, hidden), BF16), shape_of((n, d), BF16),
            shape_of((n, 3 * d), BF16), shape_of((1, d), F32), shape_of((1, d), F32), shape_of((1, d), F32),
        ],
        scratch_shapes=[pltpu.VMEM((patches, d), BF16)],
        compiler_params=params(),
        cost_estimate=cost(2 * n * d * (4 * d + 2 * hidden + 5 * patches), 30 * n * d),
        name="spat_backward",
    )(base, dah, x2, gta, x, mid, gp, pk, *weights)


def mlp_grads(bt, du, dyt, h):
    d, n = bt.shape
    hidden = du.shape[1]
    steps = 4
    wide = hidden // steps
    return pl.pallas_call(
        mlp_grad_kernel,
        grid=(steps,),
        in_specs=[whole((d, n)), col_block(n, wide), whole((d, n)), col_block(n, wide)],
        out_specs=[
            pl.BlockSpec((1, d, wide), lambda i: (i, 0, 0)),
            pl.BlockSpec((2, d, wide // 2), lambda i: (i, 0, 0)),
        ],
        out_shape=[shape_of((steps, d, wide), BF16), shape_of((2 * steps, d, wide // 2), BF16)],
        compiler_params=params(),
        cost_estimate=cost(4 * n * d * hidden, 8 * n * d + 4 * n * hidden),
        name="mlp_grads",
    )(bt, du, dyt, h)


def att_grads(at, att_t, dpk, dmid, aht=None, dkvh=None):
    d, n = at.shape
    halo = aht is not None
    wide = 256
    args = [at, att_t, dpk, dpk, dpk, dmid]
    specs = [
        whole((d, n)), whole((d, n)), col_block(n, wide), col_block(n, wide, d // wide),
        col_block(n, wide, 2 * d // wide), col_block(n, wide),
    ]
    if halo:
        args += [aht, dkvh, dkvh]
        specs += [whole((d, n)), col_block(n, wide), col_block(n, wide, d // wide)]
    return pl.pallas_call(
        lambda *refs: att_grad_kernel(halo, *refs),
        grid=(d // wide,),
        in_specs=specs,
        out_specs=pl.BlockSpec((2, d, 512), lambda i: (i, 0, 0)),
        out_shape=shape_of((d // 128, d, 512), BF16),
        compiler_params=params(),
        cost_estimate=cost(2 * n * d * d * (6 if halo else 4), 16 * n * d),
        name="att_grads",
    )(*args)


def bits_of(count):
    bits = count.bit_length() - 1
    assert count == 1 << bits
    return bits


def swap(value, axis, bit):
    count = lax.axis_size(axis)
    return lax.ppermute(value, axis, [(i, i ^ (1 << bit)) for i in range(count)])


def my_bit(axis, bit):
    return (lax.axis_index(axis) >> bit) & 1


def reduce_pieces(grad, labels, order):
    names = []
    for axis in labels:
        names += [(axis, b) for b in reversed(range(bits_of(lax.axis_size(axis))))]
    tail = grad.shape[len(labels) :]
    cur = grad.reshape((2,) * len(names) + tail)
    for axis, bit in order:
        at = names.index((axis, bit))
        me = my_bit(axis, bit)
        kept = lax.dynamic_index_in_dim(cur, me, at, keepdims=False)
        sent = lax.dynamic_index_in_dim(cur, 1 - me, at, keepdims=False)
        cur = (kept.astype(F32) + swap(sent, axis, bit).astype(F32)).astype(BF16)
        names.pop(at)
    cur = cur[None]
    for bit in reversed(range(bits_of(lax.axis_size("batch")))):
        other = swap(cur, "batch", bit)
        low = my_bit("batch", bit) == 0
        cur = jnp.stack([jnp.where(low, cur, other), jnp.where(low, other, cur)], 1)
        cur = cur.reshape((-1,) + tail)
    return cur.astype(F32)


def orders():
    fb, bb = bits_of(lax.axis_size("frame")), bits_of(lax.axis_size("batch"))
    frame = [("frame", b) for b in [0] + list(reversed(range(1, fb)))]
    batch = [("batch", b) for b in range(bb)]
    return batch + frame, batch[:1] + frame[:1] + batch[1:] + frame[1:]


def local(
    frames_in, spat_gain_a, spat_qkv, spat_out, spat_gain_b, spat_up, spat_down,
    temp_gain_a, temp_qkv, temp_out, temp_gain_b, temp_up, temp_down,
    quant_proj, codebook, code_index, clip_index, dead_codes, source_rows, latent_cot,
):
    frame_count, patches, d = frames_in.shape[1:]
    cdim = quant_proj.shape[1]
    row_count = frame_count * patches
    frame_size, batch_size = lax.axis_size("frame"), lax.axis_size("batch")
    assert frame_count == SPAN
    spat = (spat_gain_a.reshape(1, d), spat_qkv, spat_out, spat_gain_b.reshape(1, d), spat_up, spat_down)
    temp = (temp_gain_a.reshape(1, d), temp_qkv, temp_out, temp_gain_b.reshape(1, d), temp_up, temp_down)
    x = frames_in[0]

    first = lax.axis_index("frame") * frame_count
    clips = jnp.concatenate([jnp.full((SPAN,), -1, jnp.int32), clip_index[0]])
    key_clips = lax.dynamic_slice_in_dim(clips, first, SPAN + frame_count)
    query_clips = key_clips[SPAN:]
    qi, qp = jnp.arange(frame_count * SUB) // SUB, jnp.arange(frame_count * SUB) % SUB
    kj, kp = jnp.arange((SPAN + frame_count) * SUB) // SUB, jnp.arange((SPAN + frame_count) * SUB) % SUB
    offset = qi[:, None] + SPAN - kj[None, :]
    allowed = (
        (qp[:, None] == kp[None, :]) & (offset >= 0) & (offset <= SPAN)
        & (jnp.repeat(query_clips, SUB)[:, None] == jnp.repeat(key_clips, SUB)[None, :])
    )
    bias = jnp.where(allowed, 0.0, NEG).astype(F32)

    x2, s_at, s_pk, s_att_t, s_mid, s_bt, s_h, s_gp, halo = spat_forward(x, spat)
    latent3, x3, t_at, t_aht, t_pk, t_kvh, t_att_t, t_mid, t_bt, t_h, t_gp = temp_forward(
        x2, halo, bias, temp, quant_proj
    )

    latent = latent3.reshape(-1, cdim)
    codes_flat = code_index.reshape(-1)
    chosen = jnp.take(codebook, codes_flat, axis=0)
    differ = latent - chosen
    commit_part = jnp.sum(differ * differ)
    grad_latent = (latent_cot.reshape(-1, cdim) + 2.0 * BETA * differ).astype(BF16)
    grad_book = jax.ops.segment_sum(-2.0 * BETA * differ, codes_flat, num_segments=codebook.shape[0])

    dyt, du, dmid, dpk, dkvh, base, dah_back, dg_ta, dg_tb, dproj = temp_backward(
        grad_latent.reshape(latent3.shape), quant_proj, x3, x2, t_mid, t_gp, t_pk, t_kvh, bias.T, temp
    )
    t_up, t_down = mlp_grads(t_bt, du, dyt, t_h)
    t_att = att_grads(
        t_at, t_att_t, dpk.reshape(row_count, -1), dmid, t_aht, dkvh.reshape(row_count, -1)
    )
    dx, dyt, du, dmid, dpk, dg_ta2, dg_sa, dg_sb = spat_backward(
        base, dah_back, x2, temp[0], x, s_mid, s_gp, s_pk, spat
    )
    s_up, s_down = mlp_grads(s_bt, du, dyt, s_h)
    s_att = att_grads(s_at, s_att_t, dpk, dmid)

    dead_match = (codes_flat[:, None] == dead_codes[None, :]).astype(F32)
    usage_part = jnp.sum(dead_match, 0)
    row_base = (lax.axis_index("batch") * frame_size + lax.axis_index("frame")) * row_count
    pick_table = ((source_rows - row_base)[:, None] == jnp.arange(row_count)[None, :]).astype(F32)
    picked = jnp.dot(pick_table, latent, precision=HIGH)
    usage_count, candidate, commit_total = lax.psum((usage_part, picked, commit_part), ("frame", "batch"))
    gain_ta, gain_tb, gain_sa, gain_sb = lax.psum(
        ((dg_ta + dg_ta2)[0], dg_tb[0], dg_sa[0], dg_sb[0]), ("frame", "batch")
    )
    old_rows = jnp.take(codebook, dead_codes, axis=0)
    fresh_rows = jnp.where((usage_count < USE_MIN)[:, None], candidate, old_rows)
    refreshed = codebook.at[dead_codes].set(fresh_rows)
    commit_loss = commit_total / (frame_size * batch_size * row_count * cdim)

    one, two = orders()
    piece = d // frame_size

    def by_rows(grad, order):
        return reduce_pieces(
            grad.reshape(batch_size, frame_size, -1, grad.shape[-1]), ("batch", "frame"), order
        )

    def finish_up(grad):
        return by_rows(grad, one).transpose(1, 0, 2).reshape(piece, -1)

    def finish_down(grad):
        hidden = grad.shape[0] * grad.shape[2]
        wide = hidden // frame_size
        if grad.shape[2] != wide:
            grad = grad.transpose(1, 0, 2).reshape(d, frame_size, wide).transpose(1, 0, 2)
        out = reduce_pieces(
            grad.reshape(frame_size, batch_size, d // batch_size, wide), ("frame", "batch"), two
        )
        return out.reshape(d, wide).T

    def finish_att(grad, order):
        out = by_rows(grad, order)
        qkv = out[:, :, :384].reshape(batch_size, piece, 3, -1).transpose(1, 2, 0, 3).reshape(piece, 3 * d)
        return qkv, out[:, :, 384:].transpose(1, 0, 2).reshape(piece, d)

    book = grad_book.reshape(frame_size, batch_size, -1, 128)
    proj = dproj.T.reshape(frame_size, batch_size, -1)
    proj_size = proj.shape[2]
    proj = jnp.pad(proj, ((0, 0), (0, 0), (0, -proj_size % 128))).reshape(frame_size, batch_size, -1, 128)
    small = jnp.concatenate([book, proj], 2).astype(BF16)
    small = reduce_pieces(small, ("frame", "batch"), two)
    book_rows = book.shape[2]
    g_book = small[:, :book_rows].reshape(-1, cdim)
    g_proj = small[:, book_rows:].reshape(batch_size, -1)[:, :proj_size].reshape(piece, cdim)
    gt_qkv, gt_out = finish_att(t_att, one)
    gs_qkv, gs_out = finish_att(s_att, one)
    return (
        latent.reshape(latent_cot.shape),
        commit_loss,
        dx[None],
        gain_sa,
        gs_qkv,
        gs_out,
        gain_sb,
        finish_up(s_up),
        finish_down(s_down),
        gain_ta,
        gt_qkv,
        gt_out,
        gain_tb,
        finish_up(t_up),
        finish_down(t_down),
        g_proj,
        g_book,
        refreshed,
    )


def solution(mesh):
    return jax.shard_map(
        local,
        mesh=mesh,
        in_specs=(
            P("batch", "frame", None, None),
            *([P()] * 14),
            P("batch", "frame", None),
            P("batch", None),
            P(),
            P(),
            P("batch", "frame", None, None),
        ),
        out_specs=(
            P("batch", "frame", None, None),
            P(),
            P("batch", "frame", None, None),
            P(),
            P("frame", None),
            P("frame", None),
            P(),
            P("frame", None),
            P("frame", None),
            P(),
            P("frame", None),
            P("frame", None),
            P(),
            P("frame", None),
            P("frame", None),
            P("frame", None),
            P("frame", None),
            P(),
        ),
        check_vma=False,
    )
```

```python
import types

import jax
import jax.numpy as jnp
from jax import lax
from jax.experimental import pallas as pl
from jax.experimental.pallas import tpu as pltpu
from jax.sharding import PartitionSpec as P

HEADS = 8
EPS = 1e-05
BETA = 0.25
USE_MIN = 2.0
NEG = -1e30
HIGH = lax.Precision.HIGHEST
SPAN = 4
F32 = jnp.float32
BF16 = jnp.bfloat16
MESH = pl.DeviceIdType.MESH
GELU_C = 0.7978845608028654
GELU_A = 0.044715
VMEM_BYTES = 56 * 1024 * 1024
TAIL_BYTES = 62 * 1024 * 1024
SUB = 32
GROUP = 64


def mm(a, b):
    return jnp.dot(a, b, preferred_element_type=F32)


def mm_t(a, b):
    return lax.dot_general(a, b, (((1,), (1,)), ((), ())), preferred_element_type=F32)


def t_mm(a, b):
    return lax.dot_general(a, b, (((0,), (0,)), ((), ())), preferred_element_type=F32)


def norm(x):
    c = x - jnp.mean(x, -1, keepdims=True)
    r = lax.rsqrt(jnp.mean(c * c, -1, keepdims=True) + EPS)
    return c * r, r


def norm_back(dy, xhat, r, gain):
    d = dy * gain
    return r * (d - jnp.mean(d, -1, keepdims=True) - xhat * jnp.mean(d * xhat, -1, keepdims=True))


def add_row(ref, rows):
    ref[...] += jnp.sum(rows, 0, keepdims=True)


def head_masks(rows, width):
    lane = lax.broadcasted_iota(jnp.int32, (rows, width), 1)
    return (lane < width // 2, lane >= width // 2)


def attend_pair(q, k, v, bias):
    width = q.shape[1]
    scale = (width // 2) ** -0.5
    zero = jnp.zeros((), BF16)
    qs = q * jnp.asarray(scale, BF16)
    v_ext = jnp.concatenate([v, jnp.ones_like(v)], axis=1)
    masks = head_masks(q.shape[0], width)
    halves = []
    for mask in masks:
        s = mm_t(jnp.where(mask, qs, zero), k)
        if bias is not None:
            s = s + bias
        e = jnp.exp(s - jnp.max(s, -1, keepdims=True)).astype(BF16)
        r = mm(e, v_ext)
        halves.append(r[:, :width] / r[:, width:])
    return jnp.where(masks[0], halves[0], halves[1]).astype(BF16)


def attend_pair_back(q, k, v, do, bias_t):
    width = q.shape[1]
    scale = jnp.asarray((width // 2) ** -0.5, BF16)
    zero = jnp.zeros((), BF16)
    qs = q * scale
    ks = k * scale
    q_masks = head_masks(q.shape[0], width)
    k_masks = head_masks(k.shape[0], width)
    dq = dk = dv = None
    for q_mask, k_mask in zip(q_masks, k_masks):
        qm = jnp.where(q_mask, qs, zero)
        dom = jnp.where(q_mask, do, zero)
        st = mm_t(k, qm)
        if bias_t is not None:
            st = st + bias_t
        e = jnp.exp(st - jnp.max(st, 0, keepdims=True))
        p = e * (1.0 / jnp.sum(e, 0, keepdims=True))
        dp = mm_t(v, dom)
        inner = jnp.sum(p * dp, 0, keepdims=True)
        ds = (p * (dp - inner)).astype(BF16)
        dv_one = mm(p.astype(BF16), dom)
        dk_one = mm(ds, qm)
        dq_one = t_mm(ds, jnp.where(k_mask, ks, zero))
        dq = dq_one if dq is None else dq + dq_one
        dk = dk_one if dk is None else dk + dk_one
        dv = dv_one if dv is None else dv + dv_one
    return dq, dk, dv


def mlp_forward(mid, gain, w_up, w_down, bt_ref, h_ref, gp_ref, tile=512):
    xhat, _ = norm(mid)
    b = (xhat * gain).astype(BF16)
    bt_ref[...] = b.T
    out = mid
    for start in range(0, w_up.shape[1], tile):
        cols = slice(start, start + tile)
        u = mm(b, w_up[:, cols])
        u2 = u * u
        th = jnp.tanh(u * (GELU_C + (GELU_C * GELU_A) * u2))
        half = 0.5 + 0.5 * th
        h = (u * half).astype(BF16)
        slope = half + u * (half * (1.0 - th)) * (GELU_C + (3.0 * GELU_C * GELU_A) * u2)
        h_ref[:, cols] = h
        gp_ref[:, cols] = slope.astype(BF16)
        out = out + mm(h, w_down[cols, :])
    return out


def mlp_backward(dy, dy_low, mid, gain, w_up, w_down, gp_ref, du_ref, dgain_ref, tile=512):
    db = None
    for start in range(0, w_up.shape[1], tile):
        cols = slice(start, start + tile)
        dh = mm_t(dy_low, w_down[cols, :])
        du = (gp_ref[:, cols].astype(F32) * dh).astype(BF16)
        du_ref[:, cols] = du
        one = mm_t(du, w_up[:, cols])
        db = one if db is None else db + one
    xhat, r = norm(mid)
    add_row(dgain_ref, db * xhat)
    return dy + norm_back(db, xhat, r, gain)


def greet_ring(step):
    n = lax.axis_size("frame")
    me = lax.axis_index("frame")
    left, right = lax.rem(me + n - 1, n), lax.rem(me + 1, n)

    @pl.when(step == 0)
    def _():
        barrier = pltpu.get_barrier_semaphore()
        for peer in (left, right):
            pl.semaphore_signal(barrier, inc=1, device_id={"frame": peer}, device_id_type=MESH)

    return left, right


def meet_ring(step):
    @pl.when(step == 0)
    def _():
        pl.semaphore_wait(pltpu.get_barrier_semaphore(), 2)


def ring_copy(src, dst, send_sem, recv_sem, peer):
    return pltpu.make_async_remote_copy(
        src_ref=src, dst_ref=dst, send_sem=send_sem, recv_sem=recv_sem,
        device_id={"frame": peer}, device_id_type=MESH,
    )


def spat_fwd_kernel(
    x_ref, ga, w_qkv, w_out, gb, w_up, w_down,
    y_ref, at_ref, pk_ref, att_t_ref, mid_ref, bt_ref, h_ref, gp_ref, halo_ref,
    att_ref, keep_ref, send_sem, recv_sem,
):
    step = pl.program_id(0)
    steps = pl.num_programs(0)
    feature = x_ref.shape[-1]
    left, right = greet_ring(step)
    x = x_ref[0].astype(F32)
    xhat, _ = norm(x)
    a = (xhat * ga[...]).astype(BF16)
    at_ref[...] = a.T
    for start in range(0, 3 * feature, 512):
        pk_ref[:, start : start + 512] = mm(a, w_qkv[:, start : start + 512]).astype(BF16)
    for lane in range(0, feature, 128):
        att_ref[:, lane : lane + 128] = attend_pair(
            pk_ref[:, lane : lane + 128],
            pk_ref[:, feature + lane : feature + lane + 128],
            pk_ref[:, 2 * feature + lane : 2 * feature + lane + 128],
            None,
        )
    att = att_ref[...]
    att_t_ref[...] = att.T
    mid = x + mm(att, w_out[...])
    mid_ref[...] = mid
    y = mlp_forward(mid, gb[...], w_up, w_down, bt_ref, h_ref, gp_ref).astype(BF16)
    y_ref[0] = y
    keep_ref[step] = y
    meet_ring(step)

    def copy(i):
        return ring_copy(keep_ref.at[i], halo_ref.at[i], send_sem.at[i], recv_sem.at[i], right)

    copy(step).start()

    @pl.when(step == steps - 1)
    def _():
        for i in range(keep_ref.shape[0]):
            copy(i).wait()


def temp_fwd_kernel(
    x_ref, halo_ref, bias_ref, ga, w_qkv, w_out, gb, w_up, w_down, proj,
    lat_ref, x3_ref, at_ref, aht_ref, pk_ref, kvh_ref, att_t_ref, mid_ref, bt_ref, h_ref, gp_ref, att_ref,
):
    frames, group, feature = x_ref.shape
    rows = frames * group
    x = x_ref[...].reshape(rows, feature).astype(F32)
    xhat, _ = norm(x)
    a = (xhat * ga[...]).astype(BF16)
    at_ref[...] = a.T
    for start in range(0, 3 * feature, 512):
        pk_ref[:, :, start : start + 512] = (
            mm(a, w_qkv[:, start : start + 512]).astype(BF16).reshape(frames, group, 512)
        )
    xhat_h, _ = norm(halo_ref[...].reshape(rows, feature).astype(F32))
    ah = (xhat_h * ga[...]).astype(BF16)
    aht_ref[...] = ah.T
    for start in range(0, 2 * feature, 512):
        kvh_ref[:, :, start : start + 512] = (
            mm(ah, w_qkv[:, feature + start : feature + start + 512])
            .astype(BF16)
            .reshape(frames, group, 512)
        )
    bias = bias_ref[...]
    for sub in range(0, group, SUB):
        here = slice(sub, sub + SUB)
        for lane in range(0, feature, 128):
            q = pk_ref[:, here, lane : lane + 128].reshape(frames * SUB, 128)
            k = jnp.concatenate(
                [kvh_ref[:, here, lane : lane + 128],
                 pk_ref[:, here, feature + lane : feature + lane + 128]], 0
            ).reshape(2 * frames * SUB, 128)
            v = jnp.concatenate(
                [kvh_ref[:, here, feature + lane : feature + lane + 128],
                 pk_ref[:, here, 2 * feature + lane : 2 * feature + lane + 128]], 0
            ).reshape(2 * frames * SUB, 128)
            att_ref[:, here, lane : lane + 128] = attend_pair(q, k, v, bias).reshape(frames, SUB, 128)
    att = att_ref[...].reshape(rows, feature)
    att_t_ref[...] = att.T
    mid = x + mm(att, w_out[...])
    mid_ref[...] = mid
    y = mlp_forward(mid, gb[...], w_up, w_down, bt_ref, h_ref, gp_ref).astype(BF16)
    x3_ref[...] = y
    lat_ref[...] = mm(y, proj[...]).reshape(frames, group, proj.shape[1])


def temp_bwd_kernel(
    gl_ref, proj, x3_ref, x_ref, mid_ref, gp_ref, pk_ref, kvh_ref, bias_ref,
    ga, w_qkv, w_out, gb, w_up, w_down,
    dyt_ref, du_ref, dmid_ref, dpk_ref, dkvh_ref, base_ref, back_ref, dga_ref, dgb_ref, dproj_ref,
    datt_ref, dah_ref, send_sem, recv_sem,
):
    step = pl.program_id(0)
    steps = pl.num_programs(0)
    frames, group, feature = x_ref.shape
    rows = frames * group
    left, right = greet_ring(step)

    @pl.when(step == 0)
    def _():
        for ref in (dga_ref, dgb_ref, dproj_ref):
            ref[...] = jnp.zeros_like(ref)

    gl = gl_ref[...].reshape(rows, gl_ref.shape[2])
    dproj_ref[...] += t_mm(gl, x3_ref[...])
    dy_low = mm_t(gl, proj[...]).astype(BF16)
    dyt_ref[...] = dy_low.T
    dmid = mlp_backward(
        dy_low.astype(F32), dy_low, mid_ref[...], gb[...], w_up, w_down, gp_ref, du_ref, dgb_ref
    )
    dmid_low = dmid.astype(BF16)
    dmid_ref[...] = dmid_low
    datt_ref[...] = mm_t(dmid_low, w_out[...]).astype(BF16).reshape(frames, group, feature)
    bias = bias_ref[...]
    half = frames * SUB
    for sub in range(0, group, SUB):
        here = slice(sub, sub + SUB)
        for lane in range(0, feature, 128):
            l0 = slice(lane, lane + 128)
            l1 = slice(feature + lane, feature + lane + 128)
            l2 = slice(2 * feature + lane, 2 * feature + lane + 128)
            q = pk_ref[:, here, l0].reshape(half, 128)
            k = jnp.concatenate([kvh_ref[:, here, l0], pk_ref[:, here, l1]], 0).reshape(2 * half, 128)
            v = jnp.concatenate([kvh_ref[:, here, l1], pk_ref[:, here, l2]], 0).reshape(2 * half, 128)
            do = datt_ref[:, here, l0].reshape(half, 128)
            dq, dk, dv = attend_pair_back(q, k, v, do, bias)
            dk, dv = dk.astype(BF16), dv.astype(BF16)
            dpk_ref[:, here, l0] = dq.astype(BF16).reshape(frames, SUB, 128)
            dpk_ref[:, here, l1] = dk[half:].reshape(frames, SUB, 128)
            dpk_ref[:, here, l2] = dv[half:].reshape(frames, SUB, 128)
            dkvh_ref[:, here, l0] = dk[:half].reshape(frames, SUB, 128)
            dkvh_ref[:, here, l1] = dv[:half].reshape(frames, SUB, 128)
    da = mm_t(dpk_ref[...].reshape(rows, 3 * feature), w_qkv[...])
    dah = mm_t(dkvh_ref[...].reshape(rows, 2 * feature), w_qkv[:, feature:])
    dah_ref[step] = dah.astype(BF16).reshape(frames, group, feature)
    meet_ring(step)

    def copy(i):
        there = back_ref.at[:, pl.ds(i * group, group), :]
        return ring_copy(dah_ref.at[i], there, send_sem.at[i], recv_sem.at[i], left)

    copy(step).start()
    xhat, r = norm(x_ref[...].reshape(rows, feature).astype(F32))
    add_row(dga_ref, da * xhat)
    base_ref[...] = (dmid + norm_back(da, xhat, r, ga[...])).reshape(frames, group, feature)

    @pl.when(step == steps - 1)
    def _():
        for i in range(dah_ref.shape[0]):
            copy(i).wait()


def spat_bwd_kernel(
    base_ref, dah_ref, x2_ref, gta, x_ref, mid_ref, gp_ref, pk_ref,
    ga, w_qkv, w_out, gb, w_up, w_down,
    dx_ref, dyt_ref, du_ref, dmid_ref, dpk_ref, dgt_ref, dga_ref, dgb_ref,
    datt_ref,
):
    feature = x_ref.shape[-1]

    @pl.when(pl.program_id(0) == 0)
    def _():
        for ref in (dgt_ref, dga_ref, dgb_ref):
            ref[...] = jnp.zeros_like(ref)

    xhat2, r2 = norm(x2_ref[0].astype(F32))
    dah = dah_ref[0].astype(F32)
    add_row(dgt_ref, dah * xhat2)
    dy_low = (base_ref[0] + norm_back(dah, xhat2, r2, gta[...])).astype(BF16)
    dyt_ref[...] = dy_low.T
    dmid = mlp_backward(
        dy_low.astype(F32), dy_low, mid_ref[...], gb[...], w_up, w_down, gp_ref, du_ref, dgb_ref
    )
    dmid_low = dmid.astype(BF16)
    dmid_ref[...] = dmid_low
    datt_ref[...] = mm_t(dmid_low, w_out[...]).astype(BF16)
    for lane in range(0, feature, 128):
        l0 = slice(lane, lane + 128)
        l1 = slice(feature + lane, feature + lane + 128)
        l2 = slice(2 * feature + lane, 2 * feature + lane + 128)
        dq, dk, dv = attend_pair_back(pk_ref[:, l0], pk_ref[:, l1], pk_ref[:, l2], datt_ref[:, l0], None)
        dpk_ref[:, l0] = dq.astype(BF16)
        dpk_ref[:, l1] = dk.astype(BF16)
        dpk_ref[:, l2] = dv.astype(BF16)
    da = mm_t(dpk_ref[...], w_qkv[...])
    xhat, r = norm(x_ref[0].astype(F32))
    add_row(dga_ref, da * xhat)
    dx_ref[0] = (dmid + norm_back(da, xhat, r, ga[...])).astype(BF16)


def mlp_grad_kernel(bt_ref, du_ref, dyt_ref, h_ref, up_ref, down_ref):
    up_ref[0] = mm(bt_ref[...], du_ref[...]).astype(BF16)
    width = down_ref.shape[2]
    for j in range(down_ref.shape[0]):
        down_ref[j] = mm(dyt_ref[...], h_ref[:, j * width : (j + 1) * width]).astype(BF16)


def att_grad_kernel(halo, *refs):
    if halo:
        at_ref, att_t_ref, dq_ref, dk_ref, dv_ref, dm_ref, aht_ref, dkh_ref, dvh_ref, out_ref = refs
    else:
        at_ref, att_t_ref, dq_ref, dk_ref, dv_ref, dm_ref, out_ref = refs
    dq = mm(at_ref[...], dq_ref[...])
    dk = mm(at_ref[...], dk_ref[...])
    dv = mm(at_ref[...], dv_ref[...])
    if halo:
        dk = dk + mm(aht_ref[...], dkh_ref[...])
        dv = dv + mm(aht_ref[...], dvh_ref[...])
    do = mm(att_t_ref[...], dm_ref[...])
    for i, part in enumerate((dq, dk, dv, do)):
        part = part.astype(BF16)
        for j in range(2):
            out_ref[j, :, 128 * i : 128 * (i + 1)] = part[:, 128 * j : 128 * (j + 1)]


def whole(shape):
    zeros = (0,) * len(shape)
    return pl.BlockSpec(shape, lambda i: zeros)


def col_block(rows, width, offset=0):
    return pl.BlockSpec((rows, width), lambda i: (0, i + offset))


def row_block(rows, width):
    return pl.BlockSpec((rows, width), lambda i: (i, 0))


def shape_of(shape, dtype):
    return jax.ShapeDtypeStruct(shape, dtype)


def params(collective=None):
    return pltpu.CompilerParams(
        vmem_limit_bytes=VMEM_BYTES, dimension_semantics=("arbitrary",), collective_id=collective,
        has_side_effects=collective is not None,
    )


def cost(flops, nbytes):
    return pl.CostEstimate(flops=int(flops), bytes_accessed=int(nbytes), transcendentals=0)


def weight_specs(feature, hidden):
    return [
        whole((1, feature)), whole((feature, 3 * feature)), whole((feature, feature)),
        whole((1, feature)), whole((feature, hidden)), whole((hidden, feature)),
    ]


def spat_forward(x, weights):
    frames, patches, d = x.shape
    hidden = weights[4].shape[1]
    n = frames * patches
    blk = pl.BlockSpec((1, patches, d), lambda i: (i, 0, 0))
    return pl.pallas_call(
        spat_fwd_kernel,
        grid=(frames,),
        in_specs=[blk] + weight_specs(d, hidden),
        out_specs=[
            blk, col_block(d, patches), row_block(patches, 3 * d), col_block(d, patches),
            row_block(patches, d), col_block(d, patches), row_block(patches, hidden), row_block(patches, hidden),
            pl.BlockSpec(memory_space=pl.ANY),
        ],
        out_shape=[
            shape_of(x.shape, BF16), shape_of((d, n), BF16), shape_of((n, 3 * d), BF16), shape_of((d, n), BF16),
            shape_of((n, d), F32), shape_of((d, n), BF16), shape_of((n, hidden), BF16), shape_of((n, hidden), BF16),
            shape_of(x.shape, BF16),
        ],
        scratch_shapes=[
            pltpu.VMEM((patches, d), BF16), pltpu.VMEM(x.shape, BF16),
            pltpu.SemaphoreType.DMA((frames,)), pltpu.SemaphoreType.DMA((frames,)),
        ],
        compiler_params=params(1),
        cost_estimate=cost(2 * n * d * (4 * d + 2 * hidden + 2 * patches), 24 * n * d),
        name="spat_forward",
    )(x, *weights)


def temp_forward(x, halo, bias, weights, proj):
    frames, patches, d = x.shape
    hidden = weights[4].shape[1]
    n = frames * patches
    steps = patches // GROUP
    rows = frames * GROUP
    cdim = proj.shape[1]
    blk = pl.BlockSpec((frames, GROUP, d), lambda i: (0, i, 0))
    stacked = lambda width: pl.BlockSpec((frames, GROUP, width), lambda i: (i, 0, 0))
    return pl.pallas_call(
        temp_fwd_kernel,
        grid=(steps,),
        in_specs=[blk, blk, whole(bias.shape)] + weight_specs(d, hidden) + [whole(proj.shape)],
        out_specs=[
            pl.BlockSpec((frames, GROUP, cdim), lambda i: (0, i, 0)), row_block(rows, d),
            col_block(d, rows), col_block(d, rows), stacked(3 * d), stacked(2 * d), col_block(d, rows),
            row_block(rows, d), col_block(d, rows), row_block(rows, hidden), row_block(rows, hidden),
        ],
        out_shape=[
            shape_of((frames, patches, cdim), F32), shape_of((n, d), BF16),
            shape_of((d, n), BF16), shape_of((d, n), BF16),
            shape_of((frames * steps, GROUP, 3 * d), BF16), shape_of((frames * steps, GROUP, 2 * d), BF16),
            shape_of((d, n), BF16), shape_of((n, d), F32), shape_of((d, n), BF16),
            shape_of((n, hidden), BF16), shape_of((n, hidden), BF16),
        ],
        scratch_shapes=[pltpu.VMEM((frames, GROUP, d), BF16)],
        compiler_params=params(),
        cost_estimate=cost(2 * n * d * (6 * d + 2 * hidden + 2 * patches), 30 * n * d),
        name="temp_forward",
    )(x, halo, bias, *weights, proj)


def temp_backward(gl, proj, x3, x, mid, gp, pk, kvh, bias_t, weights):
    frames, patches, d = x.shape
    hidden = weights[4].shape[1]
    n = frames * patches
    steps = patches // GROUP
    rows = frames * GROUP
    cdim = proj.shape[1]
    nat = lambda width: pl.BlockSpec((frames, GROUP, width), lambda i: (0, i, 0))
    stacked = lambda width: pl.BlockSpec((frames, GROUP, width), lambda i: (i, 0, 0))
    return pl.pallas_call(
        temp_bwd_kernel,
        grid=(steps,),
        in_specs=[
            nat(cdim), whole(proj.shape), row_block(rows, d), nat(d), row_block(rows, d),
            row_block(rows, hidden), stacked(3 * d), stacked(2 * d), whole(bias_t.shape),
        ] + weight_specs(d, hidden),
        out_specs=[
            col_block(d, rows), row_block(rows, hidden), row_block(rows, d), stacked(3 * d), stacked(2 * d),
            nat(d), pl.BlockSpec(memory_space=pl.ANY), whole((1, d)), whole((1, d)), whole((cdim, d)),
        ],
        out_shape=[
            shape_of((d, n), BF16), shape_of((n, hidden), BF16), shape_of((n, d), BF16),
            shape_of((frames * steps, GROUP, 3 * d), BF16), shape_of((frames * steps, GROUP, 2 * d), BF16),
            shape_of((frames, patches, d), F32), shape_of((frames, patches, d), BF16),
            shape_of((1, d), F32), shape_of((1, d), F32), shape_of((cdim, d), F32),
        ],
        scratch_shapes=[
            pltpu.VMEM((frames, GROUP, d), BF16), pltpu.VMEM((steps, frames, GROUP, d), BF16),
            pltpu.SemaphoreType.DMA((steps,)), pltpu.SemaphoreType.DMA((steps,)),
        ],
        compiler_params=params(2),
        cost_estimate=cost(2 * n * d * (6 * d + 2 * hidden + 5 * patches), 40 * n * d),
        name="temp_backward",
    )(gl, proj, x3, x, mid, gp, pk, kvh, bias_t, *weights)


def spat_backward(base, dah, x2, gta, x, mid, gp, pk, weights):
    frames, patches, d = x.shape
    hidden = weights[4].shape[1]
    n = frames * patches
    blk = pl.BlockSpec((1, patches, d), lambda i: (i, 0, 0))
    return pl.pallas_call(
        spat_bwd_kernel,
        grid=(frames,),
        in_specs=[
            blk, blk, blk, whole((1, d)), blk, row_block(patches, d), row_block(patches, hidden),
            row_block(patches, 3 * d),
        ] + weight_specs(d, hidden),
        out_specs=[
            blk, col_block(d, patches), row_block(patches, hidden), row_block(patches, d),
            row_block(patches, 3 * d), whole((1, d)), whole((1, d)), whole((1, d)),
        ],
        out_shape=[
            shape_of(x.shape, BF16), shape_of((d, n), BF16), shape_of((n, hidden), BF16), shape_of((n, d), BF16),
            shape_of((n, 3 * d), BF16), shape_of((1, d), F32), shape_of((1, d), F32), shape_of((1, d), F32),
        ],
        scratch_shapes=[pltpu.VMEM((patches, d), BF16)],
        compiler_params=params(),
        cost_estimate=cost(2 * n * d * (4 * d + 2 * hidden + 5 * patches), 30 * n * d),
        name="spat_backward",
    )(base, dah, x2, gta, x, mid, gp, pk, *weights)


def mlp_grads(bt, du, dyt, h):
    d, n = bt.shape
    hidden = du.shape[1]
    steps = 4
    wide = hidden // steps
    return pl.pallas_call(
        mlp_grad_kernel,
        grid=(steps,),
        in_specs=[whole((d, n)), col_block(n, wide), whole((d, n)), col_block(n, wide)],
        out_specs=[
            pl.BlockSpec((1, d, wide), lambda i: (i, 0, 0)),
            pl.BlockSpec((2, d, wide // 2), lambda i: (i, 0, 0)),
        ],
        out_shape=[shape_of((steps, d, wide), BF16), shape_of((2 * steps, d, wide // 2), BF16)],
        compiler_params=params(),
        cost_estimate=cost(4 * n * d * hidden, 8 * n * d + 4 * n * hidden),
        name="mlp_grads",
    )(bt, du, dyt, h)


def att_grads(at, att_t, dpk, dmid, aht=None, dkvh=None):
    d, n = at.shape
    halo = aht is not None
    wide = 256
    args = [at, att_t, dpk, dpk, dpk, dmid]
    specs = [
        whole((d, n)), whole((d, n)), col_block(n, wide), col_block(n, wide, d // wide),
        col_block(n, wide, 2 * d // wide), col_block(n, wide),
    ]
    if halo:
        args += [aht, dkvh, dkvh]
        specs += [whole((d, n)), col_block(n, wide), col_block(n, wide, d // wide)]
    return pl.pallas_call(
        lambda *refs: att_grad_kernel(halo, *refs),
        grid=(d // wide,),
        in_specs=specs,
        out_specs=pl.BlockSpec((2, d, 512), lambda i: (i, 0, 0)),
        out_shape=shape_of((d // 128, d, 512), BF16),
        compiler_params=params(),
        cost_estimate=cost(2 * n * d * d * (6 if halo else 4), 16 * n * d),
        name="att_grads",
    )(*args)


def bits_of(count):
    bits = count.bit_length() - 1
    assert count == 1 << bits
    return bits


def swap(value, axis, bit):
    count = lax.axis_size(axis)
    return lax.ppermute(value, axis, [(i, i ^ (1 << bit)) for i in range(count)])


def my_bit(axis, bit):
    return (lax.axis_index(axis) >> bit) & 1


def reduce_pieces(grad, labels, order):
    names = []
    for axis in labels:
        names += [(axis, b) for b in reversed(range(bits_of(lax.axis_size(axis))))]
    tail = grad.shape[len(labels) :]
    cur = grad.reshape((2,) * len(names) + tail)
    for axis, bit in order:
        at = names.index((axis, bit))
        me = my_bit(axis, bit)
        kept = lax.dynamic_index_in_dim(cur, me, at, keepdims=False)
        sent = lax.dynamic_index_in_dim(cur, 1 - me, at, keepdims=False)
        cur = (kept.astype(F32) + swap(sent, axis, bit).astype(F32)).astype(BF16)
        names.pop(at)
    cur = cur[None]
    for bit in reversed(range(bits_of(lax.axis_size("batch")))):
        other = swap(cur, "batch", bit)
        low = my_bit("batch", bit) == 0
        cur = jnp.stack([jnp.where(low, cur, other), jnp.where(low, other, cur)], 1)
        cur = cur.reshape((-1,) + tail)
    return cur.astype(F32)


def orders():
    fb, bb = bits_of(lax.axis_size("frame")), bits_of(lax.axis_size("batch"))
    frame = [("frame", b) for b in [0] + list(reversed(range(1, fb)))]
    batch = [("batch", b) for b in range(bb)]
    return batch + frame, batch[:1] + frame[:1] + batch[1:] + frame[1:]


def local_general(
    frames_in, spat_gain_a, spat_qkv, spat_out, spat_gain_b, spat_up, spat_down,
    temp_gain_a, temp_qkv, temp_out, temp_gain_b, temp_up, temp_down,
    quant_proj, codebook, code_index, clip_index, dead_codes, source_rows, latent_cot,
):
    frame_count, patches, d = frames_in.shape[1:]
    cdim = quant_proj.shape[1]
    row_count = frame_count * patches
    frame_size, batch_size = lax.axis_size("frame"), lax.axis_size("batch")
    assert frame_count == SPAN
    spat = (spat_gain_a.reshape(1, d), spat_qkv, spat_out, spat_gain_b.reshape(1, d), spat_up, spat_down)
    temp = (temp_gain_a.reshape(1, d), temp_qkv, temp_out, temp_gain_b.reshape(1, d), temp_up, temp_down)
    x = frames_in[0]

    first = lax.axis_index("frame") * frame_count
    clips = jnp.concatenate([jnp.full((SPAN,), -1, jnp.int32), clip_index[0]])
    key_clips = lax.dynamic_slice_in_dim(clips, first, SPAN + frame_count)
    query_clips = key_clips[SPAN:]
    qi, qp = jnp.arange(frame_count * SUB) // SUB, jnp.arange(frame_count * SUB) % SUB
    kj, kp = jnp.arange((SPAN + frame_count) * SUB) // SUB, jnp.arange((SPAN + frame_count) * SUB) % SUB
    offset = qi[:, None] + SPAN - kj[None, :]
    allowed = (
        (qp[:, None] == kp[None, :]) & (offset >= 0) & (offset <= SPAN)
        & (jnp.repeat(query_clips, SUB)[:, None] == jnp.repeat(key_clips, SUB)[None, :])
    )
    bias = jnp.where(allowed, 0.0, NEG).astype(F32)

    x2, s_at, s_pk, s_att_t, s_mid, s_bt, s_h, s_gp, halo = spat_forward(x, spat)
    latent3, x3, t_at, t_aht, t_pk, t_kvh, t_att_t, t_mid, t_bt, t_h, t_gp = temp_forward(
        x2, halo, bias, temp, quant_proj
    )

    latent = latent3.reshape(-1, cdim)
    codes_flat = code_index.reshape(-1)
    chosen = jnp.take(codebook, codes_flat, axis=0)
    differ = latent - chosen
    commit_part = jnp.sum(differ * differ)
    grad_latent = (latent_cot.reshape(-1, cdim) + 2.0 * BETA * differ).astype(BF16)
    grad_book = jax.ops.segment_sum(-2.0 * BETA * differ, codes_flat, num_segments=codebook.shape[0])

    dyt, du, dmid, dpk, dkvh, base, dah_back, dg_ta, dg_tb, dproj = temp_backward(
        grad_latent.reshape(latent3.shape), quant_proj, x3, x2, t_mid, t_gp, t_pk, t_kvh, bias.T, temp
    )
    t_up, t_down = mlp_grads(t_bt, du, dyt, t_h)
    t_att = att_grads(
        t_at, t_att_t, dpk.reshape(row_count, -1), dmid, t_aht, dkvh.reshape(row_count, -1)
    )
    dx, dyt, du, dmid, dpk, dg_ta2, dg_sa, dg_sb = spat_backward(
        base, dah_back, x2, temp[0], x, s_mid, s_gp, s_pk, spat
    )
    s_up, s_down = mlp_grads(s_bt, du, dyt, s_h)
    s_att = att_grads(s_at, s_att_t, dpk, dmid)

    dead_match = (codes_flat[:, None] == dead_codes[None, :]).astype(F32)
    usage_part = jnp.sum(dead_match, 0)
    row_base = (lax.axis_index("batch") * frame_size + lax.axis_index("frame")) * row_count
    pick_table = ((source_rows - row_base)[:, None] == jnp.arange(row_count)[None, :]).astype(F32)
    picked = jnp.dot(pick_table, latent, precision=HIGH)
    usage_count, candidate, commit_total = lax.psum((usage_part, picked, commit_part), ("frame", "batch"))
    gain_ta, gain_tb, gain_sa, gain_sb = lax.psum(
        ((dg_ta + dg_ta2)[0], dg_tb[0], dg_sa[0], dg_sb[0]), ("frame", "batch")
    )
    old_rows = jnp.take(codebook, dead_codes, axis=0)
    fresh_rows = jnp.where((usage_count < USE_MIN)[:, None], candidate, old_rows)
    refreshed = codebook.at[dead_codes].set(fresh_rows)
    commit_loss = commit_total / (frame_size * batch_size * row_count * cdim)

    one, two = orders()
    piece = d // frame_size

    def by_rows(grad, order):
        return reduce_pieces(
            grad.reshape(batch_size, frame_size, -1, grad.shape[-1]), ("batch", "frame"), order
        )

    def finish_up(grad):
        return by_rows(grad, one).transpose(1, 0, 2).reshape(piece, -1)

    def finish_down(grad):
        hidden = grad.shape[0] * grad.shape[2]
        wide = hidden // frame_size
        if grad.shape[2] != wide:
            grad = grad.transpose(1, 0, 2).reshape(d, frame_size, wide).transpose(1, 0, 2)
        out = reduce_pieces(
            grad.reshape(frame_size, batch_size, d // batch_size, wide), ("frame", "batch"), two
        )
        return out.reshape(d, wide).T

    def finish_att(grad, order):
        out = by_rows(grad, order)
        qkv = out[:, :, :384].reshape(batch_size, piece, 3, -1).transpose(1, 2, 0, 3).reshape(piece, 3 * d)
        return qkv, out[:, :, 384:].transpose(1, 0, 2).reshape(piece, d)

    book = grad_book.reshape(frame_size, batch_size, -1, 128)
    proj = dproj.T.reshape(frame_size, batch_size, -1)
    proj_size = proj.shape[2]
    proj = jnp.pad(proj, ((0, 0), (0, 0), (0, -proj_size % 128))).reshape(frame_size, batch_size, -1, 128)
    small = jnp.concatenate([book, proj], 2).astype(BF16)
    small = reduce_pieces(small, ("frame", "batch"), two)
    book_rows = book.shape[2]
    g_book = small[:, :book_rows].reshape(-1, cdim)
    g_proj = small[:, book_rows:].reshape(batch_size, -1)[:, :proj_size].reshape(piece, cdim)
    gt_qkv, gt_out = finish_att(t_att, one)
    gs_qkv, gs_out = finish_att(s_att, one)
    return (
        latent.reshape(latent_cot.shape),
        commit_loss,
        dx[None],
        gain_sa,
        gs_qkv,
        gs_out,
        gain_sb,
        finish_up(s_up),
        finish_down(s_down),
        gain_ta,
        gt_qkv,
        gt_out,
        gain_tb,
        finish_up(t_up),
        finish_down(t_down),
        g_proj,
        g_book,
        refreshed,
    )


SIZE = {"y": 2, "c": 2, "z": 4, "x": 2}
PEERS = ({"y": 1}, {"c": 1}, {"y": 1, "c": 1}, {"x": 1}, {"z": 1}, {"z": 2}, {"z": 3})
ROWS_DIMS = ("y", "c", "z", "x")
COLS_DIMS = ("z", "x", "y", "c")
Y_FIRST = ("c", "y", "x", "z")
X_FIRST = ("c", "x", "y", "z")
WIDE = 128
TILE = 512


class Place:
    def __init__(self):
        batch, frame = lax.axis_index("batch"), lax.axis_index("frame")
        self.me = {"y": lax.div(batch, 2), "c": lax.rem(batch, 2), "z": lax.div(frame, 2), "x": lax.rem(frame, 2)}

    def next(self, dim, shift):
        return lax.rem(self.me[dim] + shift, SIZE[dim])

    def peer(self, shifts):
        at = {d: self.next(d, shifts[d]) if d in shifts else self.me[d] for d in SIZE}
        return {"batch": 2 * at["y"] + at["c"], "frame": 2 * at["z"] + at["x"]}

    def copy(self, src, dst, send, recv, shifts):
        return pltpu.make_async_remote_copy(
            src_ref=src, dst_ref=dst, send_sem=send, recv_sem=recv,
            device_id=self.peer(shifts), device_id_type=MESH,
        )

    def greet(self):
        for shifts in PEERS:
            pl.semaphore_signal(
                pltpu.get_barrier_semaphore(), inc=1, device_id=self.peer(shifts), device_id_type=MESH
            )


def sizes(dims):
    return tuple(SIZE[d] for d in dims)


class Sum:
    def __init__(self, dims, tail, order, source=None, shared=None, fixed=(), gather=True):
        self.dims, self.tail, self.order, self.source, self.shared = dims, tail, order, source, shared
        self.fixed, self.with_gather = dict(fixed), gather
        self.counts = [SIZE[d] - 1 for d in order]

    def left(self, k):
        free = [d for d in self.dims if d not in self.fixed]
        return [d for d in free if d not in self.order or self.order.index(d) > k]

    def scratch(self):
        out = []
        if self.shared is None:
            kept = self.left(0 if self.source else -1)
            out.append(pltpu.VMEM(sizes(kept) + self.tail, BF16))
        for k, count in enumerate(self.counts):
            out.append(pltpu.VMEM((count,) + sizes(self.left(k)) + self.tail, BF16))
        if self.with_gather:
            out.append(pltpu.VMEM((2, 2) + self.tail, BF16))
        copies = sum(self.counts) + 3
        out += [pltpu.SemaphoreType.DMA((copies,))] * 2
        if self.source:
            out.append(pltpu.SemaphoreType.DMA)
        return out

    def bind(self, refs, r, place):
        self.place = place
        self.src = self.source(r) if self.source else None
        self.acc = self.shared(r) if self.shared else next(refs)
        self.got = [next(refs) for _ in self.counts]
        self.all = next(refs) if self.with_gather else None
        self.send, self.recv = next(refs), next(refs)
        self.load = next(refs) if self.source else None
        return self

    def index(self, dims, k, at_k, rest=None):
        out = []
        for d in dims:
            at = self.order.index(d) if d in self.order else len(self.order)
            if d in self.fixed:
                out.append(self.fixed[d])
            elif at < k:
                out.append(self.place.me[d])
            elif at == k and d in self.order:
                out.append(at_k)
            else:
                out.append(slice(None) if rest is None else rest[d])
        return tuple(out)

    def held(self):
        if self.shared:
            return self.dims
        return self.left(0 if self.source else -1)

    def copies(self, k):
        early = k == 0 and self.source
        src, dims = (self.src, self.dims) if early else (self.acc, self.held())
        base = sum(self.counts[:k])
        for i in range(self.counts[k]):
            there = self.index(dims, k, self.place.next(self.order[k], i + 1))
            yield self.place.copy(
                src.at[there], self.got[k].at[i], self.send.at[base + i], self.recv.at[base + i], {self.order[k]: i + 1}
            )

    def keep(self):
        here = self.index(self.dims, 0, self.place.me[self.order[0]])
        return pltpu.make_async_copy(self.src.at[here], self.acc, self.load)

    def start(self, k):
        for copy in self.copies(k):
            copy.start()
        if k == 0 and self.source:
            self.keep().start()

    def finish(self, k):
        for copy in self.copies(k):
            copy.wait()
        if k == 0 and self.source:
            self.keep().wait()
        left, got, count = self.left(k), self.got[k], self.counts[k]
        total = 1
        for d in left:
            total *= SIZE[d]

        def add(i):
            rest, stride = {}, total
            for d in left:
                stride //= SIZE[d]
                rest[d] = lax.rem(lax.div(i, stride), SIZE[d])
            here = self.index(self.held(), k, self.place.me[self.order[k]], rest)
            there = tuple(rest[d] for d in left)
            if count == 1:
                self.acc[here] = self.acc[here] + got[(0,) + there]
            else:
                value = self.acc[here].astype(F32)
                for j in range(count):
                    value = value + got[(j,) + there].astype(F32)
                self.acc[here] = value.astype(BF16)

        if total == 1:
            add(0)
        else:
            lax.fori_loop(0, total, lambda i, c: (add(i), c)[1], 0)

    def move(self, k):
        self.finish(k)
        self.start(k + 1)

    def piece(self):
        return self.acc[self.index(self.held(), len(self.order), None)]

    def gathers(self):
        base = sum(self.counts)
        here = self.all.at[self.place.me["y"], self.place.me["c"]]
        for j, shifts in enumerate(PEERS[:3]):
            yield self.place.copy(here, here, self.send.at[base + j], self.recv.at[base + j], shifts)

    def gather(self):
        self.finish(len(self.order) - 1)
        self.all[self.place.me["y"], self.place.me["c"]] = self.piece()
        for copy in self.gathers():
            copy.start()

    def gathered(self, out):
        for copy in self.gathers():
            copy.wait()
        out[...] = self.all[...]


class Total:
    order = Y_FIRST

    def __init__(self, rows):
        self.rows = rows

    def scratch(self):
        copies = sum(SIZE[d] - 1 for d in self.order)
        return [
            pltpu.VMEM((self.rows, 128), F32), pltpu.VMEM((copies, self.rows, 128), F32),
            pltpu.SemaphoreType.DMA((copies,)), pltpu.SemaphoreType.DMA((copies,)),
        ]

    def bind(self, refs, r, place):
        self.place = place
        self.acc, self.got, self.send, self.recv = (next(refs) for _ in range(4))
        return self

    def copies(self, k):
        base = sum(SIZE[d] - 1 for d in self.order[:k])
        for i in range(SIZE[self.order[k]] - 1):
            at = base + i
            yield at, self.place.copy(
                self.acc, self.got.at[at], self.send.at[at], self.recv.at[at], {self.order[k]: i + 1}
            )

    def start(self, k):
        for _, copy in self.copies(k):
            copy.start()

    def finish(self, k):
        arrived = []
        for at, copy in self.copies(k):
            copy.wait()
            arrived.append(at)
        for at in arrived:
            self.acc[...] = self.acc[...] + self.got[at]

    def move(self, k):
        self.finish(k)
        self.start(k + 1)


def launch(body, name, steps, ins, outs, scratch, moves, collective, flops, limit=VMEM_BYTES):
    keys = [*ins, *outs, *scratch]
    extra = [spec for part in moves.values() for spec in part.scratch()]

    def kernel(*refs):
        r = types.SimpleNamespace(**dict(zip(keys, refs)))
        rest = iter(refs[len(keys) :])
        place = Place()
        m = types.SimpleNamespace(**{k: v.bind(rest, r, place) for k, v in moves.items()})
        body(r, m, place, pl.program_id(0))

    got = pl.pallas_call(
        kernel,
        grid=(steps,),
        in_specs=[x[1] for x in ins.values()],
        out_specs=[x[1] for x in outs.values()],
        out_shape=[x[0] for x in outs.values()],
        scratch_shapes=list(scratch.values()) + extra,
        compiler_params=pltpu.CompilerParams(
            vmem_limit_bytes=limit, dimension_semantics=("arbitrary",), collective_id=collective,
            has_side_effects=collective is not None,
        ),
        cost_estimate=cost(flops, 40 << 20),
        name=name,
    )(*[x[0] for x in ins.values()])
    return types.SimpleNamespace(**dict(zip(outs, got)))


ANY = pl.BlockSpec(memory_space=pl.ANY)


def fixed_spec(shape):
    zeros = (0,) * len(shape)
    return pl.BlockSpec(shape, lambda i: zeros, pipeline_mode=pl.Buffered(1))


def fixed(array):
    return (array, fixed_spec(array.shape))


def fixed_out(shape, dtype):
    return (shape_of(shape, dtype), fixed_spec(shape))


def part_of(first, count):
    return lambda i: jnp.clip(i - first, 0, count - 1)


def on(step, value):
    return lambda f: pl.when(step == value)(f)


def within(step, first, count):
    return lambda f: pl.when((step >= first) & (step < first + count))(f)


def split_parts(value, count):
    out = []
    for _ in range(count):
        low = value.astype(BF16)
        out.append(low)
        value = value - low.astype(F32)
    return out


def code_masks(codes, rows):
    major = lax.div(codes, 128)
    minor = codes - 128 * major
    return major, jnp.where(lax.broadcasted_iota(jnp.int32, (128, codes.shape[1]), 0) == minor, 1.0, 0.0).astype(BF16)


def spat_forward_step(r, m, place, step):
    frames = r.keep.shape[0]
    d = r.x.shape[-1]
    left, right = greet_ring(step)

    @pl.when(step < frames)
    def _():
        x = r.x[0].astype(F32)
        xhat, _ = norm(x)
        a = (xhat * r.ga[...]).astype(BF16)
        r.at[...] = a.T
        for start in range(0, 3 * d, 512):
            r.pk[:, start : start + 512] = mm(a, r.w_qkv[:, start : start + 512]).astype(BF16)
        for lane in range(0, d, 128):
            cols = [slice(part * d + lane, part * d + lane + 128) for part in range(3)]
            r.att[:, cols[0]] = attend_pair(*[r.pk[:, c] for c in cols], None)
        att = r.att[...]
        r.att_t[...] = att.T
        mid = x + mm(att, r.w_out[...])
        r.mid[...] = mid
        y = mlp_forward(mid, r.gb[...], r.w_up, r.w_down, r.bt, r.h, r.gp).astype(BF16)
        r.y[0] = y
        r.keep[step] = y

    meet_ring(step)

    def copy(i):
        return ring_copy(r.keep.at[i], r.halo.at[i], r.send.at[i], r.recv.at[i], right)

    @pl.when(step < frames)
    def _():
        copy(step).start()

    @on(step, frames)
    def _():
        codes = r.codes[...]
        cdim, count = r.book.shape
        major, onehot = code_masks(codes, count // 128)
        both = jnp.concatenate([onehot, onehot], 0)
        total = jnp.zeros(r.chosen.shape, F32)
        for first in range(0, count // 128, 8):
            book = jnp.concatenate([r.book[:, 128 * a : 128 * (a + 1)] for a in range(first, first + 8)], 0)
            found = mm(jnp.concatenate(split_parts(book, 2), 1), both)
            for i in range(8):
                total = total + jnp.where(major == first + i, found[cdim * i : cdim * (i + 1)], 0.0)
        r.chosen[...] = total
        for i in range(frames):
            copy(i).wait()


def spat_forward_call(x, weights, codes, book_t):
    frames, patches, d = x.shape
    hidden = weights[4].shape[1]
    n = frames * patches
    at = part_of(0, frames)
    blk = pl.BlockSpec((1, patches, d), lambda i: (at(i), 0, 0))
    cols = pl.BlockSpec((d, patches), lambda i: (0, at(i)))
    rows = lambda width: pl.BlockSpec((patches, width), lambda i: (at(i), 0))
    ga, w_qkv, w_out, gb, w_up, w_down = weights
    wide = lambda width, dtype=BF16: (shape_of((n, width), dtype), rows(width))
    tall = (shape_of((d, n), BF16), cols)
    return launch(
        spat_forward_step, "spat_forward", frames + 1,
        dict(
            x=(x, blk), ga=fixed(ga), w_qkv=fixed(w_qkv), w_out=fixed(w_out), gb=fixed(gb), w_up=fixed(w_up),
            w_down=fixed(w_down), codes=fixed(codes), book=fixed(book_t),
        ),
        dict(
            y=(shape_of(x.shape, BF16), blk), at=tall, pk=wide(3 * d), att_t=tall, mid=wide(d, F32), bt=tall,
            h=wide(hidden), gp=wide(hidden), halo=(shape_of(x.shape, BF16), ANY),
            chosen=fixed_out((book_t.shape[0], n), F32),
        ),
        dict(
            att=pltpu.VMEM((patches, d), BF16), keep=pltpu.VMEM(x.shape, BF16),
            send=pltpu.SemaphoreType.DMA((frames,)), recv=pltpu.SemaphoreType.DMA((frames,)),
        ),
        {}, 11, 2 * n * d * (4 * d + 2 * hidden + 2 * patches),
    )


def temp_forward_step(r, m, place, step):
    frames, group, d = r.x.shape
    rows = frames * group
    x = r.x[...].reshape(rows, d).astype(F32)
    xhat, _ = norm(x)
    a = (xhat * r.ga[...]).astype(BF16)
    r.at[...] = a.T
    for start in range(0, 3 * d, 512):
        part = mm(a, r.w_qkv[:, start : start + 512]).astype(BF16)
        r.pk[:, :, start : start + 512] = part.reshape(frames, group, 512)
    xhat_h, _ = norm(r.halo[...].reshape(rows, d).astype(F32))
    ah = (xhat_h * r.ga[...]).astype(BF16)
    r.aht[...] = ah.T
    for start in range(0, 2 * d, 512):
        part = mm(ah, r.w_qkv[:, d + start : d + start + 512]).astype(BF16)
        r.kvh[:, :, start : start + 512] = part.reshape(frames, group, 512)
    bias = r.bias[...]
    for sub in range(0, group, SUB):
        here = slice(sub, sub + SUB)
        for lane in range(0, d, 128):
            c0, c1, c2 = (slice(part * d + lane, part * d + lane + 128) for part in range(3))
            q = r.pk[:, here, c0].reshape(frames * SUB, 128)
            k = jnp.concatenate([r.kvh[:, here, c0], r.pk[:, here, c1]], 0).reshape(2 * frames * SUB, 128)
            v = jnp.concatenate([r.kvh[:, here, c1], r.pk[:, here, c2]], 0).reshape(2 * frames * SUB, 128)
            r.att[:, here, c0] = attend_pair(q, k, v, bias).reshape(frames, SUB, 128)
    att = r.att[...].reshape(rows, d)
    r.att_t[...] = att.T
    mid = x + mm(att, r.w_out[...])
    r.mid[...] = mid
    y = mlp_forward(mid, r.gb[...], r.w_up, r.w_down, r.bt, r.h, r.gp).astype(BF16)
    r.x3[...] = y
    for f in range(frames):
        r.lat[f] = mm_t(r.proj[...], y[f * group : (f + 1) * group])


def temp_forward_call(x, halo, bias, weights, proj_t):
    frames, patches, d = x.shape
    hidden = weights[4].shape[1]
    n = frames * patches
    steps = patches // WIDE
    rows = frames * WIDE
    cdim = proj_t.shape[0]
    blk = pl.BlockSpec((frames, WIDE, d), lambda i: (0, i, 0))
    ga, w_qkv, w_out, gb, w_up, w_down = weights
    tall = (shape_of((d, n), BF16), pl.BlockSpec((d, rows), lambda i: (0, i)))
    wide = lambda width, dtype=BF16: (shape_of((n, width), dtype), row_block(rows, width))
    deep = lambda width: (
        shape_of((frames * steps, WIDE, width), BF16), pl.BlockSpec((frames, WIDE, width), lambda i: (i, 0, 0))
    )
    return launch(
        temp_forward_step, "temp_forward", steps,
        dict(
            x=(x, blk), halo=(halo, blk), bias=fixed(bias), ga=fixed(ga), w_qkv=fixed(w_qkv), w_out=fixed(w_out),
            gb=fixed(gb), w_up=fixed(w_up), w_down=fixed(w_down), proj=fixed(proj_t),
        ),
        dict(
            lat=(shape_of((frames, cdim, patches), F32), pl.BlockSpec((frames, cdim, WIDE), lambda i: (0, 0, i))),
            x3=wide(d), at=tall, aht=tall, pk=deep(3 * d), kvh=deep(2 * d), att_t=tall, mid=wide(d, F32), bt=tall,
            h=wide(hidden), gp=wide(hidden),
        ),
        dict(att=pltpu.VMEM((frames, WIDE, d), BF16)),
        {}, None, 2 * n * d * (6 * d + 2 * hidden + 2 * patches),
    )


class Fetch:
    def __init__(self, r, names):
        self.pairs = [(getattr(r, n), getattr(r, n + "_")) for n in names]
        self.sem = r.fetch

    def copy(self, i):
        return pltpu.make_async_copy(*self.pairs[i], self.sem.at[i])

    def start(self):
        for i in range(len(self.pairs)):
            self.copy(i).start()

    def wait(self, *which):
        for i in which:
            self.copy(i).wait()


def mlp_tile(r, put_up, put_down):
    lead, per, d = r.db.shape
    for i in range(4):
        rows = slice(i * 256, (i + 1) * 256)
        these = slice(i * lead // 4, (i + 1) * lead // 4)
        dh = mm_t(r.dy[rows, :], r.w_down[...])
        du = (r.gp[rows, :].astype(F32) * dh).astype(BF16)
        r.du[rows, :] = du
        r.db[these] += mm_t(du, r.w_up[...]).reshape(lead // 4, per, d)
    put_up(mm(r.bt_[...], r.du[...]).astype(BF16))
    for i in range(2):
        put_down(i, mm(r.dyt[...], r.h[:, i * 256 : (i + 1) * 256]).astype(BF16))


def middle(r, put):
    lead, per, d = r.db.shape
    for i in range(4):
        rows = slice(i * 256, (i + 1) * 256)
        these = slice(i * lead // 4, (i + 1) * lead // 4)
        xhat, rs = norm(r.mid_[rows, :])
        db = r.db[these].reshape(256, d)
        add_row(r.dg_b, db * xhat)
        dmid = r.dy[rows, :].astype(F32) + norm_back(db, xhat, rs, r.gb[...])
        r.db[these] = dmid.reshape(lead // 4, per, d)
        low = dmid.astype(BF16)
        put(i, low, mm_t(low, r.w_out_[...]).astype(BF16))


T_MLP, T_MID, T_ATT, T_GRAD = 1, 5, 6, 10


def temp_backward_step(r, m, place, step):
    frames, group, d = r.x.shape
    cdim, n = r.chosen.shape
    rows = frames * group
    left, right = greet_ring(step)
    fetch = Fetch(r, ("bt", "mid", "w_out", "w_qkv", "at", "aht", "att_t"))

    @on(step, 0)
    def _():
        place.greet()
        fetch.start()
        for ref in (r.dg_a, r.dg_b, r.db, m.q.acc):
            ref[...] = jnp.zeros_like(ref)
        patches = r.lat.shape[2]
        commit = jnp.zeros((1, 1), F32)
        for f in range(frames):
            here = slice(f * patches, (f + 1) * patches)
            differ = r.lat[f] - r.chosen[:, here]
            commit = commit + jnp.sum(jnp.sum(differ * differ, 1, keepdims=True), 0, keepdims=True)
            grad = (r.cot[f] + (2.0 * BETA) * differ).astype(BF16)
            for g in range(patches // WIDE):
                to = (g * frames + f) * WIDE
                r.gl[:, to : to + WIDE] = grad[:, g * WIDE : (g + 1) * WIDE]
            r.dbook[:, here] = ((-2.0 * BETA) * differ).astype(BF16)
        for i in range(4):
            part = slice(i * 256, (i + 1) * 256)
            r.dy[part, :] = t_mm(r.gl[:, part], r.proj[...]).astype(BF16)
        r.dyt[...] = t_mm(r.proj[...], r.gl[...]).astype(BF16)
        dproj = mm(r.gl[...], r.x3[...])
        for j in range(d // 128):
            m.q.acc[cdim * j : cdim * (j + 1), :] = dproj[:, 128 * j : 128 * (j + 1)]
        codes = r.codes[...]
        major, onehot = code_masks(codes, 64)
        dbook = r.dbook[...]
        for z in range(4):
            for x in range(2):
                first = 8 * (2 * z + x)
                picked = [jnp.where(major == first + i, dbook, jnp.zeros((), BF16)) for i in range(8)]
                book = mm_t(jnp.concatenate(picked, 0), onehot).astype(BF16)
                m.d.acc[z, x] = book.reshape(m.d.acc.shape[2:])
        dead = r.dead.shape[0]
        used = jnp.where(r.dead[...] == codes, 1.0, 0.0).astype(BF16)
        usage = mm_t(jnp.ones((8, n), BF16), used)
        pick = jnp.where(r.source[...] == lax.broadcasted_iota(jnp.int32, (dead, n), 1), 1.0, 0.0).astype(BF16)
        latent = jnp.concatenate([r.lat[f] for f in range(frames)], 1)
        candidate = jnp.zeros((cdim, dead), F32)
        for part in split_parts(latent, 3):
            candidate = candidate + mm_t(part, pick)
        m.q.acc[d // 128 * cdim : d // 128 * cdim + cdim, :dead] = candidate
        m.q.acc[d // 128 * cdim + cdim :, :dead] = usage
        m.q.acc[d // 128 * cdim + cdim :, dead:] = jnp.broadcast_to(commit, (8, 128 - dead))

    @on(step, T_MLP)
    def _():
        fetch.wait(0)

    @within(step, T_MLP, 4)
    def _():
        j = step - T_MLP

        def put_up(value):
            m.a.acc[lax.div(j, 2), lax.rem(j, 2)] = value.reshape(m.a.acc.shape[2:])

        def put_down(i, value):
            m.b.acc[j, i] = value.reshape(m.b.acc.shape[2:])

        mlp_tile(r, put_up, put_down)

    @on(step, T_MID)
    def _():
        fetch.wait(1, 2)

        def put(i, low, datt):
            for t in range(2):
                r.dm[t, 2 * i : 2 * i + 2] = low[:, 256 * t : 256 * (t + 1)].reshape(2, WIDE, 256)
            r.datt[2 * i : 2 * i + 2] = datt.reshape(2, WIDE, d)

        middle(r, put)
        fetch.wait(3)

    @within(step, T_ATT, 4)
    def _():
        s = step - T_ATT
        lead = pl.ds(pl.multiple_of(frames * lax.div(s, 2), frames), frames)
        side = lax.rem(s, 2) * group
        here = pl.ds(pl.multiple_of(side, group), group)
        bias = r.bias[...]
        half = frames * SUB
        for sub in range(0, group, SUB):
            near = slice(sub, sub + SUB)
            far = pl.ds(pl.multiple_of(side + sub, SUB), SUB)
            for lane in range(0, d, 128):
                c0, c1, c2 = (slice(part * d + lane, part * d + lane + 128) for part in range(3))
                q = r.pk[:, near, c0].reshape(half, 128)
                k = jnp.concatenate([r.kvh[:, near, c0], r.pk[:, near, c1]], 0).reshape(2 * half, 128)
                v = jnp.concatenate([r.kvh[:, near, c1], r.pk[:, near, c2]], 0).reshape(2 * half, 128)
                do = r.datt[lead, far, c0].reshape(half, 128)
                dq, dk, dv = attend_pair_back(q, k, v, do, bias)
                tile, to = lane // 256, slice(lane % 256, lane % 256 + 128)
                for part, grad in enumerate((dq, dk[half:], dv[half:])):
                    r.dpk[2 * part + tile, lead, far, to] = grad.astype(BF16).reshape(frames, SUB, 128)
                for part, grad in enumerate((dk[:half], dv[:half])):
                    r.dkvh[2 * part + tile, lead, far, to] = grad.astype(BF16).reshape(frames, SUB, 128)
        da = jnp.zeros((rows, d), F32)
        for i in range(6):
            da = da + mm_t(r.dpk[i, lead, here, :].reshape(rows, 256), r.w_qkv_[:, 256 * i : 256 * (i + 1)])
        dah = jnp.zeros((rows, d), F32)
        for i in range(4):
            dah = dah + mm_t(r.dkvh[i, lead, here, :].reshape(rows, 256), r.w_qkv_[:, d + 256 * i : d + 256 * (i + 1)])
        r.dah[s] = dah.astype(BF16).reshape(frames, group, d)
        xhat, rs = norm(r.x[...].reshape(rows, d).astype(F32))
        add_row(r.dg_a, da * xhat)
        dmid = r.db[lead, here, :].reshape(rows, d)
        r.base[...] = (dmid + norm_back(da, xhat, rs, r.ga[...])).reshape(frames, group, d)

    def copy(i):
        there = r.back.at[:, pl.ds(i * group, group), :]
        return ring_copy(r.dah.at[i], there, r.send.at[i], r.recv.at[i], left)

    @on(step, T_GRAD)
    def _():
        fetch.wait(4, 5, 6)

    @within(step, T_GRAD, 2)
    def _():
        t = step - T_GRAD
        whole_rows = lambda value: value.reshape(n, 256)
        a, ah, att = r.at_[...], r.aht_[...], r.att_t_[...]
        parts = (
            mm(a, whole_rows(r.dpk[t])),
            mm(a, whole_rows(r.dpk[2 + t])) + mm(ah, whole_rows(r.dkvh[t])),
            mm(a, whole_rows(r.dpk[4 + t])) + mm(ah, whole_rows(r.dkvh[2 + t])),
            mm(att, whole_rows(r.dm[t])),
        )
        for kind, part in enumerate(parts):
            part = part.astype(BF16)
            for j in range(2):
                r.t_att[0, j, :, :, :, 128 * kind : 128 * (kind + 1)] = part[:, 128 * j : 128 * (j + 1)].reshape(
                    r.t_att.shape[2:5] + (128,)
                )

    @on(step, 0)
    def _():
        pl.semaphore_wait(pltpu.get_barrier_semaphore(), len(PEERS) + 2)
        m.d.start(0)
        m.q.start(0)

    for k in range(3):

        @on(step, 1 + k)
        def _(k=k):
            m.d.move(k)
            m.q.move(k)

    @on(step, 4)
    def _():
        m.a.start(0)
        m.b.start(0)
        m.d.gather()
        m.q.finish(3)

    @on(step, 5)
    def _():
        m.a.move(0)
        m.b.move(0)

    @within(step, T_ATT, 4)
    def _():
        copy(step - T_ATT).start()

    @on(step, T_GRAD + 1)
    def _():
        m.d.gathered(r.d_all)
        r.q_all[...] = m.q.acc[...]
        for part, out in ((m.a, r.a_part), (m.b, r.b_part)):
            part.finish(1)
            out[...] = part.piece()
        for i in range(r.dah.shape[0]):
            copy(i).wait()


def temp_backward_call(f, lat, cot_t, chosen, codes, dead, source, proj_t, x, bias_t, weights):
    frames, patches, d = x.shape
    ga, w_qkv, w_out, gb, w_up, w_down = weights
    hidden = w_up.shape[1]
    n = frames * patches
    cdim = proj_t.shape[0]
    lead = n // WIDE
    mlp, att, grad = part_of(T_MLP, 4), part_of(T_ATT, 4), part_of(T_GRAD, 2)
    natural = pl.BlockSpec((frames, GROUP, d), lambda i: (0, att(i), 0))
    tile = pl.BlockSpec((n, TILE), lambda i: (0, mlp(i)))
    deep = lambda width: pl.BlockSpec((frames, GROUP, width), lambda i: (att(i) // 2, att(i) % 2, 0))
    row_tail, col_tail, book_tail = (d // 8, TILE), (d // 4, hidden // 8), (2 * cdim, 128)
    early = d // 128 * cdim + cdim + 8
    vmem = lambda array: pltpu.VMEM(array.shape, array.dtype)
    moves = dict(
        a=Sum(ROWS_DIMS, row_tail, ("c", "y"), gather=False), b=Sum(COLS_DIMS, col_tail, ("c", "y"), gather=False),
        d=Sum(COLS_DIMS, book_tail, Y_FIRST), q=Total(early),
    )
    return launch(
        temp_backward_step, "temp_backward", 12,
        dict(
            lat=fixed(lat), cot=fixed(cot_t), chosen=fixed(chosen), codes=fixed(codes), dead=fixed(dead),
            source=fixed(source), proj=fixed(proj_t), x3=fixed(f.x3), x=(x, natural), gp=(f.gp, tile), h=(f.h, tile),
            pk=(f.pk, deep(3 * d)), kvh=(f.kvh, deep(2 * d)), bias=fixed(bias_t), ga=fixed(ga), gb=fixed(gb),
            w_up=(w_up, pl.BlockSpec((d, TILE), lambda i: (0, mlp(i)))),
            w_down=(w_down, pl.BlockSpec((TILE, d), lambda i: (mlp(i), 0))),
            bt=(f.bt, ANY), mid=(f.mid, ANY), w_out=(w_out, ANY), w_qkv=(w_qkv, ANY), at=(f.at, ANY),
            aht=(f.aht, ANY), att_t=(f.att_t, ANY),
        ),
        dict(
            base=(shape_of(x.shape, F32), natural), back=(shape_of(x.shape, BF16), ANY),
            dg_a=fixed_out((1, d), F32), dg_b=fixed_out((1, d), F32),
            t_att=(
                shape_of((2, 2, 4, 2, d // 8, d), BF16),
                pl.BlockSpec((1, 2, 4, 2, d // 8, d), lambda i: (grad(i), 0, 0, 0, 0, 0)),
            ),
            a_part=fixed_out((4, 2) + row_tail, BF16), b_part=fixed_out((4, 2) + col_tail, BF16),
            d_all=fixed_out((2, 2) + book_tail, BF16), q_all=fixed_out((early, 128), F32),
        ),
        dict(
            gl=pltpu.VMEM((cdim, n), BF16), dbook=pltpu.VMEM((cdim, n), BF16), dy=pltpu.VMEM((n, d), BF16),
            dyt=pltpu.VMEM((d, n), BF16), du=pltpu.VMEM((n, TILE), BF16), db=pltpu.VMEM((lead, WIDE, d), F32),
            dm=pltpu.VMEM((2, lead, WIDE, 256), BF16), datt=pltpu.VMEM((lead, WIDE, d), BF16),
            dpk=pltpu.VMEM((6, lead, WIDE, 256), BF16), dkvh=pltpu.VMEM((4, lead, WIDE, 256), BF16),
            dah=pltpu.VMEM((patches // GROUP, frames, GROUP, d), BF16),
            send=pltpu.SemaphoreType.DMA((patches // GROUP,)), recv=pltpu.SemaphoreType.DMA((patches // GROUP,)),
            fetch=pltpu.SemaphoreType.DMA((7,)), bt_=vmem(f.bt), mid_=vmem(f.mid), w_out_=vmem(w_out),
            w_qkv_=vmem(w_qkv), at_=vmem(f.at), aht_=vmem(f.aht), att_t_=vmem(f.att_t),
        ),
        moves, 12, 4 * n * d * (6 * d + 2 * hidden) + 10 * n * d * patches,
    )


S_MLP, S_MID, S_ATT, S_END = 1, 5, 6, 10


def spat_backward_step(r, m, place, step):
    frames, patches, d = r.x.shape
    n = frames * patches
    fetch = Fetch(r, ("bt", "mid", "w_out", "att_t", "at"))

    @on(step, 0)
    def _():
        place.greet()
        fetch.start()
        for ref in (r.dg_t, r.dg_a, r.dg_b, r.db, r.da):
            ref[...] = jnp.zeros_like(ref)
        for f in range(frames):
            xhat, rs = norm(r.x2[f].astype(F32))
            dah = r.dah[f].astype(F32)
            add_row(r.dg_t, dah * xhat)
            low = (r.base[f] + norm_back(dah, xhat, rs, r.gta[...])).astype(BF16)
            here = slice(f * patches, (f + 1) * patches)
            r.dy[here, :] = low
            r.dyt[:, here] = low.T

    @on(step, S_MLP)
    def _():
        fetch.wait(0)

    @within(step, S_MLP, 4)
    def _():
        j = step - S_MLP

        def put_up(value):
            r.e_acc[lax.div(j, 2), lax.rem(j, 2)] = value.reshape(r.e_acc.shape[2:])

        def put_down(i, value):
            m.g.acc[j, i] = value.reshape(m.g.acc.shape[2:])

        mlp_tile(r, put_up, put_down)

    @on(step, S_MID)
    def _():
        fetch.wait(1, 2)

        def put(i, low, datt):
            rows = slice(i * 256, (i + 1) * 256)
            r.dm[rows, :] = low
            for p in range(d // 128):
                r.datt[p, rows, :] = datt[:, 128 * p : 128 * (p + 1)]

        middle(r, put)
        fetch.wait(3)
        grad = mm(r.att_t_[...], r.dm[...]).astype(BF16)
        for q in range(4):
            r.h_acc[q // 2, 1, q % 2, :, :, :, :, 128:] = grad[:, 128 * q : 128 * (q + 1)].reshape(
                r.h_acc.shape[3:7] + (128,)
            )
        fetch.wait(4)

    @within(step, S_ATT, 4)
    def _():
        p = step - S_ATT
        for f in range(frames):
            here = slice(f * patches, (f + 1) * patches)
            grads = attend_pair_back(r.q[here, :], r.k[here, :], r.v[here, :], r.datt[p, here, :], None)
            for part, grad in enumerate(grads):
                r.dpk[here, 128 * part : 128 * (part + 1)] = grad.astype(BF16)
        grad = mm(r.at_[...], r.dpk[...]).astype(BF16)
        u, c = lax.div(p, 2), lax.rem(p, 2)
        shape = r.h_acc.shape[3:7]
        r.h_acc[u, 0, c] = grad[:, :256].reshape(shape + (256,))
        r.h_acc[u, 1, c, :, :, :, :, :128] = grad[:, 256:].reshape(shape + (128,))
        weights = jnp.concatenate([r.w_q[...], r.w_k[...], r.w_v[...]], 1)
        for f in range(frames):
            r.da[f] += mm_t(r.dpk[f * patches : (f + 1) * patches, :], weights)

    @on(step, S_END)
    def _():
        for f in range(frames):
            xhat, rs = norm(r.x[f].astype(F32))
            da = r.da[f]
            add_row(r.dg_a, da * xhat)
            r.dx[f] = (r.db[f] + norm_back(da, xhat, rs, r.ga[...])).astype(BF16)
        gains = (r.dg_t[...] + r.dgt_own[...], r.dgt_mid[...], r.dg_a[...], r.dg_b[...])
        for i, gain in enumerate(gains):
            for j in range(d // 128):
                row = i * (d // 128) + j
                m.w.acc[row : row + 1, :] = gain[:, 128 * j : 128 * (j + 1)]

    first, second = (m.h0a, m.h0b), (m.h1a, m.h1b)

    def each(parts, what, k):
        for part in parts:
            getattr(part, what)(k)

    start = lambda k, *parts: [part.start(k) for part in parts]
    move = lambda k, *parts: [part.move(k) for part in parts]
    gather = lambda *parts: [part.gather() for part in parts]

    @on(step, 0)
    def _():
        pl.semaphore_wait(pltpu.get_barrier_semaphore(), len(PEERS))
        start(0, m.a, m.b, m.c)

    @on(step, 1)
    def _():
        move(0, m.c)

    @on(step, 2)
    def _():
        start(0, m.e0)

    @on(step, 3)
    def _():
        move(0, m.a, m.b)
        move(0, m.e0)

    @on(step, 4)
    def _():
        move(1, m.c)
        start(0, m.e1, m.g)

    @on(step, 5)
    def _():
        move(1, m.e0)
        move(0, m.e1, m.g)

    @on(step, 6)
    def _():
        gather(m.a, m.b)
        move(2, m.c)
        move(2, m.e0)

    @on(step, 7)
    def _():
        start(0, *first)
        gather(m.e0)

    @on(step, 8)
    def _():
        move(1, m.e1, m.g)
        move(0, *first)
        gather(m.c)

    @on(step, 9)
    def _():
        start(0, *second)
        move(1, *first)
        move(2, m.e1, m.g)

    @on(step, 10)
    def _():
        move(0, *second)
        start(0, m.w)
        move(2, *first)

    @on(step, 11)
    def _():
        move(0, m.w)
        move(1, *second)
        move(1, m.w)
        gather(m.e1, m.g)
        move(2, *second)
        move(2, m.w)
        gather(*first)
        m.w.finish(3)
        gather(*second)
        outs = (
            (m.a, r.a_all), (m.b, r.b_all), (m.c, r.c_all), (m.e0, r.e0_all), (m.e1, r.e1_all), (m.g, r.g_all),
            (m.h0a, r.h00_all), (m.h0b, r.h01_all), (m.h1a, r.h10_all), (m.h1b, r.h11_all),
        )
        for part, out in outs:
            part.gathered(out)
        r.w_all[...] = m.w.acc[...]


def spat_backward_call(f, t, x2, gta, x, weights):
    frames, patches, d = x.shape
    ga, w_qkv, w_out, gb, w_up, w_down = weights
    hidden = w_up.shape[1]
    n = frames * patches
    mlp, att = part_of(S_MLP, 4), part_of(S_ATT, 4)
    tile = pl.BlockSpec((n, TILE), lambda i: (0, mlp(i)))
    heads = lambda rows, part: pl.BlockSpec((rows, 128), lambda i: (0, att(i) + part * (d // 128)))
    row_tail, col_tail = (d // 8, TILE), (d // 4, hidden // 8)
    half_tail, quarter_tail = (d // 16, TILE), (d // 16, 256)
    e_dims, h_dims = ("u", "c", "z", "x", "y"), ("u", "w", "c", "z", "x", "y")
    e_acc, h_acc = (lambda r: r.e_acc), (lambda r: r.h_acc)
    vmem = lambda array: pltpu.VMEM(array.shape, array.dtype)
    moves = dict(
        a=Sum(("z", "x"), row_tail, ("x", "z"), source=lambda r: r.a_part),
        b=Sum(("z", "x"), col_tail, ("x", "z"), source=lambda r: r.b_part),
        c=Sum(ROWS_DIMS, (d // 8, d), Y_FIRST, source=lambda r: r.t_att),
        e0=Sum(e_dims, half_tail, Y_FIRST, shared=e_acc, fixed={"u": 0}),
        e1=Sum(e_dims, half_tail, Y_FIRST, shared=e_acc, fixed={"u": 1}),
        g=Sum(COLS_DIMS, col_tail, X_FIRST),
        h0a=Sum(h_dims, quarter_tail, Y_FIRST, shared=h_acc, fixed={"u": 0, "w": 0}),
        h0b=Sum(h_dims, quarter_tail, X_FIRST, shared=h_acc, fixed={"u": 0, "w": 1}),
        h1a=Sum(h_dims, quarter_tail, Y_FIRST, shared=h_acc, fixed={"u": 1, "w": 0}),
        h1b=Sum(h_dims, quarter_tail, X_FIRST, shared=h_acc, fixed={"u": 1, "w": 1}),
        w=Total(4 * d // 128),
    )
    pieces = lambda tail: fixed_out((2, 2) + tail, BF16)
    return launch(
        spat_backward_step, "spat_backward", 12,
        dict(
            base=fixed(t.base), dah=fixed(t.back), x2=fixed(x2), gta=fixed(gta), x=fixed(x), gp=(f.gp, tile),
            h=(f.h, tile), q=(f.pk, heads(n, 0)), k=(f.pk, heads(n, 1)), v=(f.pk, heads(n, 2)),
            w_q=(w_qkv, heads(d, 0)), w_k=(w_qkv, heads(d, 1)), w_v=(w_qkv, heads(d, 2)), ga=fixed(ga), gb=fixed(gb),
            w_up=(w_up, pl.BlockSpec((d, TILE), lambda i: (0, mlp(i)))),
            w_down=(w_down, pl.BlockSpec((TILE, d), lambda i: (mlp(i), 0))),
            dgt_own=fixed(t.dg_a), dgt_mid=fixed(t.dg_b), bt=(f.bt, ANY), mid=(f.mid, ANY), w_out=(w_out, ANY),
            att_t=(f.att_t, ANY), at=(f.at, ANY), a_part=(t.a_part, ANY), b_part=(t.b_part, ANY), t_att=(t.t_att, ANY),
        ),
        dict(
            dx=fixed_out(x.shape, BF16), a_all=pieces(row_tail), b_all=pieces(col_tail), c_all=pieces((d // 8, d)),
            e0_all=pieces(half_tail), e1_all=pieces(half_tail), g_all=pieces(col_tail), h00_all=pieces(quarter_tail),
            h01_all=pieces(quarter_tail), h10_all=pieces(quarter_tail), h11_all=pieces(quarter_tail),
            w_all=fixed_out((4 * d // 128, 128), F32),
        ),
        dict(
            dg_t=pltpu.VMEM((1, d), F32), dg_a=pltpu.VMEM((1, d), F32), dg_b=pltpu.VMEM((1, d), F32),
            dy=pltpu.VMEM((n, d), BF16), dyt=pltpu.VMEM((d, n), BF16), du=pltpu.VMEM((n, TILE), BF16),
            db=pltpu.VMEM(x.shape, F32), da=pltpu.VMEM(x.shape, F32), dm=pltpu.VMEM((n, d), BF16),
            datt=pltpu.VMEM((d // 128, n, 128), BF16), dpk=pltpu.VMEM((n, 384), BF16),
            e_acc=pltpu.VMEM((2, 2, 4, 2, 2) + half_tail, BF16), h_acc=pltpu.VMEM((2, 2, 2, 4, 2, 2) + quarter_tail, BF16),
            fetch=pltpu.SemaphoreType.DMA((5,)), bt_=vmem(f.bt), mid_=vmem(f.mid), w_out_=vmem(w_out),
            att_t_=vmem(f.att_t), at_=vmem(f.at),
        ),
        moves, 13, 4 * n * d * (4 * d + 2 * hidden) + 10 * n * d * patches, TAIL_BYTES,
    )


def finish_step(r, m, place, step):
    d = r.t_out.shape[1]
    half = d // 16
    for y in range(2):
        for c in range(2):
            q = 2 * y + c
            lanes = slice(128 * q, 128 * (q + 1))
            wide = slice(TILE * q, TILE * (q + 1))
            r.t_up[:, wide] = r.a_all[y, c].astype(F32)
            r.t_down[:, lanes] = r.b_all[y, c].astype(F32).T
            r.s_down[:, lanes] = r.g_all[y, c].astype(F32).T
            value = r.c_all[y, c].astype(F32)
            for kind in range(3):
                r.t_qkv[:, d * kind + 128 * q : d * kind + 128 * (q + 1)] = value[:, 128 * kind : 128 * (kind + 1)]
            r.t_out[:, lanes] = value[:, 384:]
            book = r.d_all[y, c].astype(F32)
            cdim = book.shape[0] // 2
            for i in range(2):
                r.book_grad[:, 128 * (2 * q + i) : 128 * (2 * q + i + 1)] = book[cdim * i : cdim * (i + 1)]
            rows = slice(half * y, half * (y + 1))
            for u, up, left, right in ((0, r.e0_all, r.h00_all, r.h01_all), (1, r.e1_all, r.h10_all, r.h11_all)):
                at = 2 * u + c
                r.s_up[rows, TILE * at : TILE * (at + 1)] = up[y, c].astype(F32)
                pair, other = left[y, c].astype(F32), right[y, c].astype(F32)
                for kind, part in enumerate((pair[:, :128], pair[:, 128:], other[:, :128])):
                    r.s_qkv[rows, d * kind + 128 * at : d * kind + 128 * (at + 1)] = part
                r.s_out[rows, 128 * at : 128 * (at + 1)] = other[:, 128:]
    for i, gain in enumerate((r.g_ta, r.g_tb, r.g_sa, r.g_sb)):
        for j in range(d // 128):
            row = i * (d // 128) + j
            gain[:, 128 * j : 128 * (j + 1)] = r.w_all[row : row + 1, :]
    frame = lax.axis_index("frame")
    proj = r.q_all[pl.ds(pl.multiple_of(lax.div(frame, 2) * cdim, cdim), cdim), :]
    r.proj_grad[...] = jnp.where(lax.rem(frame, 2) == 0, proj[:, :64], proj[:, 64:])
    first = d // 128 * cdim
    dead = r.dead_row.shape[1]
    candidate = r.q_all[first : first + cdim, :dead]
    low = r.q_all[first + cdim : first + cdim + 1, :dead] < USE_MIN
    r.commit[...] = r.q_all[first + cdim : first + cdim + 1, dead : dead + 1] * (1.0 / r.scale)
    major = lax.div(r.dead_row[...], 128)
    minor = lax.rem(r.dead_col[...], 128)
    onehot = jnp.where(lax.broadcasted_iota(jnp.int32, (dead, 128), 1) == minor, 1.0, 0.0).astype(BF16)
    parts = split_parts(jnp.where(low, candidate, 0.0), 3)
    count = r.book.shape[1] // 128
    a_rows = lax.broadcasted_iota(jnp.int32, (count, dead), 0)
    replaced = mm(jnp.where((major == a_rows) & low, 1.0, 0.0).astype(BF16), onehot)
    for begin in range(0, count, 8):
        fresh = jnp.zeros((8 * cdim, 128), F32)
        for part in parts:
            chosen = [jnp.where(major == begin + i, part, jnp.zeros((), BF16)) for i in range(8)]
            fresh = fresh + mm(jnp.concatenate(chosen, 0), onehot)
        for i in range(8):
            at = begin + i
            lanes = slice(128 * at, 128 * (at + 1))
            r.refreshed[:, lanes] = jnp.where(
                replaced[at : at + 1] > 0.5, fresh[cdim * i : cdim * (i + 1)], r.book[:, lanes]
            )


def finish_call(t, s, book_t, dead, total, d, hidden):
    cdim, codes = book_t.shape
    piece = d // 8
    ins = dict(
        a_all=s.a_all, b_all=s.b_all, c_all=s.c_all, d_all=t.d_all, e0_all=s.e0_all, e1_all=s.e1_all, g_all=s.g_all,
        h00_all=s.h00_all, h01_all=s.h01_all, h10_all=s.h10_all, h11_all=s.h11_all, w_all=s.w_all, q_all=t.q_all,
        book=book_t, dead_row=dead.reshape(1, -1), dead_col=dead.reshape(-1, 1),
    )
    outs = dict(
        t_up=(piece, hidden), t_down=(hidden // 8, d), t_qkv=(piece, 3 * d), t_out=(piece, d),
        s_up=(piece, hidden), s_down=(hidden // 8, d), s_qkv=(piece, 3 * d), s_out=(piece, d),
        g_ta=(1, d), g_tb=(1, d), g_sa=(1, d), g_sb=(1, d), proj_grad=(cdim, piece), commit=(1, 1),
        book_grad=(cdim, codes // 8), refreshed=(cdim, codes),
    )

    def body(r, m, place, step):
        r.scale = total
        finish_step(r, m, place, step)

    return launch(
        body, "finish", 1, {k: fixed(v) for k, v in ins.items()}, {k: fixed_out(v, F32) for k, v in outs.items()},
        {}, {}, None, 1 << 28,
    )


def frame_bias(clip_row, frame_count):
    first = lax.axis_index("frame") * frame_count
    clips = jnp.concatenate([jnp.full((SPAN,), -1, jnp.int32), clip_row])
    key_clips = lax.dynamic_slice_in_dim(clips, first, SPAN + frame_count)
    qi, qp = jnp.arange(frame_count * SUB) // SUB, jnp.arange(frame_count * SUB) % SUB
    kj, kp = jnp.arange((SPAN + frame_count) * SUB) // SUB, jnp.arange((SPAN + frame_count) * SUB) % SUB
    offset = qi[:, None] + SPAN - kj[None, :]
    allowed = (
        (qp[:, None] == kp[None, :]) & (offset >= 0) & (offset <= SPAN)
        & (jnp.repeat(key_clips[SPAN:], SUB)[:, None] == jnp.repeat(key_clips, SUB)[None, :])
    )
    return jnp.where(allowed, 0.0, NEG).astype(F32)


def local_fused(
    frames_in, spat_gain_a, spat_qkv, spat_out, spat_gain_b, spat_up, spat_down,
    temp_gain_a, temp_qkv, temp_out, temp_gain_b, temp_up, temp_down,
    quant_proj, codebook, code_index, clip_index, dead_codes, source_rows, latent_cot,
):
    frame_count, patches, d = frames_in.shape[1:]
    cdim = quant_proj.shape[1]
    row_count = frame_count * patches
    frame_size, batch_size = lax.axis_size("frame"), lax.axis_size("batch")
    assert frame_count == SPAN
    spat = (spat_gain_a.reshape(1, d), spat_qkv, spat_out, spat_gain_b.reshape(1, d), spat_up, spat_down)
    temp = (temp_gain_a.reshape(1, d), temp_qkv, temp_out, temp_gain_b.reshape(1, d), temp_up, temp_down)
    x = frames_in[0]
    codes = code_index.reshape(1, -1)
    book_t, proj_t = codebook.T, quant_proj.T
    bias = frame_bias(clip_index[0], frame_count)
    row_base = (lax.axis_index("batch") * frame_size + lax.axis_index("frame")) * row_count
    sf = spat_forward_call(x, spat, codes, book_t)
    tf = temp_forward_call(sf.y, sf.halo, bias, temp, proj_t)
    tb = temp_backward_call(
        tf, tf.lat, latent_cot[0].transpose(0, 2, 1), sf.chosen, codes, dead_codes.reshape(-1, 1),
        (source_rows - row_base).reshape(-1, 1), proj_t, sf.y, bias.T, temp,
    )
    sb = spat_backward_call(sf, tb, sf.y, temp[0], x, spat)
    out = finish_call(
        tb, sb, book_t, dead_codes, frame_size * batch_size * row_count * cdim, d, spat_up.shape[1]
    )
    return (
        tf.lat.transpose(0, 2, 1)[None], out.commit[0, 0], sb.dx[None],
        out.g_sa[0], out.s_qkv, out.s_out, out.g_sb[0], out.s_up, out.s_down,
        out.g_ta[0], out.t_qkv, out.t_out, out.g_tb[0], out.t_up, out.t_down,
        out.proj_grad.T, out.book_grad.T, out.refreshed.T,
    )


def solution(mesh):
    fused = (mesh.shape["frame"], mesh.shape["batch"]) == (8, 4)
    return jax.shard_map(
        local_fused if fused else local_general,
        mesh=mesh,
        in_specs=(
            P("batch", "frame", None, None),
            *([P()] * 14),
            P("batch", "frame", None),
            P("batch", None),
            P(),
            P(),
            P("batch", "frame", None, None),
        ),
        out_specs=(
            P("batch", "frame", None, None),
            P(),
            P("batch", "frame", None, None),
            P(),
            P("frame", None),
            P("frame", None),
            P(),
            P("frame", None),
            P("frame", None),
            P(),
            P("frame", None),
            P("frame", None),
            P(),
            P("frame", None),
            P("frame", None),
            P("frame", None),
            P("frame", None),
            P(),
        ),
        check_vma=False,
    )
```

```python
import types

import jax
import jax.numpy as jnp
from jax import lax
from jax.experimental import pallas as pl
from jax.experimental.pallas import tpu as pltpu
from jax.sharding import PartitionSpec as P

HEADS = 8
EPS = 1e-05
BETA = 0.25
USE_MIN = 2.0
NEG = -1e30
HIGH = lax.Precision.HIGHEST
SPAN = 4
F32 = jnp.float32
BF16 = jnp.bfloat16
MESH = pl.DeviceIdType.MESH
GELU_C = 0.7978845608028654
GELU_A = 0.044715
VMEM_BYTES = 56 * 1024 * 1024
TAIL_BYTES = 62 * 1024 * 1024
SUB = 32
GROUP = 64


def mm(a, b):
    return jnp.dot(a, b, preferred_element_type=F32)


def mm_t(a, b):
    return lax.dot_general(a, b, (((1,), (1,)), ((), ())), preferred_element_type=F32)


def t_mm(a, b):
    return lax.dot_general(a, b, (((0,), (0,)), ((), ())), preferred_element_type=F32)


def norm(x):
    c = x - jnp.mean(x, -1, keepdims=True)
    r = lax.rsqrt(jnp.mean(c * c, -1, keepdims=True) + EPS)
    return c * r, r


def norm_back(dy, xhat, r, gain):
    d = dy * gain
    return r * (d - jnp.mean(d, -1, keepdims=True) - xhat * jnp.mean(d * xhat, -1, keepdims=True))


def add_row(ref, rows):
    ref[...] += jnp.sum(rows, 0, keepdims=True)


def head_masks(rows, width):
    lane = lax.broadcasted_iota(jnp.int32, (rows, width), 1)
    return (lane < width // 2, lane >= width // 2)


def attend_pair(q, k, v, bias):
    width = q.shape[1]
    scale = (width // 2) ** -0.5
    zero = jnp.zeros((), BF16)
    qs = q * jnp.asarray(scale, BF16)
    v_ext = jnp.concatenate([v, jnp.ones_like(v)], axis=1)
    masks = head_masks(q.shape[0], width)
    halves = []
    for mask in masks:
        s = mm_t(jnp.where(mask, qs, zero), k)
        if bias is not None:
            s = s + bias
        e = jnp.exp(s - jnp.max(s, -1, keepdims=True)).astype(BF16)
        r = mm(e, v_ext)
        halves.append(r[:, :width] / r[:, width:])
    return jnp.where(masks[0], halves[0], halves[1]).astype(BF16)


def attend_pair_back(q, k, v, do, bias_t):
    width = q.shape[1]
    scale = jnp.asarray((width // 2) ** -0.5, BF16)
    zero = jnp.zeros((), BF16)
    qs = q * scale
    ks = k * scale
    q_masks = head_masks(q.shape[0], width)
    k_masks = head_masks(k.shape[0], width)
    dq = dk = dv = None
    for q_mask, k_mask in zip(q_masks, k_masks):
        qm = jnp.where(q_mask, qs, zero)
        dom = jnp.where(q_mask, do, zero)
        st = mm_t(k, qm)
        if bias_t is not None:
            st = st + bias_t
        e = jnp.exp(st - jnp.max(st, 0, keepdims=True))
        p = e * (1.0 / jnp.sum(e, 0, keepdims=True))
        dp = mm_t(v, dom)
        inner = jnp.sum(p * dp, 0, keepdims=True)
        ds = (p * (dp - inner)).astype(BF16)
        dv_one = mm(p.astype(BF16), dom)
        dk_one = mm(ds, qm)
        dq_one = t_mm(ds, jnp.where(k_mask, ks, zero))
        dq = dq_one if dq is None else dq + dq_one
        dk = dk_one if dk is None else dk + dk_one
        dv = dv_one if dv is None else dv + dv_one
    return dq, dk, dv


def mlp_forward(mid, gain, w_up, w_down, bt_ref, h_ref, gp_ref, tile=512):
    xhat, _ = norm(mid)
    b = (xhat * gain).astype(BF16)
    bt_ref[...] = b.T
    out = mid
    for start in range(0, w_up.shape[1], tile):
        cols = slice(start, start + tile)
        u = mm(b, w_up[:, cols])
        u2 = u * u
        th = jnp.tanh(u * (GELU_C + (GELU_C * GELU_A) * u2))
        half = 0.5 + 0.5 * th
        h = (u * half).astype(BF16)
        slope = half + u * (half * (1.0 - th)) * (GELU_C + (3.0 * GELU_C * GELU_A) * u2)
        h_ref[:, cols] = h
        gp_ref[:, cols] = slope.astype(BF16)
        out = out + mm(h, w_down[cols, :])
    return out


def mlp_backward(dy, dy_low, mid, gain, w_up, w_down, gp_ref, du_ref, dgain_ref, tile=512):
    db = None
    for start in range(0, w_up.shape[1], tile):
        cols = slice(start, start + tile)
        dh = mm_t(dy_low, w_down[cols, :])
        du = (gp_ref[:, cols].astype(F32) * dh).astype(BF16)
        du_ref[:, cols] = du
        one = mm_t(du, w_up[:, cols])
        db = one if db is None else db + one
    xhat, r = norm(mid)
    add_row(dgain_ref, db * xhat)
    return dy + norm_back(db, xhat, r, gain)


def greet_ring(step):
    n = lax.axis_size("frame")
    me = lax.axis_index("frame")
    left, right = lax.rem(me + n - 1, n), lax.rem(me + 1, n)

    @pl.when(step == 0)
    def _():
        barrier = pltpu.get_barrier_semaphore()
        for peer in (left, right):
            pl.semaphore_signal(barrier, inc=1, device_id={"frame": peer}, device_id_type=MESH)

    return left, right


def meet_ring(step):
    @pl.when(step == 0)
    def _():
        pl.semaphore_wait(pltpu.get_barrier_semaphore(), 2)


def ring_copy(src, dst, send_sem, recv_sem, peer):
    return pltpu.make_async_remote_copy(
        src_ref=src, dst_ref=dst, send_sem=send_sem, recv_sem=recv_sem,
        device_id={"frame": peer}, device_id_type=MESH,
    )


def spat_fwd_kernel(
    x_ref, ga, w_qkv, w_out, gb, w_up, w_down,
    y_ref, at_ref, pk_ref, att_t_ref, mid_ref, bt_ref, h_ref, gp_ref, halo_ref,
    att_ref, keep_ref, send_sem, recv_sem,
):
    step = pl.program_id(0)
    steps = pl.num_programs(0)
    feature = x_ref.shape[-1]
    left, right = greet_ring(step)
    x = x_ref[0].astype(F32)
    xhat, _ = norm(x)
    a = (xhat * ga[...]).astype(BF16)
    at_ref[...] = a.T
    for start in range(0, 3 * feature, 512):
        pk_ref[:, start : start + 512] = mm(a, w_qkv[:, start : start + 512]).astype(BF16)
    for lane in range(0, feature, 128):
        att_ref[:, lane : lane + 128] = attend_pair(
            pk_ref[:, lane : lane + 128],
            pk_ref[:, feature + lane : feature + lane + 128],
            pk_ref[:, 2 * feature + lane : 2 * feature + lane + 128],
            None,
        )
    att = att_ref[...]
    att_t_ref[...] = att.T
    mid = x + mm(att, w_out[...])
    mid_ref[...] = mid
    y = mlp_forward(mid, gb[...], w_up, w_down, bt_ref, h_ref, gp_ref).astype(BF16)
    y_ref[0] = y
    keep_ref[step] = y
    meet_ring(step)

    def copy(i):
        return ring_copy(keep_ref.at[i], halo_ref.at[i], send_sem.at[i], recv_sem.at[i], right)

    copy(step).start()

    @pl.when(step == steps - 1)
    def _():
        for i in range(keep_ref.shape[0]):
            copy(i).wait()


def temp_fwd_kernel(
    x_ref, halo_ref, bias_ref, ga, w_qkv, w_out, gb, w_up, w_down, proj,
    lat_ref, x3_ref, at_ref, aht_ref, pk_ref, kvh_ref, att_t_ref, mid_ref, bt_ref, h_ref, gp_ref, att_ref,
):
    frames, group, feature = x_ref.shape
    rows = frames * group
    x = x_ref[...].reshape(rows, feature).astype(F32)
    xhat, _ = norm(x)
    a = (xhat * ga[...]).astype(BF16)
    at_ref[...] = a.T
    for start in range(0, 3 * feature, 512):
        pk_ref[:, :, start : start + 512] = (
            mm(a, w_qkv[:, start : start + 512]).astype(BF16).reshape(frames, group, 512)
        )
    xhat_h, _ = norm(halo_ref[...].reshape(rows, feature).astype(F32))
    ah = (xhat_h * ga[...]).astype(BF16)
    aht_ref[...] = ah.T
    for start in range(0, 2 * feature, 512):
        kvh_ref[:, :, start : start + 512] = (
            mm(ah, w_qkv[:, feature + start : feature + start + 512])
            .astype(BF16)
            .reshape(frames, group, 512)
        )
    bias = bias_ref[...]
    for sub in range(0, group, SUB):
        here = slice(sub, sub + SUB)
        for lane in range(0, feature, 128):
            q = pk_ref[:, here, lane : lane + 128].reshape(frames * SUB, 128)
            k = jnp.concatenate(
                [kvh_ref[:, here, lane : lane + 128],
                 pk_ref[:, here, feature + lane : feature + lane + 128]], 0
            ).reshape(2 * frames * SUB, 128)
            v = jnp.concatenate(
                [kvh_ref[:, here, feature + lane : feature + lane + 128],
                 pk_ref[:, here, 2 * feature + lane : 2 * feature + lane + 128]], 0
            ).reshape(2 * frames * SUB, 128)
            att_ref[:, here, lane : lane + 128] = attend_pair(q, k, v, bias).reshape(frames, SUB, 128)
    att = att_ref[...].reshape(rows, feature)
    att_t_ref[...] = att.T
    mid = x + mm(att, w_out[...])
    mid_ref[...] = mid
    y = mlp_forward(mid, gb[...], w_up, w_down, bt_ref, h_ref, gp_ref).astype(BF16)
    x3_ref[...] = y
    lat_ref[...] = mm(y, proj[...]).reshape(frames, group, proj.shape[1])


def temp_bwd_kernel(
    gl_ref, proj, x3_ref, x_ref, mid_ref, gp_ref, pk_ref, kvh_ref, bias_ref,
    ga, w_qkv, w_out, gb, w_up, w_down,
    dyt_ref, du_ref, dmid_ref, dpk_ref, dkvh_ref, base_ref, back_ref, dga_ref, dgb_ref, dproj_ref,
    datt_ref, dah_ref, send_sem, recv_sem,
):
    step = pl.program_id(0)
    steps = pl.num_programs(0)
    frames, group, feature = x_ref.shape
    rows = frames * group
    left, right = greet_ring(step)

    @pl.when(step == 0)
    def _():
        for ref in (dga_ref, dgb_ref, dproj_ref):
            ref[...] = jnp.zeros_like(ref)

    gl = gl_ref[...].reshape(rows, gl_ref.shape[2])
    dproj_ref[...] += t_mm(gl, x3_ref[...])
    dy_low = mm_t(gl, proj[...]).astype(BF16)
    dyt_ref[...] = dy_low.T
    dmid = mlp_backward(
        dy_low.astype(F32), dy_low, mid_ref[...], gb[...], w_up, w_down, gp_ref, du_ref, dgb_ref
    )
    dmid_low = dmid.astype(BF16)
    dmid_ref[...] = dmid_low
    datt_ref[...] = mm_t(dmid_low, w_out[...]).astype(BF16).reshape(frames, group, feature)
    bias = bias_ref[...]
    half = frames * SUB
    for sub in range(0, group, SUB):
        here = slice(sub, sub + SUB)
        for lane in range(0, feature, 128):
            l0 = slice(lane, lane + 128)
            l1 = slice(feature + lane, feature + lane + 128)
            l2 = slice(2 * feature + lane, 2 * feature + lane + 128)
            q = pk_ref[:, here, l0].reshape(half, 128)
            k = jnp.concatenate([kvh_ref[:, here, l0], pk_ref[:, here, l1]], 0).reshape(2 * half, 128)
            v = jnp.concatenate([kvh_ref[:, here, l1], pk_ref[:, here, l2]], 0).reshape(2 * half, 128)
            do = datt_ref[:, here, l0].reshape(half, 128)
            dq, dk, dv = attend_pair_back(q, k, v, do, bias)
            dk, dv = dk.astype(BF16), dv.astype(BF16)
            dpk_ref[:, here, l0] = dq.astype(BF16).reshape(frames, SUB, 128)
            dpk_ref[:, here, l1] = dk[half:].reshape(frames, SUB, 128)
            dpk_ref[:, here, l2] = dv[half:].reshape(frames, SUB, 128)
            dkvh_ref[:, here, l0] = dk[:half].reshape(frames, SUB, 128)
            dkvh_ref[:, here, l1] = dv[:half].reshape(frames, SUB, 128)
    da = mm_t(dpk_ref[...].reshape(rows, 3 * feature), w_qkv[...])
    dah = mm_t(dkvh_ref[...].reshape(rows, 2 * feature), w_qkv[:, feature:])
    dah_ref[step] = dah.astype(BF16).reshape(frames, group, feature)
    meet_ring(step)

    def copy(i):
        there = back_ref.at[:, pl.ds(i * group, group), :]
        return ring_copy(dah_ref.at[i], there, send_sem.at[i], recv_sem.at[i], left)

    copy(step).start()
    xhat, r = norm(x_ref[...].reshape(rows, feature).astype(F32))
    add_row(dga_ref, da * xhat)
    base_ref[...] = (dmid + norm_back(da, xhat, r, ga[...])).reshape(frames, group, feature)

    @pl.when(step == steps - 1)
    def _():
        for i in range(dah_ref.shape[0]):
            copy(i).wait()


def spat_bwd_kernel(
    base_ref, dah_ref, x2_ref, gta, x_ref, mid_ref, gp_ref, pk_ref,
    ga, w_qkv, w_out, gb, w_up, w_down,
    dx_ref, dyt_ref, du_ref, dmid_ref, dpk_ref, dgt_ref, dga_ref, dgb_ref,
    datt_ref,
):
    feature = x_ref.shape[-1]

    @pl.when(pl.program_id(0) == 0)
    def _():
        for ref in (dgt_ref, dga_ref, dgb_ref):
            ref[...] = jnp.zeros_like(ref)

    xhat2, r2 = norm(x2_ref[0].astype(F32))
    dah = dah_ref[0].astype(F32)
    add_row(dgt_ref, dah * xhat2)
    dy_low = (base_ref[0] + norm_back(dah, xhat2, r2, gta[...])).astype(BF16)
    dyt_ref[...] = dy_low.T
    dmid = mlp_backward(
        dy_low.astype(F32), dy_low, mid_ref[...], gb[...], w_up, w_down, gp_ref, du_ref, dgb_ref
    )
    dmid_low = dmid.astype(BF16)
    dmid_ref[...] = dmid_low
    datt_ref[...] = mm_t(dmid_low, w_out[...]).astype(BF16)
    for lane in range(0, feature, 128):
        l0 = slice(lane, lane + 128)
        l1 = slice(feature + lane, feature + lane + 128)
        l2 = slice(2 * feature + lane, 2 * feature + lane + 128)
        dq, dk, dv = attend_pair_back(pk_ref[:, l0], pk_ref[:, l1], pk_ref[:, l2], datt_ref[:, l0], None)
        dpk_ref[:, l0] = dq.astype(BF16)
        dpk_ref[:, l1] = dk.astype(BF16)
        dpk_ref[:, l2] = dv.astype(BF16)
    da = mm_t(dpk_ref[...], w_qkv[...])
    xhat, r = norm(x_ref[0].astype(F32))
    add_row(dga_ref, da * xhat)
    dx_ref[0] = (dmid + norm_back(da, xhat, r, ga[...])).astype(BF16)


def mlp_grad_kernel(bt_ref, du_ref, dyt_ref, h_ref, up_ref, down_ref):
    up_ref[0] = mm(bt_ref[...], du_ref[...]).astype(BF16)
    width = down_ref.shape[2]
    for j in range(down_ref.shape[0]):
        down_ref[j] = mm(dyt_ref[...], h_ref[:, j * width : (j + 1) * width]).astype(BF16)


def att_grad_kernel(halo, *refs):
    if halo:
        at_ref, att_t_ref, dq_ref, dk_ref, dv_ref, dm_ref, aht_ref, dkh_ref, dvh_ref, out_ref = refs
    else:
        at_ref, att_t_ref, dq_ref, dk_ref, dv_ref, dm_ref, out_ref = refs
    dq = mm(at_ref[...], dq_ref[...])
    dk = mm(at_ref[...], dk_ref[...])
    dv = mm(at_ref[...], dv_ref[...])
    if halo:
        dk = dk + mm(aht_ref[...], dkh_ref[...])
        dv = dv + mm(aht_ref[...], dvh_ref[...])
    do = mm(att_t_ref[...], dm_ref[...])
    for i, part in enumerate((dq, dk, dv, do)):
        part = part.astype(BF16)
        for j in range(2):
            out_ref[j, :, 128 * i : 128 * (i + 1)] = part[:, 128 * j : 128 * (j + 1)]


def whole(shape):
    zeros = (0,) * len(shape)
    return pl.BlockSpec(shape, lambda i: zeros)


def col_block(rows, width, offset=0):
    return pl.BlockSpec((rows, width), lambda i: (0, i + offset))


def row_block(rows, width):
    return pl.BlockSpec((rows, width), lambda i: (i, 0))


def shape_of(shape, dtype):
    return jax.ShapeDtypeStruct(shape, dtype)


def params(collective=None):
    return pltpu.CompilerParams(
        vmem_limit_bytes=VMEM_BYTES, dimension_semantics=("arbitrary",), collective_id=collective,
        has_side_effects=collective is not None,
    )


def cost(flops, nbytes):
    return pl.CostEstimate(flops=int(flops), bytes_accessed=int(nbytes), transcendentals=0)


def weight_specs(feature, hidden):
    return [
        whole((1, feature)), whole((feature, 3 * feature)), whole((feature, feature)),
        whole((1, feature)), whole((feature, hidden)), whole((hidden, feature)),
    ]


def spat_forward(x, weights):
    frames, patches, d = x.shape
    hidden = weights[4].shape[1]
    n = frames * patches
    blk = pl.BlockSpec((1, patches, d), lambda i: (i, 0, 0))
    return pl.pallas_call(
        spat_fwd_kernel,
        grid=(frames,),
        in_specs=[blk] + weight_specs(d, hidden),
        out_specs=[
            blk, col_block(d, patches), row_block(patches, 3 * d), col_block(d, patches),
            row_block(patches, d), col_block(d, patches), row_block(patches, hidden), row_block(patches, hidden),
            pl.BlockSpec(memory_space=pl.ANY),
        ],
        out_shape=[
            shape_of(x.shape, BF16), shape_of((d, n), BF16), shape_of((n, 3 * d), BF16), shape_of((d, n), BF16),
            shape_of((n, d), F32), shape_of((d, n), BF16), shape_of((n, hidden), BF16), shape_of((n, hidden), BF16),
            shape_of(x.shape, BF16),
        ],
        scratch_shapes=[
            pltpu.VMEM((patches, d), BF16), pltpu.VMEM(x.shape, BF16),
            pltpu.SemaphoreType.DMA((frames,)), pltpu.SemaphoreType.DMA((frames,)),
        ],
        compiler_params=params(1),
        cost_estimate=cost(2 * n * d * (4 * d + 2 * hidden + 2 * patches), 24 * n * d),
        name="spat_forward",
    )(x, *weights)


def temp_forward(x, halo, bias, weights, proj):
    frames, patches, d = x.shape
    hidden = weights[4].shape[1]
    n = frames * patches
    steps = patches // GROUP
    rows = frames * GROUP
    cdim = proj.shape[1]
    blk = pl.BlockSpec((frames, GROUP, d), lambda i: (0, i, 0))
    stacked = lambda width: pl.BlockSpec((frames, GROUP, width), lambda i: (i, 0, 0))
    return pl.pallas_call(
        temp_fwd_kernel,
        grid=(steps,),
        in_specs=[blk, blk, whole(bias.shape)] + weight_specs(d, hidden) + [whole(proj.shape)],
        out_specs=[
            pl.BlockSpec((frames, GROUP, cdim), lambda i: (0, i, 0)), row_block(rows, d),
            col_block(d, rows), col_block(d, rows), stacked(3 * d), stacked(2 * d), col_block(d, rows),
            row_block(rows, d), col_block(d, rows), row_block(rows, hidden), row_block(rows, hidden),
        ],
        out_shape=[
            shape_of((frames, patches, cdim), F32), shape_of((n, d), BF16),
            shape_of((d, n), BF16), shape_of((d, n), BF16),
            shape_of((frames * steps, GROUP, 3 * d), BF16), shape_of((frames * steps, GROUP, 2 * d), BF16),
            shape_of((d, n), BF16), shape_of((n, d), F32), shape_of((d, n), BF16),
            shape_of((n, hidden), BF16), shape_of((n, hidden), BF16),
        ],
        scratch_shapes=[pltpu.VMEM((frames, GROUP, d), BF16)],
        compiler_params=params(),
        cost_estimate=cost(2 * n * d * (6 * d + 2 * hidden + 2 * patches), 30 * n * d),
        name="temp_forward",
    )(x, halo, bias, *weights, proj)


def temp_backward(gl, proj, x3, x, mid, gp, pk, kvh, bias_t, weights):
    frames, patches, d = x.shape
    hidden = weights[4].shape[1]
    n = frames * patches
    steps = patches // GROUP
    rows = frames * GROUP
    cdim = proj.shape[1]
    nat = lambda width: pl.BlockSpec((frames, GROUP, width), lambda i: (0, i, 0))
    stacked = lambda width: pl.BlockSpec((frames, GROUP, width), lambda i: (i, 0, 0))
    return pl.pallas_call(
        temp_bwd_kernel,
        grid=(steps,),
        in_specs=[
            nat(cdim), whole(proj.shape), row_block(rows, d), nat(d), row_block(rows, d),
            row_block(rows, hidden), stacked(3 * d), stacked(2 * d), whole(bias_t.shape),
        ] + weight_specs(d, hidden),
        out_specs=[
            col_block(d, rows), row_block(rows, hidden), row_block(rows, d), stacked(3 * d), stacked(2 * d),
            nat(d), pl.BlockSpec(memory_space=pl.ANY), whole((1, d)), whole((1, d)), whole((cdim, d)),
        ],
        out_shape=[
            shape_of((d, n), BF16), shape_of((n, hidden), BF16), shape_of((n, d), BF16),
            shape_of((frames * steps, GROUP, 3 * d), BF16), shape_of((frames * steps, GROUP, 2 * d), BF16),
            shape_of((frames, patches, d), F32), shape_of((frames, patches, d), BF16),
            shape_of((1, d), F32), shape_of((1, d), F32), shape_of((cdim, d), F32),
        ],
        scratch_shapes=[
            pltpu.VMEM((frames, GROUP, d), BF16), pltpu.VMEM((steps, frames, GROUP, d), BF16),
            pltpu.SemaphoreType.DMA((steps,)), pltpu.SemaphoreType.DMA((steps,)),
        ],
        compiler_params=params(2),
        cost_estimate=cost(2 * n * d * (6 * d + 2 * hidden + 5 * patches), 40 * n * d),
        name="temp_backward",
    )(gl, proj, x3, x, mid, gp, pk, kvh, bias_t, *weights)


def spat_backward(base, dah, x2, gta, x, mid, gp, pk, weights):
    frames, patches, d = x.shape
    hidden = weights[4].shape[1]
    n = frames * patches
    blk = pl.BlockSpec((1, patches, d), lambda i: (i, 0, 0))
    return pl.pallas_call(
        spat_bwd_kernel,
        grid=(frames,),
        in_specs=[
            blk, blk, blk, whole((1, d)), blk, row_block(patches, d), row_block(patches, hidden),
            row_block(patches, 3 * d),
        ] + weight_specs(d, hidden),
        out_specs=[
            blk, col_block(d, patches), row_block(patches, hidden), row_block(patches, d),
            row_block(patches, 3 * d), whole((1, d)), whole((1, d)), whole((1, d)),
        ],
        out_shape=[
            shape_of(x.shape, BF16), shape_of((d, n), BF16), shape_of((n, hidden), BF16), shape_of((n, d), BF16),
            shape_of((n, 3 * d), BF16), shape_of((1, d), F32), shape_of((1, d), F32), shape_of((1, d), F32),
        ],
        scratch_shapes=[pltpu.VMEM((patches, d), BF16)],
        compiler_params=params(),
        cost_estimate=cost(2 * n * d * (4 * d + 2 * hidden + 5 * patches), 30 * n * d),
        name="spat_backward",
    )(base, dah, x2, gta, x, mid, gp, pk, *weights)


def mlp_grads(bt, du, dyt, h):
    d, n = bt.shape
    hidden = du.shape[1]
    steps = 4
    wide = hidden // steps
    return pl.pallas_call(
        mlp_grad_kernel,
        grid=(steps,),
        in_specs=[whole((d, n)), col_block(n, wide), whole((d, n)), col_block(n, wide)],
        out_specs=[
            pl.BlockSpec((1, d, wide), lambda i: (i, 0, 0)),
            pl.BlockSpec((2, d, wide // 2), lambda i: (i, 0, 0)),
        ],
        out_shape=[shape_of((steps, d, wide), BF16), shape_of((2 * steps, d, wide // 2), BF16)],
        compiler_params=params(),
        cost_estimate=cost(4 * n * d * hidden, 8 * n * d + 4 * n * hidden),
        name="mlp_grads",
    )(bt, du, dyt, h)


def att_grads(at, att_t, dpk, dmid, aht=None, dkvh=None):
    d, n = at.shape
    halo = aht is not None
    wide = 256
    args = [at, att_t, dpk, dpk, dpk, dmid]
    specs = [
        whole((d, n)), whole((d, n)), col_block(n, wide), col_block(n, wide, d // wide),
        col_block(n, wide, 2 * d // wide), col_block(n, wide),
    ]
    if halo:
        args += [aht, dkvh, dkvh]
        specs += [whole((d, n)), col_block(n, wide), col_block(n, wide, d // wide)]
    return pl.pallas_call(
        lambda *refs: att_grad_kernel(halo, *refs),
        grid=(d // wide,),
        in_specs=specs,
        out_specs=pl.BlockSpec((2, d, 512), lambda i: (i, 0, 0)),
        out_shape=shape_of((d // 128, d, 512), BF16),
        compiler_params=params(),
        cost_estimate=cost(2 * n * d * d * (6 if halo else 4), 16 * n * d),
        name="att_grads",
    )(*args)


def bits_of(count):
    bits = count.bit_length() - 1
    assert count == 1 << bits
    return bits


def swap(value, axis, bit):
    count = lax.axis_size(axis)
    return lax.ppermute(value, axis, [(i, i ^ (1 << bit)) for i in range(count)])


def my_bit(axis, bit):
    return (lax.axis_index(axis) >> bit) & 1


def reduce_pieces(grad, labels, order):
    names = []
    for axis in labels:
        names += [(axis, b) for b in reversed(range(bits_of(lax.axis_size(axis))))]
    tail = grad.shape[len(labels) :]
    cur = grad.reshape((2,) * len(names) + tail)
    for axis, bit in order:
        at = names.index((axis, bit))
        me = my_bit(axis, bit)
        kept = lax.dynamic_index_in_dim(cur, me, at, keepdims=False)
        sent = lax.dynamic_index_in_dim(cur, 1 - me, at, keepdims=False)
        cur = (kept.astype(F32) + swap(sent, axis, bit).astype(F32)).astype(BF16)
        names.pop(at)
    cur = cur[None]
    for bit in reversed(range(bits_of(lax.axis_size("batch")))):
        other = swap(cur, "batch", bit)
        low = my_bit("batch", bit) == 0
        cur = jnp.stack([jnp.where(low, cur, other), jnp.where(low, other, cur)], 1)
        cur = cur.reshape((-1,) + tail)
    return cur.astype(F32)


def orders():
    fb, bb = bits_of(lax.axis_size("frame")), bits_of(lax.axis_size("batch"))
    frame = [("frame", b) for b in [0] + list(reversed(range(1, fb)))]
    batch = [("batch", b) for b in range(bb)]
    return batch + frame, batch[:1] + frame[:1] + batch[1:] + frame[1:]


def local_general(
    frames_in, spat_gain_a, spat_qkv, spat_out, spat_gain_b, spat_up, spat_down,
    temp_gain_a, temp_qkv, temp_out, temp_gain_b, temp_up, temp_down,
    quant_proj, codebook, code_index, clip_index, dead_codes, source_rows, latent_cot,
):
    frame_count, patches, d = frames_in.shape[1:]
    cdim = quant_proj.shape[1]
    row_count = frame_count * patches
    frame_size, batch_size = lax.axis_size("frame"), lax.axis_size("batch")
    assert frame_count == SPAN
    spat = (spat_gain_a.reshape(1, d), spat_qkv, spat_out, spat_gain_b.reshape(1, d), spat_up, spat_down)
    temp = (temp_gain_a.reshape(1, d), temp_qkv, temp_out, temp_gain_b.reshape(1, d), temp_up, temp_down)
    x = frames_in[0]

    first = lax.axis_index("frame") * frame_count
    clips = jnp.concatenate([jnp.full((SPAN,), -1, jnp.int32), clip_index[0]])
    key_clips = lax.dynamic_slice_in_dim(clips, first, SPAN + frame_count)
    query_clips = key_clips[SPAN:]
    qi, qp = jnp.arange(frame_count * SUB) // SUB, jnp.arange(frame_count * SUB) % SUB
    kj, kp = jnp.arange((SPAN + frame_count) * SUB) // SUB, jnp.arange((SPAN + frame_count) * SUB) % SUB
    offset = qi[:, None] + SPAN - kj[None, :]
    allowed = (
        (qp[:, None] == kp[None, :]) & (offset >= 0) & (offset <= SPAN)
        & (jnp.repeat(query_clips, SUB)[:, None] == jnp.repeat(key_clips, SUB)[None, :])
    )
    bias = jnp.where(allowed, 0.0, NEG).astype(F32)

    x2, s_at, s_pk, s_att_t, s_mid, s_bt, s_h, s_gp, halo = spat_forward(x, spat)
    latent3, x3, t_at, t_aht, t_pk, t_kvh, t_att_t, t_mid, t_bt, t_h, t_gp = temp_forward(
        x2, halo, bias, temp, quant_proj
    )

    latent = latent3.reshape(-1, cdim)
    codes_flat = code_index.reshape(-1)
    chosen = jnp.take(codebook, codes_flat, axis=0)
    differ = latent - chosen
    commit_part = jnp.sum(differ * differ)
    grad_latent = (latent_cot.reshape(-1, cdim) + 2.0 * BETA * differ).astype(BF16)
    grad_book = jax.ops.segment_sum(-2.0 * BETA * differ, codes_flat, num_segments=codebook.shape[0])

    dyt, du, dmid, dpk, dkvh, base, dah_back, dg_ta, dg_tb, dproj = temp_backward(
        grad_latent.reshape(latent3.shape), quant_proj, x3, x2, t_mid, t_gp, t_pk, t_kvh, bias.T, temp
    )
    t_up, t_down = mlp_grads(t_bt, du, dyt, t_h)
    t_att = att_grads(
        t_at, t_att_t, dpk.reshape(row_count, -1), dmid, t_aht, dkvh.reshape(row_count, -1)
    )
    dx, dyt, du, dmid, dpk, dg_ta2, dg_sa, dg_sb = spat_backward(
        base, dah_back, x2, temp[0], x, s_mid, s_gp, s_pk, spat
    )
    s_up, s_down = mlp_grads(s_bt, du, dyt, s_h)
    s_att = att_grads(s_at, s_att_t, dpk, dmid)

    dead_match = (codes_flat[:, None] == dead_codes[None, :]).astype(F32)
    usage_part = jnp.sum(dead_match, 0)
    row_base = (lax.axis_index("batch") * frame_size + lax.axis_index("frame")) * row_count
    pick_table = ((source_rows - row_base)[:, None] == jnp.arange(row_count)[None, :]).astype(F32)
    picked = jnp.dot(pick_table, latent, precision=HIGH)
    usage_count, candidate, commit_total = lax.psum((usage_part, picked, commit_part), ("frame", "batch"))
    gain_ta, gain_tb, gain_sa, gain_sb = lax.psum(
        ((dg_ta + dg_ta2)[0], dg_tb[0], dg_sa[0], dg_sb[0]), ("frame", "batch")
    )
    old_rows = jnp.take(codebook, dead_codes, axis=0)
    fresh_rows = jnp.where((usage_count < USE_MIN)[:, None], candidate, old_rows)
    refreshed = codebook.at[dead_codes].set(fresh_rows)
    commit_loss = commit_total / (frame_size * batch_size * row_count * cdim)

    one, two = orders()
    piece = d // frame_size

    def by_rows(grad, order):
        return reduce_pieces(
            grad.reshape(batch_size, frame_size, -1, grad.shape[-1]), ("batch", "frame"), order
        )

    def finish_up(grad):
        return by_rows(grad, one).transpose(1, 0, 2).reshape(piece, -1)

    def finish_down(grad):
        hidden = grad.shape[0] * grad.shape[2]
        wide = hidden // frame_size
        if grad.shape[2] != wide:
            grad = grad.transpose(1, 0, 2).reshape(d, frame_size, wide).transpose(1, 0, 2)
        out = reduce_pieces(
            grad.reshape(frame_size, batch_size, d // batch_size, wide), ("frame", "batch"), two
        )
        return out.reshape(d, wide).T

    def finish_att(grad, order):
        out = by_rows(grad, order)
        qkv = out[:, :, :384].reshape(batch_size, piece, 3, -1).transpose(1, 2, 0, 3).reshape(piece, 3 * d)
        return qkv, out[:, :, 384:].transpose(1, 0, 2).reshape(piece, d)

    book = grad_book.reshape(frame_size, batch_size, -1, 128)
    proj = dproj.T.reshape(frame_size, batch_size, -1)
    proj_size = proj.shape[2]
    proj = jnp.pad(proj, ((0, 0), (0, 0), (0, -proj_size % 128))).reshape(frame_size, batch_size, -1, 128)
    small = jnp.concatenate([book, proj], 2).astype(BF16)
    small = reduce_pieces(small, ("frame", "batch"), two)
    book_rows = book.shape[2]
    g_book = small[:, :book_rows].reshape(-1, cdim)
    g_proj = small[:, book_rows:].reshape(batch_size, -1)[:, :proj_size].reshape(piece, cdim)
    gt_qkv, gt_out = finish_att(t_att, one)
    gs_qkv, gs_out = finish_att(s_att, one)
    return (
        latent.reshape(latent_cot.shape),
        commit_loss,
        dx[None],
        gain_sa,
        gs_qkv,
        gs_out,
        gain_sb,
        finish_up(s_up),
        finish_down(s_down),
        gain_ta,
        gt_qkv,
        gt_out,
        gain_tb,
        finish_up(t_up),
        finish_down(t_down),
        g_proj,
        g_book,
        refreshed,
    )


SIZE = {"y": 2, "c": 2, "z": 4, "x": 2}
PEERS = ({"y": 1}, {"c": 1}, {"y": 1, "c": 1}, {"x": 1}, {"z": 1}, {"z": 2}, {"z": 3})
ROWS_DIMS = ("y", "c", "z", "x")
COLS_DIMS = ("z", "x", "y", "c")
E_DIMS = ("u", "c", "z", "x", "y")
H_DIMS = ("u", "w", "c", "z", "x", "y")
Y_FIRST = ("c", "y", "x", "z")
X_FIRST = ("c", "x", "y", "z")
TILE = 512


class Place:
    def __init__(self):
        batch, frame = lax.axis_index("batch"), lax.axis_index("frame")
        self.me = {"y": lax.div(batch, 2), "c": lax.rem(batch, 2), "z": lax.div(frame, 2), "x": lax.rem(frame, 2)}

    def next(self, dim, shift):
        return lax.rem(self.me[dim] + shift, SIZE[dim])

    def peer(self, shifts):
        at = {d: self.next(d, shifts[d]) if d in shifts else self.me[d] for d in SIZE}
        return {"batch": 2 * at["y"] + at["c"], "frame": 2 * at["z"] + at["x"]}

    def copy(self, src, dst, send, recv, shifts):
        return pltpu.make_async_remote_copy(
            src_ref=src, dst_ref=dst, send_sem=send, recv_sem=recv,
            device_id=self.peer(shifts), device_id_type=MESH,
        )

    def greet(self):
        for shifts in PEERS:
            pl.semaphore_signal(
                pltpu.get_barrier_semaphore(), inc=1, device_id=self.peer(shifts), device_id_type=MESH
            )


def sizes(dims):
    return tuple(SIZE[d] for d in dims)


class Sum:
    def __init__(self, dims, tail, order, source=None, shared=None, fixed=(), gather=True, direct=False):
        self.dims, self.tail, self.order, self.source, self.shared = dims, tail, order, source, shared
        self.fixed, self.with_gather, self.direct = dict(fixed), gather, direct
        self.counts = [SIZE[d] - 1 for d in order]

    def left(self, k):
        free = [d for d in self.dims if d not in self.fixed]
        return [d for d in free if d not in self.order or self.order.index(d) > k]

    def scratch(self):
        out = []
        if self.shared is None:
            kept = self.left(0 if self.source else -1)
            out.append(pltpu.VMEM(sizes(kept) + self.tail, BF16))
        for k, count in enumerate(self.counts):
            out.append(pltpu.VMEM((count,) + sizes(self.left(k)) + self.tail, BF16))
        if self.with_gather:
            out.append(pltpu.VMEM((2, 2) + self.tail, BF16))
        copies = sum(self.counts) + 3
        out += [pltpu.SemaphoreType.DMA((copies,))] * 2
        if self.source:
            out.append(pltpu.SemaphoreType.DMA)
        return out

    def bind(self, refs, r, place):
        self.place = place
        self.src = self.source(r) if self.source else None
        self.acc = self.shared(r) if self.shared else next(refs)
        self.got = [next(refs) for _ in self.counts]
        self.all = next(refs) if self.with_gather else None
        self.send, self.recv = next(refs), next(refs)
        self.load = next(refs) if self.source else None
        return self

    def index(self, dims, k, at_k, rest=None):
        out = []
        for d in dims:
            at = self.order.index(d) if d in self.order else len(self.order)
            if d in self.fixed:
                out.append(self.fixed[d])
            elif at < k:
                out.append(self.place.me[d])
            elif at == k and d in self.order:
                out.append(at_k)
            else:
                out.append(slice(None) if rest is None else rest[d])
        return tuple(out)

    def held(self):
        if self.shared:
            return self.dims
        return self.left(0 if self.source else -1)

    def copies(self, k):
        early = k == 0 and self.source
        src, dims = (self.src, self.dims) if early else (self.acc, self.held())
        base = sum(self.counts[:k])
        for i in range(self.counts[k]):
            there = self.index(dims, k, self.place.next(self.order[k], i + 1))
            yield self.place.copy(
                src.at[there], self.got[k].at[i], self.send.at[base + i], self.recv.at[base + i], {self.order[k]: i + 1}
            )

    def keep(self):
        here = self.index(self.dims, 0, self.place.me[self.order[0]])
        return pltpu.make_async_copy(self.src.at[here], self.acc, self.load)

    def start(self, k):
        for copy in self.copies(k):
            copy.start()
        if k == 0 and self.source:
            self.keep().start()

    def finish(self, k):
        for copy in self.copies(k):
            copy.wait()
        if k == 0 and self.source:
            self.keep().wait()
        left, got, count = self.left(k), self.got[k], self.counts[k]
        total = 1
        for d in left:
            total *= SIZE[d]

        def add(i):
            rest, stride = {}, total
            for d in left:
                stride //= SIZE[d]
                rest[d] = lax.rem(lax.div(i, stride), SIZE[d])
            here = self.index(self.held(), k, self.place.me[self.order[k]], rest)
            there = tuple(rest[d] for d in left)
            if count == 1:
                self.acc[here] = self.acc[here] + got[(0,) + there]
            else:
                value = self.acc[here].astype(F32)
                for j in range(count):
                    value = value + got[(j,) + there].astype(F32)
                self.acc[here] = value.astype(BF16)

        if total == 1:
            add(0)
        else:
            lax.fori_loop(0, total, lambda i, c: (add(i), c)[1], 0)

    def move(self, k):
        self.finish(k)
        self.start(k + 1)

    def piece(self):
        return self.acc[self.index(self.held(), len(self.order), None)]

    def hops(self, which):
        base = sum(self.counts)
        y, c = self.place.me["y"], self.place.me["c"]
        here = self.all.at[y, c]
        if self.direct:
            todo = [(here, shifts) for shifts in PEERS[:3]] if which == 0 else []
        else:
            todo = [(here, PEERS[0])] if which == 0 else [(self.all.at[:, c], PEERS[1])]
        for j, (ref, shifts) in enumerate(todo):
            at = base + which + j
            yield self.place.copy(ref, ref, self.send.at[at], self.recv.at[at], shifts)

    def gather(self):
        self.finish(len(self.order) - 1)
        self.all[self.place.me["y"], self.place.me["c"]] = self.piece()
        for copy in self.hops(0):
            copy.start()

    def spread(self):
        for copy in self.hops(0):
            copy.wait()
        for copy in self.hops(1):
            copy.start()

    def gathered(self, out):
        for copy in self.hops(0 if self.direct else 1):
            copy.wait()
        out[...] = self.all[...]


class Total:
    order = Y_FIRST

    def __init__(self, rows):
        self.rows = rows

    def scratch(self):
        copies = sum(SIZE[d] - 1 for d in self.order)
        return [
            pltpu.VMEM((self.rows, 128), F32), pltpu.VMEM((copies, self.rows, 128), F32),
            pltpu.SemaphoreType.DMA((copies,)), pltpu.SemaphoreType.DMA((copies,)),
        ]

    def bind(self, refs, r, place):
        self.place = place
        self.acc, self.got, self.send, self.recv = (next(refs) for _ in range(4))
        return self

    def copies(self, k):
        base = sum(SIZE[d] - 1 for d in self.order[:k])
        for i in range(SIZE[self.order[k]] - 1):
            at = base + i
            yield at, self.place.copy(
                self.acc, self.got.at[at], self.send.at[at], self.recv.at[at], {self.order[k]: i + 1}
            )

    def start(self, k):
        for _, copy in self.copies(k):
            copy.start()

    def finish(self, k):
        arrived = []
        for at, copy in self.copies(k):
            copy.wait()
            arrived.append(at)
        for at in arrived:
            self.acc[...] = self.acc[...] + self.got[at]

    def move(self, k):
        self.finish(k)
        self.start(k + 1)


def launch(body, name, steps, ins, outs, scratch, moves, collective, flops, limit=VMEM_BYTES, unroll=False):
    keys = [*ins, *outs, *scratch]
    extra = [spec for part in moves.values() for spec in part.scratch()]

    def kernel(*refs):
        r = types.SimpleNamespace(**dict(zip(keys, refs)))
        rest = iter(refs[len(keys) :])
        place = Place()
        m = types.SimpleNamespace(**{k: v.bind(rest, r, place) for k, v in moves.items()})
        if unroll:
            for step in range(steps):
                body(r, m, place, step)
        else:
            body(r, m, place, pl.program_id(0))

    got = pl.pallas_call(
        kernel,
        grid=(1 if unroll else steps,),
        in_specs=[x[1] for x in ins.values()],
        out_specs=[x[1] for x in outs.values()],
        out_shape=[x[0] for x in outs.values()],
        scratch_shapes=list(scratch.values()) + extra,
        compiler_params=pltpu.CompilerParams(
            vmem_limit_bytes=limit, dimension_semantics=("arbitrary",), collective_id=collective,
            has_side_effects=collective is not None,
        ),
        cost_estimate=cost(flops, 40 << 20),
        name=name,
    )(*[x[0] for x in ins.values()])
    return types.SimpleNamespace(**dict(zip(outs, got)))


ANY = pl.BlockSpec(memory_space=pl.ANY)


def fixed_spec(shape):
    zeros = (0,) * len(shape)
    return pl.BlockSpec(shape, lambda i: zeros, pipeline_mode=pl.Buffered(1))


def fixed(array):
    return (array, fixed_spec(array.shape))


def fixed_out(shape, dtype):
    return (shape_of(shape, dtype), fixed_spec(shape))


def part_of(first, count):
    return lambda i: jnp.clip(i - first, 0, count - 1)


def on(step, value):
    if isinstance(step, int):
        return lambda f: f() if step == value else None
    return lambda f: pl.when(step == value)(f)


def within(step, first, count):
    if isinstance(step, int):
        return lambda f: f() if first <= step < first + count else None
    return lambda f: pl.when((step >= first) & (step < first + count))(f)


def split_parts(value, count):
    out = []
    for _ in range(count):
        low = value.astype(BF16)
        out.append(low)
        value = value - low.astype(F32)
    return out


def code_masks(codes, rows):
    major = lax.div(codes, 128)
    minor = codes - 128 * major
    return major, jnp.where(lax.broadcasted_iota(jnp.int32, (128, codes.shape[1]), 0) == minor, 1.0, 0.0).astype(BF16)


def spat_forward_step(r, m, place, step):
    frames = r.keep.shape[0]
    d = r.x.shape[-1]
    tiles = r.w_up_.shape[0]
    left, right = greet_ring(step)
    ends = frame_ends()
    fetch = Fetch(r.fetch)
    first = [fetch.add(r.w_qkv, r.w_qkv_), fetch.add(r.w_out, r.w_out_)]
    later = [fetch_mlp(fetch, r, j) for j in range(tiles)]

    @on(step, 0)
    def _():
        fetch.start()
        fetch.wait(first[0])

    @pl.when(step < frames)
    def _():
        x = r.x[0].astype(F32)
        xhat, _ = norm(x)
        a = (xhat * r.ga[...]).astype(BF16)
        r.at[...] = a.T
        for start in range(0, 3 * d, 512):
            r.pk[:, start : start + 512] = mm(a, r.w_qkv_[:, start : start + 512]).astype(BF16)
        for lane in range(0, d, 128):
            cols = [slice(part * d + lane, part * d + lane + 128) for part in range(3)]
            r.att[:, cols[0]] = attend_pair(*[r.pk[:, c] for c in cols], None)
        att = r.att[...]
        r.att_t[...] = att.T

        @on(step, 0)
        def _():
            fetch.wait(first[1])
            for pair in later:
                fetch.wait(*pair)

        mid = x + mm(att, r.w_out_[...])
        r.mid[...] = mid

        def put_bt(value):
            r.bt[...] = value

        def put(j, h, slope):
            for i in range(2):
                r.h[2 * j + i] = h[:, 256 * i : 256 * (i + 1)]
            r.gp[j] = slope

        y = mlp_up(mid, r.gb[...], r.w_up_, r.w_down_, put_bt, put).astype(BF16)
        r.y[0] = y
        r.keep[step] = y

    meet_ring(step)

    def copy(i):
        return ring_copy(r.keep.at[i], r.halo.at[i], r.send.at[i], r.recv.at[i], right)

    @pl.when((step < frames) & ends.not_last)
    def _():
        copy(step).start()

    def clear(i):
        return pltpu.make_async_copy(r.none, r.halo.at[i], r.recv.at[i])

    @pl.when((step == 0) & ends.is_first)
    def _():
        r.none[...] = jnp.zeros_like(r.none)
        for i in range(frames):
            clear(i).start()

    @on(step, frames)
    def _():
        codes = r.codes[...]
        cdim, count = r.book.shape
        major, onehot = code_masks(codes, count // 128)
        both = jnp.concatenate([onehot, onehot], 0)
        total = jnp.zeros(r.chosen.shape, F32)
        for first in range(0, count // 128, 8):
            book = jnp.concatenate([r.book[:, 128 * a : 128 * (a + 1)] for a in range(first, first + 8)], 0)
            found = mm(jnp.concatenate(split_parts(book, 2), 1), both)
            for i in range(8):
                total = total + jnp.where(major == first + i, found[cdim * i : cdim * (i + 1)], 0.0)
        r.chosen[...] = total

    @pl.when((step == frames) & ends.not_last)
    def _():
        for i in range(frames):
            copy(i).wait_send()

    @pl.when((step == frames) & ends.not_first)
    def _():
        for i in range(frames):
            copy(i).wait_recv()

    @pl.when((step == frames) & ends.is_first)
    def _():
        for i in range(frames):
            clear(i).wait()


def frame_ends():
    me, n = lax.axis_index("frame"), lax.axis_size("frame")
    return types.SimpleNamespace(
        is_first=me == 0, not_first=me > 0, is_last=me == n - 1, not_last=me < n - 1
    )


def spat_forward_call(x, weights, codes, book_t):
    frames, patches, d = x.shape
    hidden = weights[4].shape[1]
    n = frames * patches
    tiles = hidden // TILE
    at = part_of(0, frames)
    blk = pl.BlockSpec((1, patches, d), lambda i: (at(i), 0, 0))
    cols = pl.BlockSpec((d, patches), lambda i: (0, at(i)))
    rows = lambda width: pl.BlockSpec((patches, width), lambda i: (at(i), 0))
    tiled = lambda count, width: (
        shape_of((count, n, width), BF16), pl.BlockSpec((count, patches, width), lambda i: (0, at(i), 0))
    )
    ga, w_qkv, w_out, gb, w_up, w_down = weights
    wide = lambda width, dtype=BF16: (shape_of((n, width), dtype), rows(width))
    tall = (shape_of((d, n), BF16), cols)
    vmem = lambda array: pltpu.VMEM(array.shape, array.dtype)
    return launch(
        spat_forward_step, "spat_forward", frames + 1,
        dict(
            x=(x, blk), ga=fixed(ga), w_qkv=(w_qkv, ANY), w_out=(w_out, ANY), gb=fixed(gb), w_up=(w_up, ANY),
            w_down=(w_down, ANY), codes=fixed(codes), book=fixed(book_t),
        ),
        dict(
            y=(shape_of(x.shape, BF16), blk), at=tall, pk=wide(3 * d), att_t=tall, mid=wide(d, F32), bt=tall,
            h=tiled(hidden // 256, 256), gp=tiled(tiles, TILE), halo=(shape_of(x.shape, BF16), ANY),
            chosen=fixed_out((book_t.shape[0], n), F32),
        ),
        dict(
            att=pltpu.VMEM((patches, d), BF16), keep=pltpu.VMEM(x.shape, BF16), none=pltpu.VMEM((patches, d), BF16),
            send=pltpu.SemaphoreType.DMA((frames,)), recv=pltpu.SemaphoreType.DMA((frames,)),
            fetch=pltpu.SemaphoreType.DMA((2 + 2 * tiles,)), w_qkv_=vmem(w_qkv), w_out_=vmem(w_out),
            w_up_=pltpu.VMEM((tiles, d, TILE), BF16), w_down_=pltpu.VMEM((tiles, TILE, d), BF16),
        ),
        {}, 11, 2 * n * d * (4 * d + 2 * hidden + 2 * patches),
    )


class Fetch:
    def __init__(self, sem):
        self.sem, self.items = sem, []

    def add(self, src, dst):
        self.items.append((src, dst))
        return len(self.items) - 1

    def copy(self, i):
        return pltpu.make_async_copy(*self.items[i], self.sem.at[i])

    def start(self, first=0, stop=None):
        for i in range(len(self.items))[first:stop]:
            self.copy(i).start()

    def wait(self, *which):
        for i in which:
            self.copy(i).wait()


def mlp_tile(r, j, put_up, half_way=lambda: None):
    lead, per, d = r.db.shape
    for i in range(4):
        rows = slice(i * 256, (i + 1) * 256)
        these = slice(i * lead // 4, (i + 1) * lead // 4)
        dh = mm_t(r.dy[rows, :], r.w_down_[j])
        du = (r.gp_[j, rows, :].astype(F32) * dh).astype(BF16)
        r.du[rows, :] = du
        r.db[these] += mm_t(du, r.w_up_[j]).reshape(lead // 4, per, d)
        if i == 1:
            half_way()
    put_up(mm(r.bt_[...], r.du[...]).astype(BF16))


def down_tile(r, acc, j):
    for i in range(4):
        grad = mm(r.dyt[...], r.h_[4 * j + i]).astype(BF16)
        acc[2 * j + i // 2, i % 2] = grad.reshape(acc.shape[2:])


def mlp_up(mid, gain, w_up_, w_down_, put_bt, put):
    xhat, _ = norm(mid)
    b = (xhat * gain).astype(BF16)
    put_bt(b.T)
    out = mid
    for j in range(w_up_.shape[0]):
        u = mm(b, w_up_[j])
        u2 = u * u
        th = jnp.tanh(u * (GELU_C + (GELU_C * GELU_A) * u2))
        half = 0.5 + 0.5 * th
        h = (u * half).astype(BF16)
        slope = half + u * (half * (1.0 - th)) * (GELU_C + (3.0 * GELU_C * GELU_A) * u2)
        put(j, h, slope.astype(BF16))
        out = out + mm(h, w_down_[j])
    return out


def fetch_mlp(fetch, r, j):
    cols = pl.ds(j * TILE, TILE)
    return fetch.add(r.w_up.at[:, cols], r.w_up_.at[j]), fetch.add(r.w_down.at[cols, :], r.w_down_.at[j])


def middle(r, put):
    lead, per, d = r.db.shape
    for i in range(4):
        rows = slice(i * 256, (i + 1) * 256)
        these = slice(i * lead // 4, (i + 1) * lead // 4)
        xhat, rs = norm(r.mid_[rows, :])
        db = r.db[these].reshape(256, d)
        add_row(r.dg_b, db * xhat)
        dmid = r.dy[rows, :].astype(F32) + norm_back(db, xhat, rs, r.gb[...])
        r.db[these] = dmid.reshape(lead // 4, per, d)
        low = dmid.astype(BF16)
        put(i, low, mm_t(low, r.w_out_[...]).astype(BF16))


T_LOSS, T_MLP, T_MID, T_ATT, T_DOWN, T_GRAD = 4, 5, 9, 10, 12, 16


def temporal_forward(r, step, fetch, wait_first):
    frames, group, d = r.att.shape
    rows = frames * group
    lead = pl.ds(pl.multiple_of(frames * step, frames), frames)
    here = pl.ds(pl.multiple_of(rows * step, rows), rows)
    mine = pl.ds(pl.multiple_of(group * step, group), group)
    x = r.x[:, mine, :].reshape(rows, d).astype(F32)
    xhat, _ = norm(x)
    a = (xhat * r.ga[...]).astype(BF16)
    r.at_[:, here] = a.T
    for start in range(0, 3 * d, 512):
        part = mm(a, r.w_qkv_[:, start : start + 512]).astype(BF16)
        r.pk[lead, :, start : start + 512] = part.reshape(frames, group, 512)
    xhat_h, _ = norm(r.halo[:, mine, :].reshape(rows, d).astype(F32))
    ah = (xhat_h * r.ga[...]).astype(BF16)
    r.aht_[:, here] = ah.T
    for start in range(0, 2 * d, 512):
        part = mm(ah, r.w_qkv_[:, d + start : d + start + 512]).astype(BF16)
        r.kvh[lead, :, start : start + 512] = part.reshape(frames, group, 512)
    bias = r.bias[...]
    def one_sub(i_, c_):
        near = pl.ds(pl.multiple_of(i_ * SUB, SUB), SUB)
        for lane in range(0, d, 128):
            c0, c1, c2 = (slice(part * d + lane, part * d + lane + 128) for part in range(3))
            q = r.pk[lead, near, c0].reshape(frames * SUB, 128)
            k = jnp.concatenate([r.kvh[lead, near, c0], r.pk[lead, near, c1]], 0).reshape(2 * frames * SUB, 128)
            v = jnp.concatenate([r.kvh[lead, near, c1], r.pk[lead, near, c2]], 0).reshape(2 * frames * SUB, 128)
            r.att[:, near, c0] = attend_pair(q, k, v, bias).reshape(frames, SUB, 128)
        return c_

    lax.fori_loop(0, group // SUB, one_sub, 0)
    att = r.att[...].reshape(rows, d)
    r.att_t_[:, here] = att.T
    wait_first()
    mid = x + mm(att, r.w_out_[...])
    r.mid_[here, :] = mid

    def put_bt(value):
        r.bt_[:, here] = value

    def put(j, h, slope):
        for i in range(2):
            r.h_[2 * j + i, here, :] = h[:, 256 * i : 256 * (i + 1)]
        r.gp_[j, here, :] = slope

    r.x3[here, :] = mlp_up(mid, r.gb[...], r.w_up_, r.w_down_, put_bt, put).astype(BF16)


def temporal_step(r, m, place, step):
    frames, group, d = r.att.shape
    cdim, n = r.chosen.shape
    rows = frames * group
    ring = lax.axis_size("frame")
    me = lax.axis_index("frame")
    left, right = lax.rem(me + ring - 1, ring), lax.rem(me + 1, ring)
    ends = frame_ends()
    tiles = r.w_up_.shape[0]
    fetch = Fetch(r.fetch)
    first = [fetch.add(r.w_qkv, r.w_qkv_), fetch.add(r.w_out, r.w_out_)]
    later = [fetch_mlp(fetch, r, j) for j in range(tiles)]

    @on(step, 0)
    def _():
        place.greet()
        for peer in (left, right):
            pl.semaphore_signal(
                pltpu.get_barrier_semaphore(), inc=1, device_id={"frame": peer}, device_id_type=MESH
            )
        fetch.start()
        for ref in (r.dg_a, r.dg_b, r.db):
            ref[...] = jnp.zeros_like(ref)
        fetch.wait(first[0])

    @on(step, 0)
    def _():
        def wait_first():
            fetch.wait(first[1])
            for pair in later:
                fetch.wait(*pair)

        temporal_forward(r, 0, fetch, wait_first)

    @on(step, 1)
    def _():
        def one(i, carry):
            temporal_forward(r, i, fetch, lambda: None)
            return carry

        lax.fori_loop(1, r.lat.shape[2] // group, one, 0)

    @on(step, T_LOSS)
    def _():
        patches = r.lat.shape[2]
        commit = jnp.zeros((1, 1), F32)
        latent = mm_t(r.proj[...], r.x3[...])
        for f in range(frames):
            for g in range(patches // group):
                at = (g * frames + f) * group
                r.lat[f, :, g * group : (g + 1) * group] = latent[:, at : at + group]
            here = slice(f * patches, (f + 1) * patches)
            differ = r.lat[f] - r.chosen[:, here]
            commit = commit + jnp.sum(jnp.sum(differ * differ, 1, keepdims=True), 0, keepdims=True)
            grad = (r.cot[f] + (2.0 * BETA) * differ).astype(BF16)
            for g in range(patches // group):
                at = (g * frames + f) * group
                r.gl[:, at : at + group] = grad[:, g * group : (g + 1) * group]
            r.dbook[:, here] = ((-2.0 * BETA) * differ).astype(BF16)
        for i in range(4):
            part = slice(i * 256, (i + 1) * 256)
            r.dy[part, :] = t_mm(r.gl[:, part], r.proj[...]).astype(BF16)
        r.dyt[...] = t_mm(r.proj[...], r.gl[...]).astype(BF16)
        r.commit[...] = commit

    @within(step, T_MLP, 4)
    def _():
        j = step - T_MLP

        def put_up(value):
            r.a_acc[j // 2, j % 2] = value.reshape(r.a_acc.shape[2:])

        mlp_tile(r, j, put_up)

    @within(step, T_DOWN, 2)
    def _():
        down_tile(r, m.b.acc, step - T_DOWN)

    @on(step, T_MID)
    def _():
        def put(i, low, datt):
            for t in range(2):
                r.dm[t, 4 * i : 4 * i + 4] = low[:, 256 * t : 256 * (t + 1)].reshape(4, group, 256)
            r.datt[4 * i : 4 * i + 4] = datt.reshape(4, group, d)

        middle(r, put)

    s = att_step(step)
    attending = T_ATT <= step < T_DOWN or T_DOWN + 2 <= step < T_GRAD

    @on(int(attending), 1)
    def _():
        lead = pl.ds(frames * s, frames)
        bias = r.bias_t[...]
        half = frames * SUB
        def one_sub(i_, c_):
            near = pl.ds(pl.multiple_of(i_ * SUB, SUB), SUB)
            for lane in range(0, d, 128):
                c0, c1, c2 = (slice(part * d + lane, part * d + lane + 128) for part in range(3))
                q = r.pk[lead, near, c0].reshape(half, 128)
                k = jnp.concatenate([r.kvh[lead, near, c0], r.pk[lead, near, c1]], 0).reshape(2 * half, 128)
                v = jnp.concatenate([r.kvh[lead, near, c1], r.pk[lead, near, c2]], 0).reshape(2 * half, 128)
                do = r.datt[lead, near, c0].reshape(half, 128)
                dq, dk, dv = attend_pair_back(q, k, v, do, bias)
                tile, to = lane // 256, slice(lane % 256, lane % 256 + 128)
                for part, grad in enumerate((dq, dk[half:], dv[half:])):
                    r.dpk[2 * part + tile, lead, near, to] = grad.astype(BF16).reshape(frames, SUB, 128)
                for part, grad in enumerate((dk[:half], dv[:half])):
                    r.dkvh[2 * part + tile, lead, near, to] = grad.astype(BF16).reshape(frames, SUB, 128)
            return c_

        lax.fori_loop(0, group // SUB, one_sub, 0)
        dah = jnp.zeros((rows, d), F32)
        for i in range(4):
            dah = dah + mm_t(r.dkvh[i, lead].reshape(rows, 256), r.w_qkv_[:, d + 256 * i : d + 256 * (i + 1)])
        r.dah[s] = dah.astype(BF16).reshape(frames, group, d)
        da = jnp.zeros((rows, d), F32)
        for i in range(6):
            da = da + mm_t(r.dpk[i, lead].reshape(rows, 256), r.w_qkv_[:, 256 * i : 256 * (i + 1)])
        xhat, rs = norm(r.x[:, s * group : (s + 1) * group, :].reshape(rows, d).astype(F32))
        add_row(r.dg_a, da * xhat)
        dmid = r.db[lead].reshape(rows, d)
        r.base[:, s * group : (s + 1) * group, :] = (dmid + norm_back(da, xhat, rs, r.ga[...])).reshape(
            frames, group, d
        )

    def copy(i):
        there = r.back.at[:, pl.ds(i * group, group), :]
        return ring_copy(r.dah.at[i], there, r.send.at[i], r.recv.at[i], left)

    def clear(i):
        return pltpu.make_async_copy(r.none, r.back.at[:, pl.ds(i * group, group), :], r.recv.at[i])

    @on(step, T_GRAD)
    def _():
        codes = r.codes[...]
        major, onehot = code_masks(codes, 64)
        dbook = r.dbook[...]
        dproj = mm(r.gl[...], r.x3[...]).astype(BF16)
        part = cdim // 4
        for z in range(4):
            for x in range(2):
                f = 2 * z + x
                picked = [jnp.where(major == 8 * f + i, dbook, jnp.zeros((), BF16)) for i in range(8)]
                book = mm_t(jnp.concatenate(picked, 0), onehot).astype(BF16)
                r.d_part[z, x, :, :, : 2 * cdim] = book.reshape(2, 2, 2 * cdim, 128)
                r.d_part[z, x, :, :, 2 * cdim :] = jnp.zeros((2, 2, 16, 128), BF16)
                for q in range(4):
                    r.d_part[z, x, q // 2, q % 2, 2 * cdim : 2 * cdim + part, :64] = dproj[
                        part * q : part * (q + 1), 64 * f : 64 * (f + 1)
                    ]
        dead = r.dead.shape[0]
        used = jnp.where(r.dead[...] == codes, 1.0, 0.0).astype(BF16)
        usage = mm_t(jnp.ones((8, n), BF16), used)
        pick = jnp.where(r.source[...] == lax.broadcasted_iota(jnp.int32, (dead, n), 1), 1.0, 0.0).astype(BF16)
        latent = jnp.concatenate([r.lat[f] for f in range(frames)], 1)
        candidate = jnp.zeros((cdim, dead), F32)
        for one in split_parts(latent, 3):
            candidate = candidate + mm_t(one, pick)
        r.q_part[...] = jnp.zeros_like(r.q_part)
        r.q_part[:cdim, :dead] = candidate
        r.q_part[cdim:, :dead] = usage
        r.q_part[cdim:, dead:] = jnp.broadcast_to(r.commit[...], (8, 128 - dead))

    @within(step, T_GRAD, 2)
    def _():
        t = step - T_GRAD
        whole_rows = lambda value: value.reshape(n, 256)
        a, ah, att = r.at_[...], r.aht_[...], r.att_t_[...]
        parts = (
            mm(a, whole_rows(r.dpk[t])),
            mm(a, whole_rows(r.dpk[2 + t])) + mm(ah, whole_rows(r.dkvh[t])),
            mm(a, whole_rows(r.dpk[4 + t])) + mm(ah, whole_rows(r.dkvh[2 + t])),
            mm(att, whole_rows(r.dm[t])),
        )
        for kind, part in enumerate(parts):
            part = part.astype(BF16)
            for j in range(2):
                r.t_att[t, j, :, :, :, 128 * kind : 128 * (kind + 1)] = part[:, 128 * j : 128 * (j + 1)].reshape(
                    r.t_att.shape[2:5] + (128,)
                )

    @on(step, 0)
    def _():
        pl.semaphore_wait(pltpu.get_barrier_semaphore(), len(PEERS) + 2)

    @on(step, 0)
    def _():
        @pl.when(ends.is_last)
        def _():
            r.none[...] = jnp.zeros_like(r.none)
            for i in range(r.dah.shape[0]):
                clear(i).start()

    @on(int(attending), 1)
    def _():
        @pl.when(ends.not_first)
        def _():
            copy(s).start()

    @on(step, T_MLP + 1)
    def _():
        m.a0.start(0)

    @on(step, T_MLP + 2)
    def _():
        m.a0.move(0)

    @on(step, T_MLP + 3)
    def _():
        m.a1.start(0)

    @on(step, T_MID)
    def _():
        m.a1.move(0)

    @on(step, T_DOWN + 1)
    def _():
        m.b.start(0)

    @on(step, T_DOWN + 2)
    def _():
        m.b.move(0)

    @on(step, T_GRAD + 1)
    def _():
        for part in (m.a0, m.a1, m.b):
            part.finish(1)
        r.a_part[0] = m.a0.piece()
        r.a_part[1] = m.a1.piece()
        r.b_part[...] = m.b.piece()

        @pl.when(ends.not_first)
        def _():
            for i in range(r.dah.shape[0]):
                copy(i).wait_send()

        @pl.when(ends.not_last)
        def _():
            for i in range(r.dah.shape[0]):
                copy(i).wait_recv()

        @pl.when(ends.is_last)
        def _():
            for i in range(r.dah.shape[0]):
                clear(i).wait()


def att_step(step):
    return min(max(step - T_ATT, 0), 1) + min(max(step - T_DOWN - 1, 0), 2)


def temporal_call(x, halo, bias, cot_t, chosen, codes, dead, source, proj_t, weights):
    frames, patches, d = x.shape
    ga, w_qkv, w_out, gb, w_up, w_down = weights
    hidden = w_up.shape[1]
    n = frames * patches
    cdim = proj_t.shape[0]
    groups = patches // GROUP
    lead, tiles = frames * groups, hidden // TILE
    half_tail, col_tail, book_tail = (d // 16, TILE), (d // 4, hidden // 8), (2 * cdim + 16, 128)
    vmem = lambda array: pltpu.VMEM(array.shape, array.dtype)
    low = lambda *shape: pltpu.VMEM(shape, BF16)
    moves = dict(
        a0=Sum(E_DIMS, half_tail, ("c", "y"), shared=lambda r: r.a_acc, fixed={"u": 0}, gather=False),
        a1=Sum(E_DIMS, half_tail, ("c", "y"), shared=lambda r: r.a_acc, fixed={"u": 1}, gather=False),
        b=Sum(COLS_DIMS, col_tail, ("c", "y"), gather=False),
    )
    return launch(
        temporal_step, "temporal", T_GRAD + 2,
        dict(
            x=fixed(x), halo=fixed(halo), bias=fixed(bias), bias_t=fixed(bias.T),
            cot=fixed(cot_t), chosen=fixed(chosen), codes=fixed(codes), dead=fixed(dead), source=fixed(source),
            proj=fixed(proj_t), ga=fixed(ga), gb=fixed(gb), w_qkv=(w_qkv, ANY), w_out=(w_out, ANY), w_up=(w_up, ANY),
            w_down=(w_down, ANY),
        ),
        dict(
            lat=fixed_out((frames, cdim, patches), F32), base=fixed_out(x.shape, F32),
            back=(shape_of(x.shape, BF16), ANY), dg_a=fixed_out((1, d), F32), dg_b=fixed_out((1, d), F32),
            t_att=fixed_out((2, 2, 4, 2, d // 8, d), BF16),
            a_part=fixed_out((2, 4, 2) + half_tail, BF16),
            b_part=fixed_out((4, 2) + col_tail, BF16), d_part=fixed_out((4, 2, 2, 2) + book_tail, BF16),
            q_part=fixed_out((cdim + 8, 128), F32),
        ),
        dict(
            commit=pltpu.VMEM((1, 1), F32), gl=low(cdim, n), dbook=low(cdim, n), dy=low(n, d), dyt=low(d, n),
            du=low(n, TILE), db=pltpu.VMEM((lead, GROUP, d), F32), dm=low(2, lead, GROUP, 256),
            datt=low(lead, GROUP, d), dpk=low(6, lead, GROUP, 256), dkvh=low(4, lead, GROUP, 256),
            a_acc=low(2, 2, 4, 2, 2, *half_tail), dah=low(groups, frames, GROUP, d), none=low(frames, GROUP, d),
            send=pltpu.SemaphoreType.DMA((groups,)), recv=pltpu.SemaphoreType.DMA((groups,)),
            fetch=pltpu.SemaphoreType.DMA((2 + 2 * tiles,)), w_qkv_=vmem(w_qkv), w_out_=vmem(w_out),
            w_up_=low(tiles, d, TILE), w_down_=low(tiles, TILE, d), att=low(frames, GROUP, d),
            pk=low(lead, GROUP, 3 * d), kvh=low(lead, GROUP, 2 * d), at_=low(d, n), aht_=low(d, n), att_t_=low(d, n),
            bt_=low(d, n), mid_=pltpu.VMEM((n, d), F32), h_=low(hidden // 256, n, 256), gp_=low(tiles, n, TILE),
            x3=low(n, d),
        ),
        moves, 12, 6 * n * d * (6 * d + 2 * hidden) + 14 * n * d * patches, TAIL_BYTES, True,
    )


S_DOWN, S_MLP, S_MID, S_ATT, S_END = 1, 3, 7, 8, 12


def spat_backward_step(r, m, place, step):
    frames, patches, d = r.db.shape
    n = frames * patches
    tiles = r.w_up_.shape[0]
    fetch = Fetch(r.fetch)
    by_frame = [
        [fetch.add(a.at[f], b.at[f]) for a, b in ((r.base, r.base_), (r.dah, r.dah_), (r.x2, r.x2_))]
        for f in range(frames)
    ]
    h_tiles = [fetch.add(r.h.at[i], r.h_.at[i]) for i in range(r.h_.shape[0])]
    bt = fetch.add(r.bt, r.bt_)
    mlp = [(*fetch_mlp(fetch, r, j), fetch.add(r.gp.at[j], r.gp_.at[j])) for j in range(tiles)]
    mid, w_out, att_t = fetch.add(r.mid, r.mid_), fetch.add(r.w_out, r.w_out_), fetch.add(r.att_t, r.att_t_)
    pk, at, w_qkv, x = (
        fetch.add(a, b) for a, b in ((r.pk, r.pk_), (r.at, r.at_), (r.w_qkv, r.w_qkv_), (r.x, r.x_))
    )

    def transfers(point):
        start = lambda k, *parts: [part.start(k) for part in parts]
        move = lambda k, *parts: [part.move(k) for part in parts]
        finish = lambda k, *parts: [part.finish(k) for part in parts]
        gather = lambda *parts: [part.gather() for part in parts]
        spread = lambda *parts: [part.spread() for part in parts]
        todo = (
            ((start, 0, m.c, m.d, m.b, m.a0, m.q, m.a1),),
            ((move, 0, m.q),),
            ((start, 0, m.g), (move, 0, m.d),),
            ((move, 1, m.q),),
            ((move, 0, m.c), (move, 2, m.q), (move, 0, m.g),),
            ((finish, 3, m.q),),
            ((start, 0, m.e0), (move, 1, m.d),),
            ((move, 0, m.a0, m.a1),),
            ((move, 0, m.e0),),
            (),
            ((start, 0, m.e1),),
            ((move, 2, m.d), (move, 0, m.b, m.e1), (gather, m.a0, m.a1),),
            (),
            ((move, 1, m.c), (gather, m.d), (spread, m.a0, m.a1),),
            ((move, 1, m.g),),
            ((start, 0, m.h0a, m.h0b), (spread, m.d), (gather, m.b), (move, 1, m.e0),),
            ((move, 2, m.c), (move, 0, m.h0a, m.h0b),),
            ((spread, m.b), (move, 1, m.e1), (move, 2, m.e0),),
            ((move, 1, m.h0b),),
            ((start, 0, m.h1b, m.h1a), (move, 1, m.h0a), (move, 2, m.e1, m.g),),
            ((start, 0, m.w), (gather, m.c), (move, 0, m.h1b), (move, 2, m.h0a, m.h0b), (move, 0, m.w),
                (gather, m.e0), (move, 0, m.h1a),),
            ((move, 1, m.w), (spread, m.c, m.e0), (move, 1, m.h1b), (move, 2, m.w), (gather, m.e1), (move,
                1, m.h1a), (gather, m.h0a, m.h0b), (finish, 3, m.w), (move, 2, m.h1b), (spread, m.e1),
                (gather, m.g), (move, 2, m.h1a), (gather, m.h1b), (spread, m.g), (gather, m.h1a),),
        )
        for what, *args in todo[point]:
            what(*args)

    @on(step, 0)
    def _():
        place.greet()
        fetch.start(0, 3 * frames)
        m.q.acc[...] = r.q_part[...]
        pl.semaphore_wait(pltpu.get_barrier_semaphore(), len(PEERS))
        transfers(0)
        fetch.start(3 * frames)
        for ref in (r.dg_t, r.dg_a, r.dg_b, r.db, r.da):
            ref[...] = jnp.zeros_like(ref)
        for f in range(frames):
            fetch.wait(*by_frame[f])
            xhat, rs = norm(r.x2_[f].astype(F32))
            dah = r.dah_[f].astype(F32)
            add_row(r.dg_t, dah * xhat)
            low = (r.base_[f] + norm_back(dah, xhat, rs, r.gta[...])).astype(BF16)
            here = slice(f * patches, (f + 1) * patches)
            r.dy[here, :] = low
            r.dyt[:, here] = low.T
    for j in range(2):

        @on(step, S_DOWN + j)
        def _(j=j):
            fetch.wait(*h_tiles[4 * j : 4 * j + 4])

    @on(step, S_MLP)
    def _():
        fetch.wait(bt)

    for j in range(tiles):

        @on(step, S_MLP + j)
        def _(j=j):
            fetch.wait(*mlp[j])

    @within(step, S_MLP, 4)
    def _():
        j = step - S_MLP

        def put_up(value):
            r.e_acc[j // 2, j % 2] = value.reshape(r.e_acc.shape[2:])

        mlp_tile(r, j, put_up, lambda: transfers(3 + 2 * j))
        transfers(4 + 2 * j)

    @within(step, S_DOWN, 2)
    def _():
        down_tile(r, m.g.acc, step - S_DOWN)
        transfers(1 + step - S_DOWN)

    @on(step, S_MID)
    def _():
        fetch.wait(mid, w_out)

        def put(i, low, datt):
            rows = slice(i * 256, (i + 1) * 256)
            r.dm[rows, :] = low
            for p in range(d // 128):
                r.datt[p, rows, :] = datt[:, 128 * p : 128 * (p + 1)]

        middle(r, put)
        fetch.wait(att_t)
        grad = mm(r.att_t_[...], r.dm[...]).astype(BF16)
        for q in range(4):
            r.h_acc[q // 2, 1, q % 2, :, :, :, :, 128:] = grad[:, 128 * q : 128 * (q + 1)].reshape(
                r.h_acc.shape[3:7] + (128,)
            )
        fetch.wait(pk, at, w_qkv)
        transfers(11)

    @within(step, S_ATT, 4)
    def _():
        p = step - S_ATT
        cols = [slice(part * d + 128 * p, part * d + 128 * (p + 1)) for part in range(3)]
        for f in range(frames):
            here = slice(f * patches, (f + 1) * patches)
            grads = attend_pair_back(*[r.pk_[here, c] for c in cols], r.datt[p, here, :], None)
            for part, grad in enumerate(grads):
                r.dpk[here, 128 * part : 128 * (part + 1)] = grad.astype(BF16)
            if f == 1:
                transfers(12 + 2 * p)
        grad = mm(r.at_[...], r.dpk[...]).astype(BF16)
        u, c = p // 2, p % 2
        shape = r.h_acc.shape[3:7]
        r.h_acc[u, 0, c] = grad[:, :256].reshape(shape + (256,))
        r.h_acc[u, 1, c, :, :, :, :, :128] = grad[:, 256:].reshape(shape + (128,))
        weights = jnp.concatenate([r.w_qkv_[:, c] for c in cols], 1)
        for f in range(frames):
            r.da[f] += mm_t(r.dpk[f * patches : (f + 1) * patches, :], weights)
        transfers(13 + 2 * p)

    @on(step, S_END)
    def _():
        fetch.wait(x)
        for f in range(frames):
            xhat, rs = norm(r.x_[f].astype(F32))
            da = r.da[f]
            add_row(r.dg_a, da * xhat)
            r.dx[f] = (r.db[f] + norm_back(da, xhat, rs, r.ga[...])).astype(BF16)
        gains = (r.dg_t[...] + r.dgt_own[...], r.dgt_mid[...], r.dg_a[...], r.dg_b[...])
        for i, gain in enumerate(gains):
            for j in range(d // 128):
                row = i * (d // 128) + j
                m.w.acc[row : row + 1, :] = gain[:, 128 * j : 128 * (j + 1)]
        transfers(20)

    @on(step, S_END + 1)
    def _():
        transfers(21)
        outs = (
            (m.a0, r.a0_all), (m.a1, r.a1_all), (m.b, r.b_all), (m.c, r.c_all), (m.d, r.d_all), (m.e0, r.e0_all),
            (m.e1, r.e1_all), (m.g, r.g_all), (m.h0a, r.h00_all), (m.h0b, r.h01_all), (m.h1a, r.h10_all),
            (m.h1b, r.h11_all),
        )
        for part, out in outs:
            part.gathered(out)
        r.w_all[...] = m.w.acc[...]
        r.q_all[...] = m.q.acc[...]


def spat_backward_call(f, t, x2, gta, x, weights):
    frames, patches, d = x.shape
    ga, w_qkv, w_out, gb, w_up, w_down = weights
    hidden = w_up.shape[1]
    n = frames * patches
    tiles = hidden // TILE
    col_tail = (d // 4, hidden // 8)
    half_tail, quarter_tail = (d // 16, TILE), (d // 16, 256)
    e_acc, h_acc = (lambda r: r.e_acc), (lambda r: r.h_acc)
    vmem = lambda array: pltpu.VMEM(array.shape, array.dtype)
    moves = dict(
        b=Sum(("z", "x"), col_tail, ("x", "z"), source=lambda r: r.b_part),
        a0=Sum(("u", "z", "x"), half_tail, ("x", "z"), source=lambda r: r.a_part, fixed={"u": 0}),
        a1=Sum(("u", "z", "x"), half_tail, ("x", "z"), source=lambda r: r.a_part, fixed={"u": 1}),
        c=Sum(ROWS_DIMS, (d // 8, d), Y_FIRST, source=lambda r: r.t_att),
        e0=Sum(E_DIMS, half_tail, Y_FIRST, shared=e_acc, fixed={"u": 0}),
        e1=Sum(E_DIMS, half_tail, Y_FIRST, shared=e_acc, fixed={"u": 1}),
        g=Sum(COLS_DIMS, col_tail, X_FIRST),
        h0a=Sum(H_DIMS, quarter_tail, Y_FIRST, shared=h_acc, fixed={"u": 0, "w": 0}, direct=True),
        h0b=Sum(H_DIMS, quarter_tail, X_FIRST, shared=h_acc, fixed={"u": 0, "w": 1}, direct=True),
        h1a=Sum(H_DIMS, quarter_tail, Y_FIRST, shared=h_acc, fixed={"u": 1, "w": 0}, direct=True),
        h1b=Sum(H_DIMS, quarter_tail, X_FIRST, shared=h_acc, fixed={"u": 1, "w": 1}, direct=True),
        d=Sum(COLS_DIMS, t.d_part.shape[4:], Y_FIRST, source=lambda r: r.d_part), q=Total(t.q_part.shape[0]),
        w=Total(4 * d // 128),
    )
    pieces = lambda tail: fixed_out((2, 2) + tail, BF16)
    return launch(
        spat_backward_step, "spat_backward", 14,
        dict(
            base=(t.base, ANY), dah=(t.back, ANY), x2=(x2, ANY), gta=fixed(gta), x=(x, ANY), gp=(f.gp, ANY), h=(f.h, ANY),
            pk=(f.pk, ANY), w_qkv=(w_qkv, ANY), ga=fixed(ga), gb=fixed(gb), w_up=(w_up, ANY), w_down=(w_down, ANY),
            dgt_own=fixed(t.dg_a), dgt_mid=fixed(t.dg_b), bt=(f.bt, ANY), mid=(f.mid, ANY), w_out=(w_out, ANY),
            att_t=(f.att_t, ANY), at=(f.at, ANY), a_part=(t.a_part, ANY), b_part=(t.b_part, ANY), t_att=(t.t_att, ANY),
            d_part=(t.d_part, ANY), q_part=fixed(t.q_part),
        ),
        dict(
            dx=fixed_out(x.shape, BF16), a0_all=pieces(half_tail), a1_all=pieces(half_tail), b_all=pieces(col_tail), c_all=pieces((d // 8, d)),
            e0_all=pieces(half_tail), e1_all=pieces(half_tail), g_all=pieces(col_tail), h00_all=pieces(quarter_tail),
            h01_all=pieces(quarter_tail), h10_all=pieces(quarter_tail), h11_all=pieces(quarter_tail),
            w_all=fixed_out((4 * d // 128, 128), F32), q_all=fixed_out(t.q_part.shape, F32),
            d_all=pieces(t.d_part.shape[4:]),
        ),
        dict(
            dg_t=pltpu.VMEM((1, d), F32), dg_a=pltpu.VMEM((1, d), F32), dg_b=pltpu.VMEM((1, d), F32),
            dy=pltpu.VMEM((n, d), BF16), dyt=pltpu.VMEM((d, n), BF16), du=pltpu.VMEM((n, TILE), BF16),
            db=pltpu.VMEM(x.shape, F32), da=pltpu.VMEM(x.shape, F32), dm=pltpu.VMEM((n, d), BF16),
            datt=pltpu.VMEM((d // 128, n, 128), BF16), dpk=pltpu.VMEM((n, 384), BF16),
            e_acc=pltpu.VMEM((2, 2, 4, 2, 2) + half_tail, BF16), h_acc=pltpu.VMEM((2, 2, 2, 4, 2, 2) + quarter_tail, BF16),
            fetch=pltpu.SemaphoreType.DMA((3 * frames + 3 * tiles + hidden // 256 + 8,)), bt_=vmem(f.bt), mid_=vmem(f.mid),
            w_out_=vmem(w_out), att_t_=vmem(f.att_t), at_=vmem(f.at), x_=vmem(x), base_=vmem(t.base), dah_=vmem(t.back),
            x2_=vmem(x2), h_=vmem(f.h), gp_=vmem(f.gp), pk_=vmem(f.pk), w_qkv_=vmem(w_qkv),
            w_up_=pltpu.VMEM((tiles, d, TILE), BF16), w_down_=pltpu.VMEM((tiles, TILE, d), BF16),
        ),
        moves, 13, 4 * n * d * (4 * d + 2 * hidden) + 10 * n * d * patches, TAIL_BYTES, True,
    )


def finish_step(r, m, place, step):
    d = r.t_out.shape[1]
    half = d // 16
    for y in range(2):
        for c in range(2):
            q = 2 * y + c
            lanes = slice(128 * q, 128 * (q + 1))
            r.t_down[:, lanes] = r.b_all[y, c].astype(F32).T
            r.s_down[:, lanes] = r.g_all[y, c].astype(F32).T
            value = r.c_all[y, c].astype(F32)
            for kind in range(3):
                r.t_qkv[:, d * kind + 128 * q : d * kind + 128 * (q + 1)] = value[:, 128 * kind : 128 * (kind + 1)]
            r.t_out[:, lanes] = value[:, 384:]
            book = r.d_all[y, c].astype(F32)
            cdim = r.book.shape[0]
            r.proj_grad[cdim // 4 * q : cdim // 4 * (q + 1), :] = book[2 * cdim : 2 * cdim + cdim // 4, :64]
            for i in range(2):
                r.book_grad[:, 128 * (2 * q + i) : 128 * (2 * q + i + 1)] = book[cdim * i : cdim * (i + 1)]
            rows = slice(half * y, half * (y + 1))
            for u, t_up, up, left, right in (
                (0, r.a0_all, r.e0_all, r.h00_all, r.h01_all), (1, r.a1_all, r.e1_all, r.h10_all, r.h11_all)
            ):
                at = 2 * u + c
                r.t_up[rows, TILE * at : TILE * (at + 1)] = t_up[y, c].astype(F32)
                r.s_up[rows, TILE * at : TILE * (at + 1)] = up[y, c].astype(F32)
                pair, other = left[y, c].astype(F32), right[y, c].astype(F32)
                for kind, part in enumerate((pair[:, :128], pair[:, 128:], other[:, :128])):
                    r.s_qkv[rows, d * kind + 128 * at : d * kind + 128 * (at + 1)] = part
                r.s_out[rows, 128 * at : 128 * (at + 1)] = other[:, 128:]
    for i, gain in enumerate((r.g_ta, r.g_tb, r.g_sa, r.g_sb)):
        for j in range(d // 128):
            row = i * (d // 128) + j
            gain[:, 128 * j : 128 * (j + 1)] = r.w_all[row : row + 1, :]
    dead = r.dead_row.shape[1]
    candidate = r.q_all[:cdim, :dead]
    low = r.q_all[cdim : cdim + 1, :dead] < USE_MIN
    r.commit[...] = r.q_all[cdim : cdim + 1, dead : dead + 1] * (1.0 / r.scale)
    major = lax.div(r.dead_row[...], 128)
    minor = lax.rem(r.dead_col[...], 128)
    onehot = jnp.where(lax.broadcasted_iota(jnp.int32, (dead, 128), 1) == minor, 1.0, 0.0).astype(BF16)
    parts = split_parts(jnp.where(low, candidate, 0.0), 3)
    count = r.book.shape[1] // 128
    a_rows = lax.broadcasted_iota(jnp.int32, (count, dead), 0)
    replaced = mm(jnp.where((major == a_rows) & low, 1.0, 0.0).astype(BF16), onehot)
    for begin in range(0, count, 8):
        fresh = jnp.zeros((8 * cdim, 128), F32)
        for part in parts:
            chosen = [jnp.where(major == begin + i, part, jnp.zeros((), BF16)) for i in range(8)]
            fresh = fresh + mm(jnp.concatenate(chosen, 0), onehot)
        for i in range(8):
            at = begin + i
            lanes = slice(128 * at, 128 * (at + 1))
            r.refreshed[:, lanes] = jnp.where(
                replaced[at : at + 1] > 0.5, fresh[cdim * i : cdim * (i + 1)], r.book[:, lanes]
            )


def finish_call(t, s, book_t, dead, total, d, hidden):
    cdim, codes = book_t.shape
    piece = d // 8
    ins = dict(
        a0_all=s.a0_all, a1_all=s.a1_all, b_all=s.b_all, c_all=s.c_all, d_all=s.d_all, e0_all=s.e0_all, e1_all=s.e1_all, g_all=s.g_all,
        h00_all=s.h00_all, h01_all=s.h01_all, h10_all=s.h10_all, h11_all=s.h11_all, w_all=s.w_all, q_all=s.q_all,
        book=book_t, dead_row=dead.reshape(1, -1), dead_col=dead.reshape(-1, 1),
    )
    outs = dict(
        t_up=(piece, hidden), t_down=(hidden // 8, d), t_qkv=(piece, 3 * d), t_out=(piece, d),
        s_up=(piece, hidden), s_down=(hidden // 8, d), s_qkv=(piece, 3 * d), s_out=(piece, d),
        g_ta=(1, d), g_tb=(1, d), g_sa=(1, d), g_sb=(1, d), proj_grad=(cdim, piece), commit=(1, 1),
        book_grad=(cdim, codes // 8), refreshed=(cdim, codes),
    )

    def body(r, m, place, step):
        r.scale = total
        finish_step(r, m, place, step)

    return launch(
        body, "finish", 1, {k: fixed(v) for k, v in ins.items()}, {k: fixed_out(v, F32) for k, v in outs.items()},
        {}, {}, None, 1 << 28,
    )


def frame_bias(clip_row, frame_count):
    first = lax.axis_index("frame") * frame_count
    clips = jnp.concatenate([jnp.full((SPAN,), -1, jnp.int32), clip_row])
    key_clips = lax.dynamic_slice_in_dim(clips, first, SPAN + frame_count)
    qi, qp = jnp.arange(frame_count * SUB) // SUB, jnp.arange(frame_count * SUB) % SUB
    kj, kp = jnp.arange((SPAN + frame_count) * SUB) // SUB, jnp.arange((SPAN + frame_count) * SUB) % SUB
    offset = qi[:, None] + SPAN - kj[None, :]
    allowed = (
        (qp[:, None] == kp[None, :]) & (offset >= 0) & (offset <= SPAN)
        & (jnp.repeat(key_clips[SPAN:], SUB)[:, None] == jnp.repeat(key_clips, SUB)[None, :])
    )
    return jnp.where(allowed, 0.0, NEG).astype(F32)


def local_fused(
    frames_in, spat_gain_a, spat_qkv, spat_out, spat_gain_b, spat_up, spat_down,
    temp_gain_a, temp_qkv, temp_out, temp_gain_b, temp_up, temp_down,
    quant_proj, codebook, code_index, clip_index, dead_codes, source_rows, latent_cot,
):
    frame_count, patches, d = frames_in.shape[1:]
    cdim = quant_proj.shape[1]
    row_count = frame_count * patches
    frame_size, batch_size = lax.axis_size("frame"), lax.axis_size("batch")
    assert frame_count == SPAN
    spat = (spat_gain_a.reshape(1, d), spat_qkv, spat_out, spat_gain_b.reshape(1, d), spat_up, spat_down)
    temp = (temp_gain_a.reshape(1, d), temp_qkv, temp_out, temp_gain_b.reshape(1, d), temp_up, temp_down)
    x = frames_in[0]
    codes = code_index.reshape(1, -1)
    book_t, proj_t = codebook.T, quant_proj.T
    bias = frame_bias(clip_index[0], frame_count)
    row_base = (lax.axis_index("batch") * frame_size + lax.axis_index("frame")) * row_count
    sf = spat_forward_call(x, spat, codes, book_t)
    tb = temporal_call(
        sf.y, sf.halo, bias, latent_cot[0].transpose(0, 2, 1), sf.chosen, codes, dead_codes.reshape(-1, 1),
        (source_rows - row_base).reshape(-1, 1), proj_t, temp,
    )
    sb = spat_backward_call(sf, tb, sf.y, temp[0], x, spat)
    out = finish_call(
        tb, sb, book_t, dead_codes, frame_size * batch_size * row_count * cdim, d, spat_up.shape[1]
    )
    return (
        tb.lat.transpose(0, 2, 1)[None], out.commit[0, 0], sb.dx[None],
        out.g_sa[0], out.s_qkv, out.s_out, out.g_sb[0], out.s_up, out.s_down,
        out.g_ta[0], out.t_qkv, out.t_out, out.g_tb[0], out.t_up, out.t_down,
        out.proj_grad.T, out.book_grad.T, out.refreshed.T,
    )


def solution(mesh):
    fused = (mesh.shape["frame"], mesh.shape["batch"]) == (8, 4)
    return jax.shard_map(
        local_fused if fused else local_general,
        mesh=mesh,
        in_specs=(
            P("batch", "frame", None, None),
            *([P()] * 14),
            P("batch", "frame", None),
            P("batch", None),
            P(),
            P(),
            P("batch", "frame", None, None),
        ),
        out_specs=(
            P("batch", "frame", None, None),
            P(),
            P("batch", "frame", None, None),
            P(),
            P("frame", None),
            P("frame", None),
            P(),
            P("frame", None),
            P("frame", None),
            P(),
            P("frame", None),
            P("frame", None),
            P(),
            P("frame", None),
            P("frame", None),
            P("frame", None),
            P("frame", None),
            P(),
        ),
        check_vma=False,
    )
```

```python
import types

import jax
import jax.numpy as jnp
from jax import lax
from jax.experimental import pallas as pl
from jax.experimental.pallas import tpu as pltpu
from jax.sharding import PartitionSpec as P

HEADS = 8
EPS = 1e-05
BETA = 0.25
USE_MIN = 2.0
NEG = -1e30
HIGH = lax.Precision.HIGHEST
SPAN = 4
F32 = jnp.float32
BF16 = jnp.bfloat16
MESH = pl.DeviceIdType.MESH
GELU_C = 0.7978845608028654
GELU_A = 0.044715
VMEM_BYTES = 56 * 1024 * 1024
TAIL_BYTES = 62 * 1024 * 1024
SUB = 32
GROUP = 64


def mm(a, b):
    return jnp.dot(a, b, preferred_element_type=F32)


def mm_t(a, b):
    return lax.dot_general(a, b, (((1,), (1,)), ((), ())), preferred_element_type=F32)


def t_mm(a, b):
    return lax.dot_general(a, b, (((0,), (0,)), ((), ())), preferred_element_type=F32)


def norm(x):
    c = x - jnp.mean(x, -1, keepdims=True)
    r = lax.rsqrt(jnp.mean(c * c, -1, keepdims=True) + EPS)
    return c * r, r


def norm_back(dy, xhat, r, gain):
    d = dy * gain
    return r * (d - jnp.mean(d, -1, keepdims=True) - xhat * jnp.mean(d * xhat, -1, keepdims=True))


def add_row(ref, rows):
    ref[...] += jnp.sum(rows, 0, keepdims=True)


def head_masks(rows, width):
    lane = lax.broadcasted_iota(jnp.int32, (rows, width), 1)
    return (lane < width // 2, lane >= width // 2)


def attend_pair(q, k, v, bias):
    width = q.shape[1]
    scale = (width // 2) ** -0.5
    zero = jnp.zeros((), BF16)
    qs = q * jnp.asarray(scale, BF16)
    v_ext = jnp.concatenate([v, jnp.ones_like(v)], axis=1)
    masks = head_masks(q.shape[0], width)
    halves = []
    for mask in masks:
        s = mm_t(jnp.where(mask, qs, zero), k)
        if bias is not None:
            s = s + bias
        e = jnp.exp(s - jnp.max(s, -1, keepdims=True)).astype(BF16)
        r = mm(e, v_ext)
        halves.append(r[:, :width] / r[:, width:])
    return jnp.where(masks[0], halves[0], halves[1]).astype(BF16)


def attend_pair_back(q, k, v, do, bias_t):
    width = q.shape[1]
    scale = jnp.asarray((width // 2) ** -0.5, BF16)
    zero = jnp.zeros((), BF16)
    qs = q * scale
    ks = k * scale
    q_masks = head_masks(q.shape[0], width)
    k_masks = head_masks(k.shape[0], width)
    dq = dk = dv = None
    for q_mask, k_mask in zip(q_masks, k_masks):
        qm = jnp.where(q_mask, qs, zero)
        dom = jnp.where(q_mask, do, zero)
        st = mm_t(k, qm)
        if bias_t is not None:
            st = st + bias_t
        e = jnp.exp(st - jnp.max(st, 0, keepdims=True))
        p = e * (1.0 / jnp.sum(e, 0, keepdims=True))
        dp = mm_t(v, dom)
        inner = jnp.sum(p * dp, 0, keepdims=True)
        ds = (p * (dp - inner)).astype(BF16)
        dv_one = mm(p.astype(BF16), dom)
        dk_one = mm(ds, qm)
        dq_one = t_mm(ds, jnp.where(k_mask, ks, zero))
        dq = dq_one if dq is None else dq + dq_one
        dk = dk_one if dk is None else dk + dk_one
        dv = dv_one if dv is None else dv + dv_one
    return dq, dk, dv


def mlp_forward(mid, gain, w_up, w_down, bt_ref, h_ref, gp_ref, tile=512):
    xhat, _ = norm(mid)
    b = (xhat * gain).astype(BF16)
    bt_ref[...] = b.T
    out = mid
    for start in range(0, w_up.shape[1], tile):
        cols = slice(start, start + tile)
        u = mm(b, w_up[:, cols])
        u2 = u * u
        th = jnp.tanh(u * (GELU_C + (GELU_C * GELU_A) * u2))
        half = 0.5 + 0.5 * th
        h = (u * half).astype(BF16)
        slope = half + u * (half * (1.0 - th)) * (GELU_C + (3.0 * GELU_C * GELU_A) * u2)
        h_ref[:, cols] = h
        gp_ref[:, cols] = slope.astype(BF16)
        out = out + mm(h, w_down[cols, :])
    return out


def mlp_backward(dy, dy_low, mid, gain, w_up, w_down, gp_ref, du_ref, dgain_ref, tile=512):
    db = None
    for start in range(0, w_up.shape[1], tile):
        cols = slice(start, start + tile)
        dh = mm_t(dy_low, w_down[cols, :])
        du = (gp_ref[:, cols].astype(F32) * dh).astype(BF16)
        du_ref[:, cols] = du
        one = mm_t(du, w_up[:, cols])
        db = one if db is None else db + one
    xhat, r = norm(mid)
    add_row(dgain_ref, db * xhat)
    return dy + norm_back(db, xhat, r, gain)


def greet_ring(step):
    n = lax.axis_size("frame")
    me = lax.axis_index("frame")
    left, right = lax.rem(me + n - 1, n), lax.rem(me + 1, n)

    @pl.when(step == 0)
    def _():
        barrier = pltpu.get_barrier_semaphore()
        for peer in (left, right):
            pl.semaphore_signal(barrier, inc=1, device_id={"frame": peer}, device_id_type=MESH)

    return left, right


def meet_ring(step):
    @pl.when(step == 0)
    def _():
        pl.semaphore_wait(pltpu.get_barrier_semaphore(), 2)


def ring_copy(src, dst, send_sem, recv_sem, peer):
    return pltpu.make_async_remote_copy(
        src_ref=src, dst_ref=dst, send_sem=send_sem, recv_sem=recv_sem,
        device_id={"frame": peer}, device_id_type=MESH,
    )


def spat_fwd_kernel(
    x_ref, ga, w_qkv, w_out, gb, w_up, w_down,
    y_ref, at_ref, pk_ref, att_t_ref, mid_ref, bt_ref, h_ref, gp_ref, halo_ref,
    att_ref, keep_ref, send_sem, recv_sem,
):
    step = pl.program_id(0)
    steps = pl.num_programs(0)
    feature = x_ref.shape[-1]
    left, right = greet_ring(step)
    x = x_ref[0].astype(F32)
    xhat, _ = norm(x)
    a = (xhat * ga[...]).astype(BF16)
    at_ref[...] = a.T
    for start in range(0, 3 * feature, 512):
        pk_ref[:, start : start + 512] = mm(a, w_qkv[:, start : start + 512]).astype(BF16)
    for lane in range(0, feature, 128):
        att_ref[:, lane : lane + 128] = attend_pair(
            pk_ref[:, lane : lane + 128],
            pk_ref[:, feature + lane : feature + lane + 128],
            pk_ref[:, 2 * feature + lane : 2 * feature + lane + 128],
            None,
        )
    att = att_ref[...]
    att_t_ref[...] = att.T
    mid = x + mm(att, w_out[...])
    mid_ref[...] = mid
    y = mlp_forward(mid, gb[...], w_up, w_down, bt_ref, h_ref, gp_ref).astype(BF16)
    y_ref[0] = y
    keep_ref[step] = y
    meet_ring(step)

    def copy(i):
        return ring_copy(keep_ref.at[i], halo_ref.at[i], send_sem.at[i], recv_sem.at[i], right)

    copy(step).start()

    @pl.when(step == steps - 1)
    def _():
        for i in range(keep_ref.shape[0]):
            copy(i).wait()


def temp_fwd_kernel(
    x_ref, halo_ref, bias_ref, ga, w_qkv, w_out, gb, w_up, w_down, proj,
    lat_ref, x3_ref, at_ref, aht_ref, pk_ref, kvh_ref, att_t_ref, mid_ref, bt_ref, h_ref, gp_ref, att_ref,
):
    frames, group, feature = x_ref.shape
    rows = frames * group
    x = x_ref[...].reshape(rows, feature).astype(F32)
    xhat, _ = norm(x)
    a = (xhat * ga[...]).astype(BF16)
    at_ref[...] = a.T
    for start in range(0, 3 * feature, 512):
        pk_ref[:, :, start : start + 512] = (
            mm(a, w_qkv[:, start : start + 512]).astype(BF16).reshape(frames, group, 512)
        )
    xhat_h, _ = norm(halo_ref[...].reshape(rows, feature).astype(F32))
    ah = (xhat_h * ga[...]).astype(BF16)
    aht_ref[...] = ah.T
    for start in range(0, 2 * feature, 512):
        kvh_ref[:, :, start : start + 512] = (
            mm(ah, w_qkv[:, feature + start : feature + start + 512])
            .astype(BF16)
            .reshape(frames, group, 512)
        )
    bias = bias_ref[...]
    for sub in range(0, group, SUB):
        here = slice(sub, sub + SUB)
        for lane in range(0, feature, 128):
            q = pk_ref[:, here, lane : lane + 128].reshape(frames * SUB, 128)
            k = jnp.concatenate(
                [kvh_ref[:, here, lane : lane + 128],
                 pk_ref[:, here, feature + lane : feature + lane + 128]], 0
            ).reshape(2 * frames * SUB, 128)
            v = jnp.concatenate(
                [kvh_ref[:, here, feature + lane : feature + lane + 128],
                 pk_ref[:, here, 2 * feature + lane : 2 * feature + lane + 128]], 0
            ).reshape(2 * frames * SUB, 128)
            att_ref[:, here, lane : lane + 128] = attend_pair(q, k, v, bias).reshape(frames, SUB, 128)
    att = att_ref[...].reshape(rows, feature)
    att_t_ref[...] = att.T
    mid = x + mm(att, w_out[...])
    mid_ref[...] = mid
    y = mlp_forward(mid, gb[...], w_up, w_down, bt_ref, h_ref, gp_ref).astype(BF16)
    x3_ref[...] = y
    lat_ref[...] = mm(y, proj[...]).reshape(frames, group, proj.shape[1])


def temp_bwd_kernel(
    gl_ref, proj, x3_ref, x_ref, mid_ref, gp_ref, pk_ref, kvh_ref, bias_ref,
    ga, w_qkv, w_out, gb, w_up, w_down,
    dyt_ref, du_ref, dmid_ref, dpk_ref, dkvh_ref, base_ref, back_ref, dga_ref, dgb_ref, dproj_ref,
    datt_ref, dah_ref, send_sem, recv_sem,
):
    step = pl.program_id(0)
    steps = pl.num_programs(0)
    frames, group, feature = x_ref.shape
    rows = frames * group
    left, right = greet_ring(step)

    @pl.when(step == 0)
    def _():
        for ref in (dga_ref, dgb_ref, dproj_ref):
            ref[...] = jnp.zeros_like(ref)

    gl = gl_ref[...].reshape(rows, gl_ref.shape[2])
    dproj_ref[...] += t_mm(gl, x3_ref[...])
    dy_low = mm_t(gl, proj[...]).astype(BF16)
    dyt_ref[...] = dy_low.T
    dmid = mlp_backward(
        dy_low.astype(F32), dy_low, mid_ref[...], gb[...], w_up, w_down, gp_ref, du_ref, dgb_ref
    )
    dmid_low = dmid.astype(BF16)
    dmid_ref[...] = dmid_low
    datt_ref[...] = mm_t(dmid_low, w_out[...]).astype(BF16).reshape(frames, group, feature)
    bias = bias_ref[...]
    half = frames * SUB
    for sub in range(0, group, SUB):
        here = slice(sub, sub + SUB)
        for lane in range(0, feature, 128):
            l0 = slice(lane, lane + 128)
            l1 = slice(feature + lane, feature + lane + 128)
            l2 = slice(2 * feature + lane, 2 * feature + lane + 128)
            q = pk_ref[:, here, l0].reshape(half, 128)
            k = jnp.concatenate([kvh_ref[:, here, l0], pk_ref[:, here, l1]], 0).reshape(2 * half, 128)
            v = jnp.concatenate([kvh_ref[:, here, l1], pk_ref[:, here, l2]], 0).reshape(2 * half, 128)
            do = datt_ref[:, here, l0].reshape(half, 128)
            dq, dk, dv = attend_pair_back(q, k, v, do, bias)
            dk, dv = dk.astype(BF16), dv.astype(BF16)
            dpk_ref[:, here, l0] = dq.astype(BF16).reshape(frames, SUB, 128)
            dpk_ref[:, here, l1] = dk[half:].reshape(frames, SUB, 128)
            dpk_ref[:, here, l2] = dv[half:].reshape(frames, SUB, 128)
            dkvh_ref[:, here, l0] = dk[:half].reshape(frames, SUB, 128)
            dkvh_ref[:, here, l1] = dv[:half].reshape(frames, SUB, 128)
    da = mm_t(dpk_ref[...].reshape(rows, 3 * feature), w_qkv[...])
    dah = mm_t(dkvh_ref[...].reshape(rows, 2 * feature), w_qkv[:, feature:])
    dah_ref[step] = dah.astype(BF16).reshape(frames, group, feature)
    meet_ring(step)

    def copy(i):
        there = back_ref.at[:, pl.ds(i * group, group), :]
        return ring_copy(dah_ref.at[i], there, send_sem.at[i], recv_sem.at[i], left)

    copy(step).start()
    xhat, r = norm(x_ref[...].reshape(rows, feature).astype(F32))
    add_row(dga_ref, da * xhat)
    base_ref[...] = (dmid + norm_back(da, xhat, r, ga[...])).reshape(frames, group, feature)

    @pl.when(step == steps - 1)
    def _():
        for i in range(dah_ref.shape[0]):
            copy(i).wait()


def spat_bwd_kernel(
    base_ref, dah_ref, x2_ref, gta, x_ref, mid_ref, gp_ref, pk_ref,
    ga, w_qkv, w_out, gb, w_up, w_down,
    dx_ref, dyt_ref, du_ref, dmid_ref, dpk_ref, dgt_ref, dga_ref, dgb_ref,
    datt_ref,
):
    feature = x_ref.shape[-1]

    @pl.when(pl.program_id(0) == 0)
    def _():
        for ref in (dgt_ref, dga_ref, dgb_ref):
            ref[...] = jnp.zeros_like(ref)

    xhat2, r2 = norm(x2_ref[0].astype(F32))
    dah = dah_ref[0].astype(F32)
    add_row(dgt_ref, dah * xhat2)
    dy_low = (base_ref[0] + norm_back(dah, xhat2, r2, gta[...])).astype(BF16)
    dyt_ref[...] = dy_low.T
    dmid = mlp_backward(
        dy_low.astype(F32), dy_low, mid_ref[...], gb[...], w_up, w_down, gp_ref, du_ref, dgb_ref
    )
    dmid_low = dmid.astype(BF16)
    dmid_ref[...] = dmid_low
    datt_ref[...] = mm_t(dmid_low, w_out[...]).astype(BF16)
    for lane in range(0, feature, 128):
        l0 = slice(lane, lane + 128)
        l1 = slice(feature + lane, feature + lane + 128)
        l2 = slice(2 * feature + lane, 2 * feature + lane + 128)
        dq, dk, dv = attend_pair_back(pk_ref[:, l0], pk_ref[:, l1], pk_ref[:, l2], datt_ref[:, l0], None)
        dpk_ref[:, l0] = dq.astype(BF16)
        dpk_ref[:, l1] = dk.astype(BF16)
        dpk_ref[:, l2] = dv.astype(BF16)
    da = mm_t(dpk_ref[...], w_qkv[...])
    xhat, r = norm(x_ref[0].astype(F32))
    add_row(dga_ref, da * xhat)
    dx_ref[0] = (dmid + norm_back(da, xhat, r, ga[...])).astype(BF16)


def mlp_grad_kernel(bt_ref, du_ref, dyt_ref, h_ref, up_ref, down_ref):
    up_ref[0] = mm(bt_ref[...], du_ref[...]).astype(BF16)
    width = down_ref.shape[2]
    for j in range(down_ref.shape[0]):
        down_ref[j] = mm(dyt_ref[...], h_ref[:, j * width : (j + 1) * width]).astype(BF16)


def att_grad_kernel(halo, *refs):
    if halo:
        at_ref, att_t_ref, dq_ref, dk_ref, dv_ref, dm_ref, aht_ref, dkh_ref, dvh_ref, out_ref = refs
    else:
        at_ref, att_t_ref, dq_ref, dk_ref, dv_ref, dm_ref, out_ref = refs
    dq = mm(at_ref[...], dq_ref[...])
    dk = mm(at_ref[...], dk_ref[...])
    dv = mm(at_ref[...], dv_ref[...])
    if halo:
        dk = dk + mm(aht_ref[...], dkh_ref[...])
        dv = dv + mm(aht_ref[...], dvh_ref[...])
    do = mm(att_t_ref[...], dm_ref[...])
    for i, part in enumerate((dq, dk, dv, do)):
        part = part.astype(BF16)
        for j in range(2):
            out_ref[j, :, 128 * i : 128 * (i + 1)] = part[:, 128 * j : 128 * (j + 1)]


def whole(shape):
    zeros = (0,) * len(shape)
    return pl.BlockSpec(shape, lambda i: zeros)


def col_block(rows, width, offset=0):
    return pl.BlockSpec((rows, width), lambda i: (0, i + offset))


def row_block(rows, width):
    return pl.BlockSpec((rows, width), lambda i: (i, 0))


def shape_of(shape, dtype):
    return jax.ShapeDtypeStruct(shape, dtype)


def params(collective=None):
    return pltpu.CompilerParams(
        vmem_limit_bytes=VMEM_BYTES, dimension_semantics=("arbitrary",), collective_id=collective,
        has_side_effects=collective is not None,
    )


def cost(flops, nbytes):
    return pl.CostEstimate(flops=int(flops), bytes_accessed=int(nbytes), transcendentals=0)


def weight_specs(feature, hidden):
    return [
        whole((1, feature)), whole((feature, 3 * feature)), whole((feature, feature)),
        whole((1, feature)), whole((feature, hidden)), whole((hidden, feature)),
    ]


def spat_forward(x, weights):
    frames, patches, d = x.shape
    hidden = weights[4].shape[1]
    n = frames * patches
    blk = pl.BlockSpec((1, patches, d), lambda i: (i, 0, 0))
    return pl.pallas_call(
        spat_fwd_kernel,
        grid=(frames,),
        in_specs=[blk] + weight_specs(d, hidden),
        out_specs=[
            blk, col_block(d, patches), row_block(patches, 3 * d), col_block(d, patches),
            row_block(patches, d), col_block(d, patches), row_block(patches, hidden), row_block(patches, hidden),
            pl.BlockSpec(memory_space=pl.ANY),
        ],
        out_shape=[
            shape_of(x.shape, BF16), shape_of((d, n), BF16), shape_of((n, 3 * d), BF16), shape_of((d, n), BF16),
            shape_of((n, d), F32), shape_of((d, n), BF16), shape_of((n, hidden), BF16), shape_of((n, hidden), BF16),
            shape_of(x.shape, BF16),
        ],
        scratch_shapes=[
            pltpu.VMEM((patches, d), BF16), pltpu.VMEM(x.shape, BF16),
            pltpu.SemaphoreType.DMA((frames,)), pltpu.SemaphoreType.DMA((frames,)),
        ],
        compiler_params=params(1),
        cost_estimate=cost(2 * n * d * (4 * d + 2 * hidden + 2 * patches), 24 * n * d),
        name="spat_forward",
    )(x, *weights)


def temp_forward(x, halo, bias, weights, proj):
    frames, patches, d = x.shape
    hidden = weights[4].shape[1]
    n = frames * patches
    steps = patches // GROUP
    rows = frames * GROUP
    cdim = proj.shape[1]
    blk = pl.BlockSpec((frames, GROUP, d), lambda i: (0, i, 0))
    stacked = lambda width: pl.BlockSpec((frames, GROUP, width), lambda i: (i, 0, 0))
    return pl.pallas_call(
        temp_fwd_kernel,
        grid=(steps,),
        in_specs=[blk, blk, whole(bias.shape)] + weight_specs(d, hidden) + [whole(proj.shape)],
        out_specs=[
            pl.BlockSpec((frames, GROUP, cdim), lambda i: (0, i, 0)), row_block(rows, d),
            col_block(d, rows), col_block(d, rows), stacked(3 * d), stacked(2 * d), col_block(d, rows),
            row_block(rows, d), col_block(d, rows), row_block(rows, hidden), row_block(rows, hidden),
        ],
        out_shape=[
            shape_of((frames, patches, cdim), F32), shape_of((n, d), BF16),
            shape_of((d, n), BF16), shape_of((d, n), BF16),
            shape_of((frames * steps, GROUP, 3 * d), BF16), shape_of((frames * steps, GROUP, 2 * d), BF16),
            shape_of((d, n), BF16), shape_of((n, d), F32), shape_of((d, n), BF16),
            shape_of((n, hidden), BF16), shape_of((n, hidden), BF16),
        ],
        scratch_shapes=[pltpu.VMEM((frames, GROUP, d), BF16)],
        compiler_params=params(),
        cost_estimate=cost(2 * n * d * (6 * d + 2 * hidden + 2 * patches), 30 * n * d),
        name="temp_forward",
    )(x, halo, bias, *weights, proj)


def temp_backward(gl, proj, x3, x, mid, gp, pk, kvh, bias_t, weights):
    frames, patches, d = x.shape
    hidden = weights[4].shape[1]
    n = frames * patches
    steps = patches // GROUP
    rows = frames * GROUP
    cdim = proj.shape[1]
    nat = lambda width: pl.BlockSpec((frames, GROUP, width), lambda i: (0, i, 0))
    stacked = lambda width: pl.BlockSpec((frames, GROUP, width), lambda i: (i, 0, 0))
    return pl.pallas_call(
        temp_bwd_kernel,
        grid=(steps,),
        in_specs=[
            nat(cdim), whole(proj.shape), row_block(rows, d), nat(d), row_block(rows, d),
            row_block(rows, hidden), stacked(3 * d), stacked(2 * d), whole(bias_t.shape),
        ] + weight_specs(d, hidden),
        out_specs=[
            col_block(d, rows), row_block(rows, hidden), row_block(rows, d), stacked(3 * d), stacked(2 * d),
            nat(d), pl.BlockSpec(memory_space=pl.ANY), whole((1, d)), whole((1, d)), whole((cdim, d)),
        ],
        out_shape=[
            shape_of((d, n), BF16), shape_of((n, hidden), BF16), shape_of((n, d), BF16),
            shape_of((frames * steps, GROUP, 3 * d), BF16), shape_of((frames * steps, GROUP, 2 * d), BF16),
            shape_of((frames, patches, d), F32), shape_of((frames, patches, d), BF16),
            shape_of((1, d), F32), shape_of((1, d), F32), shape_of((cdim, d), F32),
        ],
        scratch_shapes=[
            pltpu.VMEM((frames, GROUP, d), BF16), pltpu.VMEM((steps, frames, GROUP, d), BF16),
            pltpu.SemaphoreType.DMA((steps,)), pltpu.SemaphoreType.DMA((steps,)),
        ],
        compiler_params=params(2),
        cost_estimate=cost(2 * n * d * (6 * d + 2 * hidden + 5 * patches), 40 * n * d),
        name="temp_backward",
    )(gl, proj, x3, x, mid, gp, pk, kvh, bias_t, *weights)


def spat_backward(base, dah, x2, gta, x, mid, gp, pk, weights):
    frames, patches, d = x.shape
    hidden = weights[4].shape[1]
    n = frames * patches
    blk = pl.BlockSpec((1, patches, d), lambda i: (i, 0, 0))
    return pl.pallas_call(
        spat_bwd_kernel,
        grid=(frames,),
        in_specs=[
            blk, blk, blk, whole((1, d)), blk, row_block(patches, d), row_block(patches, hidden),
            row_block(patches, 3 * d),
        ] + weight_specs(d, hidden),
        out_specs=[
            blk, col_block(d, patches), row_block(patches, hidden), row_block(patches, d),
            row_block(patches, 3 * d), whole((1, d)), whole((1, d)), whole((1, d)),
        ],
        out_shape=[
            shape_of(x.shape, BF16), shape_of((d, n), BF16), shape_of((n, hidden), BF16), shape_of((n, d), BF16),
            shape_of((n, 3 * d), BF16), shape_of((1, d), F32), shape_of((1, d), F32), shape_of((1, d), F32),
        ],
        scratch_shapes=[pltpu.VMEM((patches, d), BF16)],
        compiler_params=params(),
        cost_estimate=cost(2 * n * d * (4 * d + 2 * hidden + 5 * patches), 30 * n * d),
        name="spat_backward",
    )(base, dah, x2, gta, x, mid, gp, pk, *weights)


def mlp_grads(bt, du, dyt, h):
    d, n = bt.shape
    hidden = du.shape[1]
    steps = 4
    wide = hidden // steps
    return pl.pallas_call(
        mlp_grad_kernel,
        grid=(steps,),
        in_specs=[whole((d, n)), col_block(n, wide), whole((d, n)), col_block(n, wide)],
        out_specs=[
            pl.BlockSpec((1, d, wide), lambda i: (i, 0, 0)),
            pl.BlockSpec((2, d, wide // 2), lambda i: (i, 0, 0)),
        ],
        out_shape=[shape_of((steps, d, wide), BF16), shape_of((2 * steps, d, wide // 2), BF16)],
        compiler_params=params(),
        cost_estimate=cost(4 * n * d * hidden, 8 * n * d + 4 * n * hidden),
        name="mlp_grads",
    )(bt, du, dyt, h)


def att_grads(at, att_t, dpk, dmid, aht=None, dkvh=None):
    d, n = at.shape
    halo = aht is not None
    wide = 256
    args = [at, att_t, dpk, dpk, dpk, dmid]
    specs = [
        whole((d, n)), whole((d, n)), col_block(n, wide), col_block(n, wide, d // wide),
        col_block(n, wide, 2 * d // wide), col_block(n, wide),
    ]
    if halo:
        args += [aht, dkvh, dkvh]
        specs += [whole((d, n)), col_block(n, wide), col_block(n, wide, d // wide)]
    return pl.pallas_call(
        lambda *refs: att_grad_kernel(halo, *refs),
        grid=(d // wide,),
        in_specs=specs,
        out_specs=pl.BlockSpec((2, d, 512), lambda i: (i, 0, 0)),
        out_shape=shape_of((d // 128, d, 512), BF16),
        compiler_params=params(),
        cost_estimate=cost(2 * n * d * d * (6 if halo else 4), 16 * n * d),
        name="att_grads",
    )(*args)


def bits_of(count):
    bits = count.bit_length() - 1
    assert count == 1 << bits
    return bits


def swap(value, axis, bit):
    count = lax.axis_size(axis)
    return lax.ppermute(value, axis, [(i, i ^ (1 << bit)) for i in range(count)])


def my_bit(axis, bit):
    return (lax.axis_index(axis) >> bit) & 1


def reduce_pieces(grad, labels, order):
    names = []
    for axis in labels:
        names += [(axis, b) for b in reversed(range(bits_of(lax.axis_size(axis))))]
    tail = grad.shape[len(labels) :]
    cur = grad.reshape((2,) * len(names) + tail)
    for axis, bit in order:
        at = names.index((axis, bit))
        me = my_bit(axis, bit)
        kept = lax.dynamic_index_in_dim(cur, me, at, keepdims=False)
        sent = lax.dynamic_index_in_dim(cur, 1 - me, at, keepdims=False)
        cur = (kept.astype(F32) + swap(sent, axis, bit).astype(F32)).astype(BF16)
        names.pop(at)
    cur = cur[None]
    for bit in reversed(range(bits_of(lax.axis_size("batch")))):
        other = swap(cur, "batch", bit)
        low = my_bit("batch", bit) == 0
        cur = jnp.stack([jnp.where(low, cur, other), jnp.where(low, other, cur)], 1)
        cur = cur.reshape((-1,) + tail)
    return cur.astype(F32)


def orders():
    fb, bb = bits_of(lax.axis_size("frame")), bits_of(lax.axis_size("batch"))
    frame = [("frame", b) for b in [0] + list(reversed(range(1, fb)))]
    batch = [("batch", b) for b in range(bb)]
    return batch + frame, batch[:1] + frame[:1] + batch[1:] + frame[1:]


def local_general(
    frames_in, spat_gain_a, spat_qkv, spat_out, spat_gain_b, spat_up, spat_down,
    temp_gain_a, temp_qkv, temp_out, temp_gain_b, temp_up, temp_down,
    quant_proj, codebook, code_index, clip_index, dead_codes, source_rows, latent_cot,
):
    frame_count, patches, d = frames_in.shape[1:]
    cdim = quant_proj.shape[1]
    row_count = frame_count * patches
    frame_size, batch_size = lax.axis_size("frame"), lax.axis_size("batch")
    assert frame_count == SPAN
    spat = (spat_gain_a.reshape(1, d), spat_qkv, spat_out, spat_gain_b.reshape(1, d), spat_up, spat_down)
    temp = (temp_gain_a.reshape(1, d), temp_qkv, temp_out, temp_gain_b.reshape(1, d), temp_up, temp_down)
    x = frames_in[0]

    first = lax.axis_index("frame") * frame_count
    clips = jnp.concatenate([jnp.full((SPAN,), -1, jnp.int32), clip_index[0]])
    key_clips = lax.dynamic_slice_in_dim(clips, first, SPAN + frame_count)
    query_clips = key_clips[SPAN:]
    qi, qp = jnp.arange(frame_count * SUB) // SUB, jnp.arange(frame_count * SUB) % SUB
    kj, kp = jnp.arange((SPAN + frame_count) * SUB) // SUB, jnp.arange((SPAN + frame_count) * SUB) % SUB
    offset = qi[:, None] + SPAN - kj[None, :]
    allowed = (
        (qp[:, None] == kp[None, :]) & (offset >= 0) & (offset <= SPAN)
        & (jnp.repeat(query_clips, SUB)[:, None] == jnp.repeat(key_clips, SUB)[None, :])
    )
    bias = jnp.where(allowed, 0.0, NEG).astype(F32)

    x2, s_at, s_pk, s_att_t, s_mid, s_bt, s_h, s_gp, halo = spat_forward(x, spat)
    latent3, x3, t_at, t_aht, t_pk, t_kvh, t_att_t, t_mid, t_bt, t_h, t_gp = temp_forward(
        x2, halo, bias, temp, quant_proj
    )

    latent = latent3.reshape(-1, cdim)
    codes_flat = code_index.reshape(-1)
    chosen = jnp.take(codebook, codes_flat, axis=0)
    differ = latent - chosen
    commit_part = jnp.sum(differ * differ)
    grad_latent = (latent_cot.reshape(-1, cdim) + 2.0 * BETA * differ).astype(BF16)
    grad_book = jax.ops.segment_sum(-2.0 * BETA * differ, codes_flat, num_segments=codebook.shape[0])

    dyt, du, dmid, dpk, dkvh, base, dah_back, dg_ta, dg_tb, dproj = temp_backward(
        grad_latent.reshape(latent3.shape), quant_proj, x3, x2, t_mid, t_gp, t_pk, t_kvh, bias.T, temp
    )
    t_up, t_down = mlp_grads(t_bt, du, dyt, t_h)
    t_att = att_grads(
        t_at, t_att_t, dpk.reshape(row_count, -1), dmid, t_aht, dkvh.reshape(row_count, -1)
    )
    dx, dyt, du, dmid, dpk, dg_ta2, dg_sa, dg_sb = spat_backward(
        base, dah_back, x2, temp[0], x, s_mid, s_gp, s_pk, spat
    )
    s_up, s_down = mlp_grads(s_bt, du, dyt, s_h)
    s_att = att_grads(s_at, s_att_t, dpk, dmid)

    dead_match = (codes_flat[:, None] == dead_codes[None, :]).astype(F32)
    usage_part = jnp.sum(dead_match, 0)
    row_base = (lax.axis_index("batch") * frame_size + lax.axis_index("frame")) * row_count
    pick_table = ((source_rows - row_base)[:, None] == jnp.arange(row_count)[None, :]).astype(F32)
    picked = jnp.dot(pick_table, latent, precision=HIGH)
    usage_count, candidate, commit_total = lax.psum((usage_part, picked, commit_part), ("frame", "batch"))
    gain_ta, gain_tb, gain_sa, gain_sb = lax.psum(
        ((dg_ta + dg_ta2)[0], dg_tb[0], dg_sa[0], dg_sb[0]), ("frame", "batch")
    )
    old_rows = jnp.take(codebook, dead_codes, axis=0)
    fresh_rows = jnp.where((usage_count < USE_MIN)[:, None], candidate, old_rows)
    refreshed = codebook.at[dead_codes].set(fresh_rows)
    commit_loss = commit_total / (frame_size * batch_size * row_count * cdim)

    one, two = orders()
    piece = d // frame_size

    def by_rows(grad, order):
        return reduce_pieces(
            grad.reshape(batch_size, frame_size, -1, grad.shape[-1]), ("batch", "frame"), order
        )

    def finish_up(grad):
        return by_rows(grad, one).transpose(1, 0, 2).reshape(piece, -1)

    def finish_down(grad):
        hidden = grad.shape[0] * grad.shape[2]
        wide = hidden // frame_size
        if grad.shape[2] != wide:
            grad = grad.transpose(1, 0, 2).reshape(d, frame_size, wide).transpose(1, 0, 2)
        out = reduce_pieces(
            grad.reshape(frame_size, batch_size, d // batch_size, wide), ("frame", "batch"), two
        )
        return out.reshape(d, wide).T

    def finish_att(grad, order):
        out = by_rows(grad, order)
        qkv = out[:, :, :384].reshape(batch_size, piece, 3, -1).transpose(1, 2, 0, 3).reshape(piece, 3 * d)
        return qkv, out[:, :, 384:].transpose(1, 0, 2).reshape(piece, d)

    book = grad_book.reshape(frame_size, batch_size, -1, 128)
    proj = dproj.T.reshape(frame_size, batch_size, -1)
    proj_size = proj.shape[2]
    proj = jnp.pad(proj, ((0, 0), (0, 0), (0, -proj_size % 128))).reshape(frame_size, batch_size, -1, 128)
    small = jnp.concatenate([book, proj], 2).astype(BF16)
    small = reduce_pieces(small, ("frame", "batch"), two)
    book_rows = book.shape[2]
    g_book = small[:, :book_rows].reshape(-1, cdim)
    g_proj = small[:, book_rows:].reshape(batch_size, -1)[:, :proj_size].reshape(piece, cdim)
    gt_qkv, gt_out = finish_att(t_att, one)
    gs_qkv, gs_out = finish_att(s_att, one)
    return (
        latent.reshape(latent_cot.shape),
        commit_loss,
        dx[None],
        gain_sa,
        gs_qkv,
        gs_out,
        gain_sb,
        finish_up(s_up),
        finish_down(s_down),
        gain_ta,
        gt_qkv,
        gt_out,
        gain_tb,
        finish_up(t_up),
        finish_down(t_down),
        g_proj,
        g_book,
        refreshed,
    )


def stack_heads(x, masks):
    zero = jnp.zeros((), BF16)
    return jnp.concatenate([jnp.where(mask, x, zero) for mask in masks], 0)


def attend_both(q, k, v, bias):
    rows, width = q.shape
    masks = head_masks(rows, width)
    s = mm_t(stack_heads(q * jnp.asarray((width // 2) ** -0.5, BF16), masks), k)
    if bias is not None:
        s = s + bias
    e = jnp.exp(s - jnp.max(s, -1, keepdims=True)).astype(BF16)
    r = mm(e, jnp.concatenate([v, jnp.ones_like(v)], axis=1))
    r = r[:, :width] / r[:, width:]
    return jnp.where(masks[0], r[:rows], r[rows:]).astype(BF16)


def attend_both_back(q, k, v, do, bias_t):
    rows, width = q.shape
    scale = jnp.asarray((width // 2) ** -0.5, BF16)
    masks = head_masks(rows, width)
    q2, do2 = stack_heads(q * scale, masks), stack_heads(do, masks)
    st = mm_t(k, q2)
    if bias_t is not None:
        st = st + bias_t
    e = jnp.exp(st - jnp.max(st, 0, keepdims=True))
    p = e * (1.0 / jnp.sum(e, 0, keepdims=True))
    dp = mm_t(v, do2)
    inner = jnp.sum(p * dp, 0, keepdims=True)
    ds = (p * (dp - inner)).astype(BF16)
    dq = t_mm(ds, k * scale)
    return jnp.where(masks[0], dq[:rows], dq[rows:]), mm(ds, q2), mm(p.astype(BF16), do2)


SIZE = {"y": 2, "c": 2, "z": 4, "x": 2}
PEERS = ({"y": 1}, {"c": 1}, {"y": 1, "c": 1}, {"x": 1}, {"z": 1}, {"z": 2}, {"z": 3})
ROWS_DIMS = ("y", "c", "z", "x")
COLS_DIMS = ("z", "x", "y", "c")
E_DIMS = ("u", "c", "z", "x", "y")
H_DIMS = ("u", "w", "c", "z", "x", "y")
Y_FIRST = ("c", "y", "x", "z")
X_FIRST = ("c", "x", "y", "z")
TILE = 512


class Place:
    def __init__(self):
        batch, frame = lax.axis_index("batch"), lax.axis_index("frame")
        self.me = {"y": lax.div(batch, 2), "c": lax.rem(batch, 2), "z": lax.div(frame, 2), "x": lax.rem(frame, 2)}

    def next(self, dim, shift):
        return lax.rem(self.me[dim] + shift, SIZE[dim])

    def peer(self, shifts):
        at = {d: self.next(d, shifts[d]) if d in shifts else self.me[d] for d in SIZE}
        return {"batch": 2 * at["y"] + at["c"], "frame": 2 * at["z"] + at["x"]}

    def copy(self, src, dst, send, recv, shifts):
        return pltpu.make_async_remote_copy(
            src_ref=src, dst_ref=dst, send_sem=send, recv_sem=recv,
            device_id=self.peer(shifts), device_id_type=MESH,
        )

    def greet(self):
        for shifts in PEERS:
            pl.semaphore_signal(
                pltpu.get_barrier_semaphore(), inc=1, device_id=self.peer(shifts), device_id_type=MESH
            )


def sizes(dims):
    return tuple(SIZE[d] for d in dims)


class Sum:
    def __init__(self, dims, tail, order, source=None, shared=None, fixed=(), gather=True, direct=False):
        self.dims, self.tail, self.order, self.source, self.shared = dims, tail, order, source, shared
        self.fixed, self.with_gather, self.direct = dict(fixed), gather, direct
        self.counts = [SIZE[d] - 1 for d in order]

    def left(self, k):
        free = [d for d in self.dims if d not in self.fixed]
        return [d for d in free if d not in self.order or self.order.index(d) > k]

    def scratch(self):
        out = []
        if self.shared is None:
            kept = self.left(0 if self.source else -1)
            out.append(pltpu.VMEM(sizes(kept) + self.tail, BF16))
        for k, count in enumerate(self.counts):
            out.append(pltpu.VMEM((count,) + sizes(self.left(k)) + self.tail, BF16))
        if self.with_gather:
            out.append(pltpu.VMEM((2, 2) + self.tail, BF16))
        copies = sum(self.counts) + 3
        out += [pltpu.SemaphoreType.DMA((copies,))] * 2
        if self.source:
            out.append(pltpu.SemaphoreType.DMA)
        return out

    def bind(self, refs, r, place):
        self.place = place
        self.src = self.source(r) if self.source else None
        self.acc = self.shared(r) if self.shared else next(refs)
        self.got = [next(refs) for _ in self.counts]
        self.all = next(refs) if self.with_gather else None
        self.send, self.recv = next(refs), next(refs)
        self.load = next(refs) if self.source else None
        return self

    def index(self, dims, k, at_k, rest=None):
        out = []
        for d in dims:
            at = self.order.index(d) if d in self.order else len(self.order)
            if d in self.fixed:
                out.append(self.fixed[d])
            elif at < k:
                out.append(self.place.me[d])
            elif at == k and d in self.order:
                out.append(at_k)
            else:
                out.append(slice(None) if rest is None else rest[d])
        return tuple(out)

    def held(self):
        if self.shared:
            return self.dims
        return self.left(0 if self.source else -1)

    def copies(self, k):
        early = k == 0 and self.source
        src, dims = (self.src, self.dims) if early else (self.acc, self.held())
        base = sum(self.counts[:k])
        for i in range(self.counts[k]):
            there = self.index(dims, k, self.place.next(self.order[k], i + 1))
            yield self.place.copy(
                src.at[there], self.got[k].at[i], self.send.at[base + i], self.recv.at[base + i], {self.order[k]: i + 1}
            )

    def keep(self):
        here = self.index(self.dims, 0, self.place.me[self.order[0]])
        return pltpu.make_async_copy(self.src.at[here], self.acc, self.load)

    def start(self, k):
        for copy in self.copies(k):
            copy.start()
        if k == 0 and self.source:
            self.keep().start()

    def finish(self, k):
        for copy in self.copies(k):
            copy.wait()
        if k == 0 and self.source:
            self.keep().wait()
        left, got, count = self.left(k), self.got[k], self.counts[k]
        total = 1
        for d in left:
            total *= SIZE[d]

        def add(i):
            rest, stride = {}, total
            for d in left:
                stride //= SIZE[d]
                rest[d] = lax.rem(lax.div(i, stride), SIZE[d])
            here = self.index(self.held(), k, self.place.me[self.order[k]], rest)
            there = tuple(rest[d] for d in left)
            if count == 1:
                self.acc[here] = self.acc[here] + got[(0,) + there]
            else:
                value = self.acc[here].astype(F32)
                for j in range(count):
                    value = value + got[(j,) + there].astype(F32)
                self.acc[here] = value.astype(BF16)

        if total == 1:
            add(0)
        else:
            lax.fori_loop(0, total, lambda i, c: (add(i), c)[1], 0)

    def move(self, k):
        self.finish(k)
        self.start(k + 1)

    def piece(self):
        return self.acc[self.index(self.held(), len(self.order), None)]

    def hops(self, which):
        base = sum(self.counts)
        y, c = self.place.me["y"], self.place.me["c"]
        here = self.all.at[y, c]
        if self.direct:
            todo = [(here, shifts) for shifts in PEERS[:3]] if which == 0 else []
        else:
            todo = [(here, PEERS[0])] if which == 0 else [(self.all.at[:, c], PEERS[1])]
        for j, (ref, shifts) in enumerate(todo):
            at = base + which + j
            yield self.place.copy(ref, ref, self.send.at[at], self.recv.at[at], shifts)

    def gather(self):
        self.finish(len(self.order) - 1)
        self.all[self.place.me["y"], self.place.me["c"]] = self.piece()
        for copy in self.hops(0):
            copy.start()

    def spread(self):
        for copy in self.hops(0):
            copy.wait()
        for copy in self.hops(1):
            copy.start()

    def gathered(self, out):
        for copy in self.hops(0 if self.direct else 1):
            copy.wait()
        out[...] = self.all[...]


class Total:
    order = Y_FIRST

    def __init__(self, rows):
        self.rows = rows

    def scratch(self):
        copies = sum(SIZE[d] - 1 for d in self.order)
        return [
            pltpu.VMEM((self.rows, 128), F32), pltpu.VMEM((copies, self.rows, 128), F32),
            pltpu.SemaphoreType.DMA((copies,)), pltpu.SemaphoreType.DMA((copies,)),
        ]

    def bind(self, refs, r, place):
        self.place = place
        self.acc, self.got, self.send, self.recv = (next(refs) for _ in range(4))
        return self

    def copies(self, k):
        base = sum(SIZE[d] - 1 for d in self.order[:k])
        for i in range(SIZE[self.order[k]] - 1):
            at = base + i
            yield at, self.place.copy(
                self.acc, self.got.at[at], self.send.at[at], self.recv.at[at], {self.order[k]: i + 1}
            )

    def start(self, k):
        for _, copy in self.copies(k):
            copy.start()

    def finish(self, k):
        arrived = []
        for at, copy in self.copies(k):
            copy.wait()
            arrived.append(at)
        for at in arrived:
            self.acc[...] = self.acc[...] + self.got[at]

    def move(self, k):
        self.finish(k)
        self.start(k + 1)


def launch(body, name, steps, ins, outs, scratch, moves, collective, flops, limit=VMEM_BYTES, unroll=False):
    keys = [*ins, *outs, *scratch]
    extra = [spec for part in moves.values() for spec in part.scratch()]

    def kernel(*refs):
        r = types.SimpleNamespace(**dict(zip(keys, refs)))
        rest = iter(refs[len(keys) :])
        place = Place()
        m = types.SimpleNamespace(**{k: v.bind(rest, r, place) for k, v in moves.items()})
        if unroll:
            for step in range(steps):
                body(r, m, place, step)
        else:
            body(r, m, place, pl.program_id(0))

    got = pl.pallas_call(
        kernel,
        grid=(1 if unroll else steps,),
        in_specs=[x[1] for x in ins.values()],
        out_specs=[x[1] for x in outs.values()],
        out_shape=[x[0] for x in outs.values()],
        scratch_shapes=list(scratch.values()) + extra,
        compiler_params=pltpu.CompilerParams(
            vmem_limit_bytes=limit, dimension_semantics=("arbitrary",), collective_id=collective,
            has_side_effects=collective is not None,
        ),
        cost_estimate=cost(flops, 40 << 20),
        name=name,
    )(*[x[0] for x in ins.values()])
    return types.SimpleNamespace(**dict(zip(outs, got)))


ANY = pl.BlockSpec(memory_space=pl.ANY)


def fixed_spec(shape):
    zeros = (0,) * len(shape)
    return pl.BlockSpec(shape, lambda i: zeros, pipeline_mode=pl.Buffered(1))


def fixed(array):
    return (array, fixed_spec(array.shape))


def fixed_out(shape, dtype):
    return (shape_of(shape, dtype), fixed_spec(shape))


def part_of(first, count):
    return lambda i: jnp.clip(i - first, 0, count - 1)


def on(step, value):
    if isinstance(step, int):
        return lambda f: f() if step == value else None
    return lambda f: pl.when(step == value)(f)


def within(step, first, count):
    if isinstance(step, int):
        return lambda f: f() if first <= step < first + count else None
    return lambda f: pl.when((step >= first) & (step < first + count))(f)


def split_parts(value, count):
    out = []
    for _ in range(count):
        low = value.astype(BF16)
        out.append(low)
        value = value - low.astype(F32)
    return out


def one_row(ref):
    return jnp.concatenate([ref[i : i + 1, :] for i in range(ref.shape[0])], 1)


def as_column(row):
    n = row.shape[1]
    same = lax.broadcasted_iota(jnp.int32, (n, n), 0) == lax.broadcasted_iota(jnp.int32, (n, n), 1)
    return jnp.sum(jnp.where(same, row.astype(F32), 0.0), 1, keepdims=True)


def code_masks(codes, rows):
    major = lax.div(codes, 128)
    minor = codes - 128 * major
    return major, jnp.where(lax.broadcasted_iota(jnp.int32, (128, codes.shape[1]), 0) == minor, 1.0, 0.0).astype(BF16)


def spat_forward_step(r, m, place, step):
    frames = r.keep.shape[0]
    d = r.x.shape[-1]
    tiles = r.w_up_.shape[0]
    left, right = greet_ring(step)
    ends = frame_ends()
    fetch = Fetch(r.fetch)
    first = [fetch.add(r.w_qkv, r.w_qkv_), fetch.add(r.w_out, r.w_out_)]
    later = [fetch_mlp(fetch, r, j) for j in range(tiles)]

    @on(step, 0)
    def _():
        fetch.start()
        fetch.wait(first[0])

    @pl.when(step < frames)
    def _():
        x = r.x[0].astype(F32)
        xhat, _ = norm(x)
        a = (xhat * r.ga[...]).astype(BF16)
        r.at[...] = a.T
        for start in range(0, 3 * d, 512):
            r.pk[:, start : start + 512] = mm(a, r.w_qkv_[:, start : start + 512]).astype(BF16)
        for lane in range(0, d, 128):
            cols = [slice(part * d + lane, part * d + lane + 128) for part in range(3)]
            r.att[:, cols[0]] = attend_both(*[r.pk[:, c] for c in cols], None)
        att = r.att[...]
        r.att_t[...] = att.T

        @on(step, 0)
        def _():
            fetch.wait(first[1])
            for pair in later:
                fetch.wait(*pair)

        mid = x + mm(att, r.w_out_[...])
        r.mid[...] = mid

        def put_bt(value):
            r.bt[...] = value

        def put(j, h, slope):
            for i in range(2):
                r.h[2 * j + i] = h[:, 256 * i : 256 * (i + 1)]
            r.gp[j] = slope

        y = mlp_up(mid, r.gb[...], r.w_up_, r.w_down_, put_bt, put).astype(BF16)
        r.y[0] = y
        r.keep[step] = y

    meet_ring(step)

    def copy(i):
        return ring_copy(r.keep.at[i], r.halo.at[i], r.send.at[i], r.recv.at[i], right)

    @pl.when((step < frames) & ends.not_last)
    def _():
        copy(step).start()

    def clear(i):
        return pltpu.make_async_copy(r.none, r.halo.at[i], r.recv.at[i])

    @pl.when((step == 0) & ends.is_first)
    def _():
        r.none[...] = jnp.zeros_like(r.none)
        for i in range(frames):
            clear(i).start()

    @on(step, frames)
    def _():
        codes = one_row(r.codes)
        cdim, count = r.book.shape
        major, onehot = code_masks(codes, count // 128)
        both = jnp.concatenate([onehot, onehot], 0)
        total = jnp.zeros(r.chosen.shape, F32)
        for first in range(0, count // 128, 8):
            book = jnp.concatenate([r.book[:, 128 * a : 128 * (a + 1)] for a in range(first, first + 8)], 0)
            found = mm(jnp.concatenate(split_parts(book, 2), 1), both)
            for i in range(8):
                total = total + jnp.where(major == first + i, found[cdim * i : cdim * (i + 1)], 0.0)
        r.chosen[...] = total

    @pl.when((step == frames) & ends.not_last)
    def _():
        for i in range(frames):
            copy(i).wait_send()

    @pl.when((step == frames) & ends.not_first)
    def _():
        for i in range(frames):
            copy(i).wait_recv()

    @pl.when((step == frames) & ends.is_first)
    def _():
        for i in range(frames):
            clear(i).wait()


def frame_ends():
    me, n = lax.axis_index("frame"), lax.axis_size("frame")
    return types.SimpleNamespace(
        is_first=me == 0, not_first=me > 0, is_last=me == n - 1, not_last=me < n - 1
    )


def spat_forward_call(x, weights, codes, book_t):
    frames, patches, d = x.shape
    hidden = weights[4].shape[1]
    n = frames * patches
    tiles = hidden // TILE
    at = part_of(0, frames)
    blk = pl.BlockSpec((1, patches, d), lambda i: (at(i), 0, 0))
    cols = pl.BlockSpec((d, patches), lambda i: (0, at(i)))
    rows = lambda width: pl.BlockSpec((patches, width), lambda i: (at(i), 0))
    tiled = lambda count, width: (
        shape_of((count, n, width), BF16), pl.BlockSpec((count, patches, width), lambda i: (0, at(i), 0))
    )
    ga, w_qkv, w_out, gb, w_up, w_down = weights
    wide = lambda width, dtype=BF16: (shape_of((n, width), dtype), rows(width))
    tall = (shape_of((d, n), BF16), cols)
    vmem = lambda array: pltpu.VMEM(array.shape, array.dtype)
    return launch(
        spat_forward_step, "spat_forward", frames + 1,
        dict(
            x=(x, blk), ga=fixed(ga), w_qkv=(w_qkv, ANY), w_out=(w_out, ANY), gb=fixed(gb), w_up=(w_up, ANY),
            w_down=(w_down, ANY), codes=fixed(codes), book=fixed(book_t),
        ),
        dict(
            y=(shape_of(x.shape, BF16), blk), at=tall, pk=wide(3 * d), att_t=tall, mid=wide(d, F32), bt=tall,
            h=tiled(hidden // 256, 256), gp=tiled(tiles, TILE), halo=(shape_of(x.shape, BF16), ANY),
            chosen=fixed_out((book_t.shape[0], n), F32),
        ),
        dict(
            att=pltpu.VMEM((patches, d), BF16), keep=pltpu.VMEM(x.shape, BF16), none=pltpu.VMEM((patches, d), BF16),
            send=pltpu.SemaphoreType.DMA((frames,)), recv=pltpu.SemaphoreType.DMA((frames,)),
            fetch=pltpu.SemaphoreType.DMA((2 + 2 * tiles,)), w_qkv_=vmem(w_qkv), w_out_=vmem(w_out),
            w_up_=pltpu.VMEM((tiles, d, TILE), BF16), w_down_=pltpu.VMEM((tiles, TILE, d), BF16),
        ),
        {}, 11, 2 * n * d * (4 * d + 2 * hidden + 2 * patches),
    )


class Fetch:
    def __init__(self, sem):
        self.sem, self.items = sem, []

    def add(self, src, dst):
        self.items.append((src, dst))
        return len(self.items) - 1

    def copy(self, i):
        return pltpu.make_async_copy(*self.items[i], self.sem.at[i])

    def start(self, first=0, stop=None):
        for i in range(len(self.items))[first:stop]:
            self.copy(i).start()

    def wait(self, *which):
        for i in which:
            self.copy(i).wait()


def mlp_tile(r, j, put_up, half_way=lambda: None):
    lead, per, d = r.db.shape
    for i in range(4):
        rows = slice(i * 256, (i + 1) * 256)
        these = slice(i * lead // 4, (i + 1) * lead // 4)
        dh = mm_t(r.dy[rows, :], r.w_down_[j])
        du = (r.gp_[j, rows, :].astype(F32) * dh).astype(BF16)
        r.du[rows, :] = du
        r.db[these] += mm_t(du, r.w_up_[j]).reshape(lead // 4, per, d)
        if i == 1:
            half_way()
    put_up(mm(r.bt_[...], r.du[...]).astype(BF16))


def down_tile(r, acc, j):
    for i in range(4):
        grad = mm(r.dyt[...], r.h_[4 * j + i]).astype(BF16)
        acc[2 * j + i // 2, i % 2] = grad.reshape(acc.shape[2:])


def mlp_up(mid, gain, w_up_, w_down_, put_bt, put):
    xhat, _ = norm(mid)
    b = (xhat * gain).astype(BF16)
    put_bt(b.T)
    out = mid
    for j in range(w_up_.shape[0]):
        u = mm(b, w_up_[j])
        u2 = u * u
        th = jnp.tanh(u * (GELU_C + (GELU_C * GELU_A) * u2))
        half = 0.5 + 0.5 * th
        h = (u * half).astype(BF16)
        slope = half + u * (half * (1.0 - th)) * (GELU_C + (3.0 * GELU_C * GELU_A) * u2)
        put(j, h, slope.astype(BF16))
        out = out + mm(h, w_down_[j])
    return out


def fetch_mlp(fetch, r, j):
    cols = pl.ds(j * TILE, TILE)
    return fetch.add(r.w_up.at[:, cols], r.w_up_.at[j]), fetch.add(r.w_down.at[cols, :], r.w_down_.at[j])


def middle(r, put):
    lead, per, d = r.db.shape
    for i in range(4):
        rows = slice(i * 256, (i + 1) * 256)
        these = slice(i * lead // 4, (i + 1) * lead // 4)
        xhat, rs = norm(r.mid_[rows, :])
        db = r.db[these].reshape(256, d)
        add_row(r.dg_b, db * xhat)
        dmid = r.dy[rows, :].astype(F32) + norm_back(db, xhat, rs, r.gb[...])
        r.db[these] = dmid.reshape(lead // 4, per, d)
        low = dmid.astype(BF16)
        put(i, low, mm_t(low, r.w_out_[...]).astype(BF16))


T_LOSS, T_MLP, T_MID, T_ATT, T_DOWN, T_GRAD = 4, 5, 9, 10, 12, 16


def temporal_forward(r, step, fetch, wait_first):
    frames, group, d = r.att.shape
    rows = frames * group
    lead = pl.ds(pl.multiple_of(frames * step, frames), frames)
    here = pl.ds(pl.multiple_of(rows * step, rows), rows)
    mine = pl.ds(pl.multiple_of(group * step, group), group)
    x = r.x[:, mine, :].reshape(rows, d).astype(F32)
    xhat, _ = norm(x)
    a = (xhat * r.ga[...]).astype(BF16)
    r.at_[:, here] = a.T
    for start in range(0, 3 * d, 512):
        part = mm(a, r.w_qkv_[:, start : start + 512]).astype(BF16)
        r.pk[lead, :, start : start + 512] = part.reshape(frames, group, 512)
    xhat_h, _ = norm(r.halo[:, mine, :].reshape(rows, d).astype(F32))
    ah = (xhat_h * r.ga[...]).astype(BF16)
    r.aht_[:, here] = ah.T
    for start in range(0, 2 * d, 512):
        part = mm(ah, r.w_qkv_[:, d + start : d + start + 512]).astype(BF16)
        r.kvh[lead, :, start : start + 512] = part.reshape(frames, group, 512)
    bias = jnp.concatenate([r.bias[...]] * 2, 0)
    def one_sub(i_, c_):
        near = pl.ds(pl.multiple_of(i_ * SUB, SUB), SUB)
        for lane in range(0, d, 128):
            c0, c1, c2 = (slice(part * d + lane, part * d + lane + 128) for part in range(3))
            q = r.pk[lead, near, c0].reshape(frames * SUB, 128)
            k = jnp.concatenate([r.kvh[lead, near, c0], r.pk[lead, near, c1]], 0).reshape(2 * frames * SUB, 128)
            v = jnp.concatenate([r.kvh[lead, near, c1], r.pk[lead, near, c2]], 0).reshape(2 * frames * SUB, 128)
            r.att[:, near, c0] = attend_both(q, k, v, bias).reshape(frames, SUB, 128)
        return c_

    lax.fori_loop(0, group // SUB, one_sub, 0)
    att = r.att[...].reshape(rows, d)
    r.att_t_[:, here] = att.T
    wait_first()
    mid = x + mm(att, r.w_out_[...])
    r.mid_[here, :] = mid

    def put_bt(value):
        r.bt_[:, here] = value

    def put(j, h, slope):
        for i in range(2):
            r.h_[2 * j + i, here, :] = h[:, 256 * i : 256 * (i + 1)]
        r.gp_[j, here, :] = slope

    r.x3[here, :] = mlp_up(mid, r.gb[...], r.w_up_, r.w_down_, put_bt, put).astype(BF16)


def temporal_step(r, m, place, step):
    frames, group, d = r.att.shape
    cdim, n = r.chosen.shape
    rows = frames * group
    ring = lax.axis_size("frame")
    me = lax.axis_index("frame")
    left, right = lax.rem(me + ring - 1, ring), lax.rem(me + 1, ring)
    ends = frame_ends()
    tiles = r.w_up_.shape[0]
    fetch = Fetch(r.fetch)
    first = [fetch.add(r.w_qkv, r.w_qkv_), fetch.add(r.w_out, r.w_out_)]
    later = [fetch_mlp(fetch, r, j) for j in range(tiles)]

    @on(step, 0)
    def _():
        place.greet()
        for peer in (left, right):
            pl.semaphore_signal(
                pltpu.get_barrier_semaphore(), inc=1, device_id={"frame": peer}, device_id_type=MESH
            )
        fetch.start()
        for ref in (r.dg_a, r.dg_b, r.db):
            ref[...] = jnp.zeros_like(ref)
        fetch.wait(first[0])

    @on(step, 0)
    def _():
        def wait_first():
            fetch.wait(first[1])
            for pair in later:
                fetch.wait(*pair)

        temporal_forward(r, 0, fetch, wait_first)

    @on(step, 1)
    def _():
        def one(i, carry):
            temporal_forward(r, i, fetch, lambda: None)
            return carry

        lax.fori_loop(1, r.lat.shape[2] // group, one, 0)

    @on(step, T_LOSS)
    def _():
        patches = r.lat.shape[2]
        commit = jnp.zeros((1, 1), F32)
        latent = mm_t(r.proj[...], r.x3[...])
        for f in range(frames):
            for g in range(patches // group):
                at = (g * frames + f) * group
                r.lat[f, :, g * group : (g + 1) * group] = latent[:, at : at + group]
            here = slice(f * patches, (f + 1) * patches)
            differ = r.lat[f] - r.chosen[:, here]
            commit = commit + jnp.sum(jnp.sum(differ * differ, 1, keepdims=True), 0, keepdims=True)
            grad = (r.cot[f] + (2.0 * BETA) * differ).astype(BF16)
            for g in range(patches // group):
                at = (g * frames + f) * group
                r.gl[:, at : at + group] = grad[:, g * group : (g + 1) * group]
            r.dbook[:, here] = ((-2.0 * BETA) * differ).astype(BF16)
        for i in range(4):
            part = slice(i * 256, (i + 1) * 256)
            r.dy[part, :] = t_mm(r.gl[:, part], r.proj[...]).astype(BF16)
        r.dyt[...] = t_mm(r.proj[...], r.gl[...]).astype(BF16)
        r.commit[...] = commit

    @within(step, T_MLP, 4)
    def _():
        j = step - T_MLP

        def put_up(value):
            r.a_acc[j // 2, j % 2] = value.reshape(r.a_acc.shape[2:])

        mlp_tile(r, j, put_up)

    @within(step, T_DOWN, 2)
    def _():
        down_tile(r, m.b.acc, step - T_DOWN)

    @on(step, T_MID)
    def _():
        def put(i, low, datt):
            for t in range(2):
                r.dm[t, 4 * i : 4 * i + 4] = low[:, 256 * t : 256 * (t + 1)].reshape(4, group, 256)
            r.datt[4 * i : 4 * i + 4] = datt.reshape(4, group, d)

        middle(r, put)

    s = att_step(step)
    attending = T_ATT <= step < T_DOWN or T_DOWN + 2 <= step < T_GRAD

    @on(int(attending), 1)
    def _():
        lead = pl.ds(frames * s, frames)
        bias = jnp.concatenate([r.bias_t[...]] * 2, 1)
        half = frames * SUB
        def one_sub(i_, c_):
            near = pl.ds(pl.multiple_of(i_ * SUB, SUB), SUB)
            for lane in range(0, d, 128):
                c0, c1, c2 = (slice(part * d + lane, part * d + lane + 128) for part in range(3))
                q = r.pk[lead, near, c0].reshape(half, 128)
                k = jnp.concatenate([r.kvh[lead, near, c0], r.pk[lead, near, c1]], 0).reshape(2 * half, 128)
                v = jnp.concatenate([r.kvh[lead, near, c1], r.pk[lead, near, c2]], 0).reshape(2 * half, 128)
                do = r.datt[lead, near, c0].reshape(half, 128)
                dq, dk, dv = attend_both_back(q, k, v, do, bias)
                tile, to = lane // 256, slice(lane % 256, lane % 256 + 128)
                for part, grad in enumerate((dq, dk[half:], dv[half:])):
                    r.dpk[2 * part + tile, lead, near, to] = grad.astype(BF16).reshape(frames, SUB, 128)
                for part, grad in enumerate((dk[:half], dv[:half])):
                    r.dkvh[2 * part + tile, lead, near, to] = grad.astype(BF16).reshape(frames, SUB, 128)
            return c_

        lax.fori_loop(0, group // SUB, one_sub, 0)
        dah = jnp.zeros((rows, d), F32)
        for i in range(4):
            dah = dah + mm_t(r.dkvh[i, lead].reshape(rows, 256), r.w_qkv_[:, d + 256 * i : d + 256 * (i + 1)])
        r.dah[s] = dah.astype(BF16).reshape(frames, group, d)
        da = jnp.zeros((rows, d), F32)
        for i in range(6):
            da = da + mm_t(r.dpk[i, lead].reshape(rows, 256), r.w_qkv_[:, 256 * i : 256 * (i + 1)])
        xhat, rs = norm(r.x[:, s * group : (s + 1) * group, :].reshape(rows, d).astype(F32))
        add_row(r.dg_a, da * xhat)
        dmid = r.db[lead].reshape(rows, d)
        r.base[:, s * group : (s + 1) * group, :] = (dmid + norm_back(da, xhat, rs, r.ga[...])).reshape(
            frames, group, d
        )

    def copy(i):
        there = r.back.at[:, pl.ds(i * group, group), :]
        return ring_copy(r.dah.at[i], there, r.send.at[i], r.recv.at[i], left)

    def clear(i):
        return pltpu.make_async_copy(r.none, r.back.at[:, pl.ds(i * group, group), :], r.recv.at[i])

    @on(step, T_GRAD)
    def _():
        codes = one_row(r.codes)
        major, onehot = code_masks(codes, 64)
        dbook = r.dbook[...]
        dproj = mm(r.gl[...], r.x3[...]).astype(BF16)
        part = cdim // 4
        for z in range(4):
            for x in range(2):
                f = 2 * z + x
                picked = [jnp.where(major == 8 * f + i, dbook, jnp.zeros((), BF16)) for i in range(8)]
                book = mm_t(jnp.concatenate(picked, 0), onehot).astype(BF16)
                r.d_part[z, x, :, :, : 2 * cdim] = book.reshape(2, 2, 2 * cdim, 128)
                r.d_part[z, x, :, :, 2 * cdim :] = jnp.zeros((2, 2, 16, 128), BF16)
                for q in range(4):
                    r.d_part[z, x, q // 2, q % 2, 2 * cdim : 2 * cdim + part, :64] = dproj[
                        part * q : part * (q + 1), 64 * f : 64 * (f + 1)
                    ]
        dead = r.dead.shape[1]
        used = jnp.where(as_column(r.dead[...]) == codes.astype(F32), 1.0, 0.0).astype(BF16)
        usage = mm_t(jnp.ones((8, n), BF16), used)
        places = lax.broadcasted_iota(jnp.int32, (dead, n), 1).astype(F32)
        pick = jnp.where(as_column(r.source[...]) == places, 1.0, 0.0).astype(BF16)
        latent = jnp.concatenate([r.lat[f] for f in range(frames)], 1)
        candidate = jnp.zeros((cdim, dead), F32)
        for one in split_parts(latent, 3):
            candidate = candidate + mm_t(one, pick)
        r.q_part[...] = jnp.zeros_like(r.q_part)
        r.q_part[:cdim, :dead] = candidate
        r.q_part[cdim:, :dead] = usage
        r.q_part[cdim:, dead:] = jnp.broadcast_to(r.commit[...], (8, 128 - dead))

    @within(step, T_GRAD, 2)
    def _():
        t = step - T_GRAD
        whole_rows = lambda value: value.reshape(n, 256)
        a, ah, att = r.at_[...], r.aht_[...], r.att_t_[...]
        parts = (
            mm(a, whole_rows(r.dpk[t])),
            mm(a, whole_rows(r.dpk[2 + t])) + mm(ah, whole_rows(r.dkvh[t])),
            mm(a, whole_rows(r.dpk[4 + t])) + mm(ah, whole_rows(r.dkvh[2 + t])),
            mm(att, whole_rows(r.dm[t])),
        )
        for kind, part in enumerate(parts):
            part = part.astype(BF16)
            for j in range(2):
                r.t_att[t, j, :, :, :, 128 * kind : 128 * (kind + 1)] = part[:, 128 * j : 128 * (j + 1)].reshape(
                    r.t_att.shape[2:5] + (128,)
                )

    @on(step, 0)
    def _():
        pl.semaphore_wait(pltpu.get_barrier_semaphore(), len(PEERS) + 2)

    @on(step, 0)
    def _():
        @pl.when(ends.is_last)
        def _():
            r.none[...] = jnp.zeros_like(r.none)
            for i in range(r.dah.shape[0]):
                clear(i).start()

    @on(int(attending), 1)
    def _():
        @pl.when(ends.not_first)
        def _():
            copy(s).start()

    @on(step, T_MLP + 1)
    def _():
        m.a0.start(0)

    @on(step, T_MLP + 2)
    def _():
        m.a0.move(0)

    @on(step, T_MLP + 3)
    def _():
        m.a1.start(0)

    @on(step, T_MID)
    def _():
        m.a1.move(0)

    @on(step, T_DOWN + 1)
    def _():
        m.b.start(0)

    @on(step, T_DOWN + 2)
    def _():
        m.b.move(0)

    @on(step, T_GRAD + 1)
    def _():
        for part in (m.a0, m.a1, m.b):
            part.finish(1)
        r.a_part[0] = m.a0.piece()
        r.a_part[1] = m.a1.piece()
        r.b_part[...] = m.b.piece()

        @pl.when(ends.not_first)
        def _():
            for i in range(r.dah.shape[0]):
                copy(i).wait_send()

        @pl.when(ends.not_last)
        def _():
            for i in range(r.dah.shape[0]):
                copy(i).wait_recv()

        @pl.when(ends.is_last)
        def _():
            for i in range(r.dah.shape[0]):
                clear(i).wait()


def att_step(step):
    return min(max(step - T_ATT, 0), 1) + min(max(step - T_DOWN - 1, 0), 2)


def temporal_call(x, halo, bias, cot_t, chosen, codes, dead, source, proj_t, weights):
    frames, patches, d = x.shape
    ga, w_qkv, w_out, gb, w_up, w_down = weights
    hidden = w_up.shape[1]
    n = frames * patches
    cdim = proj_t.shape[0]
    groups = patches // GROUP
    lead, tiles = frames * groups, hidden // TILE
    half_tail, col_tail, book_tail = (d // 16, TILE), (d // 4, hidden // 8), (2 * cdim + 16, 128)
    vmem = lambda array: pltpu.VMEM(array.shape, array.dtype)
    low = lambda *shape: pltpu.VMEM(shape, BF16)
    moves = dict(
        a0=Sum(E_DIMS, half_tail, ("c", "y"), shared=lambda r: r.a_acc, fixed={"u": 0}, gather=False),
        a1=Sum(E_DIMS, half_tail, ("c", "y"), shared=lambda r: r.a_acc, fixed={"u": 1}, gather=False),
        b=Sum(COLS_DIMS, col_tail, ("c", "y"), gather=False),
    )
    return launch(
        temporal_step, "temporal", T_GRAD + 2,
        dict(
            x=fixed(x), halo=fixed(halo), bias=fixed(bias), bias_t=fixed(bias.T),
            cot=fixed(cot_t), chosen=fixed(chosen), codes=fixed(codes), dead=fixed(dead), source=fixed(source),
            proj=fixed(proj_t), ga=fixed(ga), gb=fixed(gb), w_qkv=(w_qkv, ANY), w_out=(w_out, ANY), w_up=(w_up, ANY),
            w_down=(w_down, ANY),
        ),
        dict(
            lat=fixed_out((frames, cdim, patches), F32), base=fixed_out(x.shape, F32),
            back=(shape_of(x.shape, BF16), ANY), dg_a=fixed_out((1, d), F32), dg_b=fixed_out((1, d), F32),
            t_att=fixed_out((2, 2, 4, 2, d // 8, d), BF16),
            a_part=fixed_out((2, 4, 2) + half_tail, BF16),
            b_part=fixed_out((4, 2) + col_tail, BF16), d_part=fixed_out((4, 2, 2, 2) + book_tail, BF16),
            q_part=fixed_out((cdim + 8, 128), F32),
        ),
        dict(
            commit=pltpu.VMEM((1, 1), F32), gl=low(cdim, n), dbook=low(cdim, n), dy=low(n, d), dyt=low(d, n),
            du=low(n, TILE), db=pltpu.VMEM((lead, GROUP, d), F32), dm=low(2, lead, GROUP, 256),
            datt=low(lead, GROUP, d), dpk=low(6, lead, GROUP, 256), dkvh=low(4, lead, GROUP, 256),
            a_acc=low(2, 2, 4, 2, 2, *half_tail), dah=low(groups, frames, GROUP, d), none=low(frames, GROUP, d),
            send=pltpu.SemaphoreType.DMA((groups,)), recv=pltpu.SemaphoreType.DMA((groups,)),
            fetch=pltpu.SemaphoreType.DMA((2 + 2 * tiles,)), w_qkv_=vmem(w_qkv), w_out_=vmem(w_out),
            w_up_=low(tiles, d, TILE), w_down_=low(tiles, TILE, d), att=low(frames, GROUP, d),
            pk=low(lead, GROUP, 3 * d), kvh=low(lead, GROUP, 2 * d), at_=low(d, n), aht_=low(d, n), att_t_=low(d, n),
            bt_=low(d, n), mid_=pltpu.VMEM((n, d), F32), h_=low(hidden // 256, n, 256), gp_=low(tiles, n, TILE),
            x3=low(n, d),
        ),
        moves, 12, 6 * n * d * (6 * d + 2 * hidden) + 14 * n * d * patches, TAIL_BYTES, True,
    )


S_DOWN, S_MLP, S_MID, S_ATT, S_END = 1, 3, 7, 8, 12


def spat_backward_step(r, m, place, step):
    frames, patches, d = r.db.shape
    n = frames * patches
    tiles = r.w_up_.shape[0]
    fetch = Fetch(r.fetch)
    by_frame = [
        [fetch.add(a.at[f], b.at[f]) for a, b in ((r.base, r.base_), (r.dah, r.dah_), (r.x2, r.x2_))]
        for f in range(frames)
    ]
    h_tiles = [fetch.add(r.h.at[i], r.h_.at[i]) for i in range(r.h_.shape[0])]
    bt = fetch.add(r.bt, r.bt_)
    mlp = [(*fetch_mlp(fetch, r, j), fetch.add(r.gp.at[j], r.gp_.at[j])) for j in range(tiles)]
    mid, w_out, att_t = fetch.add(r.mid, r.mid_), fetch.add(r.w_out, r.w_out_), fetch.add(r.att_t, r.att_t_)
    pk, at, w_qkv, x = (
        fetch.add(a, b) for a, b in ((r.pk, r.pk_), (r.at, r.at_), (r.w_qkv, r.w_qkv_), (r.x, r.x_))
    )

    def transfers(point):
        start = lambda k, *parts: [part.start(k) for part in parts]
        move = lambda k, *parts: [part.move(k) for part in parts]
        finish = lambda k, *parts: [part.finish(k) for part in parts]
        gather = lambda *parts: [part.gather() for part in parts]
        spread = lambda *parts: [part.spread() for part in parts]
        todo = (
            ((start, 0, m.c, m.d, m.b, m.a0, m.q, m.a1),),
            ((move, 0, m.q),),
            ((start, 0, m.g), (move, 0, m.d),),
            ((move, 1, m.q),),
            ((move, 0, m.c), (move, 2, m.q), (move, 0, m.g),),
            ((finish, 3, m.q),),
            ((start, 0, m.e0), (move, 1, m.d),),
            ((move, 0, m.a0, m.a1),),
            ((move, 0, m.e0),),
            (),
            ((start, 0, m.e1),),
            ((move, 2, m.d), (move, 0, m.b, m.e1), (gather, m.a0, m.a1),),
            (),
            ((move, 1, m.c), (gather, m.d), (spread, m.a0, m.a1),),
            ((move, 1, m.g),),
            ((start, 0, m.h0a, m.h0b), (spread, m.d), (gather, m.b), (move, 1, m.e0),),
            ((move, 2, m.c), (move, 0, m.h0a, m.h0b),),
            ((spread, m.b), (move, 1, m.e1), (move, 2, m.e0),),
            ((move, 1, m.h0b),),
            ((start, 0, m.h1b, m.h1a), (move, 1, m.h0a), (move, 2, m.e1, m.g),),
            ((move, 0, m.h1b, m.h1a), (gather, m.c)),
            ((move, 2, m.h0b, m.h0a),),
            ((gather, m.e0),),
            ((start, 0, m.w), (move, 1, m.h1b, m.h1a)),
            (
                (move, 0, m.w), (spread, m.c, m.e0), (gather, m.e1), (move, 1, m.w), (gather, m.h0a, m.h0b),
                (move, 2, m.h1b, m.h1a), (move, 2, m.w), (spread, m.e1), (gather, m.g), (gather, m.h1b, m.h1a),
                (spread, m.g), (finish, 3, m.w),
            ),
        )
        for what, *args in todo[point]:
            what(*args)

    @on(step, 0)
    def _():
        place.greet()
        fetch.start(0, 3 * frames)
        m.q.acc[...] = r.q_part[...]
        pl.semaphore_wait(pltpu.get_barrier_semaphore(), len(PEERS))
        transfers(0)
        fetch.start(3 * frames)
        for ref in (r.dg_t, r.dg_a, r.dg_b, r.db):
            ref[...] = jnp.zeros_like(ref)
        for f in range(frames):
            fetch.wait(*by_frame[f])
            xhat, rs = norm(r.x2_[f].astype(F32))
            dah = r.dah_[f].astype(F32)
            add_row(r.dg_t, dah * xhat)
            low = (r.base_[f] + norm_back(dah, xhat, rs, r.gta[...])).astype(BF16)
            here = slice(f * patches, (f + 1) * patches)
            r.dy[here, :] = low
            r.dyt[:, here] = low.T
    for j in range(2):

        @on(step, S_DOWN + j)
        def _(j=j):
            fetch.wait(*h_tiles[4 * j : 4 * j + 4])

    @on(step, S_MLP)
    def _():
        fetch.wait(bt)

    for j in range(tiles):

        @on(step, S_MLP + j)
        def _(j=j):
            fetch.wait(*mlp[j])

    @within(step, S_MLP, 4)
    def _():
        j = step - S_MLP

        def put_up(value):
            r.e_acc[j // 2, j % 2] = value.reshape(r.e_acc.shape[2:])

        mlp_tile(r, j, put_up, lambda: transfers(3 + 2 * j))
        transfers(4 + 2 * j)

    @within(step, S_DOWN, 2)
    def _():
        down_tile(r, m.g.acc, step - S_DOWN)
        transfers(1 + step - S_DOWN)

    @on(step, S_MID)
    def _():
        fetch.wait(mid, w_out)

        def put(i, low, datt):
            rows = slice(i * 256, (i + 1) * 256)
            r.dm[rows, :] = low
            for p in range(d // 128):
                r.datt[p, rows, :] = datt[:, 128 * p : 128 * (p + 1)]

        middle(r, put)
        fetch.wait(att_t)
        grad = mm(r.att_t_[...], r.dm[...]).astype(BF16)
        for q in range(4):
            r.h_acc[q // 2, 1, q % 2, :, :, :, :, 128:] = grad[:, 128 * q : 128 * (q + 1)].reshape(
                r.h_acc.shape[3:7] + (128,)
            )
        fetch.wait(pk, at, w_qkv)
        transfers(11)

    @within(step, S_ATT, 4)
    def _():
        p = step - S_ATT
        cols = [slice(part * d + 128 * p, part * d + 128 * (p + 1)) for part in range(3)]
        for f in range(frames):
            here = slice(f * patches, (f + 1) * patches)
            grads = attend_both_back(*[r.pk_[here, c] for c in cols], r.datt[p, here, :], None)
            for part, grad in enumerate(grads):
                r.dpk[here, cols[part]] = grad.astype(BF16)
            if f == 1:
                transfers(12 + 2 * p)
        grad = mm(r.at_[...], jnp.concatenate([r.dpk[:, c] for c in cols], 1)).astype(BF16)
        u, c = p // 2, p % 2
        shape = r.h_acc.shape[3:7]
        r.h_acc[u, 0, c] = grad[:, :256].reshape(shape + (256,))
        r.h_acc[u, 1, c, :, :, :, :, :128] = grad[:, 256:].reshape(shape + (128,))
        transfers(13 + 2 * p)

    @on(step, S_END)
    def _():
        fetch.wait(x)
        for f in range(frames):
            rows = slice(f * patches, (f + 1) * patches)
            da = mm_t(r.dpk[rows, :], r.w_qkv_[...])
            xhat, rs = norm(r.x_[f].astype(F32))
            add_row(r.dg_a, da * xhat)
            r.dx[f] = (r.db[f] + norm_back(da, xhat, rs, r.ga[...])).astype(BF16)
            if f < frames - 1:
                transfers(20 + f)
        gains = (r.dg_t[...] + r.dgt_own[...], r.dgt_mid[...], r.dg_a[...], r.dg_b[...])
        for i, gain in enumerate(gains):
            for j in range(d // 128):
                row = i * (d // 128) + j
                m.w.acc[row : row + 1, :] = gain[:, 128 * j : 128 * (j + 1)]
        transfers(23)

    @on(step, S_END + 1)
    def _():
        transfers(24)
        outs = (
            (m.a0, r.a0_all), (m.a1, r.a1_all), (m.b, r.b_all), (m.c, r.c_all), (m.d, r.d_all), (m.e0, r.e0_all),
            (m.e1, r.e1_all), (m.g, r.g_all), (m.h0a, r.h00_all), (m.h0b, r.h01_all), (m.h1a, r.h10_all),
            (m.h1b, r.h11_all),
        )
        for part, out in outs:
            part.gathered(out)
        r.w_all[...] = m.w.acc[...]
        r.q_all[...] = m.q.acc[...]


def spat_backward_call(f, t, x2, gta, x, weights):
    frames, patches, d = x.shape
    ga, w_qkv, w_out, gb, w_up, w_down = weights
    hidden = w_up.shape[1]
    n = frames * patches
    tiles = hidden // TILE
    col_tail = (d // 4, hidden // 8)
    half_tail, quarter_tail = (d // 16, TILE), (d // 16, 256)
    e_acc, h_acc = (lambda r: r.e_acc), (lambda r: r.h_acc)
    vmem = lambda array: pltpu.VMEM(array.shape, array.dtype)
    moves = dict(
        b=Sum(("z", "x"), col_tail, ("x", "z"), source=lambda r: r.b_part),
        a0=Sum(("u", "z", "x"), half_tail, ("x", "z"), source=lambda r: r.a_part, fixed={"u": 0}),
        a1=Sum(("u", "z", "x"), half_tail, ("x", "z"), source=lambda r: r.a_part, fixed={"u": 1}),
        c=Sum(ROWS_DIMS, (d // 8, d), Y_FIRST, source=lambda r: r.t_att),
        e0=Sum(E_DIMS, half_tail, Y_FIRST, shared=e_acc, fixed={"u": 0}),
        e1=Sum(E_DIMS, half_tail, Y_FIRST, shared=e_acc, fixed={"u": 1}),
        g=Sum(COLS_DIMS, col_tail, X_FIRST),
        h0a=Sum(H_DIMS, quarter_tail, Y_FIRST, shared=h_acc, fixed={"u": 0, "w": 0}, direct=True),
        h0b=Sum(H_DIMS, quarter_tail, X_FIRST, shared=h_acc, fixed={"u": 0, "w": 1}, direct=True),
        h1a=Sum(H_DIMS, quarter_tail, Y_FIRST, shared=h_acc, fixed={"u": 1, "w": 0}, direct=True),
        h1b=Sum(H_DIMS, quarter_tail, X_FIRST, shared=h_acc, fixed={"u": 1, "w": 1}, direct=True),
        d=Sum(COLS_DIMS, t.d_part.shape[4:], Y_FIRST, source=lambda r: r.d_part), q=Total(t.q_part.shape[0]),
        w=Total(4 * d // 128),
    )
    pieces = lambda tail: fixed_out((2, 2) + tail, BF16)
    return launch(
        spat_backward_step, "spat_backward", 14,
        dict(
            base=(t.base, ANY), dah=(t.back, ANY), x2=(x2, ANY), gta=fixed(gta), x=(x, ANY), gp=(f.gp, ANY), h=(f.h, ANY),
            pk=(f.pk, ANY), w_qkv=(w_qkv, ANY), ga=fixed(ga), gb=fixed(gb), w_up=(w_up, ANY), w_down=(w_down, ANY),
            dgt_own=fixed(t.dg_a), dgt_mid=fixed(t.dg_b), bt=(f.bt, ANY), mid=(f.mid, ANY), w_out=(w_out, ANY),
            att_t=(f.att_t, ANY), at=(f.at, ANY), a_part=(t.a_part, ANY), b_part=(t.b_part, ANY), t_att=(t.t_att, ANY),
            d_part=(t.d_part, ANY), q_part=fixed(t.q_part),
        ),
        dict(
            dx=fixed_out(x.shape, BF16), a0_all=pieces(half_tail), a1_all=pieces(half_tail), b_all=pieces(col_tail), c_all=pieces((d // 8, d)),
            e0_all=pieces(half_tail), e1_all=pieces(half_tail), g_all=pieces(col_tail), h00_all=pieces(quarter_tail),
            h01_all=pieces(quarter_tail), h10_all=pieces(quarter_tail), h11_all=pieces(quarter_tail),
            w_all=fixed_out((4 * d // 128, 128), F32), q_all=fixed_out(t.q_part.shape, F32),
            d_all=pieces(t.d_part.shape[4:]),
        ),
        dict(
            dg_t=pltpu.VMEM((1, d), F32), dg_a=pltpu.VMEM((1, d), F32), dg_b=pltpu.VMEM((1, d), F32),
            dy=pltpu.VMEM((n, d), BF16), dyt=pltpu.VMEM((d, n), BF16), du=pltpu.VMEM((n, TILE), BF16),
            db=pltpu.VMEM(x.shape, F32), dm=pltpu.VMEM((n, d), BF16),
            datt=pltpu.VMEM((d // 128, n, 128), BF16), dpk=pltpu.VMEM((n, 3 * d), BF16),
            e_acc=pltpu.VMEM((2, 2, 4, 2, 2) + half_tail, BF16), h_acc=pltpu.VMEM((2, 2, 2, 4, 2, 2) + quarter_tail, BF16),
            fetch=pltpu.SemaphoreType.DMA((3 * frames + 3 * tiles + hidden // 256 + 8,)), bt_=vmem(f.bt), mid_=vmem(f.mid),
            w_out_=vmem(w_out), att_t_=vmem(f.att_t), at_=vmem(f.at), x_=vmem(x), base_=vmem(t.base), dah_=vmem(t.back),
            x2_=vmem(x2), h_=vmem(f.h), gp_=vmem(f.gp), pk_=vmem(f.pk), w_qkv_=vmem(w_qkv),
            w_up_=pltpu.VMEM((tiles, d, TILE), BF16), w_down_=pltpu.VMEM((tiles, TILE, d), BF16),
        ),
        moves, 13, 4 * n * d * (4 * d + 2 * hidden) + 10 * n * d * patches, TAIL_BYTES, True,
    )


def finish_step(r, m, place, step):
    d = r.t_out.shape[1]
    half = d // 16
    for y in range(2):
        for c in range(2):
            q = 2 * y + c
            lanes = slice(128 * q, 128 * (q + 1))
            r.t_down[:, lanes] = r.b_all[y, c].astype(F32).T
            r.s_down[:, lanes] = r.g_all[y, c].astype(F32).T
            value = r.c_all[y, c].astype(F32)
            for kind in range(3):
                r.t_qkv[:, d * kind + 128 * q : d * kind + 128 * (q + 1)] = value[:, 128 * kind : 128 * (kind + 1)]
            r.t_out[:, lanes] = value[:, 384:]
            book = r.d_all[y, c].astype(F32)
            cdim = r.book.shape[0]
            r.proj_grad[cdim // 4 * q : cdim // 4 * (q + 1), :] = book[2 * cdim : 2 * cdim + cdim // 4, :64]
            for i in range(2):
                r.book_grad[:, 128 * (2 * q + i) : 128 * (2 * q + i + 1)] = book[cdim * i : cdim * (i + 1)]
            rows = slice(half * y, half * (y + 1))
            for u, t_up, up, left, right in (
                (0, r.a0_all, r.e0_all, r.h00_all, r.h01_all), (1, r.a1_all, r.e1_all, r.h10_all, r.h11_all)
            ):
                at = 2 * u + c
                r.t_up[rows, TILE * at : TILE * (at + 1)] = t_up[y, c].astype(F32)
                r.s_up[rows, TILE * at : TILE * (at + 1)] = up[y, c].astype(F32)
                pair, other = left[y, c].astype(F32), right[y, c].astype(F32)
                for kind, part in enumerate((pair[:, :128], pair[:, 128:], other[:, :128])):
                    r.s_qkv[rows, d * kind + 128 * at : d * kind + 128 * (at + 1)] = part
                r.s_out[rows, 128 * at : 128 * (at + 1)] = other[:, 128:]
    for i, gain in enumerate((r.g_ta, r.g_tb, r.g_sa, r.g_sb)):
        for j in range(d // 128):
            row = i * (d // 128) + j
            gain[:, 128 * j : 128 * (j + 1)] = r.w_all[row : row + 1, :]
    dead = r.dead_row.shape[1]
    candidate = r.q_all[:cdim, :dead]
    low = r.q_all[cdim : cdim + 1, :dead] < USE_MIN
    r.commit[...] = r.q_all[cdim : cdim + 1, dead : dead + 1] * (1.0 / r.scale)
    major = lax.div(r.dead_row[...], 128)
    minor = as_column(lax.rem(r.dead_row[...], 128))
    lanes = lax.broadcasted_iota(jnp.int32, (dead, 128), 1).astype(F32)
    onehot = jnp.where(lanes == minor, 1.0, 0.0).astype(BF16)
    parts = split_parts(jnp.where(low, candidate, 0.0), 3)
    count = r.book.shape[1] // 128
    a_rows = lax.broadcasted_iota(jnp.int32, (count, dead), 0)
    replaced = mm(jnp.where((major == a_rows) & low, 1.0, 0.0).astype(BF16), onehot)
    for begin in range(0, count, 8):
        fresh = jnp.zeros((8 * cdim, 128), F32)
        for part in parts:
            chosen = [jnp.where(major == begin + i, part, jnp.zeros((), BF16)) for i in range(8)]
            fresh = fresh + mm(jnp.concatenate(chosen, 0), onehot)
        for i in range(8):
            at = begin + i
            lanes = slice(128 * at, 128 * (at + 1))
            r.refreshed[:, lanes] = jnp.where(
                replaced[at : at + 1] > 0.5, fresh[cdim * i : cdim * (i + 1)], r.book[:, lanes]
            )


def finish_call(t, s, book_t, dead, total, d, hidden):
    cdim, codes = book_t.shape
    piece = d // 8
    ins = dict(
        a0_all=s.a0_all, a1_all=s.a1_all, b_all=s.b_all, c_all=s.c_all, d_all=s.d_all, e0_all=s.e0_all, e1_all=s.e1_all, g_all=s.g_all,
        h00_all=s.h00_all, h01_all=s.h01_all, h10_all=s.h10_all, h11_all=s.h11_all, w_all=s.w_all, q_all=s.q_all,
        book=book_t, dead_row=dead.reshape(1, -1),
    )
    outs = dict(
        t_up=(piece, hidden), t_down=(hidden // 8, d), t_qkv=(piece, 3 * d), t_out=(piece, d),
        s_up=(piece, hidden), s_down=(hidden // 8, d), s_qkv=(piece, 3 * d), s_out=(piece, d),
        g_ta=(1, d), g_tb=(1, d), g_sa=(1, d), g_sb=(1, d), proj_grad=(cdim, piece), commit=(1, 1),
        book_grad=(cdim, codes // 8), refreshed=(cdim, codes),
    )

    def body(r, m, place, step):
        r.scale = total
        finish_step(r, m, place, step)

    return launch(
        body, "finish", 1, {k: fixed(v) for k, v in ins.items()}, {k: fixed_out(v, F32) for k, v in outs.items()},
        {}, {}, None, 1 << 28,
    )


def frame_bias(clip_row, frame_count):
    first = lax.axis_index("frame") * frame_count
    clips = jnp.concatenate([jnp.full((SPAN,), -1, jnp.int32), clip_row])
    key_clips = lax.dynamic_slice_in_dim(clips, first, SPAN + frame_count)
    qi, qp = jnp.arange(frame_count * SUB) // SUB, jnp.arange(frame_count * SUB) % SUB
    kj, kp = jnp.arange((SPAN + frame_count) * SUB) // SUB, jnp.arange((SPAN + frame_count) * SUB) % SUB
    offset = qi[:, None] + SPAN - kj[None, :]
    allowed = (
        (qp[:, None] == kp[None, :]) & (offset >= 0) & (offset <= SPAN)
        & (jnp.repeat(key_clips[SPAN:], SUB)[:, None] == jnp.repeat(key_clips, SUB)[None, :])
    )
    return jnp.where(allowed, 0.0, NEG).astype(F32)


def local_fused(
    frames_in, spat_gain_a, spat_qkv, spat_out, spat_gain_b, spat_up, spat_down,
    temp_gain_a, temp_qkv, temp_out, temp_gain_b, temp_up, temp_down,
    quant_proj, codebook, code_index, clip_index, dead_codes, source_rows, latent_cot,
):
    frame_count, patches, d = frames_in.shape[1:]
    cdim = quant_proj.shape[1]
    row_count = frame_count * patches
    frame_size, batch_size = lax.axis_size("frame"), lax.axis_size("batch")
    assert frame_count == SPAN
    spat = (spat_gain_a.reshape(1, d), spat_qkv, spat_out, spat_gain_b.reshape(1, d), spat_up, spat_down)
    temp = (temp_gain_a.reshape(1, d), temp_qkv, temp_out, temp_gain_b.reshape(1, d), temp_up, temp_down)
    x = frames_in[0]
    codes = code_index[0]
    book_t, proj_t = codebook.T, quant_proj.T
    bias = frame_bias(clip_index[0], frame_count)
    row_base = (lax.axis_index("batch") * frame_size + lax.axis_index("frame")) * row_count
    sf = spat_forward_call(x, spat, codes, book_t)
    tb = temporal_call(
        sf.y, sf.halo, bias, latent_cot[0].transpose(0, 2, 1), sf.chosen, codes, dead_codes.reshape(1, -1),
        (source_rows - row_base).reshape(1, -1), proj_t, temp,
    )
    sb = spat_backward_call(sf, tb, sf.y, temp[0], x, spat)
    out = finish_call(
        tb, sb, book_t, dead_codes, frame_size * batch_size * row_count * cdim, d, spat_up.shape[1]
    )
    return (
        tb.lat.transpose(0, 2, 1)[None], out.commit[0, 0], sb.dx[None],
        out.g_sa[0], out.s_qkv, out.s_out, out.g_sb[0], out.s_up, out.s_down,
        out.g_ta[0], out.t_qkv, out.t_out, out.g_tb[0], out.t_up, out.t_down,
        out.proj_grad.T, out.book_grad.T, out.refreshed.T,
    )


def solution(mesh):
    fused = (mesh.shape["frame"], mesh.shape["batch"]) == (8, 4)
    return jax.shard_map(
        local_fused if fused else local_general,
        mesh=mesh,
        in_specs=(
            P("batch", "frame", None, None),
            *([P()] * 14),
            P("batch", "frame", None),
            P("batch", None),
            P(),
            P(),
            P("batch", "frame", None, None),
        ),
        out_specs=(
            P("batch", "frame", None, None),
            P(),
            P("batch", "frame", None, None),
            P(),
            P("frame", None),
            P("frame", None),
            P(),
            P("frame", None),
            P("frame", None),
            P(),
            P("frame", None),
            P("frame", None),
            P(),
            P("frame", None),
            P("frame", None),
            P("frame", None),
            P("frame", None),
            P(),
        ),
        check_vma=False,
    )
```

```python
import types

import jax
import jax.numpy as jnp
from jax import lax
from jax.experimental import pallas as pl
from jax.experimental.pallas import tpu as pltpu
from jax.sharding import PartitionSpec as P

HEADS = 8
EPS = 1e-05
BETA = 0.25
USE_MIN = 2.0
NEG = -1e30
HIGH = lax.Precision.HIGHEST
SPAN = 4
F32 = jnp.float32
BF16 = jnp.bfloat16
MESH = pl.DeviceIdType.MESH
GELU_C = 0.7978845608028654
GELU_A = 0.044715
VMEM_BYTES = 56 * 1024 * 1024
TAIL_BYTES = 62 * 1024 * 1024
SUB = 32
GROUP = 64


def mm(a, b):
    return jnp.dot(a, b, preferred_element_type=F32)


def mm_t(a, b):
    return lax.dot_general(a, b, (((1,), (1,)), ((), ())), preferred_element_type=F32)


def t_mm(a, b):
    return lax.dot_general(a, b, (((0,), (0,)), ((), ())), preferred_element_type=F32)


def norm(x):
    c = x - jnp.mean(x, -1, keepdims=True)
    r = lax.rsqrt(jnp.mean(c * c, -1, keepdims=True) + EPS)
    return c * r, r


def norm_back(dy, xhat, r, gain):
    d = dy * gain
    return r * (d - jnp.mean(d, -1, keepdims=True) - xhat * jnp.mean(d * xhat, -1, keepdims=True))


def add_row(ref, rows):
    ref[...] += jnp.sum(rows, 0, keepdims=True)


def head_masks(rows, width):
    lane = lax.broadcasted_iota(jnp.int32, (rows, width), 1)
    return (lane < width // 2, lane >= width // 2)


def attend_pair(q, k, v, bias):
    width = q.shape[1]
    scale = (width // 2) ** -0.5
    zero = jnp.zeros((), BF16)
    qs = q * jnp.asarray(scale, BF16)
    v_ext = jnp.concatenate([v, jnp.ones_like(v)], axis=1)
    masks = head_masks(q.shape[0], width)
    halves = []
    for mask in masks:
        s = mm_t(jnp.where(mask, qs, zero), k)
        if bias is not None:
            s = s + bias
        e = jnp.exp(s - jnp.max(s, -1, keepdims=True)).astype(BF16)
        r = mm(e, v_ext)
        halves.append(r[:, :width] / r[:, width:])
    return jnp.where(masks[0], halves[0], halves[1]).astype(BF16)


def attend_pair_back(q, k, v, do, bias_t):
    width = q.shape[1]
    scale = jnp.asarray((width // 2) ** -0.5, BF16)
    zero = jnp.zeros((), BF16)
    qs = q * scale
    ks = k * scale
    q_masks = head_masks(q.shape[0], width)
    k_masks = head_masks(k.shape[0], width)
    dq = dk = dv = None
    for q_mask, k_mask in zip(q_masks, k_masks):
        qm = jnp.where(q_mask, qs, zero)
        dom = jnp.where(q_mask, do, zero)
        st = mm_t(k, qm)
        if bias_t is not None:
            st = st + bias_t
        e = jnp.exp(st - jnp.max(st, 0, keepdims=True))
        p = e * (1.0 / jnp.sum(e, 0, keepdims=True))
        dp = mm_t(v, dom)
        inner = jnp.sum(p * dp, 0, keepdims=True)
        ds = (p * (dp - inner)).astype(BF16)
        dv_one = mm(p.astype(BF16), dom)
        dk_one = mm(ds, qm)
        dq_one = t_mm(ds, jnp.where(k_mask, ks, zero))
        dq = dq_one if dq is None else dq + dq_one
        dk = dk_one if dk is None else dk + dk_one
        dv = dv_one if dv is None else dv + dv_one
    return dq, dk, dv


def mlp_forward(mid, gain, w_up, w_down, bt_ref, h_ref, gp_ref, tile=512):
    xhat, _ = norm(mid)
    b = (xhat * gain).astype(BF16)
    bt_ref[...] = b.T
    out = mid
    for start in range(0, w_up.shape[1], tile):
        cols = slice(start, start + tile)
        u = mm(b, w_up[:, cols])
        u2 = u * u
        th = jnp.tanh(u * (GELU_C + (GELU_C * GELU_A) * u2))
        half = 0.5 + 0.5 * th
        h = (u * half).astype(BF16)
        slope = half + u * (half * (1.0 - th)) * (GELU_C + (3.0 * GELU_C * GELU_A) * u2)
        h_ref[:, cols] = h
        gp_ref[:, cols] = slope.astype(BF16)
        out = out + mm(h, w_down[cols, :])
    return out


def mlp_backward(dy, dy_low, mid, gain, w_up, w_down, gp_ref, du_ref, dgain_ref, tile=512):
    db = None
    for start in range(0, w_up.shape[1], tile):
        cols = slice(start, start + tile)
        dh = mm_t(dy_low, w_down[cols, :])
        du = (gp_ref[:, cols].astype(F32) * dh).astype(BF16)
        du_ref[:, cols] = du
        one = mm_t(du, w_up[:, cols])
        db = one if db is None else db + one
    xhat, r = norm(mid)
    add_row(dgain_ref, db * xhat)
    return dy + norm_back(db, xhat, r, gain)


def greet_ring(step):
    n = lax.axis_size("frame")
    me = lax.axis_index("frame")
    left, right = lax.rem(me + n - 1, n), lax.rem(me + 1, n)

    @pl.when(step == 0)
    def _():
        barrier = pltpu.get_barrier_semaphore()
        for peer in (left, right):
            pl.semaphore_signal(barrier, inc=1, device_id={"frame": peer}, device_id_type=MESH)

    return left, right


def meet_ring(step):
    @pl.when(step == 0)
    def _():
        pl.semaphore_wait(pltpu.get_barrier_semaphore(), 2)


def ring_copy(src, dst, send_sem, recv_sem, peer):
    return pltpu.make_async_remote_copy(
        src_ref=src, dst_ref=dst, send_sem=send_sem, recv_sem=recv_sem,
        device_id={"frame": peer}, device_id_type=MESH,
    )


def spat_fwd_kernel(
    x_ref, ga, w_qkv, w_out, gb, w_up, w_down,
    y_ref, at_ref, pk_ref, att_t_ref, mid_ref, bt_ref, h_ref, gp_ref, halo_ref,
    att_ref, keep_ref, send_sem, recv_sem,
):
    step = pl.program_id(0)
    steps = pl.num_programs(0)
    feature = x_ref.shape[-1]
    left, right = greet_ring(step)
    x = x_ref[0].astype(F32)
    xhat, _ = norm(x)
    a = (xhat * ga[...]).astype(BF16)
    at_ref[...] = a.T
    for start in range(0, 3 * feature, 512):
        pk_ref[:, start : start + 512] = mm(a, w_qkv[:, start : start + 512]).astype(BF16)
    for lane in range(0, feature, 128):
        att_ref[:, lane : lane + 128] = attend_pair(
            pk_ref[:, lane : lane + 128],
            pk_ref[:, feature + lane : feature + lane + 128],
            pk_ref[:, 2 * feature + lane : 2 * feature + lane + 128],
            None,
        )
    att = att_ref[...]
    att_t_ref[...] = att.T
    mid = x + mm(att, w_out[...])
    mid_ref[...] = mid
    y = mlp_forward(mid, gb[...], w_up, w_down, bt_ref, h_ref, gp_ref).astype(BF16)
    y_ref[0] = y
    keep_ref[step] = y
    meet_ring(step)

    def copy(i):
        return ring_copy(keep_ref.at[i], halo_ref.at[i], send_sem.at[i], recv_sem.at[i], right)

    copy(step).start()

    @pl.when(step == steps - 1)
    def _():
        for i in range(keep_ref.shape[0]):
            copy(i).wait()


def temp_fwd_kernel(
    x_ref, halo_ref, bias_ref, ga, w_qkv, w_out, gb, w_up, w_down, proj,
    lat_ref, x3_ref, at_ref, aht_ref, pk_ref, kvh_ref, att_t_ref, mid_ref, bt_ref, h_ref, gp_ref, att_ref,
):
    frames, group, feature = x_ref.shape
    rows = frames * group
    x = x_ref[...].reshape(rows, feature).astype(F32)
    xhat, _ = norm(x)
    a = (xhat * ga[...]).astype(BF16)
    at_ref[...] = a.T
    for start in range(0, 3 * feature, 512):
        pk_ref[:, :, start : start + 512] = (
            mm(a, w_qkv[:, start : start + 512]).astype(BF16).reshape(frames, group, 512)
        )
    xhat_h, _ = norm(halo_ref[...].reshape(rows, feature).astype(F32))
    ah = (xhat_h * ga[...]).astype(BF16)
    aht_ref[...] = ah.T
    for start in range(0, 2 * feature, 512):
        kvh_ref[:, :, start : start + 512] = (
            mm(ah, w_qkv[:, feature + start : feature + start + 512])
            .astype(BF16)
            .reshape(frames, group, 512)
        )
    bias = bias_ref[...]
    for sub in range(0, group, SUB):
        here = slice(sub, sub + SUB)
        for lane in range(0, feature, 128):
            q = pk_ref[:, here, lane : lane + 128].reshape(frames * SUB, 128)
            k = jnp.concatenate(
                [kvh_ref[:, here, lane : lane + 128],
                 pk_ref[:, here, feature + lane : feature + lane + 128]], 0
            ).reshape(2 * frames * SUB, 128)
            v = jnp.concatenate(
                [kvh_ref[:, here, feature + lane : feature + lane + 128],
                 pk_ref[:, here, 2 * feature + lane : 2 * feature + lane + 128]], 0
            ).reshape(2 * frames * SUB, 128)
            att_ref[:, here, lane : lane + 128] = attend_pair(q, k, v, bias).reshape(frames, SUB, 128)
    att = att_ref[...].reshape(rows, feature)
    att_t_ref[...] = att.T
    mid = x + mm(att, w_out[...])
    mid_ref[...] = mid
    y = mlp_forward(mid, gb[...], w_up, w_down, bt_ref, h_ref, gp_ref).astype(BF16)
    x3_ref[...] = y
    lat_ref[...] = mm(y, proj[...]).reshape(frames, group, proj.shape[1])


def temp_bwd_kernel(
    gl_ref, proj, x3_ref, x_ref, mid_ref, gp_ref, pk_ref, kvh_ref, bias_ref,
    ga, w_qkv, w_out, gb, w_up, w_down,
    dyt_ref, du_ref, dmid_ref, dpk_ref, dkvh_ref, base_ref, back_ref, dga_ref, dgb_ref, dproj_ref,
    datt_ref, dah_ref, send_sem, recv_sem,
):
    step = pl.program_id(0)
    steps = pl.num_programs(0)
    frames, group, feature = x_ref.shape
    rows = frames * group
    left, right = greet_ring(step)

    @pl.when(step == 0)
    def _():
        for ref in (dga_ref, dgb_ref, dproj_ref):
            ref[...] = jnp.zeros_like(ref)

    gl = gl_ref[...].reshape(rows, gl_ref.shape[2])
    dproj_ref[...] += t_mm(gl, x3_ref[...])
    dy_low = mm_t(gl, proj[...]).astype(BF16)
    dyt_ref[...] = dy_low.T
    dmid = mlp_backward(
        dy_low.astype(F32), dy_low, mid_ref[...], gb[...], w_up, w_down, gp_ref, du_ref, dgb_ref
    )
    dmid_low = dmid.astype(BF16)
    dmid_ref[...] = dmid_low
    datt_ref[...] = mm_t(dmid_low, w_out[...]).astype(BF16).reshape(frames, group, feature)
    bias = bias_ref[...]
    half = frames * SUB
    for sub in range(0, group, SUB):
        here = slice(sub, sub + SUB)
        for lane in range(0, feature, 128):
            l0 = slice(lane, lane + 128)
            l1 = slice(feature + lane, feature + lane + 128)
            l2 = slice(2 * feature + lane, 2 * feature + lane + 128)
            q = pk_ref[:, here, l0].reshape(half, 128)
            k = jnp.concatenate([kvh_ref[:, here, l0], pk_ref[:, here, l1]], 0).reshape(2 * half, 128)
            v = jnp.concatenate([kvh_ref[:, here, l1], pk_ref[:, here, l2]], 0).reshape(2 * half, 128)
            do = datt_ref[:, here, l0].reshape(half, 128)
            dq, dk, dv = attend_pair_back(q, k, v, do, bias)
            dk, dv = dk.astype(BF16), dv.astype(BF16)
            dpk_ref[:, here, l0] = dq.astype(BF16).reshape(frames, SUB, 128)
            dpk_ref[:, here, l1] = dk[half:].reshape(frames, SUB, 128)
            dpk_ref[:, here, l2] = dv[half:].reshape(frames, SUB, 128)
            dkvh_ref[:, here, l0] = dk[:half].reshape(frames, SUB, 128)
            dkvh_ref[:, here, l1] = dv[:half].reshape(frames, SUB, 128)
    da = mm_t(dpk_ref[...].reshape(rows, 3 * feature), w_qkv[...])
    dah = mm_t(dkvh_ref[...].reshape(rows, 2 * feature), w_qkv[:, feature:])
    dah_ref[step] = dah.astype(BF16).reshape(frames, group, feature)
    meet_ring(step)

    def copy(i):
        there = back_ref.at[:, pl.ds(i * group, group), :]
        return ring_copy(dah_ref.at[i], there, send_sem.at[i], recv_sem.at[i], left)

    copy(step).start()
    xhat, r = norm(x_ref[...].reshape(rows, feature).astype(F32))
    add_row(dga_ref, da * xhat)
    base_ref[...] = (dmid + norm_back(da, xhat, r, ga[...])).reshape(frames, group, feature)

    @pl.when(step == steps - 1)
    def _():
        for i in range(dah_ref.shape[0]):
            copy(i).wait()


def spat_bwd_kernel(
    base_ref, dah_ref, x2_ref, gta, x_ref, mid_ref, gp_ref, pk_ref,
    ga, w_qkv, w_out, gb, w_up, w_down,
    dx_ref, dyt_ref, du_ref, dmid_ref, dpk_ref, dgt_ref, dga_ref, dgb_ref,
    datt_ref,
):
    feature = x_ref.shape[-1]

    @pl.when(pl.program_id(0) == 0)
    def _():
        for ref in (dgt_ref, dga_ref, dgb_ref):
            ref[...] = jnp.zeros_like(ref)

    xhat2, r2 = norm(x2_ref[0].astype(F32))
    dah = dah_ref[0].astype(F32)
    add_row(dgt_ref, dah * xhat2)
    dy_low = (base_ref[0] + norm_back(dah, xhat2, r2, gta[...])).astype(BF16)
    dyt_ref[...] = dy_low.T
    dmid = mlp_backward(
        dy_low.astype(F32), dy_low, mid_ref[...], gb[...], w_up, w_down, gp_ref, du_ref, dgb_ref
    )
    dmid_low = dmid.astype(BF16)
    dmid_ref[...] = dmid_low
    datt_ref[...] = mm_t(dmid_low, w_out[...]).astype(BF16)
    for lane in range(0, feature, 128):
        l0 = slice(lane, lane + 128)
        l1 = slice(feature + lane, feature + lane + 128)
        l2 = slice(2 * feature + lane, 2 * feature + lane + 128)
        dq, dk, dv = attend_pair_back(pk_ref[:, l0], pk_ref[:, l1], pk_ref[:, l2], datt_ref[:, l0], None)
        dpk_ref[:, l0] = dq.astype(BF16)
        dpk_ref[:, l1] = dk.astype(BF16)
        dpk_ref[:, l2] = dv.astype(BF16)
    da = mm_t(dpk_ref[...], w_qkv[...])
    xhat, r = norm(x_ref[0].astype(F32))
    add_row(dga_ref, da * xhat)
    dx_ref[0] = (dmid + norm_back(da, xhat, r, ga[...])).astype(BF16)


def mlp_grad_kernel(bt_ref, du_ref, dyt_ref, h_ref, up_ref, down_ref):
    up_ref[0] = mm(bt_ref[...], du_ref[...]).astype(BF16)
    width = down_ref.shape[2]
    for j in range(down_ref.shape[0]):
        down_ref[j] = mm(dyt_ref[...], h_ref[:, j * width : (j + 1) * width]).astype(BF16)


def att_grad_kernel(halo, *refs):
    if halo:
        at_ref, att_t_ref, dq_ref, dk_ref, dv_ref, dm_ref, aht_ref, dkh_ref, dvh_ref, out_ref = refs
    else:
        at_ref, att_t_ref, dq_ref, dk_ref, dv_ref, dm_ref, out_ref = refs
    dq = mm(at_ref[...], dq_ref[...])
    dk = mm(at_ref[...], dk_ref[...])
    dv = mm(at_ref[...], dv_ref[...])
    if halo:
        dk = dk + mm(aht_ref[...], dkh_ref[...])
        dv = dv + mm(aht_ref[...], dvh_ref[...])
    do = mm(att_t_ref[...], dm_ref[...])
    for i, part in enumerate((dq, dk, dv, do)):
        part = part.astype(BF16)
        for j in range(2):
            out_ref[j, :, 128 * i : 128 * (i + 1)] = part[:, 128 * j : 128 * (j + 1)]


def whole(shape):
    zeros = (0,) * len(shape)
    return pl.BlockSpec(shape, lambda i: zeros)


def col_block(rows, width, offset=0):
    return pl.BlockSpec((rows, width), lambda i: (0, i + offset))


def row_block(rows, width):
    return pl.BlockSpec((rows, width), lambda i: (i, 0))


def shape_of(shape, dtype):
    return jax.ShapeDtypeStruct(shape, dtype)


def params(collective=None):
    return pltpu.CompilerParams(
        vmem_limit_bytes=VMEM_BYTES, dimension_semantics=("arbitrary",), collective_id=collective,
        has_side_effects=collective is not None,
    )


def cost(flops, nbytes):
    return pl.CostEstimate(flops=int(flops), bytes_accessed=int(nbytes), transcendentals=0)


def weight_specs(feature, hidden):
    return [
        whole((1, feature)), whole((feature, 3 * feature)), whole((feature, feature)),
        whole((1, feature)), whole((feature, hidden)), whole((hidden, feature)),
    ]


def spat_forward(x, weights):
    frames, patches, d = x.shape
    hidden = weights[4].shape[1]
    n = frames * patches
    blk = pl.BlockSpec((1, patches, d), lambda i: (i, 0, 0))
    return pl.pallas_call(
        spat_fwd_kernel,
        grid=(frames,),
        in_specs=[blk] + weight_specs(d, hidden),
        out_specs=[
            blk, col_block(d, patches), row_block(patches, 3 * d), col_block(d, patches),
            row_block(patches, d), col_block(d, patches), row_block(patches, hidden), row_block(patches, hidden),
            pl.BlockSpec(memory_space=pl.ANY),
        ],
        out_shape=[
            shape_of(x.shape, BF16), shape_of((d, n), BF16), shape_of((n, 3 * d), BF16), shape_of((d, n), BF16),
            shape_of((n, d), F32), shape_of((d, n), BF16), shape_of((n, hidden), BF16), shape_of((n, hidden), BF16),
            shape_of(x.shape, BF16),
        ],
        scratch_shapes=[
            pltpu.VMEM((patches, d), BF16), pltpu.VMEM(x.shape, BF16),
            pltpu.SemaphoreType.DMA((frames,)), pltpu.SemaphoreType.DMA((frames,)),
        ],
        compiler_params=params(1),
        cost_estimate=cost(2 * n * d * (4 * d + 2 * hidden + 2 * patches), 24 * n * d),
        name="spat_forward",
    )(x, *weights)


def temp_forward(x, halo, bias, weights, proj):
    frames, patches, d = x.shape
    hidden = weights[4].shape[1]
    n = frames * patches
    steps = patches // GROUP
    rows = frames * GROUP
    cdim = proj.shape[1]
    blk = pl.BlockSpec((frames, GROUP, d), lambda i: (0, i, 0))
    stacked = lambda width: pl.BlockSpec((frames, GROUP, width), lambda i: (i, 0, 0))
    return pl.pallas_call(
        temp_fwd_kernel,
        grid=(steps,),
        in_specs=[blk, blk, whole(bias.shape)] + weight_specs(d, hidden) + [whole(proj.shape)],
        out_specs=[
            pl.BlockSpec((frames, GROUP, cdim), lambda i: (0, i, 0)), row_block(rows, d),
            col_block(d, rows), col_block(d, rows), stacked(3 * d), stacked(2 * d), col_block(d, rows),
            row_block(rows, d), col_block(d, rows), row_block(rows, hidden), row_block(rows, hidden),
        ],
        out_shape=[
            shape_of((frames, patches, cdim), F32), shape_of((n, d), BF16),
            shape_of((d, n), BF16), shape_of((d, n), BF16),
            shape_of((frames * steps, GROUP, 3 * d), BF16), shape_of((frames * steps, GROUP, 2 * d), BF16),
            shape_of((d, n), BF16), shape_of((n, d), F32), shape_of((d, n), BF16),
            shape_of((n, hidden), BF16), shape_of((n, hidden), BF16),
        ],
        scratch_shapes=[pltpu.VMEM((frames, GROUP, d), BF16)],
        compiler_params=params(),
        cost_estimate=cost(2 * n * d * (6 * d + 2 * hidden + 2 * patches), 30 * n * d),
        name="temp_forward",
    )(x, halo, bias, *weights, proj)


def temp_backward(gl, proj, x3, x, mid, gp, pk, kvh, bias_t, weights):
    frames, patches, d = x.shape
    hidden = weights[4].shape[1]
    n = frames * patches
    steps = patches // GROUP
    rows = frames * GROUP
    cdim = proj.shape[1]
    nat = lambda width: pl.BlockSpec((frames, GROUP, width), lambda i: (0, i, 0))
    stacked = lambda width: pl.BlockSpec((frames, GROUP, width), lambda i: (i, 0, 0))
    return pl.pallas_call(
        temp_bwd_kernel,
        grid=(steps,),
        in_specs=[
            nat(cdim), whole(proj.shape), row_block(rows, d), nat(d), row_block(rows, d),
            row_block(rows, hidden), stacked(3 * d), stacked(2 * d), whole(bias_t.shape),
        ] + weight_specs(d, hidden),
        out_specs=[
            col_block(d, rows), row_block(rows, hidden), row_block(rows, d), stacked(3 * d), stacked(2 * d),
            nat(d), pl.BlockSpec(memory_space=pl.ANY), whole((1, d)), whole((1, d)), whole((cdim, d)),
        ],
        out_shape=[
            shape_of((d, n), BF16), shape_of((n, hidden), BF16), shape_of((n, d), BF16),
            shape_of((frames * steps, GROUP, 3 * d), BF16), shape_of((frames * steps, GROUP, 2 * d), BF16),
            shape_of((frames, patches, d), F32), shape_of((frames, patches, d), BF16),
            shape_of((1, d), F32), shape_of((1, d), F32), shape_of((cdim, d), F32),
        ],
        scratch_shapes=[
            pltpu.VMEM((frames, GROUP, d), BF16), pltpu.VMEM((steps, frames, GROUP, d), BF16),
            pltpu.SemaphoreType.DMA((steps,)), pltpu.SemaphoreType.DMA((steps,)),
        ],
        compiler_params=params(2),
        cost_estimate=cost(2 * n * d * (6 * d + 2 * hidden + 5 * patches), 40 * n * d),
        name="temp_backward",
    )(gl, proj, x3, x, mid, gp, pk, kvh, bias_t, *weights)


def spat_backward(base, dah, x2, gta, x, mid, gp, pk, weights):
    frames, patches, d = x.shape
    hidden = weights[4].shape[1]
    n = frames * patches
    blk = pl.BlockSpec((1, patches, d), lambda i: (i, 0, 0))
    return pl.pallas_call(
        spat_bwd_kernel,
        grid=(frames,),
        in_specs=[
            blk, blk, blk, whole((1, d)), blk, row_block(patches, d), row_block(patches, hidden),
            row_block(patches, 3 * d),
        ] + weight_specs(d, hidden),
        out_specs=[
            blk, col_block(d, patches), row_block(patches, hidden), row_block(patches, d),
            row_block(patches, 3 * d), whole((1, d)), whole((1, d)), whole((1, d)),
        ],
        out_shape=[
            shape_of(x.shape, BF16), shape_of((d, n), BF16), shape_of((n, hidden), BF16), shape_of((n, d), BF16),
            shape_of((n, 3 * d), BF16), shape_of((1, d), F32), shape_of((1, d), F32), shape_of((1, d), F32),
        ],
        scratch_shapes=[pltpu.VMEM((patches, d), BF16)],
        compiler_params=params(),
        cost_estimate=cost(2 * n * d * (4 * d + 2 * hidden + 5 * patches), 30 * n * d),
        name="spat_backward",
    )(base, dah, x2, gta, x, mid, gp, pk, *weights)


def mlp_grads(bt, du, dyt, h):
    d, n = bt.shape
    hidden = du.shape[1]
    steps = 4
    wide = hidden // steps
    return pl.pallas_call(
        mlp_grad_kernel,
        grid=(steps,),
        in_specs=[whole((d, n)), col_block(n, wide), whole((d, n)), col_block(n, wide)],
        out_specs=[
            pl.BlockSpec((1, d, wide), lambda i: (i, 0, 0)),
            pl.BlockSpec((2, d, wide // 2), lambda i: (i, 0, 0)),
        ],
        out_shape=[shape_of((steps, d, wide), BF16), shape_of((2 * steps, d, wide // 2), BF16)],
        compiler_params=params(),
        cost_estimate=cost(4 * n * d * hidden, 8 * n * d + 4 * n * hidden),
        name="mlp_grads",
    )(bt, du, dyt, h)


def att_grads(at, att_t, dpk, dmid, aht=None, dkvh=None):
    d, n = at.shape
    halo = aht is not None
    wide = 256
    args = [at, att_t, dpk, dpk, dpk, dmid]
    specs = [
        whole((d, n)), whole((d, n)), col_block(n, wide), col_block(n, wide, d // wide),
        col_block(n, wide, 2 * d // wide), col_block(n, wide),
    ]
    if halo:
        args += [aht, dkvh, dkvh]
        specs += [whole((d, n)), col_block(n, wide), col_block(n, wide, d // wide)]
    return pl.pallas_call(
        lambda *refs: att_grad_kernel(halo, *refs),
        grid=(d // wide,),
        in_specs=specs,
        out_specs=pl.BlockSpec((2, d, 512), lambda i: (i, 0, 0)),
        out_shape=shape_of((d // 128, d, 512), BF16),
        compiler_params=params(),
        cost_estimate=cost(2 * n * d * d * (6 if halo else 4), 16 * n * d),
        name="att_grads",
    )(*args)


def bits_of(count):
    bits = count.bit_length() - 1
    assert count == 1 << bits
    return bits


def swap(value, axis, bit):
    count = lax.axis_size(axis)
    return lax.ppermute(value, axis, [(i, i ^ (1 << bit)) for i in range(count)])


def my_bit(axis, bit):
    return (lax.axis_index(axis) >> bit) & 1


def reduce_pieces(grad, labels, order):
    names = []
    for axis in labels:
        names += [(axis, b) for b in reversed(range(bits_of(lax.axis_size(axis))))]
    tail = grad.shape[len(labels) :]
    cur = grad.reshape((2,) * len(names) + tail)
    for axis, bit in order:
        at = names.index((axis, bit))
        me = my_bit(axis, bit)
        kept = lax.dynamic_index_in_dim(cur, me, at, keepdims=False)
        sent = lax.dynamic_index_in_dim(cur, 1 - me, at, keepdims=False)
        cur = (kept.astype(F32) + swap(sent, axis, bit).astype(F32)).astype(BF16)
        names.pop(at)
    cur = cur[None]
    for bit in reversed(range(bits_of(lax.axis_size("batch")))):
        other = swap(cur, "batch", bit)
        low = my_bit("batch", bit) == 0
        cur = jnp.stack([jnp.where(low, cur, other), jnp.where(low, other, cur)], 1)
        cur = cur.reshape((-1,) + tail)
    return cur.astype(F32)


def orders():
    fb, bb = bits_of(lax.axis_size("frame")), bits_of(lax.axis_size("batch"))
    frame = [("frame", b) for b in [0] + list(reversed(range(1, fb)))]
    batch = [("batch", b) for b in range(bb)]
    return batch + frame, batch[:1] + frame[:1] + batch[1:] + frame[1:]


def local_general(
    frames_in, spat_gain_a, spat_qkv, spat_out, spat_gain_b, spat_up, spat_down,
    temp_gain_a, temp_qkv, temp_out, temp_gain_b, temp_up, temp_down,
    quant_proj, codebook, code_index, clip_index, dead_codes, source_rows, latent_cot,
):
    frame_count, patches, d = frames_in.shape[1:]
    cdim = quant_proj.shape[1]
    row_count = frame_count * patches
    frame_size, batch_size = lax.axis_size("frame"), lax.axis_size("batch")
    assert frame_count == SPAN
    spat = (spat_gain_a.reshape(1, d), spat_qkv, spat_out, spat_gain_b.reshape(1, d), spat_up, spat_down)
    temp = (temp_gain_a.reshape(1, d), temp_qkv, temp_out, temp_gain_b.reshape(1, d), temp_up, temp_down)
    x = frames_in[0]

    first = lax.axis_index("frame") * frame_count
    clips = jnp.concatenate([jnp.full((SPAN,), -1, jnp.int32), clip_index[0]])
    key_clips = lax.dynamic_slice_in_dim(clips, first, SPAN + frame_count)
    query_clips = key_clips[SPAN:]
    qi, qp = jnp.arange(frame_count * SUB) // SUB, jnp.arange(frame_count * SUB) % SUB
    kj, kp = jnp.arange((SPAN + frame_count) * SUB) // SUB, jnp.arange((SPAN + frame_count) * SUB) % SUB
    offset = qi[:, None] + SPAN - kj[None, :]
    allowed = (
        (qp[:, None] == kp[None, :]) & (offset >= 0) & (offset <= SPAN)
        & (jnp.repeat(query_clips, SUB)[:, None] == jnp.repeat(key_clips, SUB)[None, :])
    )
    bias = jnp.where(allowed, 0.0, NEG).astype(F32)

    x2, s_at, s_pk, s_att_t, s_mid, s_bt, s_h, s_gp, halo = spat_forward(x, spat)
    latent3, x3, t_at, t_aht, t_pk, t_kvh, t_att_t, t_mid, t_bt, t_h, t_gp = temp_forward(
        x2, halo, bias, temp, quant_proj
    )

    latent = latent3.reshape(-1, cdim)
    codes_flat = code_index.reshape(-1)
    chosen = jnp.take(codebook, codes_flat, axis=0)
    differ = latent - chosen
    commit_part = jnp.sum(differ * differ)
    grad_latent = (latent_cot.reshape(-1, cdim) + 2.0 * BETA * differ).astype(BF16)
    grad_book = jax.ops.segment_sum(-2.0 * BETA * differ, codes_flat, num_segments=codebook.shape[0])

    dyt, du, dmid, dpk, dkvh, base, dah_back, dg_ta, dg_tb, dproj = temp_backward(
        grad_latent.reshape(latent3.shape), quant_proj, x3, x2, t_mid, t_gp, t_pk, t_kvh, bias.T, temp
    )
    t_up, t_down = mlp_grads(t_bt, du, dyt, t_h)
    t_att = att_grads(
        t_at, t_att_t, dpk.reshape(row_count, -1), dmid, t_aht, dkvh.reshape(row_count, -1)
    )
    dx, dyt, du, dmid, dpk, dg_ta2, dg_sa, dg_sb = spat_backward(
        base, dah_back, x2, temp[0], x, s_mid, s_gp, s_pk, spat
    )
    s_up, s_down = mlp_grads(s_bt, du, dyt, s_h)
    s_att = att_grads(s_at, s_att_t, dpk, dmid)

    dead_match = (codes_flat[:, None] == dead_codes[None, :]).astype(F32)
    usage_part = jnp.sum(dead_match, 0)
    row_base = (lax.axis_index("batch") * frame_size + lax.axis_index("frame")) * row_count
    pick_table = ((source_rows - row_base)[:, None] == jnp.arange(row_count)[None, :]).astype(F32)
    picked = jnp.dot(pick_table, latent, precision=HIGH)
    usage_count, candidate, commit_total = lax.psum((usage_part, picked, commit_part), ("frame", "batch"))
    gain_ta, gain_tb, gain_sa, gain_sb = lax.psum(
        ((dg_ta + dg_ta2)[0], dg_tb[0], dg_sa[0], dg_sb[0]), ("frame", "batch")
    )
    old_rows = jnp.take(codebook, dead_codes, axis=0)
    fresh_rows = jnp.where((usage_count < USE_MIN)[:, None], candidate, old_rows)
    refreshed = codebook.at[dead_codes].set(fresh_rows)
    commit_loss = commit_total / (frame_size * batch_size * row_count * cdim)

    one, two = orders()
    piece = d // frame_size

    def by_rows(grad, order):
        return reduce_pieces(
            grad.reshape(batch_size, frame_size, -1, grad.shape[-1]), ("batch", "frame"), order
        )

    def finish_up(grad):
        return by_rows(grad, one).transpose(1, 0, 2).reshape(piece, -1)

    def finish_down(grad):
        hidden = grad.shape[0] * grad.shape[2]
        wide = hidden // frame_size
        if grad.shape[2] != wide:
            grad = grad.transpose(1, 0, 2).reshape(d, frame_size, wide).transpose(1, 0, 2)
        out = reduce_pieces(
            grad.reshape(frame_size, batch_size, d // batch_size, wide), ("frame", "batch"), two
        )
        return out.reshape(d, wide).T

    def finish_att(grad, order):
        out = by_rows(grad, order)
        qkv = out[:, :, :384].reshape(batch_size, piece, 3, -1).transpose(1, 2, 0, 3).reshape(piece, 3 * d)
        return qkv, out[:, :, 384:].transpose(1, 0, 2).reshape(piece, d)

    book = grad_book.reshape(frame_size, batch_size, -1, 128)
    proj = dproj.T.reshape(frame_size, batch_size, -1)
    proj_size = proj.shape[2]
    proj = jnp.pad(proj, ((0, 0), (0, 0), (0, -proj_size % 128))).reshape(frame_size, batch_size, -1, 128)
    small = jnp.concatenate([book, proj], 2).astype(BF16)
    small = reduce_pieces(small, ("frame", "batch"), two)
    book_rows = book.shape[2]
    g_book = small[:, :book_rows].reshape(-1, cdim)
    g_proj = small[:, book_rows:].reshape(batch_size, -1)[:, :proj_size].reshape(piece, cdim)
    gt_qkv, gt_out = finish_att(t_att, one)
    gs_qkv, gs_out = finish_att(s_att, one)
    return (
        latent.reshape(latent_cot.shape),
        commit_loss,
        dx[None],
        gain_sa,
        gs_qkv,
        gs_out,
        gain_sb,
        finish_up(s_up),
        finish_down(s_down),
        gain_ta,
        gt_qkv,
        gt_out,
        gain_tb,
        finish_up(t_up),
        finish_down(t_down),
        g_proj,
        g_book,
        refreshed,
    )


def stack_heads(x, masks):
    zero = jnp.zeros((), BF16)
    return jnp.concatenate([jnp.where(mask, x, zero) for mask in masks], 0)


def attend_both(q, k, v, bias):
    rows, width = q.shape
    masks = head_masks(rows, width)
    s = mm_t(stack_heads(q * jnp.asarray((width // 2) ** -0.5, BF16), masks), k)
    if bias is not None:
        s = s + bias
    e = jnp.exp(s - jnp.max(s, -1, keepdims=True)).astype(BF16)
    r = mm(e, jnp.concatenate([v, jnp.ones_like(v)], axis=1))
    r = r[:, :width] / r[:, width:]
    return jnp.where(masks[0], r[:rows], r[rows:]).astype(BF16)


def attend_both_back(q, k, v, do, bias_t):
    rows, width = q.shape
    scale = jnp.asarray((width // 2) ** -0.5, BF16)
    masks = head_masks(rows, width)
    q2, do2 = stack_heads(q * scale, masks), stack_heads(do, masks)
    st = mm_t(k, q2)
    if bias_t is not None:
        st = st + bias_t
    e = jnp.exp(st - jnp.max(st, 0, keepdims=True))
    p = e * (1.0 / jnp.sum(e, 0, keepdims=True))
    dp = mm_t(v, do2)
    inner = jnp.sum(p * dp, 0, keepdims=True)
    ds = (p * (dp - inner)).astype(BF16)
    dq = t_mm(ds, k * scale)
    return jnp.where(masks[0], dq[:rows], dq[rows:]), mm(ds, q2), mm(p.astype(BF16), do2)


SIZE = {"y": 2, "c": 2, "z": 4, "x": 2}
PEERS = ({"y": 1}, {"c": 1}, {"y": 1, "c": 1}, {"x": 1}, {"z": 1}, {"z": 2}, {"z": 3})
ROWS_DIMS = ("y", "c", "z", "x")
COLS_DIMS = ("z", "x", "y", "c")
E_DIMS = ("u", "c", "z", "x", "y")
H_DIMS = ("u", "w", "c", "z", "x", "y")
Y_FIRST = ("c", "y", "x", "z")
X_FIRST = ("c", "x", "y", "z")
TILE = 512


class Place:
    def __init__(self):
        batch, frame = lax.axis_index("batch"), lax.axis_index("frame")
        self.me = {"y": lax.div(batch, 2), "c": lax.rem(batch, 2), "z": lax.div(frame, 2), "x": lax.rem(frame, 2)}

    def next(self, dim, shift):
        return lax.rem(self.me[dim] + shift, SIZE[dim])

    def peer(self, shifts):
        at = {d: self.next(d, shifts[d]) if d in shifts else self.me[d] for d in SIZE}
        return {"batch": 2 * at["y"] + at["c"], "frame": 2 * at["z"] + at["x"]}

    def copy(self, src, dst, send, recv, shifts):
        return pltpu.make_async_remote_copy(
            src_ref=src, dst_ref=dst, send_sem=send, recv_sem=recv,
            device_id=self.peer(shifts), device_id_type=MESH,
        )

    def greet(self):
        for shifts in PEERS:
            pl.semaphore_signal(
                pltpu.get_barrier_semaphore(), inc=1, device_id=self.peer(shifts), device_id_type=MESH
            )


def sizes(dims):
    return tuple(SIZE[d] for d in dims)


class Sum:
    def __init__(self, dims, tail, order, source=None, shared=None, fixed=(), gather=True, direct=False):
        self.dims, self.tail, self.order, self.source, self.shared = dims, tail, order, source, shared
        self.fixed, self.with_gather, self.direct = dict(fixed), gather, direct
        self.counts = [SIZE[d] - 1 for d in order]

    def left(self, k):
        free = [d for d in self.dims if d not in self.fixed]
        return [d for d in free if d not in self.order or self.order.index(d) > k]

    def scratch(self):
        out = []
        if self.shared is None:
            kept = self.left(0 if self.source else -1)
            out.append(pltpu.VMEM(sizes(kept) + self.tail, BF16))
        for k, count in enumerate(self.counts):
            out.append(pltpu.VMEM((count,) + sizes(self.left(k)) + self.tail, BF16))
        if self.with_gather:
            out.append(pltpu.VMEM((2, 2) + self.tail, BF16))
        copies = sum(self.counts) + 3
        out += [pltpu.SemaphoreType.DMA((copies,))] * 2
        if self.source:
            out.append(pltpu.SemaphoreType.DMA)
        return out

    def bind(self, refs, r, place):
        self.place = place
        self.src = self.source(r) if self.source else None
        self.acc = self.shared(r) if self.shared else next(refs)
        self.got = [next(refs) for _ in self.counts]
        self.all = next(refs) if self.with_gather else None
        self.send, self.recv = next(refs), next(refs)
        self.load = next(refs) if self.source else None
        return self

    def index(self, dims, k, at_k, rest=None):
        out = []
        for d in dims:
            at = self.order.index(d) if d in self.order else len(self.order)
            if d in self.fixed:
                out.append(self.fixed[d])
            elif at < k:
                out.append(self.place.me[d])
            elif at == k and d in self.order:
                out.append(at_k)
            else:
                out.append(slice(None) if rest is None else rest[d])
        return tuple(out)

    def held(self):
        if self.shared:
            return self.dims
        return self.left(0 if self.source else -1)

    def copies(self, k):
        early = k == 0 and self.source
        src, dims = (self.src, self.dims) if early else (self.acc, self.held())
        base = sum(self.counts[:k])
        for i in range(self.counts[k]):
            there = self.index(dims, k, self.place.next(self.order[k], i + 1))
            yield self.place.copy(
                src.at[there], self.got[k].at[i], self.send.at[base + i], self.recv.at[base + i], {self.order[k]: i + 1}
            )

    def keep(self):
        here = self.index(self.dims, 0, self.place.me[self.order[0]])
        return pltpu.make_async_copy(self.src.at[here], self.acc, self.load)

    def start(self, k):
        for copy in self.copies(k):
            copy.start()
        if k == 0 and self.source:
            self.keep().start()

    def finish(self, k):
        for copy in self.copies(k):
            copy.wait()
        if k == 0 and self.source:
            self.keep().wait()
        left, got, count = self.left(k), self.got[k], self.counts[k]
        total = 1
        for d in left:
            total *= SIZE[d]

        def add(i):
            rest, stride = {}, total
            for d in left:
                stride //= SIZE[d]
                rest[d] = lax.rem(lax.div(i, stride), SIZE[d])
            here = self.index(self.held(), k, self.place.me[self.order[k]], rest)
            there = tuple(rest[d] for d in left)
            if count == 1:
                self.acc[here] = self.acc[here] + got[(0,) + there]
            else:
                value = self.acc[here].astype(F32)
                for j in range(count):
                    value = value + got[(j,) + there].astype(F32)
                self.acc[here] = value.astype(BF16)

        if total == 1:
            add(0)
        else:
            lax.fori_loop(0, total, lambda i, c: (add(i), c)[1], 0)

    def move(self, k):
        self.finish(k)
        self.start(k + 1)

    def piece(self):
        return self.acc[self.index(self.held(), len(self.order), None)]

    def hops(self, which):
        base = sum(self.counts)
        y, c = self.place.me["y"], self.place.me["c"]
        here = self.all.at[y, c]
        if self.direct:
            todo = [(here, shifts) for shifts in PEERS[:3]] if which == 0 else []
        else:
            todo = [(here, PEERS[0])] if which == 0 else [(self.all.at[:, c], PEERS[1])]
        for j, (ref, shifts) in enumerate(todo):
            at = base + which + j
            yield self.place.copy(ref, ref, self.send.at[at], self.recv.at[at], shifts)

    def gather(self):
        self.finish(len(self.order) - 1)
        self.all[self.place.me["y"], self.place.me["c"]] = self.piece()
        for copy in self.hops(0):
            copy.start()

    def spread(self):
        for copy in self.hops(0):
            copy.wait()
        for copy in self.hops(1):
            copy.start()

    def gathered(self, out):
        for copy in self.hops(0 if self.direct else 1):
            copy.wait()
        out[...] = self.all[...]


class Total:
    order = Y_FIRST

    def __init__(self, rows):
        self.rows = rows

    def scratch(self):
        copies = sum(SIZE[d] - 1 for d in self.order)
        return [
            pltpu.VMEM((self.rows, 128), F32), pltpu.VMEM((copies, self.rows, 128), F32),
            pltpu.SemaphoreType.DMA((copies,)), pltpu.SemaphoreType.DMA((copies,)),
        ]

    def bind(self, refs, r, place):
        self.place = place
        self.acc, self.got, self.send, self.recv = (next(refs) for _ in range(4))
        return self

    def copies(self, k):
        base = sum(SIZE[d] - 1 for d in self.order[:k])
        for i in range(SIZE[self.order[k]] - 1):
            at = base + i
            yield at, self.place.copy(
                self.acc, self.got.at[at], self.send.at[at], self.recv.at[at], {self.order[k]: i + 1}
            )

    def start(self, k):
        for _, copy in self.copies(k):
            copy.start()

    def finish(self, k):
        arrived = []
        for at, copy in self.copies(k):
            copy.wait()
            arrived.append(at)
        for at in arrived:
            self.acc[...] = self.acc[...] + self.got[at]

    def move(self, k):
        self.finish(k)
        self.start(k + 1)


def launch(body, name, steps, ins, outs, scratch, moves, collective, flops, limit=VMEM_BYTES, unroll=False):
    keys = [*ins, *outs, *scratch]
    extra = [spec for part in moves.values() for spec in part.scratch()]

    def kernel(*refs):
        r = types.SimpleNamespace(**dict(zip(keys, refs)))
        rest = iter(refs[len(keys) :])
        place = Place()
        m = types.SimpleNamespace(**{k: v.bind(rest, r, place) for k, v in moves.items()})
        if unroll:
            for step in range(steps):
                body(r, m, place, step)
        else:
            body(r, m, place, pl.program_id(0))

    got = pl.pallas_call(
        kernel,
        grid=(1 if unroll else steps,),
        in_specs=[x[1] for x in ins.values()],
        out_specs=[x[1] for x in outs.values()],
        out_shape=[x[0] for x in outs.values()],
        scratch_shapes=list(scratch.values()) + extra,
        compiler_params=pltpu.CompilerParams(
            vmem_limit_bytes=limit, dimension_semantics=("arbitrary",), collective_id=collective,
            has_side_effects=collective is not None,
        ),
        cost_estimate=cost(flops, 40 << 20),
        name=name,
    )(*[x[0] for x in ins.values()])
    return types.SimpleNamespace(**dict(zip(outs, got)))


ANY = pl.BlockSpec(memory_space=pl.ANY)


def fixed_spec(shape):
    zeros = (0,) * len(shape)
    return pl.BlockSpec(shape, lambda i: zeros, pipeline_mode=pl.Buffered(1))


def fixed(array):
    return (array, fixed_spec(array.shape))


def fixed_out(shape, dtype):
    return (shape_of(shape, dtype), fixed_spec(shape))


def part_of(first, count):
    return lambda i: jnp.clip(i - first, 0, count - 1)


def on(step, value):
    if isinstance(step, int):
        return lambda f: f() if step == value else None
    return lambda f: pl.when(step == value)(f)


def within(step, first, count):
    if isinstance(step, int):
        return lambda f: f() if first <= step < first + count else None
    return lambda f: pl.when((step >= first) & (step < first + count))(f)


def split_parts(value, count):
    out = []
    for _ in range(count):
        low = value.astype(BF16)
        out.append(low)
        value = value - low.astype(F32)
    return out


def one_row(ref):
    return jnp.concatenate([ref[i : i + 1, :] for i in range(ref.shape[0])], 1)


def as_column(row):
    n = row.shape[1]
    same = lax.broadcasted_iota(jnp.int32, (n, n), 0) == lax.broadcasted_iota(jnp.int32, (n, n), 1)
    return jnp.sum(jnp.where(same, row.astype(F32), 0.0), 1, keepdims=True)


def code_masks(codes, rows):
    major = lax.div(codes, 128)
    minor = codes - 128 * major
    return major, jnp.where(lax.broadcasted_iota(jnp.int32, (128, codes.shape[1]), 0) == minor, 1.0, 0.0).astype(BF16)


def spat_forward_step(r, m, place, step):
    frames = r.keep.shape[0]
    d = r.x.shape[-1]
    tiles = r.w_up_.shape[0]
    left, right = greet_ring(step)
    ends = frame_ends()
    fetch = Fetch(r.fetch)
    first = [fetch.add(r.w_qkv, r.w_qkv_), fetch.add(r.w_out, r.w_out_)]
    later = [fetch_mlp(fetch, r, j) for j in range(tiles)]

    @on(step, 0)
    def _():
        fetch.start()
        fetch.wait(first[0])

    @pl.when(step < frames)
    def _():
        x = r.x[0].astype(F32)
        xhat, _ = norm(x)
        a = (xhat * r.ga[...]).astype(BF16)
        r.at[...] = a.T
        for start in range(0, 3 * d, 512):
            r.pk[:, start : start + 512] = mm(a, r.w_qkv_[:, start : start + 512]).astype(BF16)
        for lane in range(0, d, 128):
            cols = [slice(part * d + lane, part * d + lane + 128) for part in range(3)]
            r.att[:, cols[0]] = attend_both(*[r.pk[:, c] for c in cols], None)
        att = r.att[...]
        r.att_t[...] = att.T

        @on(step, 0)
        def _():
            fetch.wait(first[1])
            for pair in later:
                fetch.wait(*pair)

        mid = x + mm(att, r.w_out_[...])
        r.mid[...] = mid

        def put_bt(value):
            r.bt[...] = value

        def put(j, h, slope):
            for i in range(2):
                r.h[2 * j + i] = h[:, 256 * i : 256 * (i + 1)]
            r.gp[j] = slope

        y = mlp_up(mid, r.gb[...], r.w_up_, r.w_down_, put_bt, put).astype(BF16)
        r.y[0] = y
        r.keep[step] = y

    meet_ring(step)

    def copy(i):
        return ring_copy(r.keep.at[i], r.halo.at[i], r.send.at[i], r.recv.at[i], right)

    @pl.when((step < frames) & ends.not_last)
    def _():
        copy(step).start()

    def clear(i):
        return pltpu.make_async_copy(r.none, r.halo.at[i], r.recv.at[i])

    @pl.when((step == 0) & ends.is_first)
    def _():
        r.none[...] = jnp.zeros_like(r.none)
        for i in range(frames):
            clear(i).start()

    @on(step, frames)
    def _():
        codes = one_row(r.codes)
        cdim, count = r.book.shape
        major, onehot = code_masks(codes, count // 128)
        both = jnp.concatenate([onehot, onehot], 0)
        total = jnp.zeros(r.chosen.shape, F32)
        for first in range(0, count // 128, 8):
            book = jnp.concatenate([r.book[:, 128 * a : 128 * (a + 1)] for a in range(first, first + 8)], 0)
            found = mm(jnp.concatenate(split_parts(book, 2), 1), both)
            for i in range(8):
                total = total + jnp.where(major == first + i, found[cdim * i : cdim * (i + 1)], 0.0)
        r.chosen[...] = total

    @pl.when((step == frames) & ends.not_last)
    def _():
        for i in range(frames):
            copy(i).wait_send()

    @pl.when((step == frames) & ends.not_first)
    def _():
        for i in range(frames):
            copy(i).wait_recv()

    @pl.when((step == frames) & ends.is_first)
    def _():
        for i in range(frames):
            clear(i).wait()


def frame_ends():
    me, n = lax.axis_index("frame"), lax.axis_size("frame")
    return types.SimpleNamespace(
        is_first=me == 0, not_first=me > 0, is_last=me == n - 1, not_last=me < n - 1
    )


def spat_forward_call(x, weights, codes, book_t):
    frames, patches, d = x.shape
    hidden = weights[4].shape[1]
    n = frames * patches
    tiles = hidden // TILE
    at = part_of(0, frames)
    blk = pl.BlockSpec((1, patches, d), lambda i: (at(i), 0, 0))
    cols = pl.BlockSpec((d, patches), lambda i: (0, at(i)))
    rows = lambda width: pl.BlockSpec((patches, width), lambda i: (at(i), 0))
    tiled = lambda count, width: (
        shape_of((count, n, width), BF16), pl.BlockSpec((count, patches, width), lambda i: (0, at(i), 0))
    )
    ga, w_qkv, w_out, gb, w_up, w_down = weights
    wide = lambda width, dtype=BF16: (shape_of((n, width), dtype), rows(width))
    tall = (shape_of((d, n), BF16), cols)
    vmem = lambda array: pltpu.VMEM(array.shape, array.dtype)
    return launch(
        spat_forward_step, "spat_forward", frames + 1,
        dict(
            x=(x, blk), ga=fixed(ga), w_qkv=(w_qkv, ANY), w_out=(w_out, ANY), gb=fixed(gb), w_up=(w_up, ANY),
            w_down=(w_down, ANY), codes=fixed(codes), book=fixed(book_t),
        ),
        dict(
            y=(shape_of(x.shape, BF16), blk), at=tall, pk=wide(3 * d), att_t=tall, mid=wide(d, F32), bt=tall,
            h=tiled(hidden // 256, 256), gp=tiled(tiles, TILE), halo=(shape_of(x.shape, BF16), ANY),
            chosen=fixed_out((book_t.shape[0], n), F32),
        ),
        dict(
            att=pltpu.VMEM((patches, d), BF16), keep=pltpu.VMEM(x.shape, BF16), none=pltpu.VMEM((patches, d), BF16),
            send=pltpu.SemaphoreType.DMA((frames,)), recv=pltpu.SemaphoreType.DMA((frames,)),
            fetch=pltpu.SemaphoreType.DMA((2 + 2 * tiles,)), w_qkv_=vmem(w_qkv), w_out_=vmem(w_out),
            w_up_=pltpu.VMEM((tiles, d, TILE), BF16), w_down_=pltpu.VMEM((tiles, TILE, d), BF16),
        ),
        {}, 11, 2 * n * d * (4 * d + 2 * hidden + 2 * patches),
    )


class Fetch:
    def __init__(self, sem):
        self.sem, self.items = sem, []

    def add(self, src, dst):
        self.items.append((src, dst))
        return len(self.items) - 1

    def copy(self, i):
        return pltpu.make_async_copy(*self.items[i], self.sem.at[i])

    def start(self, first=0, stop=None):
        for i in range(len(self.items))[first:stop]:
            self.copy(i).start()

    def wait(self, *which):
        for i in which:
            self.copy(i).wait()


def mlp_tile(r, j, put_up, half_way=lambda: None):
    lead, per, d = r.db.shape
    for i in range(4):
        rows = slice(i * 256, (i + 1) * 256)
        these = slice(i * lead // 4, (i + 1) * lead // 4)
        dh = mm_t(r.dy[rows, :], r.w_down_[j])
        du = (r.gp_[j, rows, :].astype(F32) * dh).astype(BF16)
        r.du[rows, :] = du
        r.db[these] += mm_t(du, r.w_up_[j]).reshape(lead // 4, per, d)
        if i == 1:
            half_way()
    put_up(mm(r.bt_[...], r.du[...]).astype(BF16))


def down_tile(r, acc, j):
    for i in range(4):
        grad = mm(r.dyt[...], r.h_[4 * j + i]).astype(BF16)
        acc[2 * j + i // 2, i % 2] = grad.reshape(acc.shape[2:])


def mlp_up(mid, gain, w_up_, w_down_, put_bt, put):
    xhat, _ = norm(mid)
    b = (xhat * gain).astype(BF16)
    put_bt(b.T)
    out = mid
    for j in range(w_up_.shape[0]):
        u = mm(b, w_up_[j])
        u2 = u * u
        th = jnp.tanh(u * (GELU_C + (GELU_C * GELU_A) * u2))
        half = 0.5 + 0.5 * th
        h = (u * half).astype(BF16)
        slope = half + u * (half * (1.0 - th)) * (GELU_C + (3.0 * GELU_C * GELU_A) * u2)
        put(j, h, slope.astype(BF16))
        out = out + mm(h, w_down_[j])
    return out


def fetch_mlp(fetch, r, j):
    cols = pl.ds(j * TILE, TILE)
    return fetch.add(r.w_up.at[:, cols], r.w_up_.at[j]), fetch.add(r.w_down.at[cols, :], r.w_down_.at[j])


def middle(r, put):
    lead, per, d = r.db.shape
    for i in range(4):
        rows = slice(i * 256, (i + 1) * 256)
        these = slice(i * lead // 4, (i + 1) * lead // 4)
        xhat, rs = norm(r.mid_[rows, :])
        db = r.db[these].reshape(256, d)
        add_row(r.dg_b, db * xhat)
        dmid = r.dy[rows, :].astype(F32) + norm_back(db, xhat, rs, r.gb[...])
        r.db[these] = dmid.reshape(lead // 4, per, d)
        low = dmid.astype(BF16)
        put(i, low, mm_t(low, r.w_out_[...]).astype(BF16))


T_LOSS, T_MLP, T_MID, T_ATT, T_DOWN, T_GRAD = 4, 5, 9, 10, 12, 16


def temporal_forward(r, step, fetch, wait_first):
    frames, group, d = r.att.shape
    rows = frames * group
    lead = pl.ds(pl.multiple_of(frames * step, frames), frames)
    here = pl.ds(pl.multiple_of(rows * step, rows), rows)
    mine = pl.ds(pl.multiple_of(group * step, group), group)
    x = r.x[:, mine, :].reshape(rows, d).astype(F32)
    xhat, _ = norm(x)
    a = (xhat * r.ga[...]).astype(BF16)
    r.at_[:, here] = a.T
    for start in range(0, 3 * d, 512):
        part = mm(a, r.w_qkv_[:, start : start + 512]).astype(BF16)
        r.pk[lead, :, start : start + 512] = part.reshape(frames, group, 512)
    xhat_h, _ = norm(r.halo[:, mine, :].reshape(rows, d).astype(F32))
    ah = (xhat_h * r.ga[...]).astype(BF16)
    r.aht_[:, here] = ah.T
    for start in range(0, 2 * d, 512):
        part = mm(ah, r.w_qkv_[:, d + start : d + start + 512]).astype(BF16)
        r.kvh[lead, :, start : start + 512] = part.reshape(frames, group, 512)
    bias = jnp.concatenate([r.bias[...]] * 2, 0)
    for sub in range(0, group, SUB):
        near = slice(sub, sub + SUB)
        for lane in range(0, d, 128):
            c0, c1, c2 = (slice(part * d + lane, part * d + lane + 128) for part in range(3))
            q = r.pk[lead, near, c0].reshape(frames * SUB, 128)
            k = jnp.concatenate([r.kvh[lead, near, c0], r.pk[lead, near, c1]], 0).reshape(2 * frames * SUB, 128)
            v = jnp.concatenate([r.kvh[lead, near, c1], r.pk[lead, near, c2]], 0).reshape(2 * frames * SUB, 128)
            r.att[:, near, c0] = attend_both(q, k, v, bias).reshape(frames, SUB, 128)
    att = r.att[...].reshape(rows, d)
    r.att_t_[:, here] = att.T
    wait_first()
    mid = x + mm(att, r.w_out_[...])
    r.mid_[here, :] = mid

    def put_bt(value):
        r.bt_[:, here] = value

    def put(j, h, slope):
        for i in range(2):
            r.h_[2 * j + i, here, :] = h[:, 256 * i : 256 * (i + 1)]
        r.gp_[j, here, :] = slope

    r.x3[here, :] = mlp_up(mid, r.gb[...], r.w_up_, r.w_down_, put_bt, put).astype(BF16)


def temporal_step(r, m, place, step):
    frames, group, d = r.att.shape
    cdim, n = r.chosen.shape
    rows = frames * group
    ring = lax.axis_size("frame")
    me = lax.axis_index("frame")
    left, right = lax.rem(me + ring - 1, ring), lax.rem(me + 1, ring)
    ends = frame_ends()
    tiles = r.w_up_.shape[0]
    fetch = Fetch(r.fetch)
    first = [fetch.add(r.w_qkv, r.w_qkv_), fetch.add(r.w_out, r.w_out_)]
    later = [fetch_mlp(fetch, r, j) for j in range(tiles)]

    @on(step, 0)
    def _():
        place.greet()
        for peer in (left, right):
            pl.semaphore_signal(
                pltpu.get_barrier_semaphore(), inc=1, device_id={"frame": peer}, device_id_type=MESH
            )
        fetch.start()
        for ref in (r.dg_a, r.dg_b, r.db):
            ref[...] = jnp.zeros_like(ref)
        fetch.wait(first[0])

    @on(step, 0)
    def _():
        def wait_first():
            fetch.wait(first[1])
            for pair in later:
                fetch.wait(*pair)

        temporal_forward(r, 0, fetch, wait_first)

    @on(step, 1)
    def _():
        def one(i, carry):
            temporal_forward(r, i, fetch, lambda: None)
            return carry

        lax.fori_loop(1, r.lat.shape[2] // group, one, 0)

    @on(step, T_LOSS)
    def _():
        patches = r.lat.shape[2]
        commit = jnp.zeros((1, 1), F32)
        latent = mm_t(r.proj[...], r.x3[...])
        for f in range(frames):
            for g in range(patches // group):
                at = (g * frames + f) * group
                r.lat[f, :, g * group : (g + 1) * group] = latent[:, at : at + group]
            here = slice(f * patches, (f + 1) * patches)
            differ = r.lat[f] - r.chosen[:, here]
            commit = commit + jnp.sum(jnp.sum(differ * differ, 1, keepdims=True), 0, keepdims=True)
            grad = (r.cot[f] + (2.0 * BETA) * differ).astype(BF16)
            for g in range(patches // group):
                at = (g * frames + f) * group
                r.gl[:, at : at + group] = grad[:, g * group : (g + 1) * group]
            r.dbook[:, here] = ((-2.0 * BETA) * differ).astype(BF16)
        for i in range(4):
            part = slice(i * 256, (i + 1) * 256)
            r.dy[part, :] = t_mm(r.gl[:, part], r.proj[...]).astype(BF16)
        r.dyt[...] = t_mm(r.proj[...], r.gl[...]).astype(BF16)
        r.commit[...] = commit

    @within(step, T_MLP, 4)
    def _():
        j = step - T_MLP

        def put_up(value):
            r.a_acc[j // 2, j % 2] = value.reshape(r.a_acc.shape[2:])

        mlp_tile(r, j, put_up)

    @within(step, T_DOWN, 2)
    def _():
        down_tile(r, m.b.acc, step - T_DOWN)

    @on(step, T_MID)
    def _():
        def put(i, low, datt):
            for t in range(2):
                r.dm[t, 4 * i : 4 * i + 4] = low[:, 256 * t : 256 * (t + 1)].reshape(4, group, 256)
            r.datt[4 * i : 4 * i + 4] = datt.reshape(4, group, d)

        middle(r, put)

    s = att_step(step)
    attending = T_ATT <= step < T_DOWN or T_DOWN + 2 <= step < T_GRAD

    @on(int(attending), 1)
    def _():
        lead = pl.ds(frames * s, frames)
        bias = jnp.concatenate([r.bias_t[...]] * 2, 1)
        half = frames * SUB
        for sub in range(0, group, SUB):
            near = slice(sub, sub + SUB)
            for lane in range(0, d, 128):
                c0, c1, c2 = (slice(part * d + lane, part * d + lane + 128) for part in range(3))
                q = r.pk[lead, near, c0].reshape(half, 128)
                k = jnp.concatenate([r.kvh[lead, near, c0], r.pk[lead, near, c1]], 0).reshape(2 * half, 128)
                v = jnp.concatenate([r.kvh[lead, near, c1], r.pk[lead, near, c2]], 0).reshape(2 * half, 128)
                do = r.datt[lead, near, c0].reshape(half, 128)
                dq, dk, dv = attend_both_back(q, k, v, do, bias)
                tile, to = lane // 256, slice(lane % 256, lane % 256 + 128)
                for part, grad in enumerate((dq, dk[half:], dv[half:])):
                    r.dpk[2 * part + tile, lead, near, to] = grad.astype(BF16).reshape(frames, SUB, 128)
                for part, grad in enumerate((dk[:half], dv[:half])):
                    r.dkvh[2 * part + tile, lead, near, to] = grad.astype(BF16).reshape(frames, SUB, 128)
        dah = jnp.zeros((rows, d), F32)
        for i in range(4):
            dah = dah + mm_t(r.dkvh[i, lead].reshape(rows, 256), r.w_qkv_[:, d + 256 * i : d + 256 * (i + 1)])
        r.dah[s] = dah.astype(BF16).reshape(frames, group, d)
        da = jnp.zeros((rows, d), F32)
        for i in range(6):
            da = da + mm_t(r.dpk[i, lead].reshape(rows, 256), r.w_qkv_[:, 256 * i : 256 * (i + 1)])
        xhat, rs = norm(r.x[:, s * group : (s + 1) * group, :].reshape(rows, d).astype(F32))
        add_row(r.dg_a, da * xhat)
        dmid = r.db[lead].reshape(rows, d)
        r.base[:, s * group : (s + 1) * group, :] = (dmid + norm_back(da, xhat, rs, r.ga[...])).reshape(
            frames, group, d
        )

    def copy(i):
        there = r.back.at[:, pl.ds(i * group, group), :]
        return ring_copy(r.dah.at[i], there, r.send.at[i], r.recv.at[i], left)

    def clear(i):
        return pltpu.make_async_copy(r.none, r.back.at[:, pl.ds(i * group, group), :], r.recv.at[i])

    @on(step, T_GRAD)
    def _():
        codes = one_row(r.codes)
        major, onehot = code_masks(codes, 64)
        dbook = r.dbook[...]
        dproj = mm(r.gl[...], r.x3[...]).astype(BF16)
        part = cdim // 4
        for z in range(4):
            for x in range(2):
                f = 2 * z + x
                picked = [jnp.where(major == 8 * f + i, dbook, jnp.zeros((), BF16)) for i in range(8)]
                book = mm_t(jnp.concatenate(picked, 0), onehot).astype(BF16)
                r.d_part[z, x, :, :, : 2 * cdim] = book.reshape(2, 2, 2 * cdim, 128)
                r.d_part[z, x, :, :, 2 * cdim :] = jnp.zeros((2, 2, 16, 128), BF16)
                for q in range(4):
                    r.d_part[z, x, q // 2, q % 2, 2 * cdim : 2 * cdim + part, :64] = dproj[
                        part * q : part * (q + 1), 64 * f : 64 * (f + 1)
                    ]
        dead = r.dead.shape[1]
        used = jnp.where(as_column(r.dead[...]) == codes.astype(F32), 1.0, 0.0).astype(BF16)
        usage = mm_t(jnp.ones((8, n), BF16), used)
        places = lax.broadcasted_iota(jnp.int32, (dead, n), 1).astype(F32)
        pick = jnp.where(as_column(r.source[...]) == places, 1.0, 0.0).astype(BF16)
        latent = jnp.concatenate([r.lat[f] for f in range(frames)], 1)
        candidate = jnp.zeros((cdim, dead), F32)
        for one in split_parts(latent, 3):
            candidate = candidate + mm_t(one, pick)
        r.q_part[...] = jnp.zeros_like(r.q_part)
        r.q_part[:cdim, :dead] = candidate
        r.q_part[cdim:, :dead] = usage
        r.q_part[cdim:, dead:] = jnp.broadcast_to(r.commit[...], (8, 128 - dead))

    @within(step, T_GRAD, 2)
    def _():
        t = step - T_GRAD
        whole_rows = lambda value: value.reshape(n, 256)
        a, ah, att = r.at_[...], r.aht_[...], r.att_t_[...]
        parts = (
            mm(a, whole_rows(r.dpk[t])),
            mm(a, whole_rows(r.dpk[2 + t])) + mm(ah, whole_rows(r.dkvh[t])),
            mm(a, whole_rows(r.dpk[4 + t])) + mm(ah, whole_rows(r.dkvh[2 + t])),
            mm(att, whole_rows(r.dm[t])),
        )
        for kind, part in enumerate(parts):
            part = part.astype(BF16)
            for j in range(2):
                r.t_att[t, j, :, :, :, 128 * kind : 128 * (kind + 1)] = part[:, 128 * j : 128 * (j + 1)].reshape(
                    r.t_att.shape[2:5] + (128,)
                )

    @on(step, 0)
    def _():
        pl.semaphore_wait(pltpu.get_barrier_semaphore(), len(PEERS) + 2)

    @on(step, 0)
    def _():
        @pl.when(ends.is_last)
        def _():
            r.none[...] = jnp.zeros_like(r.none)
            for i in range(r.dah.shape[0]):
                clear(i).start()

    @on(int(attending), 1)
    def _():
        @pl.when(ends.not_first)
        def _():
            copy(s).start()

    @on(step, T_MLP + 1)
    def _():
        m.a0.start(0)

    @on(step, T_MLP + 2)
    def _():
        m.a0.move(0)

    @on(step, T_MLP + 3)
    def _():
        m.a1.start(0)

    @on(step, T_MID)
    def _():
        m.a1.move(0)

    @on(step, T_DOWN + 1)
    def _():
        m.b.start(0)

    @on(step, T_DOWN + 2)
    def _():
        m.b.move(0)

    @on(step, T_GRAD + 1)
    def _():
        for part in (m.a0, m.a1, m.b):
            part.finish(1)
        r.a_part[0] = m.a0.piece()
        r.a_part[1] = m.a1.piece()
        r.b_part[...] = m.b.piece()

        @pl.when(ends.not_first)
        def _():
            for i in range(r.dah.shape[0]):
                copy(i).wait_send()

        @pl.when(ends.not_last)
        def _():
            for i in range(r.dah.shape[0]):
                copy(i).wait_recv()

        @pl.when(ends.is_last)
        def _():
            for i in range(r.dah.shape[0]):
                clear(i).wait()


def att_step(step):
    return min(max(step - T_ATT, 0), 1) + min(max(step - T_DOWN - 1, 0), 2)


def temporal_call(x, halo, bias, cot_t, chosen, codes, dead, source, proj_t, weights):
    frames, patches, d = x.shape
    ga, w_qkv, w_out, gb, w_up, w_down = weights
    hidden = w_up.shape[1]
    n = frames * patches
    cdim = proj_t.shape[0]
    groups = patches // GROUP
    lead, tiles = frames * groups, hidden // TILE
    half_tail, col_tail, book_tail = (d // 16, TILE), (d // 4, hidden // 8), (2 * cdim + 16, 128)
    vmem = lambda array: pltpu.VMEM(array.shape, array.dtype)
    low = lambda *shape: pltpu.VMEM(shape, BF16)
    moves = dict(
        a0=Sum(E_DIMS, half_tail, ("c", "y"), shared=lambda r: r.a_acc, fixed={"u": 0}, gather=False),
        a1=Sum(E_DIMS, half_tail, ("c", "y"), shared=lambda r: r.a_acc, fixed={"u": 1}, gather=False),
        b=Sum(COLS_DIMS, col_tail, ("c", "y"), gather=False),
    )
    return launch(
        temporal_step, "temporal", T_GRAD + 2,
        dict(
            x=fixed(x), halo=fixed(halo), bias=fixed(bias), bias_t=fixed(bias.T),
            cot=fixed(cot_t), chosen=fixed(chosen), codes=fixed(codes), dead=fixed(dead), source=fixed(source),
            proj=fixed(proj_t), ga=fixed(ga), gb=fixed(gb), w_qkv=(w_qkv, ANY), w_out=(w_out, ANY), w_up=(w_up, ANY),
            w_down=(w_down, ANY),
        ),
        dict(
            lat=fixed_out((frames, cdim, patches), F32), base=fixed_out(x.shape, F32),
            back=(shape_of(x.shape, BF16), ANY), dg_a=fixed_out((1, d), F32), dg_b=fixed_out((1, d), F32),
            t_att=fixed_out((2, 2, 4, 2, d // 8, d), BF16),
            a_part=fixed_out((2, 4, 2) + half_tail, BF16),
            b_part=fixed_out((4, 2) + col_tail, BF16), d_part=fixed_out((4, 2, 2, 2) + book_tail, BF16),
            q_part=fixed_out((cdim + 8, 128), F32),
        ),
        dict(
            commit=pltpu.VMEM((1, 1), F32), gl=low(cdim, n), dbook=low(cdim, n), dy=low(n, d), dyt=low(d, n),
            du=low(n, TILE), db=pltpu.VMEM((lead, GROUP, d), F32), dm=low(2, lead, GROUP, 256),
            datt=low(lead, GROUP, d), dpk=low(6, lead, GROUP, 256), dkvh=low(4, lead, GROUP, 256),
            a_acc=low(2, 2, 4, 2, 2, *half_tail), dah=low(groups, frames, GROUP, d), none=low(frames, GROUP, d),
            send=pltpu.SemaphoreType.DMA((groups,)), recv=pltpu.SemaphoreType.DMA((groups,)),
            fetch=pltpu.SemaphoreType.DMA((2 + 2 * tiles,)), w_qkv_=vmem(w_qkv), w_out_=vmem(w_out),
            w_up_=low(tiles, d, TILE), w_down_=low(tiles, TILE, d), att=low(frames, GROUP, d),
            pk=low(lead, GROUP, 3 * d), kvh=low(lead, GROUP, 2 * d), at_=low(d, n), aht_=low(d, n), att_t_=low(d, n),
            bt_=low(d, n), mid_=pltpu.VMEM((n, d), F32), h_=low(hidden // 256, n, 256), gp_=low(tiles, n, TILE),
            x3=low(n, d),
        ),
        moves, 12, 6 * n * d * (6 * d + 2 * hidden) + 14 * n * d * patches, TAIL_BYTES, True,
    )


S_DOWN, S_MLP, S_MID, S_ATT, S_END = 1, 3, 7, 8, 12


def spat_backward_step(r, m, place, step):
    frames, patches, d = r.db.shape
    n = frames * patches
    tiles = r.w_up_.shape[0]
    fetch = Fetch(r.fetch)
    by_frame = [
        [fetch.add(a.at[f], b.at[f]) for a, b in ((r.base, r.base_), (r.dah, r.dah_), (r.x2, r.x2_))]
        for f in range(frames)
    ]
    h_tiles = [fetch.add(r.h.at[i], r.h_.at[i]) for i in range(r.h_.shape[0])]
    bt = fetch.add(r.bt, r.bt_)
    mlp = [(*fetch_mlp(fetch, r, j), fetch.add(r.gp.at[j], r.gp_.at[j])) for j in range(tiles)]
    mid, w_out, att_t = fetch.add(r.mid, r.mid_), fetch.add(r.w_out, r.w_out_), fetch.add(r.att_t, r.att_t_)
    pk, at, w_qkv, x = (
        fetch.add(a, b) for a, b in ((r.pk, r.pk_), (r.at, r.at_), (r.w_qkv, r.w_qkv_), (r.x, r.x_))
    )

    def transfers(point):
        start = lambda k, *parts: [part.start(k) for part in parts]
        move = lambda k, *parts: [part.move(k) for part in parts]
        finish = lambda k, *parts: [part.finish(k) for part in parts]
        gather = lambda *parts: [part.gather() for part in parts]
        spread = lambda *parts: [part.spread() for part in parts]
        todo = (
            ((start, 0, m.c, m.d, m.b, m.a0, m.q, m.a1),),
            ((move, 0, m.q),),
            ((start, 0, m.g), (move, 0, m.d),),
            ((move, 1, m.q),),
            ((move, 0, m.c), (move, 2, m.q), (move, 0, m.g),),
            ((finish, 3, m.q),),
            ((start, 0, m.e0), (move, 1, m.d),),
            ((move, 0, m.a0, m.a1),),
            ((move, 0, m.e0),),
            (),
            ((start, 0, m.e1),),
            ((move, 2, m.d), (move, 0, m.b, m.e1), (gather, m.a0, m.a1),),
            (),
            ((move, 1, m.c), (gather, m.d), (spread, m.a0, m.a1),),
            ((move, 1, m.g),),
            ((start, 0, m.h0a, m.h0b), (spread, m.d), (gather, m.b), (move, 1, m.e0),),
            ((move, 2, m.c), (move, 0, m.h0a, m.h0b),),
            ((spread, m.b), (move, 1, m.e1), (move, 2, m.e0),),
            ((move, 1, m.h0b),),
            ((start, 0, m.h1b, m.h1a), (move, 1, m.h0a), (move, 2, m.e1, m.g),),
            ((move, 0, m.h1b, m.h1a), (gather, m.c)),
            ((move, 2, m.h0b, m.h0a),),
            ((gather, m.e0),),
            ((start, 0, m.w), (move, 1, m.h1b, m.h1a)),
            (
                (move, 0, m.w), (spread, m.c, m.e0), (gather, m.e1), (move, 1, m.w), (gather, m.h0a, m.h0b),
                (move, 2, m.h1b, m.h1a), (move, 2, m.w), (spread, m.e1), (gather, m.g), (gather, m.h1b, m.h1a),
                (spread, m.g), (finish, 3, m.w),
            ),
        )
        for what, *args in todo[point]:
            what(*args)

    @on(step, 0)
    def _():
        place.greet()
        fetch.start(0, 3 * frames)
        m.q.acc[...] = r.q_part[...]
        pl.semaphore_wait(pltpu.get_barrier_semaphore(), len(PEERS))
        transfers(0)
        fetch.start(3 * frames)
        for ref in (r.dg_t, r.dg_a, r.dg_b, r.db):
            ref[...] = jnp.zeros_like(ref)
        for f in range(frames):
            fetch.wait(*by_frame[f])
            xhat, rs = norm(r.x2_[f].astype(F32))
            dah = r.dah_[f].astype(F32)
            add_row(r.dg_t, dah * xhat)
            low = (r.base_[f] + norm_back(dah, xhat, rs, r.gta[...])).astype(BF16)
            here = slice(f * patches, (f + 1) * patches)
            r.dy[here, :] = low
            r.dyt[:, here] = low.T
    for j in range(2):

        @on(step, S_DOWN + j)
        def _(j=j):
            fetch.wait(*h_tiles[4 * j : 4 * j + 4])

    @on(step, S_MLP)
    def _():
        fetch.wait(bt)

    for j in range(tiles):

        @on(step, S_MLP + j)
        def _(j=j):
            fetch.wait(*mlp[j])

    @within(step, S_MLP, 4)
    def _():
        j = step - S_MLP

        def put_up(value):
            r.e_acc[j // 2, j % 2] = value.reshape(r.e_acc.shape[2:])

        mlp_tile(r, j, put_up, lambda: transfers(3 + 2 * j))
        transfers(4 + 2 * j)

    @within(step, S_DOWN, 2)
    def _():
        down_tile(r, m.g.acc, step - S_DOWN)
        transfers(1 + step - S_DOWN)

    @on(step, S_MID)
    def _():
        fetch.wait(mid, w_out)

        def put(i, low, datt):
            rows = slice(i * 256, (i + 1) * 256)
            r.dm[rows, :] = low
            for p in range(d // 128):
                r.datt[p, rows, :] = datt[:, 128 * p : 128 * (p + 1)]

        middle(r, put)
        fetch.wait(att_t)
        grad = mm(r.att_t_[...], r.dm[...]).astype(BF16)
        for q in range(4):
            r.h_acc[q // 2, 1, q % 2, :, :, :, :, 128:] = grad[:, 128 * q : 128 * (q + 1)].reshape(
                r.h_acc.shape[3:7] + (128,)
            )
        fetch.wait(pk, at, w_qkv)
        transfers(11)

    @within(step, S_ATT, 4)
    def _():
        p = step - S_ATT
        cols = [slice(part * d + 128 * p, part * d + 128 * (p + 1)) for part in range(3)]
        for f in range(frames):
            here = slice(f * patches, (f + 1) * patches)
            grads = attend_both_back(*[r.pk_[here, c] for c in cols], r.datt[p, here, :], None)
            for part, grad in enumerate(grads):
                r.dpk[here, cols[part]] = grad.astype(BF16)
            if f == 1:
                transfers(12 + 2 * p)
        grad = mm(r.at_[...], jnp.concatenate([r.dpk[:, c] for c in cols], 1)).astype(BF16)
        u, c = p // 2, p % 2
        shape = r.h_acc.shape[3:7]
        r.h_acc[u, 0, c] = grad[:, :256].reshape(shape + (256,))
        r.h_acc[u, 1, c, :, :, :, :, :128] = grad[:, 256:].reshape(shape + (128,))
        transfers(13 + 2 * p)

    @on(step, S_END)
    def _():
        fetch.wait(x)
        for f in range(frames):
            rows = slice(f * patches, (f + 1) * patches)
            da = mm_t(r.dpk[rows, :], r.w_qkv_[...])
            xhat, rs = norm(r.x_[f].astype(F32))
            add_row(r.dg_a, da * xhat)
            r.dx[f] = (r.db[f] + norm_back(da, xhat, rs, r.ga[...])).astype(BF16)
            if f < frames - 1:
                transfers(20 + f)
        gains = (r.dg_t[...] + r.dgt_own[...], r.dgt_mid[...], r.dg_a[...], r.dg_b[...])
        for i, gain in enumerate(gains):
            for j in range(d // 128):
                row = i * (d // 128) + j
                m.w.acc[row : row + 1, :] = gain[:, 128 * j : 128 * (j + 1)]
        transfers(23)

    @on(step, S_END + 1)
    def _():
        transfers(24)
        outs = (
            (m.a0, r.a0_all), (m.a1, r.a1_all), (m.b, r.b_all), (m.c, r.c_all), (m.d, r.d_all), (m.e0, r.e0_all),
            (m.e1, r.e1_all), (m.g, r.g_all), (m.h0a, r.h00_all), (m.h0b, r.h01_all), (m.h1a, r.h10_all),
            (m.h1b, r.h11_all),
        )
        for part, out in outs:
            part.gathered(out)
        r.w_all[...] = m.w.acc[...]
        r.q_all[...] = m.q.acc[...]


def spat_backward_call(f, t, x2, gta, x, weights):
    frames, patches, d = x.shape
    ga, w_qkv, w_out, gb, w_up, w_down = weights
    hidden = w_up.shape[1]
    n = frames * patches
    tiles = hidden // TILE
    col_tail = (d // 4, hidden // 8)
    half_tail, quarter_tail = (d // 16, TILE), (d // 16, 256)
    e_acc, h_acc = (lambda r: r.e_acc), (lambda r: r.h_acc)
    vmem = lambda array: pltpu.VMEM(array.shape, array.dtype)
    moves = dict(
        b=Sum(("z", "x"), col_tail, ("x", "z"), source=lambda r: r.b_part),
        a0=Sum(("u", "z", "x"), half_tail, ("x", "z"), source=lambda r: r.a_part, fixed={"u": 0}),
        a1=Sum(("u", "z", "x"), half_tail, ("x", "z"), source=lambda r: r.a_part, fixed={"u": 1}),
        c=Sum(ROWS_DIMS, (d // 8, d), Y_FIRST, source=lambda r: r.t_att),
        e0=Sum(E_DIMS, half_tail, Y_FIRST, shared=e_acc, fixed={"u": 0}),
        e1=Sum(E_DIMS, half_tail, Y_FIRST, shared=e_acc, fixed={"u": 1}),
        g=Sum(COLS_DIMS, col_tail, X_FIRST),
        h0a=Sum(H_DIMS, quarter_tail, Y_FIRST, shared=h_acc, fixed={"u": 0, "w": 0}, direct=True),
        h0b=Sum(H_DIMS, quarter_tail, X_FIRST, shared=h_acc, fixed={"u": 0, "w": 1}, direct=True),
        h1a=Sum(H_DIMS, quarter_tail, Y_FIRST, shared=h_acc, fixed={"u": 1, "w": 0}, direct=True),
        h1b=Sum(H_DIMS, quarter_tail, X_FIRST, shared=h_acc, fixed={"u": 1, "w": 1}, direct=True),
        d=Sum(COLS_DIMS, t.d_part.shape[4:], Y_FIRST, source=lambda r: r.d_part), q=Total(t.q_part.shape[0]),
        w=Total(4 * d // 128),
    )
    pieces = lambda tail: fixed_out((2, 2) + tail, BF16)
    return launch(
        spat_backward_step, "spat_backward", 14,
        dict(
            base=(t.base, ANY), dah=(t.back, ANY), x2=(x2, ANY), gta=fixed(gta), x=(x, ANY), gp=(f.gp, ANY), h=(f.h, ANY),
            pk=(f.pk, ANY), w_qkv=(w_qkv, ANY), ga=fixed(ga), gb=fixed(gb), w_up=(w_up, ANY), w_down=(w_down, ANY),
            dgt_own=fixed(t.dg_a), dgt_mid=fixed(t.dg_b), bt=(f.bt, ANY), mid=(f.mid, ANY), w_out=(w_out, ANY),
            att_t=(f.att_t, ANY), at=(f.at, ANY), a_part=(t.a_part, ANY), b_part=(t.b_part, ANY), t_att=(t.t_att, ANY),
            d_part=(t.d_part, ANY), q_part=fixed(t.q_part),
        ),
        dict(
            dx=fixed_out(x.shape, BF16), a0_all=pieces(half_tail), a1_all=pieces(half_tail), b_all=pieces(col_tail), c_all=pieces((d // 8, d)),
            e0_all=pieces(half_tail), e1_all=pieces(half_tail), g_all=pieces(col_tail), h00_all=pieces(quarter_tail),
            h01_all=pieces(quarter_tail), h10_all=pieces(quarter_tail), h11_all=pieces(quarter_tail),
            w_all=fixed_out((4 * d // 128, 128), F32), q_all=fixed_out(t.q_part.shape, F32),
            d_all=pieces(t.d_part.shape[4:]),
        ),
        dict(
            dg_t=pltpu.VMEM((1, d), F32), dg_a=pltpu.VMEM((1, d), F32), dg_b=pltpu.VMEM((1, d), F32),
            dy=pltpu.VMEM((n, d), BF16), dyt=pltpu.VMEM((d, n), BF16), du=pltpu.VMEM((n, TILE), BF16),
            db=pltpu.VMEM(x.shape, F32), dm=pltpu.VMEM((n, d), BF16),
            datt=pltpu.VMEM((d // 128, n, 128), BF16), dpk=pltpu.VMEM((n, 3 * d), BF16),
            e_acc=pltpu.VMEM((2, 2, 4, 2, 2) + half_tail, BF16), h_acc=pltpu.VMEM((2, 2, 2, 4, 2, 2) + quarter_tail, BF16),
            fetch=pltpu.SemaphoreType.DMA((3 * frames + 3 * tiles + hidden // 256 + 8,)), bt_=vmem(f.bt), mid_=vmem(f.mid),
            w_out_=vmem(w_out), att_t_=vmem(f.att_t), at_=vmem(f.at), x_=vmem(x), base_=vmem(t.base), dah_=vmem(t.back),
            x2_=vmem(x2), h_=vmem(f.h), gp_=vmem(f.gp), pk_=vmem(f.pk), w_qkv_=vmem(w_qkv),
            w_up_=pltpu.VMEM((tiles, d, TILE), BF16), w_down_=pltpu.VMEM((tiles, TILE, d), BF16),
        ),
        moves, 13, 4 * n * d * (4 * d + 2 * hidden) + 10 * n * d * patches, TAIL_BYTES, True,
    )


def finish_step(r, m, place, step):
    d = r.t_out.shape[1]
    half = d // 16
    for y in range(2):
        for c in range(2):
            q = 2 * y + c
            lanes = slice(128 * q, 128 * (q + 1))
            r.t_down[:, lanes] = r.b_all[y, c].astype(F32).T
            r.s_down[:, lanes] = r.g_all[y, c].astype(F32).T
            value = r.c_all[y, c].astype(F32)
            for kind in range(3):
                r.t_qkv[:, d * kind + 128 * q : d * kind + 128 * (q + 1)] = value[:, 128 * kind : 128 * (kind + 1)]
            r.t_out[:, lanes] = value[:, 384:]
            book = r.d_all[y, c].astype(F32)
            cdim = r.book.shape[0]
            r.proj_grad[cdim // 4 * q : cdim // 4 * (q + 1), :] = book[2 * cdim : 2 * cdim + cdim // 4, :64]
            for i in range(2):
                r.book_grad[:, 128 * (2 * q + i) : 128 * (2 * q + i + 1)] = book[cdim * i : cdim * (i + 1)]
            rows = slice(half * y, half * (y + 1))
            for u, t_up, up, left, right in (
                (0, r.a0_all, r.e0_all, r.h00_all, r.h01_all), (1, r.a1_all, r.e1_all, r.h10_all, r.h11_all)
            ):
                at = 2 * u + c
                r.t_up[rows, TILE * at : TILE * (at + 1)] = t_up[y, c].astype(F32)
                r.s_up[rows, TILE * at : TILE * (at + 1)] = up[y, c].astype(F32)
                pair, other = left[y, c].astype(F32), right[y, c].astype(F32)
                for kind, part in enumerate((pair[:, :128], pair[:, 128:], other[:, :128])):
                    r.s_qkv[rows, d * kind + 128 * at : d * kind + 128 * (at + 1)] = part
                r.s_out[rows, 128 * at : 128 * (at + 1)] = other[:, 128:]
    for i, gain in enumerate((r.g_ta, r.g_tb, r.g_sa, r.g_sb)):
        for j in range(d // 128):
            row = i * (d // 128) + j
            gain[:, 128 * j : 128 * (j + 1)] = r.w_all[row : row + 1, :]
    dead = r.dead_row.shape[1]
    candidate = r.q_all[:cdim, :dead]
    low = r.q_all[cdim : cdim + 1, :dead] < USE_MIN
    r.commit[...] = r.q_all[cdim : cdim + 1, dead : dead + 1] * (1.0 / r.scale)
    major = lax.div(r.dead_row[...], 128)
    minor = as_column(lax.rem(r.dead_row[...], 128))
    lanes = lax.broadcasted_iota(jnp.int32, (dead, 128), 1).astype(F32)
    onehot = jnp.where(lanes == minor, 1.0, 0.0).astype(BF16)
    parts = split_parts(jnp.where(low, candidate, 0.0), 3)
    count = r.book.shape[1] // 128
    a_rows = lax.broadcasted_iota(jnp.int32, (count, dead), 0)
    replaced = mm(jnp.where((major == a_rows) & low, 1.0, 0.0).astype(BF16), onehot)
    for begin in range(0, count, 8):
        fresh = jnp.zeros((8 * cdim, 128), F32)
        for part in parts:
            chosen = [jnp.where(major == begin + i, part, jnp.zeros((), BF16)) for i in range(8)]
            fresh = fresh + mm(jnp.concatenate(chosen, 0), onehot)
        for i in range(8):
            at = begin + i
            lanes = slice(128 * at, 128 * (at + 1))
            r.refreshed[:, lanes] = jnp.where(
                replaced[at : at + 1] > 0.5, fresh[cdim * i : cdim * (i + 1)], r.book[:, lanes]
            )


def finish_call(t, s, book_t, dead, total, d, hidden):
    cdim, codes = book_t.shape
    piece = d // 8
    ins = dict(
        a0_all=s.a0_all, a1_all=s.a1_all, b_all=s.b_all, c_all=s.c_all, d_all=s.d_all, e0_all=s.e0_all, e1_all=s.e1_all, g_all=s.g_all,
        h00_all=s.h00_all, h01_all=s.h01_all, h10_all=s.h10_all, h11_all=s.h11_all, w_all=s.w_all, q_all=s.q_all,
        book=book_t, dead_row=dead.reshape(1, -1),
    )
    outs = dict(
        t_up=(piece, hidden), t_down=(hidden // 8, d), t_qkv=(piece, 3 * d), t_out=(piece, d),
        s_up=(piece, hidden), s_down=(hidden // 8, d), s_qkv=(piece, 3 * d), s_out=(piece, d),
        g_ta=(1, d), g_tb=(1, d), g_sa=(1, d), g_sb=(1, d), proj_grad=(cdim, piece), commit=(1, 1),
        book_grad=(cdim, codes // 8), refreshed=(cdim, codes),
    )

    def body(r, m, place, step):
        r.scale = total
        finish_step(r, m, place, step)

    return launch(
        body, "finish", 1, {k: fixed(v) for k, v in ins.items()}, {k: fixed_out(v, F32) for k, v in outs.items()},
        {}, {}, None, 1 << 28,
    )


def frame_bias(clip_row, frame_count):
    first = lax.axis_index("frame") * frame_count
    clips = jnp.concatenate([jnp.full((SPAN,), -1, jnp.int32), clip_row])
    key_clips = lax.dynamic_slice_in_dim(clips, first, SPAN + frame_count)
    qi, qp = jnp.arange(frame_count * SUB) // SUB, jnp.arange(frame_count * SUB) % SUB
    kj, kp = jnp.arange((SPAN + frame_count) * SUB) // SUB, jnp.arange((SPAN + frame_count) * SUB) % SUB
    offset = qi[:, None] + SPAN - kj[None, :]
    allowed = (
        (qp[:, None] == kp[None, :]) & (offset >= 0) & (offset <= SPAN)
        & (jnp.repeat(key_clips[SPAN:], SUB)[:, None] == jnp.repeat(key_clips, SUB)[None, :])
    )
    return jnp.where(allowed, 0.0, NEG).astype(F32)


def local_fused(
    frames_in, spat_gain_a, spat_qkv, spat_out, spat_gain_b, spat_up, spat_down,
    temp_gain_a, temp_qkv, temp_out, temp_gain_b, temp_up, temp_down,
    quant_proj, codebook, code_index, clip_index, dead_codes, source_rows, latent_cot,
):
    frame_count, patches, d = frames_in.shape[1:]
    cdim = quant_proj.shape[1]
    row_count = frame_count * patches
    frame_size, batch_size = lax.axis_size("frame"), lax.axis_size("batch")
    assert frame_count == SPAN
    spat = (spat_gain_a.reshape(1, d), spat_qkv, spat_out, spat_gain_b.reshape(1, d), spat_up, spat_down)
    temp = (temp_gain_a.reshape(1, d), temp_qkv, temp_out, temp_gain_b.reshape(1, d), temp_up, temp_down)
    x = frames_in[0]
    codes = code_index[0]
    book_t, proj_t = codebook.T, quant_proj.T
    bias = frame_bias(clip_index[0], frame_count)
    row_base = (lax.axis_index("batch") * frame_size + lax.axis_index("frame")) * row_count
    sf = spat_forward_call(x, spat, codes, book_t)
    tb = temporal_call(
        sf.y, sf.halo, bias, latent_cot[0].transpose(0, 2, 1), sf.chosen, codes, dead_codes.reshape(1, -1),
        (source_rows - row_base).reshape(1, -1), proj_t, temp,
    )
    sb = spat_backward_call(sf, tb, sf.y, temp[0], x, spat)
    out = finish_call(
        tb, sb, book_t, dead_codes, frame_size * batch_size * row_count * cdim, d, spat_up.shape[1]
    )
    return (
        tb.lat.transpose(0, 2, 1)[None], out.commit[0, 0], sb.dx[None],
        out.g_sa[0], out.s_qkv, out.s_out, out.g_sb[0], out.s_up, out.s_down,
        out.g_ta[0], out.t_qkv, out.t_out, out.g_tb[0], out.t_up, out.t_down,
        out.proj_grad.T, out.book_grad.T, out.refreshed.T,
    )


def solution(mesh):
    fused = (mesh.shape["frame"], mesh.shape["batch"]) == (8, 4)
    return jax.shard_map(
        local_fused if fused else local_general,
        mesh=mesh,
        in_specs=(
            P("batch", "frame", None, None),
            *([P()] * 14),
            P("batch", "frame", None),
            P("batch", None),
            P(),
            P(),
            P("batch", "frame", None, None),
        ),
        out_specs=(
            P("batch", "frame", None, None),
            P(),
            P("batch", "frame", None, None),
            P(),
            P("frame", None),
            P("frame", None),
            P(),
            P("frame", None),
            P("frame", None),
            P(),
            P("frame", None),
            P("frame", None),
            P(),
            P("frame", None),
            P("frame", None),
            P("frame", None),
            P("frame", None),
            P(),
        ),
        check_vma=False,
    )
```
